32 devices in a mesh: rep: 8 (over y, x, core), shard: 4 (over z).
Axes of the slice: x: 2, y: 2, z: 4, core: 2. Of those that a mesh axis runs over, the one named last changes fastest.
Arguments:
- tokens: bfloat16 [3, 4096, 1472], P(None, ('rep', 'shard')), may hold values from -6 to 6
- cotangent: bfloat16 [3, 4096, 1472], P(None, ('rep', 'shard')), may hold values from -6 to 6
- gate_cotangent: bfloat16 [3, 4096], P(None, ('rep', 'shard')), may hold values from -6 to 6
- slot_of: int32 [3, 8, 512], P(None, 'rep'), may hold values from 0 to 511, as said below
- seq_lengths: int32 [3, 8, 2], P(None, 'rep'), may hold values from 256 to 256, as said below
- buckets: int32 [1023], replicated, may hold values from 0 to 31
- gain_attn: bfloat16 [1472], P('shard'), may hold values from 0.099609375 to 1.8984375
- w_query: bfloat16 [1472, 384], P('shard'), may hold values from -0.078125 to 0.078125
- w_key: bfloat16 [1472, 384], P('shard'), may hold values from -0.078125 to 0.078125
- w_value: bfloat16 [1472, 384], P('shard'), may hold values from -0.15625 to 0.15625
- w_out: bfloat16 [384, 1472], P('shard'), may hold values from -1.75 to 1.75
- rel_bias: bfloat16 [32, 6], P('shard'), may hold values from -4 to 4
- gain_ffn: bfloat16 [1472], P('shard'), may hold values from 0.099609375 to 1.8984375
- w_gate: bfloat16 [1472, 3584], P('shard'), may hold values from -0.15625 to 0.15625
- w_up: bfloat16 [1472, 3584], P('shard'), may hold values from -0.15625 to 0.15625
- w_down: bfloat16 [3584, 1472], P('shard'), may hold values from -0.09375 to 0.09375
- gain_delete: bfloat16 [1472], P('shard'), may hold values from 0.099609375 to 1.8984375
- w_delete: bfloat16 [1472], P('shard'), may hold values from -0.15625 to 0.15625
Outputs:
- states: float32 [3, 4096, 1472], P(None, ('rep', 'shard'))
- delete_gate: float32 [3, 4096], P(None, ('rep', 'shard'))
- grad_tokens: bfloat16 [3, 4096, 1472], P(None, ('rep', 'shard'))
- grad_gain_attn: float32 [1472], P('shard')
- grad_w_query: float32 [1472, 384], P('shard')
- grad_w_key: float32 [1472, 384], P('shard')
- grad_w_value: float32 [1472, 384], P('shard')
- grad_w_out: float32 [384, 1472], P('shard')
- grad_rel_bias: float32 [32, 6], P('shard')
- grad_gain_ffn: float32 [1472], P('shard')
- grad_w_gate: float32 [1472, 3584], P('shard')
- grad_w_up: float32 [1472, 3584], P('shard')
- grad_w_down: float32 [3584, 1472], P('shard')
- grad_gain_delete: float32 [1472], P('shard')
- grad_w_delete: float32 [1472], P('shard')
The draws below stay inside these ranges and needn't reach their ends.
Inputs may be any that keep to these rules, and one draw needn't show every extreme that they name: `slot_of`: each row is a permutation of the 512 slots of a group; of the 128 tokens that arrive on one device, exactly 32 have slots in each block of 128 consecutive slots. `seq_lengths`: the two lengths of a group sum to 512; the first sequence takes the first slots.
All inputs are finite; a program needn't handle non-finite values.
Results may differ from the reference program's by a relative error of at most 0.02.
Values may be sent and summed in bfloat16 or wider, within the bound.
No kernel may reach another device: no remote copies, remote signals or barrier semaphores. Data moves between devices by JAX's collectives and lax.ppermute only.
A program may use at most 256 MiB of HBM per device.

```python
import jax
import jax.numpy as jnp
from jax import lax

D = 1472
H = 6
DK = 64
HD = 384
FF = 3584
NB = 32
TOK_DEV = 128
MICRO = 3
MINLEN = 256
GROUP = 512
TOKENS = 4096
OFFSETS = 1023
N_REP = 8
N_SHARD = 4


def draw_slot_of(key, part):
    per_peer = TOK_DEV // N_SHARD
    group_count = MICRO * N_REP
    source_key, target_key = jax.random.split(jax.random.fold_in(key, 17))
    source_keys = jax.random.split(source_key, group_count * N_SHARD)
    target_keys = jax.random.split(target_key, group_count * N_SHARD)
    source_perm = jax.vmap(lambda subkey: jax.random.permutation(subkey, TOK_DEV))(source_keys).astype(jnp.int32)
    target_perm = jax.vmap(lambda subkey: jax.random.permutation(subkey, TOK_DEV))(target_keys).astype(jnp.int32)
    source_perm = source_perm.reshape(group_count, N_SHARD, N_SHARD, per_peer)
    target_perm = target_perm.reshape(group_count, N_SHARD, N_SHARD, per_peer)
    starts = jnp.arange(N_SHARD, dtype=jnp.int32) * TOK_DEV
    arrival = starts[None, :, None, None] + source_perm
    packed = starts[None, None, :, None] + jnp.transpose(target_perm, (0, 2, 1, 3))
    empty = jnp.zeros((group_count, GROUP), jnp.int32)
    slot_table = jax.vmap(lambda base_row, row_index, row_value: base_row.at[row_index].set(row_value))(empty, arrival.reshape(group_count, GROUP), packed.reshape(group_count, GROUP))
    return slot_table.reshape(MICRO, N_REP, GROUP).astype(jnp.int32)


def draw_seq_lengths(key, part):
    group_count = MICRO * N_REP
    first_len = jax.random.randint(jax.random.fold_in(key, 5), (group_count,), MINLEN, GROUP - MINLEN + 1).astype(jnp.int32)
    first_len = first_len.at[0].set(GROUP - MINLEN).at[1].set(MINLEN)
    both = jnp.stack([first_len, GROUP - first_len], axis=-1)
    return both.reshape(MICRO, N_REP, 2).astype(jnp.int32)


def with_ends(entries, key, low, largest):
    longest = entries.shape.index(max(entries.shape))
    spots = []
    for shift in (0, 1):
        where = [jax.random.randint(jax.random.fold_in(key, axis), (), 0, length) for axis, length in enumerate(entries.shape)]
        where[longest] = (where[longest] + shift) % entries.shape[longest]
        spots.append(tuple(where))
    return entries.at[spots[0]].set(low).at[spots[1]].set(largest)


def block_scale(key, shape, cuts, smallest, high):
    level = 1.0
    for dim, blocks in cuts:
        draws = jax.random.uniform(jax.random.fold_in(jax.random.fold_in(key, 6), dim), (blocks,), jnp.float32, smallest / len(cuts), high / len(cuts))
        level = level * jnp.repeat(jnp.exp(draws), shape[dim] // blocks).reshape((-1,) + (1,) * (len(shape) - 1 - dim))
    return level


def gaussian(key, shape, scale, most, shards=(), kind=jnp.bfloat16):
    level = block_scale(key, shape, shards, -0.22, 0.18) if shards else 1.0
    array = jax.random.normal(key, shape, jnp.float32) * scale * level
    return jnp.minimum(jnp.maximum(array, -most), most).astype(kind)


def setup_inputs(seed: int = 0) -> dict:
    streams_of = jax.random.split(jax.random.key(seed), 19)
    return {
        "tokens": gaussian(streams_of[0], (MICRO, TOKENS, D), 1.0, 6.0, ((1, 32),)),
        "cotangent": gaussian(streams_of[1], (MICRO, TOKENS, D), 1.0, 6.0, ((1, 32),)),
        "gate_cotangent": gaussian(streams_of[2], (MICRO, TOKENS), 1.0, 6.0, ((1, 32),)),
        "slot_of": draw_slot_of(jax.random.fold_in(streams_of[18], 71), 0),
        "seq_lengths": draw_seq_lengths(jax.random.fold_in(streams_of[18], 71), 0),
        "buckets": with_ends(jax.random.randint(streams_of[5], (OFFSETS,), 0, NB), jax.random.fold_in(streams_of[5], 1), 0, NB - 1).astype(jnp.int32),
        "gain_attn": jnp.clip(1.0 + 0.18 * jax.random.normal(streams_of[6], (D,), jnp.float32), 0.099609375, 1.8984375).astype(jnp.bfloat16),
        "w_query": gaussian(streams_of[7], (D, HD), (4 * D) ** -0.5, 0.078125, ((0, 4),)),
        "w_key": gaussian(streams_of[8], (D, HD), (4 * D) ** -0.5, 0.078125, ((0, 4),)),
        "w_value": gaussian(streams_of[9], (D, HD), D ** -0.5, 0.15625, ((0, 4),)),
        "w_out": gaussian(streams_of[10], (HD, D), (HD // 32) ** -0.5, 1.75, ((0, 4),)),
        "rel_bias": gaussian(streams_of[11], (NB, H), 1.0, 4.0, ((0, 4),)),
        "gain_ffn": jnp.clip(1.0 + 0.18 * jax.random.normal(streams_of[12], (D,), jnp.float32), 0.099609375, 1.8984375).astype(jnp.bfloat16),
        "w_gate": gaussian(streams_of[13], (D, FF), D ** -0.5, 0.15625, ((0, 4),)),
        "w_up": gaussian(streams_of[14], (D, FF), D ** -0.5, 0.15625, ((0, 4),)),
        "w_down": gaussian(streams_of[15], (FF, D), FF ** -0.5, 0.09375, ((0, 4),)),
        "gain_delete": jnp.clip(1.0 + 0.18 * jax.random.normal(streams_of[16], (D,), jnp.float32), 0.099609375, 1.8984375).astype(jnp.bfloat16),
        "w_delete": gaussian(streams_of[17], (D,), D ** -0.5, 0.15625, ((0, 4),)),
    }


EPSILON = 1e-06
HIGHEST = lax.Precision.HIGHEST

@jax.custom_vjp
def low(v):
    return lax.optimization_barrier(v.astype(jnp.bfloat16)).astype(jnp.float32)

@jax.custom_vjp
def low_back(v):
    return v

def low_keep(v):
    return (low(v), None)

def low_pass(kept, grad):
    return (grad,)

def back_keep(v):
    return (v, None)

def back_low(kept, grad):
    return (low(grad),)
low.defvjp(low_keep, low_pass)
low_back.defvjp(back_keep, back_low)

def matmul(left, right):
    return jnp.dot(left, right, precision=HIGHEST, preferred_element_type=jnp.float32)

def rms_norm(hidden, gain):
    return hidden * lax.rsqrt(lax.optimization_barrier(jnp.mean(hidden * hidden, axis=-1, keepdims=True)) + EPSILON) * gain

def group_layer(weights, row_data, slot_row, length_row, buckets):
    gain_attn, w_query, w_key, w_value, w_out, rel_bias, gain_ffn, w_gate, w_up, w_down, gain_delete, w_delete = weights
    total_rows = row_data.shape[0]
    counting = jnp.arange(total_rows, dtype=jnp.int32)
    packed_from = jnp.zeros((total_rows,), jnp.int32).at[slot_row].set(counting)
    packed = row_data[packed_from]
    second = (counting >= length_row[0]).astype(jnp.int32)
    position = counting - second * length_row[0]
    same_seq = second[:, None] == second[None, :]
    offset = position[None, :] - position[:, None] + (total_rows - 1)
    bias_table = rel_bias[buckets]
    bias_grid = jnp.transpose(bias_table[offset], (2, 0, 1))
    normed_one = low(rms_norm(packed, gain_attn))
    queries = low(low_back(matmul(normed_one, w_query))).reshape(total_rows, H, DK)
    keys_proj = low(low_back(matmul(normed_one, w_key))).reshape(total_rows, H, DK)
    values_proj = low(low_back(matmul(normed_one, w_value))).reshape(total_rows, H, DK)
    scores = jnp.einsum('qhd,khd->hqk', queries, keys_proj, precision=HIGHEST) + bias_grid
    scores = low_back(scores)
    scores = jnp.where(same_seq[None], scores, -1000000000.0)
    probabilities = low(jax.nn.softmax(scores, axis=-1))
    context = jnp.einsum('hqk,khd->qhd', probabilities, values_proj, precision=HIGHEST).reshape(total_rows, HD)
    context = low(low_back(context))
    hidden_mid = packed + low_back(matmul(context, w_out))
    normed_two = low(rms_norm(hidden_mid, gain_ffn))
    gate_pre = low_back(matmul(normed_two, w_gate))
    up_pre = low_back(matmul(normed_two, w_up))
    inner_act = low(jax.nn.gelu(gate_pre, approximate=True) * up_pre)
    hidden_out = hidden_mid + low_back(matmul(inner_act, w_down))
    delete_logit = lax.optimization_barrier(jnp.sum(rms_norm(hidden_out, gain_delete) * w_delete, axis=-1))
    deleted = -30.0 * jax.nn.sigmoid(delete_logit)
    return (hidden_out[slot_row], deleted[slot_row])

def reference(tokens, cotangent, gate_cotangent, slot_of, seq_lengths, buckets, gain_attn, w_query, w_key, w_value, w_out, rel_bias, gain_ffn, w_gate, w_up, w_down, gain_delete, w_delete):
    params = tuple((weight.astype(jnp.float32) for weight in (gain_attn, w_query, w_key, w_value, w_out, rel_bias, gain_ffn, w_gate, w_up, w_down, gain_delete, w_delete)))
    group_count = MICRO * N_REP
    row_data = tokens.astype(jnp.float32).reshape(group_count, GROUP, D)
    slot_rows = slot_of.reshape(group_count, GROUP)
    length_rows = seq_lengths.reshape(group_count, 2)

    def forward(weights, inputs):

        def per_group(members):
            return group_layer(weights, members[0], members[1], members[2], buckets)
        return lax.map(jax.checkpoint(per_group), (inputs, slot_rows, length_rows))
    (hidden, deleted), pullback = jax.vjp(forward, params, row_data)
    gradients, grad_rows = pullback((cotangent.astype(jnp.float32).reshape(group_count, GROUP, D), gate_cotangent.astype(jnp.float32).reshape(group_count, GROUP)))
    return (hidden.reshape(MICRO, TOKENS, D), deleted.reshape(MICRO, TOKENS), grad_rows.astype(jnp.bfloat16).reshape(MICRO, TOKENS, D), gradients[0], gradients[1], gradients[2], gradients[3], gradients[4], gradients[5], gradients[6], gradients[7], gradients[8], gradients[9], gradients[10], gradients[11])
```

```python
import functools

import jax
import jax.numpy as jnp
from jax import lax
from jax.experimental import pallas as pl
from jax.experimental.pallas import tpu as pltpu
from jax.sharding import PartitionSpec as P

EPSILON = 1e-06
HIGHEST = lax.Precision.HIGHEST
MASKED = -1000000000.0
BF16 = jnp.bfloat16
F32 = jnp.float32


def gelu_tanh(value):
    return jax.nn.gelu(value, approximate=True)


def rms_scale(hidden):
    return lax.rsqrt(jnp.mean(hidden * hidden, axis=-1, keepdims=True) + EPSILON)


def rms_back(hidden, scale_row, gain, upstream):
    scaled = upstream * gain
    return scale_row * scaled - hidden * (scale_row * scale_row * scale_row) * jnp.mean(
        hidden * scaled, axis=-1, keepdims=True
    )


def dot(left, right, kind=F32):
    return jnp.dot(left, right, preferred_element_type=F32).astype(kind)


def bias_kernel(rows_ref, slots_ref, out_ref):
    group = out_ref.shape[2]
    row = jnp.broadcast_to(rows_ref[0], (group, rows_ref.shape[2]))
    grid = pltpu.roll(row, group + 1, 1, stride=1, stride_axis=0)[:, :group].astype(BF16)
    tokens = slots_ref.shape[0]
    pick = (slots_ref[...] == lax.broadcasted_iota(jnp.int32, (tokens, group), 1)).astype(BF16)
    out_ref[0] = jnp.dot(pick, grid, preferred_element_type=F32)


def bias_of_queries(bias_rows, slots, group):
    heads, width = bias_rows.shape
    tokens = slots.shape[0]
    return pl.pallas_call(
        bias_kernel,
        grid=(heads,),
        in_specs=[
            pl.BlockSpec((1, 1, width), lambda h: (h, 0, 0)),
            pl.BlockSpec((tokens, 1), lambda h: (0, 0)),
        ],
        out_specs=pl.BlockSpec((1, tokens, group), lambda h: (h, 0, 0)),
        out_shape=jax.ShapeDtypeStruct((heads, tokens, group), F32),
    )(bias_rows.reshape(heads, 1, width), slots.reshape(tokens, 1))


def fold_kernel(grad_ref, slots_ref, out_ref):
    tokens, group = grad_ref.shape[1:]
    place = (
        lax.broadcasted_iota(jnp.int32, (group, tokens), 0) == (group - 1) - slots_ref[...]
    ).astype(BF16)
    square = jnp.dot(place, grad_ref[0], preferred_element_type=F32)
    wide = jnp.concatenate([square, jnp.zeros_like(square)], axis=1)
    rolled = pltpu.roll(wide, 0, 1, stride=1, stride_axis=0)
    out_ref[0] = jnp.sum(rolled, axis=0, keepdims=True)


def bias_fold(score_grad, slots):
    heads, tokens, group = score_grad.shape
    return pl.pallas_call(
        fold_kernel,
        grid=(heads,),
        in_specs=[
            pl.BlockSpec((1, tokens, group), lambda h: (h, 0, 0)),
            pl.BlockSpec((1, tokens), lambda h: (0, 0)),
        ],
        out_specs=pl.BlockSpec((1, 1, 2 * group), lambda h: (h, 0, 0)),
        out_shape=jax.ShapeDtypeStruct((heads, 1, 2 * group), F32),
    )(score_grad, slots.reshape(1, tokens)).reshape(heads, 2 * group)


def on_device(
    tokens,
    cotangent,
    gate_cotangent,
    slot_of,
    seq_lengths,
    buckets,
    gain_attn,
    w_query,
    w_key,
    w_value,
    w_out,
    rel_bias,
    gain_ffn,
    w_gate,
    w_up,
    w_down,
    gain_delete,
    w_delete,
):
    shards = lax.axis_size("shard")
    reps = lax.axis_size("rep")
    chips = reps // 2
    rank = lax.axis_index("shard")
    rep_rank = lax.axis_index("rep")
    core = rep_rank % 2
    chip = rep_rank // 2
    micro_count, local_rows, width = tokens.shape
    group = local_rows * shards
    rows = micro_count * local_rows
    heads = rel_bias.shape[1]
    bucket_rows = rel_bias.shape[0]
    bucket_count = bucket_rows * shards
    proj = w_query.shape[1]
    head_size = proj // heads
    block = gain_attn.shape[0]
    inner = w_gate.shape[1]
    half_inner = inner // 2
    col_piece = inner // chips
    down_block = w_down.shape[0]
    down_half = down_block // 2
    down_piece = down_half // chips
    half_shards = shards // 2

    def swap(value, mask):
        return lax.ppermute(value, "rep", [(i, i ^ mask) for i in range(reps)])

    def shift(value):
        return lax.ppermute(value, "shard", [(i, (i + 1) % shards) for i in range(shards)])

    def cut(count):
        half = count // 2
        return half // 16 * 16 if half >= 16 else half

    def plane_gather(piece):
        if chips == 1:
            return []
        near = swap(piece, 2)
        found = [(1, 0, near)]
        if chips >= 4:
            far = swap(piece, 4)
            middle = cut(piece.shape[0])
            found += [
                (2, 0, far),
                (3, 0, swap(far[:middle], 2)),
                (3, middle, swap(near[middle:], 4)),
            ]
        bit = 4
        while bit < chips:
            found += [
                (mask ^ bit, start, swap(part, 2 * bit))
                for mask, start, part in [(0, 0, piece)] + found
            ]
            bit *= 2
        return found

    def plane_reduce(take):
        def reduce_level(get, level):
            if level == 1:
                return get(0)
            if level == 2:
                return (get(0).astype(F32) + swap(get(1), 2).astype(F32)).astype(BF16)
            if level == 4:
                diagonal = get(3)
                middle = cut(diagonal.shape[0])
                top = swap(diagonal[:middle], 2)
                low = swap(diagonal[middle:], 4)
                far, near = get(2), get(1)
                far = jnp.concatenate(
                    [(far[:middle].astype(F32) + top.astype(F32)).astype(BF16), far[middle:]]
                )
                near = jnp.concatenate(
                    [near[:middle], (near[middle:].astype(F32) + low.astype(F32)).astype(BF16)]
                )
                return (
                    get(0).astype(F32) + swap(far, 4).astype(F32) + swap(near, 2).astype(F32)
                ).astype(BF16)
            bit = level // 2
            return reduce_level(
                lambda mask: (
                    get(mask).astype(F32) + swap(get(mask ^ bit), 2 * bit).astype(F32)
                ).astype(BF16),
                bit,
            )

        return reduce_level(take, chips)

    def ring_reduce(block_of):
        total = block_of(1)
        for step in range(2, shards + 1):
            arrived = shift(total)
            total = (arrived.astype(F32) + block_of(step % shards).astype(F32)).astype(BF16)
        return total

    def source(step):
        return (rank - step) % shards

    vector_pack = jnp.concatenate(
        [gain_attn, gain_ffn, gain_delete, w_delete, rel_bias.reshape(-1)]
    ).reshape(1, -1)
    vectors = jnp.zeros((shards, vector_pack.shape[1]), BF16)
    moving = vector_pack
    vectors = lax.dynamic_update_slice(vectors, moving, (rank, 0))
    for step in range(1, shards):
        moving = shift(moving)
        vectors = lax.dynamic_update_slice(vectors, moving, (source(step), 0))
    attn_gain = vectors[:, :block].reshape(width).astype(F32)
    ffn_gain = vectors[:, block : 2 * block].reshape(width).astype(F32)
    delete_gain = vectors[:, 2 * block : 3 * block].reshape(width).astype(F32)
    delete_vec = vectors[:, 3 * block : 4 * block].reshape(width).astype(F32)
    bias_table = vectors[:, 4 * block :].reshape(bucket_count, heads)

    attn_rows = 4 * block // reps
    per_matrix = reps // 4
    attn_own = jnp.stack([w_query, w_key, w_value, w_out.reshape(block, proj)]).reshape(
        4, per_matrix, attn_rows, proj
    )
    attn_full = jnp.zeros((4, shards, per_matrix, attn_rows, proj), BF16)
    attn_full = lax.dynamic_update_slice(attn_full, attn_own[:, None], (0, rank, 0, 0, 0))
    attn_piece = lax.dynamic_index_in_dim(
        attn_own.reshape(reps, attn_rows, proj), rep_rank, 0, keepdims=False
    )
    attn_moving = attn_piece
    attn_foreign = []
    for step in range(1, shards):
        attn_moving = shift(attn_moving)
        attn_foreign.append(attn_moving)
    stacked = jnp.stack(attn_foreign)
    attn_found = [(0, 0, stacked)] + plane_gather_stack(plane_gather, stacked)
    attn_found = [(2 * mask, start, part) for mask, start, part in attn_found]
    attn_found = attn_found + [(mask ^ 1, start, swap(part, 1)) for mask, start, part in attn_found]
    for mask, start, part in attn_found:
        owner = rep_rank ^ mask
        for index in range(part.shape[0]):
            attn_full = lax.dynamic_update_slice(
                attn_full,
                part[index][None, None, None],
                (owner // per_matrix, source(start + index + 1), owner % per_matrix, 0, 0),
            )
    query_full = attn_full[0].reshape(width, proj)
    key_full = attn_full[1].reshape(width, proj)
    value_full = attn_full[2].reshape(width, proj)
    out_full = attn_full[3].reshape(proj, width)

    column = core * half_inner
    gate_up_own = jnp.concatenate(
        [
            lax.dynamic_slice_in_dim(w_gate, column, half_inner, 1),
            lax.dynamic_slice_in_dim(w_up, column, half_inner, 1),
        ],
        axis=1,
    )
    gate_up = jnp.zeros((width, inner), BF16)
    gate_up = lax.dynamic_update_slice(gate_up, gate_up_own, (rank * block, 0))
    moving = lax.dynamic_slice_in_dim(gate_up_own, chip * col_piece, col_piece, 1)
    for step in range(1, shards):
        moving = shift(moving)
        for mask, start, part in [(0, 0, moving)] + plane_gather(moving):
            gate_up = lax.dynamic_update_slice(
                gate_up, part, (source(step) * block + start, (chip ^ mask) * col_piece)
            )

    down_own = lax.dynamic_slice_in_dim(w_down, core * down_half, down_half, 0)
    carried = jnp.zeros((shards, down_half, width), BF16)
    carried = lax.dynamic_update_slice(carried, down_own[None], (rank, 0, 0))
    moving = lax.dynamic_slice_in_dim(down_own, chip * down_piece, down_piece, 0)
    for step in range(1, shards):
        moving = shift(moving)
        for mask, start, part in [(0, 0, moving)] + plane_gather(moving):
            carried = lax.dynamic_update_slice(
                carried, part[None], (source(step), (chip ^ mask) * down_piece + start, 0)
            )
    kept = lax.dynamic_slice_in_dim(carried, core * half_shards, half_shards, 0)
    given = swap(lax.dynamic_slice_in_dim(carried, (1 - core) * half_shards, half_shards, 0), 1)
    down = jnp.stack(
        [jnp.where(core == 0, kept, given), jnp.where(core == 0, given, kept)], axis=1
    ).reshape(half_inner, width)

    slots = slot_of[:, 0]
    own_slots = lax.dynamic_slice_in_dim(slots, rank * local_rows, local_rows, 1)
    order = (rank - jnp.arange(shards, dtype=jnp.int32)) % shards
    key_slots = jnp.take(slots.reshape(micro_count, shards, local_rows), order, axis=1)
    key_slots = key_slots.reshape(micro_count, group)
    to_slots = (
        key_slots[:, None, :] == jnp.arange(group, dtype=jnp.int32)[None, :, None]
    ).astype(BF16)
    onehot = (buckets[:, None] == jnp.arange(bucket_count, dtype=jnp.int32)[None, :]).astype(F32)
    onehot = jnp.pad(onehot, ((0, 1), (0, 0)))
    bias_rows = jnp.dot(onehot, bias_table.astype(F32), precision=HIGHEST).T
    bias = bias_of_queries(bias_rows, own_slots.reshape(rows), group).reshape(
        heads, micro_count, local_rows, group
    )
    first_len = seq_lengths[:, 0, 0]
    query_seg = own_slots >= first_len[:, None]
    key_seg = jnp.arange(group, dtype=jnp.int32)[None, :] >= first_len[:, None]
    same_seq = (query_seg[:, :, None] == key_seg[:, None, :])[None]

    hidden_in = tokens.reshape(rows, width).astype(F32)
    scale_one = rms_scale(hidden_in)
    normed_one = (hidden_in * scale_one * attn_gain).astype(BF16)
    queries = dot(normed_one, query_full, BF16)
    moving = jnp.concatenate(
        [dot(normed_one, key_full, BF16), dot(normed_one, value_full, BF16)], axis=1
    )
    arrived = [moving]
    for step in range(1, shards):
        moving = shift(moving)
        arrived.append(moving)
    pairs = jnp.stack([part.reshape(micro_count, local_rows, 2 * proj) for part in arrived], axis=1)
    pairs = pairs.reshape(micro_count, group, 2 * proj)
    packed = jnp.einsum("msj,mjc->msc", to_slots, pairs, preferred_element_type=F32).astype(BF16)
    packed = packed.reshape(micro_count, group, 2, heads, head_size)
    keys, values = packed[:, :, 0], packed[:, :, 1]
    queries = queries.reshape(micro_count, local_rows, heads, head_size)
    scores = jnp.einsum("mqhd,mkhd->hmqk", queries, keys, preferred_element_type=F32) + bias
    scores = jnp.where(same_seq, scores, MASKED)
    weights = jnp.exp(scores - jnp.max(scores, axis=-1, keepdims=True))
    probabilities = weights / jnp.sum(weights, axis=-1, keepdims=True)
    rounded = probabilities.astype(BF16)
    context = jnp.einsum("hmqk,mkhd->mqhd", rounded, values, preferred_element_type=F32)
    context = context.astype(BF16).reshape(rows, proj)
    hidden_mid = hidden_in + dot(context, out_full)

    scale_two = rms_scale(hidden_mid)
    normed_two = (hidden_mid * scale_two * ffn_gain).astype(BF16)
    normed_pair = jnp.concatenate([normed_two, swap(normed_two, 1)])
    both = dot(normed_pair, gate_up)
    gate_pre, up_pre = both[:, :half_inner], both[:, half_inner:]
    inner_act = (gelu_tanh(gate_pre) * up_pre).astype(BF16)
    partial = dot(inner_act, down)
    hidden_out = hidden_mid + partial[:rows] + swap(partial[rows:].astype(BF16), 1).astype(F32)
    scale_three = rms_scale(hidden_out)
    delete_norm = hidden_out * scale_three * delete_gain
    sigmoid_val = jax.nn.sigmoid(jnp.sum(delete_norm * delete_vec, axis=-1))
    deleted = -30.0 * sigmoid_val

    gate_upstream = gate_cotangent.reshape(rows).astype(F32)
    gate_slope = gate_upstream * -30.0 * sigmoid_val * (1.0 - sigmoid_val)
    grad_delete_vec = jnp.sum(gate_slope[:, None] * delete_norm, axis=0)
    delete_up = gate_slope[:, None] * delete_vec
    grad_delete_gain = jnp.sum(delete_up * hidden_out * scale_three, axis=0)
    grad_out = cotangent.reshape(rows, width).astype(F32) + rms_back(
        hidden_out, scale_three, delete_gain, delete_up
    )
    down_up = grad_out.astype(BF16)
    down_up_pair = jnp.concatenate([down_up, swap(down_up, 1)])

    grad_down = jnp.einsum("tf,td->fd", inner_act, down_up_pair, preferred_element_type=F32)
    grad_down = grad_down.astype(BF16).reshape(half_shards, 2, down_half, width)
    kept = lax.dynamic_index_in_dim(grad_down, core, 1, keepdims=False)
    given = swap(lax.dynamic_index_in_dim(grad_down, 1 - core, 1, keepdims=False), 1)
    carried = jnp.concatenate(
        [jnp.where(core == 0, kept, given), jnp.where(core == 0, given, kept)]
    )

    def down_block_of(step):
        return plane_reduce(
            lambda mask: lax.dynamic_slice(
                carried,
                (source(step), (chip ^ mask) * down_piece, 0),
                (1, down_piece, width),
            )[0]
        )

    down_sum = ring_reduce(down_block_of)

    inner_grad = jnp.einsum("td,fd->tf", down_up_pair, down, preferred_element_type=F32)
    activated, gelu_pull = jax.vjp(gelu_tanh, gate_pre)
    both_grad = jnp.concatenate(
        [
            gelu_pull(inner_grad * up_pre)[0].astype(BF16),
            (inner_grad * activated).astype(BF16),
        ],
        axis=1,
    )
    grad_gate_up = jnp.einsum("td,tf->df", normed_pair, both_grad, preferred_element_type=F32)
    grad_gate_up = grad_gate_up.astype(BF16)

    def gate_up_block_of(step):
        return plane_reduce(
            lambda mask: lax.dynamic_slice(
                grad_gate_up,
                (source(step) * block, (chip ^ mask) * col_piece),
                (block, col_piece),
            )
        )

    gate_up_sum = ring_reduce(gate_up_block_of)

    partial = jnp.einsum("tf,df->td", both_grad, gate_up, preferred_element_type=F32)
    normed_two_grad = partial[:rows] + swap(partial[rows:].astype(BF16), 1).astype(F32)
    grad_ffn_gain = jnp.sum(normed_two_grad * hidden_mid * scale_two, axis=0)
    grad_mid = grad_out + rms_back(hidden_mid, scale_two, ffn_gain, normed_two_grad)
    out_grad = grad_mid.astype(BF16)
    grad_w_out = jnp.einsum("th,td->hd", context, out_grad, preferred_element_type=F32)
    context_grad = jnp.einsum("td,hd->th", out_grad, out_full, preferred_element_type=F32)
    context_grad = context_grad.astype(BF16).reshape(micro_count, local_rows, heads, head_size)
    prob_grad = jnp.einsum("mqhd,mkhd->hmqk", context_grad, values, preferred_element_type=F32)
    inner_sum = jnp.sum(probabilities * prob_grad, axis=-1, keepdims=True)
    score_grad = (probabilities * (prob_grad - inner_sum)).astype(BF16)
    query_grad = jnp.einsum("hmqk,mkhd->mqhd", score_grad, keys, preferred_element_type=F32)
    query_grad = query_grad.astype(BF16).reshape(rows, proj)
    key_part = jnp.einsum("hmqk,mqhd->mkhd", score_grad, queries, preferred_element_type=F32)
    value_part = jnp.einsum("hmqk,mqhd->mkhd", rounded, context_grad, preferred_element_type=F32)
    pair_part = jnp.concatenate(
        [key_part.reshape(micro_count, group, proj), value_part.reshape(micro_count, group, proj)],
        axis=2,
    ).astype(BF16)
    pair_part = jnp.einsum("msj,msc->mjc", to_slots, pair_part, preferred_element_type=F32)
    pair_part = pair_part.astype(BF16).reshape(micro_count, shards, local_rows, 2 * proj)
    pair_sum = ring_reduce(lambda step: pair_part[:, step].reshape(rows, 2 * proj))
    grad_bias_rows = bias_fold(
        score_grad.reshape(heads, rows, group), own_slots.reshape(rows)
    )
    grad_bias = jnp.einsum("ob,ho->bh", onehot, grad_bias_rows, precision=HIGHEST)

    projected = jnp.concatenate([query_grad, pair_sum], axis=1)
    grad_proj = jnp.einsum("td,th->dh", normed_one, projected, preferred_element_type=F32)
    grad_proj = grad_proj.astype(BF16)
    normed_one_grad = (
        jnp.einsum("th,dh->td", query_grad, query_full, preferred_element_type=F32)
        + jnp.einsum("th,dh->td", pair_sum[:, :proj], key_full, preferred_element_type=F32)
        + jnp.einsum("th,dh->td", pair_sum[:, proj:], value_full, preferred_element_type=F32)
    )
    grad_attn_gain = jnp.sum(normed_one_grad * hidden_in * scale_one, axis=0)
    grad_in = grad_mid + rms_back(hidden_in, scale_one, attn_gain, normed_one_grad)

    attn_grads = jnp.stack(
        [
            grad_proj[:, :proj].reshape(shards, block, proj),
            grad_proj[:, proj : 2 * proj].reshape(shards, block, proj),
            grad_proj[:, 2 * proj :].reshape(shards, block, proj),
            grad_w_out.astype(BF16).reshape(shards, block, proj),
        ],
        axis=1,
    ).reshape(shards, chips, 2, attn_rows, proj)
    attn_grads = jnp.take(attn_grads, order, axis=0)
    kept = lax.dynamic_index_in_dim(attn_grads, core, 2, keepdims=False)
    given = swap(lax.dynamic_index_in_dim(attn_grads, 1 - core, 2, keepdims=False), 1)
    attn_grads = (kept.astype(F32) + given.astype(F32)).astype(BF16)
    attn_sum = plane_reduce(
        lambda mask: lax.dynamic_index_in_dim(attn_grads, chip ^ mask, 1, keepdims=False)
    )
    attn_sum = ring_reduce(lambda step: attn_sum[step])

    gate_up_half = jnp.zeros((block, inner), BF16)
    for mask, start, part in [(0, 0, gate_up_sum)] + plane_gather(gate_up_sum):
        gate_up_half = lax.dynamic_update_slice(
            gate_up_half, part, (start, (chip ^ mask) * col_piece)
        )
    gate_up_other = swap(gate_up_half, 1)
    low = jnp.where(core == 0, gate_up_half, gate_up_other).astype(F32)
    high = jnp.where(core == 0, gate_up_other, gate_up_half).astype(F32)
    grad_gate = jnp.concatenate([low[:, :half_inner], high[:, :half_inner]], axis=1)
    grad_up = jnp.concatenate([low[:, half_inner:], high[:, half_inner:]], axis=1)

    down_half_sum = jnp.zeros((down_half, width), BF16)
    for mask, start, part in [(0, 0, down_sum)] + plane_gather(down_sum):
        down_half_sum = lax.dynamic_update_slice(
            down_half_sum, part, ((chip ^ mask) * down_piece + start, 0)
        )
    down_other = swap(down_half_sum, 1)
    grad_down_out = jnp.concatenate(
        [jnp.where(core == 0, down_half_sum, down_other), jnp.where(core == 0, down_other, down_half_sum)]
    ).astype(F32)

    attn_half = jnp.zeros((chips, attn_rows, proj), BF16)
    for mask, start, part in [(0, 0, attn_sum)] + plane_gather(attn_sum):
        attn_half = lax.dynamic_update_slice(attn_half, part[None], (chip ^ mask, start, 0))
    attn_other = swap(attn_half, 1)
    attn_shard = jnp.stack(
        [jnp.where(core == 0, attn_half, attn_other), jnp.where(core == 0, attn_other, attn_half)],
        axis=1,
    ).reshape(4, block, proj).astype(F32)

    small = jnp.concatenate(
        [
            grad_attn_gain.reshape(shards, block),
            grad_ffn_gain.reshape(shards, block),
            grad_delete_gain.reshape(shards, block),
            grad_delete_vec.reshape(shards, block),
            grad_bias.reshape(shards, bucket_rows * heads),
        ],
        axis=1,
    )
    small = jnp.take(small, order, axis=0)
    bit = 1
    while bit < reps:
        small = small + swap(small, bit)
        bit *= 2
    total = small[1:2]
    for step in range(2, shards + 1):
        total = shift(total) + small[step % shards : step % shards + 1]
    total = total.reshape(-1)

    return (
        hidden_out.reshape(micro_count, local_rows, width),
        deleted.reshape(micro_count, local_rows),
        grad_in.astype(BF16).reshape(micro_count, local_rows, width),
        total[:block],
        attn_shard[0],
        attn_shard[1],
        attn_shard[2],
        attn_shard[3].reshape(proj // shards, width),
        total[4 * block :].reshape(bucket_rows, heads),
        total[block : 2 * block],
        grad_gate,
        grad_up,
        grad_down_out,
        total[2 * block : 3 * block],
        total[3 * block : 4 * block],
    )


def plane_gather_stack(plane_gather, stacked):
    return plane_gather(stacked)


def solution(mesh):
    rows = P(None, ("rep", "shard"), None)
    flat = P(None, ("rep", "shard"))
    by_rep = P(None, "rep", None)
    vector = P("shard")
    matrix = P("shard", None)
    in_specs = (
        (rows, rows, flat, by_rep, by_rep, P(), vector)
        + (matrix,) * 5
        + (vector,)
        + (matrix,) * 3
        + (vector, vector)
    )
    out_specs = (
        (rows, flat, rows, vector) + (matrix,) * 5 + (vector,) + (matrix,) * 3 + (vector, vector)
    )
    return jax.shard_map(
        on_device, mesh=mesh, in_specs=in_specs, out_specs=out_specs, check_vma=False
    )
```

```python
import functools

import math

import jax
import jax.numpy as jnp
from jax import lax
from jax.experimental import pallas as pl
from jax.experimental.pallas import tpu as pltpu
from jax.sharding import PartitionSpec as P

EPSILON = 1e-06
HIGHEST = lax.Precision.HIGHEST
MASKED = -1000000000.0
BF16 = jnp.bfloat16
F32 = jnp.float32


def gelu_tanh(value):
    return jax.nn.gelu(value, approximate=True)


def rms_scale(hidden):
    return lax.rsqrt(jnp.mean(hidden * hidden, axis=-1, keepdims=True) + EPSILON)


def rms_back(hidden, scale_row, gain, upstream):
    scaled = upstream * gain
    return scale_row * scaled - hidden * (scale_row * scale_row * scale_row) * jnp.mean(
        hidden * scaled, axis=-1, keepdims=True
    )


def dot(left, right, kind=F32):
    return jnp.dot(left, right, preferred_element_type=F32).astype(kind)


def bias_kernel(rows_ref, slots_ref, out_ref):
    group = out_ref.shape[2]
    row = jnp.broadcast_to(rows_ref[0], (group, rows_ref.shape[2]))
    grid = pltpu.roll(row, group + 1, 1, stride=1, stride_axis=0)[:, :group].astype(BF16)
    tokens = slots_ref.shape[0]
    pick = (slots_ref[...] == lax.broadcasted_iota(jnp.int32, (tokens, group), 1)).astype(BF16)
    out_ref[0] = jnp.dot(pick, grid, preferred_element_type=F32)


def bias_of_queries(bias_rows, slots, group):
    heads, width = bias_rows.shape
    tokens = slots.shape[0]
    return pl.pallas_call(
        bias_kernel,
        grid=(heads,),
        in_specs=[
            pl.BlockSpec((1, 1, width), lambda h: (h, 0, 0)),
            pl.BlockSpec((tokens, 1), lambda h: (0, 0)),
        ],
        out_specs=pl.BlockSpec((1, tokens, group), lambda h: (h, 0, 0)),
        out_shape=jax.ShapeDtypeStruct((heads, tokens, group), F32),
    )(bias_rows.reshape(heads, 1, width), slots.reshape(tokens, 1))


def fold_kernel(grad_ref, slots_ref, out_ref):
    tokens, group = grad_ref.shape[1:]
    place = (
        lax.broadcasted_iota(jnp.int32, (group, tokens), 0) == (group - 1) - slots_ref[...]
    ).astype(BF16)
    square = jnp.dot(place, grad_ref[0], preferred_element_type=F32)
    wide = jnp.concatenate([square, jnp.zeros_like(square)], axis=1)
    rolled = pltpu.roll(wide, 0, 1, stride=1, stride_axis=0)
    out_ref[0] = jnp.sum(rolled, axis=0, keepdims=True)


def bias_fold(score_grad, slots):
    heads, tokens, group = score_grad.shape
    return pl.pallas_call(
        fold_kernel,
        grid=(heads,),
        in_specs=[
            pl.BlockSpec((1, tokens, group), lambda h: (h, 0, 0)),
            pl.BlockSpec((1, tokens), lambda h: (0, 0)),
        ],
        out_specs=pl.BlockSpec((1, 1, 2 * group), lambda h: (h, 0, 0)),
        out_shape=jax.ShapeDtypeStruct((heads, 1, 2 * group), F32),
    )(score_grad, slots.reshape(1, tokens)).reshape(heads, 2 * group)


def axis_ranks():
    return lax.axis_index("shard"), lax.axis_index("rep") // 2


def gelu_parts(value):
    inner = math.sqrt(2.0 / math.pi)
    square = value * value
    bend = jnp.tanh(inner * value * (1.0 + 0.044715 * square))
    outside = 0.5 * (1.0 + bend)
    slope = outside + 0.5 * value * (1.0 - bend * bend) * (inner * (1.0 + 0.134145 * square))
    return value * outside, slope


def run_copies(copies, sems):
    started = [pltpu.make_async_copy(src, dst, sems.at[i]) for i, (src, dst) in enumerate(copies)]
    for copy in started:
        copy.start()
    return started


ANY = pl.BlockSpec(memory_space=pl.ANY)
VMEM = pl.BlockSpec(memory_space=pltpu.VMEM)


def pick_kernel(gate_ref, up_ref, out_ref):
    core = lax.axis_index("rep") % 2
    inner = gate_ref.shape[1]
    shards = lax.axis_size("shard")
    unit = inner // shards
    half = unit // 2
    for index, ref in enumerate((gate_ref, up_ref)):
        parts = []
        for shard in range(shards):
            low = ref[:, shard * unit : shard * unit + half]
            high = ref[:, shard * unit + half : (shard + 1) * unit]
            parts.append(jnp.where(core == 0, low, high))
        out_ref[:, index * (inner // 2) : (index + 1) * (inner // 2)] = jnp.concatenate(parts, 1)


def pick_columns(w_gate, w_up):
    return pl.pallas_call(
        pick_kernel,
        in_specs=[VMEM, VMEM],
        out_specs=VMEM,
        out_shape=jax.ShapeDtypeStruct(w_gate.shape, BF16),
    )(w_gate, w_up)


def spread_kernel(low_ref, high_ref, gate_ref, up_ref):
    inner = gate_ref.shape[1]
    shards = lax.axis_size("shard")
    half = inner // shards // 2
    for index, ref in enumerate((gate_ref, up_ref)):
        parts = []
        for shard in range(shards):
            start = index * (inner // 2) + shard * half
            parts += [low_ref[:, start : start + half], high_ref[:, start : start + half]]
        ref[...] = jnp.concatenate(parts, 1).astype(F32)


def spread_columns(low, high):
    shape = jax.ShapeDtypeStruct(low.shape, F32)
    return pl.pallas_call(
        spread_kernel,
        in_specs=[VMEM, VMEM],
        out_specs=[VMEM, VMEM],
        out_shape=[shape, shape],
    )(low, high)


def gate_up_call(own, other, pieces, places):
    rows, width = own.shape
    count = len(pieces)
    inner = places[0][1]
    half = inner // 2
    tile = 256

    def kernel(own_ref, other_ref, *rest):
        piece_refs = rest[:count]
        slope_ref, act_ref, hidden_ref, keep_ref, both, weights, sems = rest[count:]
        rank, chip = axis_ranks()
        copies = [(own_ref, both.at[:rows]), (other_ref, both.at[rows:])]
        for ref, place in zip(piece_refs, places[1:]):
            row, column = place(rank, chip)
            copies.append(
                (ref, weights.at[pl.ds(row, ref.shape[0]), pl.ds(column, ref.shape[1])])
            )
        for copy in run_copies(copies, sems):
            copy.wait()
        keep = pltpu.make_async_copy(weights, keep_ref, sems.at[count + 2])
        keep.start()

        def step(index, carry):
            start = pl.multiple_of(index * tile, tile)
            gate = jnp.dot(both[...], weights[:, pl.ds(start, tile)], preferred_element_type=F32)
            up = jnp.dot(
                both[...],
                weights[:, pl.ds(pl.multiple_of(half + start, tile), tile)],
                preferred_element_type=F32,
            )
            act, slope = gelu_parts(gate)
            act_ref[:, pl.ds(start, tile)] = act.astype(BF16)
            slope_ref[:, pl.ds(start, tile)] = (up * slope).astype(BF16)
            hidden_ref[:, pl.ds(start, tile)] = (act * up).astype(BF16)
            return carry

        lax.fori_loop(0, half // tile, step, 0)
        keep.wait()

    shape = jax.ShapeDtypeStruct((2 * rows, half), BF16)
    return pl.pallas_call(
        kernel,
        in_specs=[ANY] * (2 + count),
        out_specs=[VMEM, VMEM, VMEM, ANY],
        out_shape=[shape, shape, shape, jax.ShapeDtypeStruct((width, inner), BF16)],
        scratch_shapes=[
            pltpu.VMEM((2 * rows, width), BF16),
            pltpu.VMEM((width, inner), BF16),
            pltpu.SemaphoreType.DMA((count + 3,)),
        ],
        cost_estimate=pl.CostEstimate(
            flops=4 * rows * width * inner,
            bytes_accessed=4 * width * inner + 6 * rows * inner,
            transcendentals=rows * inner,
        ),
    )(own, other, *pieces)


def col_tiles(width):
    return [(start, min(512, width - start)) for start in range(0, width, 512)]


def down_call(hidden, pieces, places):
    double, half = hidden.shape
    rows = double // 2
    count = len(pieces)
    width = pieces[0].shape[1]

    def kernel(hidden_ref, *rest):
        piece_refs = rest[:count]
        own_ref, other_ref, keep_ref, weights, sems = rest[count:]
        rank, chip = axis_ranks()
        copies = []
        for ref, place in zip(piece_refs, places):
            copies.append((ref, weights.at[pl.ds(place(rank, chip), ref.shape[0])]))
        for copy in run_copies(copies, sems):
            copy.wait()
        keep = pltpu.make_async_copy(weights, keep_ref, sems.at[count])
        keep.start()
        for start, size in col_tiles(width):
            columns = slice(start, start + size)
            own_ref[:, columns] = jnp.dot(
                hidden_ref[:rows], weights[:, columns], preferred_element_type=F32
            )
            other_ref[:, columns] = jnp.dot(
                hidden_ref[rows:], weights[:, columns], preferred_element_type=F32
            ).astype(BF16)
        keep.wait()

    return pl.pallas_call(
        kernel,
        in_specs=[VMEM] + [ANY] * count,
        out_specs=[VMEM, VMEM, ANY],
        out_shape=[
            jax.ShapeDtypeStruct((rows, width), F32),
            jax.ShapeDtypeStruct((rows, width), BF16),
            jax.ShapeDtypeStruct((half, width), BF16),
        ],
        scratch_shapes=[pltpu.VMEM((half, width), BF16), pltpu.SemaphoreType.DMA((count + 1,))],
        cost_estimate=pl.CostEstimate(
            flops=4 * rows * width * half, bytes_accessed=4 * width * half, transcendentals=0
        ),
    )(hidden, *pieces)


def hidden_grad_call(own, other, down, slope, act):
    rows, width = own.shape
    half = down.shape[0]
    tile = 256

    def kernel(own_ref, other_ref, down_ref, slope_ref, act_ref, out_ref, both, sems):
        for copy in run_copies(
            [(own_ref, both.at[:rows]), (other_ref, both.at[rows:])], sems
        ):
            copy.wait()

        def step(index, carry):
            start = pl.multiple_of(index * tile, tile)
            upstream = lax.dot_general(
                both[...],
                down_ref[pl.ds(start, tile)],
                (((1,), (1,)), ((), ())),
                preferred_element_type=F32,
            )
            gate = upstream * slope_ref[:, pl.ds(start, tile)].astype(F32)
            up = upstream * act_ref[:, pl.ds(start, tile)].astype(F32)
            out_ref[:, pl.ds(start, tile)] = gate.astype(BF16)
            out_ref[:, pl.ds(pl.multiple_of(half + start, tile), tile)] = up.astype(BF16)
            return carry

        lax.fori_loop(0, half // tile, step, 0)

    return pl.pallas_call(
        kernel,
        in_specs=[ANY, ANY, VMEM, VMEM, VMEM],
        out_specs=VMEM,
        out_shape=jax.ShapeDtypeStruct((2 * rows, 2 * half), BF16),
        scratch_shapes=[pltpu.VMEM((2 * rows, width), BF16), pltpu.SemaphoreType.DMA((2,))],
        cost_estimate=pl.CostEstimate(
            flops=4 * rows * width * half,
            bytes_accessed=2 * width * half + 16 * rows * half,
            transcendentals=0,
        ),
    )(own, other, down, slope, act)


def weight_grad_call(left, right, outputs):
    left_own, left_other = left
    right_own, right_other = right
    rows = left_own.shape[0]
    depth, width = left_own.shape[1], right_own.shape[1]
    count = len(outputs)
    copies_out = sum(len(moves) for _, moves in outputs)
    split = left_other is not None
    total = 2 * rows if split else rows
    right_split = right_other is not None
    inputs = [left_own] + ([left_other] if split else []) + [right_own]
    inputs += [right_other] if right_split else []

    def kernel(*refs):
        in_refs = list(refs[: len(inputs)])
        out_refs = refs[len(inputs) : len(inputs) + count]
        lefts, rights, result, sems = refs[len(inputs) + count :]
        copies = []
        for target, parted in ((lefts, split), (rights, right_split)):
            first = in_refs.pop(0)
            size = first.shape[0]
            copies.append((first, target.at[:size]))
            if parted:
                copies.append((in_refs.pop(0), target.at[size:]))
        for copy in run_copies(copies, sems):
            copy.wait()
        tile = 512 if width % 512 == 0 else width
        for begin in range(0, depth, 256):
            size = min(256, depth - begin)
            turned = lefts[:, begin : begin + size].T
            if tile == width:
                for start, span in col_tiles(width):
                    result[begin : begin + size, start : start + span] = jnp.dot(
                        turned, rights[:, start : start + span], preferred_element_type=F32
                    ).astype(BF16)
            else:

                def step(index, carry):
                    start = pl.multiple_of(index * tile, tile)
                    result[begin : begin + size, pl.ds(start, tile)] = jnp.dot(
                        turned, rights[:, pl.ds(start, tile)], preferred_element_type=F32
                    ).astype(BF16)
                    return carry

                lax.fori_loop(0, width // tile, step, 0)
        rank, chip = axis_ranks()
        moves_out = []
        for ref, (shape, moves) in zip(out_refs, outputs):
            for index, place in moves:
                row, column = place(rank, chip)
                moves_out.append(
                    (result.at[pl.ds(row, shape[1]), pl.ds(column, shape[2])], ref.at[index])
                )
        for copy in run_copies(moves_out, sems):
            copy.wait()

    return pl.pallas_call(
        kernel,
        in_specs=[ANY] * len(inputs),
        out_specs=[ANY] * count,
        out_shape=[jax.ShapeDtypeStruct(shape, BF16) for shape, _ in outputs],
        scratch_shapes=[
            pltpu.VMEM((total, depth), BF16),
            pltpu.VMEM((total, width), BF16),
            pltpu.VMEM((depth, width), BF16),
            pltpu.SemaphoreType.DMA((max(4, copies_out),)),
        ],
        cost_estimate=pl.CostEstimate(
            flops=2 * total * depth * width,
            bytes_accessed=2 * (depth * width + total * (depth + width)),
            transcendentals=0,
        ),
    )(*inputs)


def on_device(
    tokens,
    cotangent,
    gate_cotangent,
    slot_of,
    seq_lengths,
    buckets,
    gain_attn,
    w_query,
    w_key,
    w_value,
    w_out,
    rel_bias,
    gain_ffn,
    w_gate,
    w_up,
    w_down,
    gain_delete,
    w_delete,
):
    shards = lax.axis_size("shard")
    reps = lax.axis_size("rep")
    chips = reps // 2
    rank = lax.axis_index("shard")
    rep_rank = lax.axis_index("rep")
    core = rep_rank % 2
    chip = rep_rank // 2
    micro_count, local_rows, width = tokens.shape
    group = local_rows * shards
    rows = micro_count * local_rows
    heads = rel_bias.shape[1]
    bucket_rows = rel_bias.shape[0]
    bucket_count = bucket_rows * shards
    proj = w_query.shape[1]
    head_size = proj // heads
    block = gain_attn.shape[0]
    inner = w_gate.shape[1]
    half_inner = inner // 2
    col_piece = inner // chips
    down_block = w_down.shape[0]
    down_half = down_block // 2
    down_piece = down_half // chips
    aligned = block % 16 == 0 and down_piece % 16 == 0 and col_piece % 128 == 0

    def swap(value, mask):
        return lax.ppermute(value, "rep", [(i, i ^ mask) for i in range(reps)])

    def shift(value):
        return lax.ppermute(value, "shard", [(i, (i + 1) % shards) for i in range(shards)])

    def cut(count):
        half = count // 2
        return half // 16 * 16 if half >= 16 else half

    def plane_gather(piece):
        if chips == 1:
            return []
        near = swap(piece, 2)
        found = [(1, 0, near)]
        if chips >= 4:
            far = swap(piece, 4)
            middle = cut(piece.shape[0])
            found += [
                (2, 0, far),
                (3, 0, swap(far[:middle], 2)),
                (3, middle, swap(near[middle:], 4)),
            ]
        bit = 4
        while bit < chips:
            found += [
                (mask ^ bit, start, swap(part, 2 * bit))
                for mask, start, part in [(0, 0, piece)] + found
            ]
            bit *= 2
        return found

    def add(*values):
        return sum(value.astype(F32) for value in values).astype(BF16)

    def plane_reduce(parts, axis):
        def level_two(get):
            if chips == 1:
                return get("own")
            if chips == 2:
                return add(get("own"), swap(get("near"), 2))
            top, low = swap(get("top"), 2), swap(get("low"), 4)
            far, near = get("far"), get("near")
            middle = top.shape[axis]

            def pair(value):
                return (
                    lax.slice_in_dim(value, 0, middle, axis=axis),
                    lax.slice_in_dim(value, middle, value.shape[axis], axis=axis),
                )

            (far_top, far_low), (near_top, near_low) = pair(far), pair(near)
            far = jnp.concatenate([add(far_top, top), far_low], axis)
            near = jnp.concatenate([near_top, add(near_low, low)], axis)
            return add(get("own"), swap(far, 4), swap(near, 2))

        def level(base, bit):
            if bit < 4:
                return lambda name: parts[base][name]
            lower, upper = level(base, bit // 2), level(base ^ bit, bit // 2)
            return lambda name: add(lower(name), swap(upper(name), 2 * bit))

        return level_two(level(0, chips // 2))

    names = {"own": 0, "near": 1, "far": 2, "top": 3, "low": 3}
    bases = [base for base in range(chips) if base & 3 == 0]
    used = ["own", "near", "far", "top", "low"] if chips >= 4 else ["own", "near"][:chips]

    def ring_reduce(block_of):
        total = block_of(1)
        for step in range(2, shards + 1):
            arrived = shift(total)
            total = (arrived.astype(F32) + block_of(step % shards).astype(F32)).astype(BF16)
        return total

    def source(step):
        return (rank - step) % shards

    vector_pack = jnp.concatenate(
        [gain_attn, gain_ffn, gain_delete, w_delete, rel_bias.reshape(-1)]
    ).reshape(1, -1)
    vectors = jnp.zeros((shards, vector_pack.shape[1]), BF16)
    moving = vector_pack
    vectors = lax.dynamic_update_slice(vectors, moving, (rank, 0))
    for step in range(1, shards):
        moving = shift(moving)
        vectors = lax.dynamic_update_slice(vectors, moving, (source(step), 0))
    attn_gain = vectors[:, :block].reshape(width).astype(F32)
    ffn_gain = vectors[:, block : 2 * block].reshape(width).astype(F32)
    delete_gain = vectors[:, 2 * block : 3 * block].reshape(width).astype(F32)
    delete_vec = vectors[:, 3 * block : 4 * block].reshape(width).astype(F32)
    bias_table = vectors[:, 4 * block :].reshape(bucket_count, heads)

    attn_rows = 4 * block // reps
    per_matrix = reps // 4
    attn_own = jnp.stack([w_query, w_key, w_value, w_out.reshape(block, proj)]).reshape(
        4, per_matrix, attn_rows, proj
    )
    attn_full = jnp.zeros((4, shards, per_matrix, attn_rows, proj), BF16)
    attn_full = lax.dynamic_update_slice(attn_full, attn_own[:, None], (0, rank, 0, 0, 0))
    attn_piece = lax.dynamic_index_in_dim(
        attn_own.reshape(reps, attn_rows, proj), rep_rank, 0, keepdims=False
    )
    attn_moving = attn_piece
    attn_foreign = []
    for step in range(1, shards):
        attn_moving = shift(attn_moving)
        attn_foreign.append(attn_moving)
    stacked = jnp.stack(attn_foreign)
    attn_found = [(0, 0, stacked)] + plane_gather_stack(plane_gather, stacked)
    attn_found = [(2 * mask, start, part) for mask, start, part in attn_found]
    attn_found = attn_found + [(mask ^ 1, start, swap(part, 1)) for mask, start, part in attn_found]
    for mask, start, part in attn_found:
        owner = rep_rank ^ mask
        for index in range(part.shape[0]):
            attn_full = lax.dynamic_update_slice(
                attn_full,
                part[index][None, None, None],
                (owner // per_matrix, source(start + index + 1), owner % per_matrix, 0, 0),
            )
    query_full = attn_full[0].reshape(width, proj)
    key_full = attn_full[1].reshape(width, proj)
    value_full = attn_full[2].reshape(width, proj)
    out_full = attn_full[3].reshape(proj, width)

    gate_up_own = pick_columns(w_gate, w_up)
    gate_up_parts = [(0, 0, 0, gate_up_own)]
    moving = lax.dynamic_slice_in_dim(gate_up_own, chip * col_piece, col_piece, 1)
    for step in range(1, shards):
        moving = shift(moving)
        gate_up_parts += [
            (step, mask, start, part) for mask, start, part in [(0, 0, moving)] + plane_gather(moving)
        ]

    def gate_up_place(step, mask, start):
        def place(at, chip_at):
            column = 0 if step == 0 else (chip_at ^ mask) * col_piece
            return (at - step) % shards * block + start, column

        return place

    down_own = lax.dynamic_slice_in_dim(w_down, core * down_half, down_half, 0)
    down_parts = [(0, 0, 0, down_own)]
    moving = lax.dynamic_slice_in_dim(down_own, chip * down_piece, down_piece, 0)
    for step in range(1, shards):
        moving = shift(moving)
        down_parts += [
            (step, mask, start, part) for mask, start, part in [(0, 0, moving)] + plane_gather(moving)
        ]

    def down_place(step, mask, start):
        def place(at, chip_at):
            row = start if step == 0 else (chip_at ^ mask) * down_piece + start
            return (at - step) % shards * down_half + row

        return place

    if aligned:
        gate_up_pieces = [part for _, _, _, part in gate_up_parts]
        gate_up_places = [tile_hint(gate_up_place(*where), 16, 128) for *where, _ in gate_up_parts]
        down_pieces = [part for _, _, _, part in down_parts]
        down_places = [row_hint(down_place(*where), 16) for *where, _ in down_parts]
    else:
        whole = jnp.zeros((width, inner), BF16)
        for *where, part in gate_up_parts:
            whole = lax.dynamic_update_slice(whole, part, gate_up_place(*where)(rank, chip))
        gate_up_pieces, gate_up_places = [whole], [lambda at, chip_at: (0, 0)]
        whole = jnp.zeros((half_inner, width), BF16)
        for *where, part in down_parts:
            whole = lax.dynamic_update_slice(whole, part, (down_place(*where)(rank, chip), 0))
        down_pieces, down_places = [whole], [lambda at, chip_at: 0]

    slots = slot_of[:, 0]
    own_slots = lax.dynamic_slice_in_dim(slots, rank * local_rows, local_rows, 1)
    order = (rank - jnp.arange(shards, dtype=jnp.int32)) % shards
    key_slots = jnp.take(slots.reshape(micro_count, shards, local_rows), order, axis=1)
    key_slots = key_slots.reshape(micro_count, group)
    to_slots = (
        key_slots[:, None, :] == jnp.arange(group, dtype=jnp.int32)[None, :, None]
    ).astype(BF16)
    onehot = (buckets[:, None] == jnp.arange(bucket_count, dtype=jnp.int32)[None, :]).astype(F32)
    onehot = jnp.pad(onehot, ((0, 1), (0, 0)))
    bias_rows = jnp.dot(onehot, bias_table.astype(F32), precision=HIGHEST).T
    bias = bias_of_queries(bias_rows, own_slots.reshape(rows), group).reshape(
        heads, micro_count, local_rows, group
    )
    first_len = seq_lengths[:, 0, 0]
    query_seg = own_slots >= first_len[:, None]
    key_seg = jnp.arange(group, dtype=jnp.int32)[None, :] >= first_len[:, None]
    same_seq = (query_seg[:, :, None] == key_seg[:, None, :])[None]

    hidden_in = tokens.reshape(rows, width).astype(F32)
    scale_one = rms_scale(hidden_in)
    normed_one = (hidden_in * scale_one * attn_gain).astype(BF16)
    queries = dot(normed_one, query_full, BF16)
    moving = jnp.concatenate(
        [dot(normed_one, key_full, BF16), dot(normed_one, value_full, BF16)], axis=1
    )
    arrived = [moving]
    for step in range(1, shards):
        moving = shift(moving)
        arrived.append(moving)
    pairs = jnp.stack([part.reshape(micro_count, local_rows, 2 * proj) for part in arrived], axis=1)
    pairs = pairs.reshape(micro_count, group, 2 * proj)
    packed = jnp.einsum("msj,mjc->msc", to_slots, pairs, preferred_element_type=F32).astype(BF16)
    packed = packed.reshape(micro_count, group, 2, heads, head_size)
    keys, values = packed[:, :, 0], packed[:, :, 1]
    queries = queries.reshape(micro_count, local_rows, heads, head_size)
    scores = jnp.einsum("mqhd,mkhd->hmqk", queries, keys, preferred_element_type=F32) + bias
    scores = jnp.where(same_seq, scores, MASKED)
    weights = jnp.exp(scores - jnp.max(scores, axis=-1, keepdims=True))
    probabilities = weights / jnp.sum(weights, axis=-1, keepdims=True)
    rounded = probabilities.astype(BF16)
    context = jnp.einsum("hmqk,mkhd->mqhd", rounded, values, preferred_element_type=F32)
    context = context.astype(BF16).reshape(rows, proj)
    hidden_mid = hidden_in + dot(context, out_full)

    scale_two = rms_scale(hidden_mid)
    normed_two = (hidden_mid * scale_two * ffn_gain).astype(BF16)
    normed_two_other = swap(normed_two, 1)
    gate_slope_act, gate_act, inner_act, gate_up = gate_up_call(
        normed_two, normed_two_other, gate_up_pieces, [("inner", inner)] + gate_up_places
    )
    down_part, down_given, down = down_call(inner_act, down_pieces, down_places)
    hidden_out = hidden_mid + down_part + swap(down_given, 1).astype(F32)
    scale_three = rms_scale(hidden_out)
    delete_norm = hidden_out * scale_three * delete_gain
    sigmoid_val = jax.nn.sigmoid(jnp.sum(delete_norm * delete_vec, axis=-1))
    deleted = -30.0 * sigmoid_val

    gate_upstream = gate_cotangent.reshape(rows).astype(F32)
    gate_slope = gate_upstream * -30.0 * sigmoid_val * (1.0 - sigmoid_val)
    grad_delete_vec = jnp.sum(gate_slope[:, None] * delete_norm, axis=0)
    delete_up = gate_slope[:, None] * delete_vec
    grad_delete_gain = jnp.sum(delete_up * hidden_out * scale_three, axis=0)
    grad_out = cotangent.reshape(rows, width).astype(F32) + rms_back(
        hidden_out, scale_three, delete_gain, delete_up
    )
    down_up = grad_out.astype(BF16)
    down_up_other = swap(down_up, 1)

    def reduce_plan(piece_rows, piece_columns, place):
        middle = cut(piece_rows)
        spans = {"own": (0, piece_rows), "near": (0, piece_rows), "far": (0, piece_rows)}
        spans["top"], spans["low"] = (0, middle), (middle, piece_rows - middle)
        first = shards // 2
        plan = []
        for steps in (range(1, first + 1), range(first + 1, shards + 1)):
            for base in bases:
                for name in used:
                    start, size = spans[name]
                    moves = [
                        (index, place(step % shards, base ^ names[name], start))
                        for index, step in enumerate(steps)
                    ]
                    plan.append(((len(moves), size, piece_columns), moves))
        return plan

    def reduce_run(plan, left, right):
        if aligned:
            buffers = weight_grad_call(left, right, plan)
        else:
            shape = (left[0].shape[1], right[0].shape[1])
            whole = weight_grad_call(
                left, right, [((1,) + shape, [(0, lambda at, chip_at: (0, 0))])]
            )[0][0]
            buffers = []
            for (_, size, columns), moves in plan:
                buffers.append(
                    jnp.stack(
                        [
                            lax.dynamic_slice(whole, place(rank, chip), (size, columns))
                            for _, place in moves
                        ]
                    )
                )
        return buffers

    def reduce_groups(buffers):
        each = len(buffers) // 2
        sums = []
        for group_index in range(2):
            chosen = buffers[group_index * each : (group_index + 1) * each]
            parts = {
                base: dict(zip(used, chosen[i * len(used) : (i + 1) * len(used)]))
                for i, base in enumerate(bases)
            }
            sums.append(plane_reduce(parts, 1))
        return sums

    def ring_of(sums):
        first = sums[0].shape[0]

        def block_of(step):
            step = step if step else shards
            return sums[0][step - 1] if step <= first else sums[1][step - 1 - first]

        return ring_reduce(block_of)

    def down_grad_place(step, mask, start):
        return tile_hint(
            lambda at, chip_at: (
                (at - step) % shards * down_half + (chip_at ^ mask) * down_piece + start,
                0,
            ),
            16,
            128,
        ) if aligned else lambda at, chip_at: (
            (at - step) % shards * down_half + (chip_at ^ mask) * down_piece + start,
            0,
        )

    def gate_up_grad_place(step, mask, start):
        plain = lambda at, chip_at: (
            (at - step) % shards * block + start,
            (chip_at ^ mask) * col_piece,
        )
        return tile_hint(plain, 16, 128) if aligned else plain

    down_buffers = reduce_run(
        reduce_plan(down_piece, width, down_grad_place), (inner_act, None), (down_up, down_up_other)
    )
    both_grad = hidden_grad_call(down_up, down_up_other, down, gate_slope_act, gate_act)
    gate_up_buffers = reduce_run(
        reduce_plan(block, col_piece, gate_up_grad_place),
        (normed_two, normed_two_other),
        (both_grad, None),
    )
    down_sum = ring_of(reduce_groups(down_buffers))
    gate_up_sum = ring_of(reduce_groups(gate_up_buffers))

    partial = jnp.einsum("tf,df->td", both_grad, gate_up, preferred_element_type=F32)
    normed_two_grad = partial[:rows] + swap(partial[rows:].astype(BF16), 1).astype(F32)
    grad_ffn_gain = jnp.sum(normed_two_grad * hidden_mid * scale_two, axis=0)
    grad_mid = grad_out + rms_back(hidden_mid, scale_two, ffn_gain, normed_two_grad)
    out_grad = grad_mid.astype(BF16)
    grad_w_out = jnp.einsum("th,td->hd", context, out_grad, preferred_element_type=F32)
    context_grad = jnp.einsum("td,hd->th", out_grad, out_full, preferred_element_type=F32)
    context_grad = context_grad.astype(BF16).reshape(micro_count, local_rows, heads, head_size)
    prob_grad = jnp.einsum("mqhd,mkhd->hmqk", context_grad, values, preferred_element_type=F32)
    inner_sum = jnp.sum(probabilities * prob_grad, axis=-1, keepdims=True)
    score_grad = (probabilities * (prob_grad - inner_sum)).astype(BF16)
    query_grad = jnp.einsum("hmqk,mkhd->mqhd", score_grad, keys, preferred_element_type=F32)
    query_grad = query_grad.astype(BF16).reshape(rows, proj)
    key_part = jnp.einsum("hmqk,mqhd->mkhd", score_grad, queries, preferred_element_type=F32)
    value_part = jnp.einsum("hmqk,mqhd->mkhd", rounded, context_grad, preferred_element_type=F32)
    pair_part = jnp.concatenate(
        [key_part.reshape(micro_count, group, proj), value_part.reshape(micro_count, group, proj)],
        axis=2,
    ).astype(BF16)
    pair_part = jnp.einsum("msj,msc->mjc", to_slots, pair_part, preferred_element_type=F32)
    pair_part = pair_part.astype(BF16).reshape(micro_count, shards, local_rows, 2 * proj)
    pair_sum = ring_reduce(lambda step: pair_part[:, step].reshape(rows, 2 * proj))
    grad_bias_rows = bias_fold(
        score_grad.reshape(heads, rows, group), own_slots.reshape(rows)
    )
    grad_bias = jnp.einsum("ob,ho->bh", onehot, grad_bias_rows, precision=HIGHEST)

    projected = jnp.concatenate([query_grad, pair_sum], axis=1)
    grad_proj = jnp.einsum("td,th->dh", normed_one, projected, preferred_element_type=F32)
    grad_proj = grad_proj.astype(BF16)
    normed_one_grad = (
        jnp.einsum("th,dh->td", query_grad, query_full, preferred_element_type=F32)
        + jnp.einsum("th,dh->td", pair_sum[:, :proj], key_full, preferred_element_type=F32)
        + jnp.einsum("th,dh->td", pair_sum[:, proj:], value_full, preferred_element_type=F32)
    )
    grad_attn_gain = jnp.sum(normed_one_grad * hidden_in * scale_one, axis=0)
    grad_in = grad_mid + rms_back(hidden_in, scale_one, attn_gain, normed_one_grad)

    attn_grads = jnp.stack(
        [
            grad_proj[:, :proj].reshape(shards, block, proj),
            grad_proj[:, proj : 2 * proj].reshape(shards, block, proj),
            grad_proj[:, 2 * proj :].reshape(shards, block, proj),
            grad_w_out.astype(BF16).reshape(shards, block, proj),
        ],
        axis=1,
    ).reshape(shards, chips, 2, attn_rows, proj)
    attn_grads = jnp.take(attn_grads, order, axis=0)
    kept = lax.dynamic_index_in_dim(attn_grads, core, 2, keepdims=False)
    given = swap(lax.dynamic_index_in_dim(attn_grads, 1 - core, 2, keepdims=False), 1)
    attn_grads = (kept.astype(F32) + given.astype(F32)).astype(BF16)
    middle = cut(shards)
    attn_parts = {}
    for base in bases:
        attn_parts[base] = {}
        for name in used:
            part = lax.dynamic_index_in_dim(
                attn_grads, chip ^ base ^ names[name], 1, keepdims=False
            )
            part = part[:middle] if name == "top" else part[middle:] if name == "low" else part
            attn_parts[base][name] = part
    attn_sum = plane_reduce(attn_parts, 0)
    attn_sum = ring_reduce(lambda step: attn_sum[step])

    gate_up_half = jnp.zeros((block, inner), BF16)
    for mask, start, part in [(0, 0, gate_up_sum)] + plane_gather(gate_up_sum):
        gate_up_half = lax.dynamic_update_slice(
            gate_up_half, part, (start, (chip ^ mask) * col_piece)
        )
    gate_up_other = swap(gate_up_half, 1)
    grad_gate, grad_up = spread_columns(
        jnp.where(core == 0, gate_up_half, gate_up_other),
        jnp.where(core == 0, gate_up_other, gate_up_half),
    )

    down_half_sum = jnp.zeros((down_half, width), BF16)
    for mask, start, part in [(0, 0, down_sum)] + plane_gather(down_sum):
        down_half_sum = lax.dynamic_update_slice(
            down_half_sum, part, ((chip ^ mask) * down_piece + start, 0)
        )
    down_other = swap(down_half_sum, 1)
    grad_down_out = jnp.concatenate(
        [jnp.where(core == 0, down_half_sum, down_other), jnp.where(core == 0, down_other, down_half_sum)]
    ).astype(F32)

    attn_half = jnp.zeros((chips, attn_rows, proj), BF16)
    for mask, start, part in [(0, 0, attn_sum)] + plane_gather(attn_sum):
        attn_half = lax.dynamic_update_slice(attn_half, part[None], (chip ^ mask, start, 0))
    attn_other = swap(attn_half, 1)
    attn_shard = jnp.stack(
        [jnp.where(core == 0, attn_half, attn_other), jnp.where(core == 0, attn_other, attn_half)],
        axis=1,
    ).reshape(4, block, proj).astype(F32)

    small = jnp.concatenate(
        [
            grad_attn_gain.reshape(shards, block),
            grad_ffn_gain.reshape(shards, block),
            grad_delete_gain.reshape(shards, block),
            grad_delete_vec.reshape(shards, block),
            grad_bias.reshape(shards, bucket_rows * heads),
        ],
        axis=1,
    )
    small = jnp.take(small, order, axis=0)
    bit = 1
    while bit < reps:
        small = small + swap(small, bit)
        bit *= 2
    total = small[1:2]
    for step in range(2, shards + 1):
        total = shift(total) + small[step % shards : step % shards + 1]
    total = total.reshape(-1)

    return (
        hidden_out.reshape(micro_count, local_rows, width),
        deleted.reshape(micro_count, local_rows),
        grad_in.astype(BF16).reshape(micro_count, local_rows, width),
        total[:block],
        attn_shard[0],
        attn_shard[1],
        attn_shard[2],
        attn_shard[3].reshape(proj // shards, width),
        total[4 * block :].reshape(bucket_rows, heads),
        total[block : 2 * block],
        grad_gate,
        grad_up,
        grad_down_out,
        total[2 * block : 3 * block],
        total[3 * block : 4 * block],
    )


def plane_gather_stack(plane_gather, stacked):
    return plane_gather(stacked)


def tile_hint(place, row_unit, column_unit):
    def hinted(at, chip_at):
        row, column = place(at, chip_at)
        return pl.multiple_of(row, row_unit), pl.multiple_of(column, column_unit)

    return hinted


def row_hint(place, unit):
    return lambda at, chip_at: pl.multiple_of(place(at, chip_at), unit)


def solution(mesh):
    rows = P(None, ("rep", "shard"), None)
    flat = P(None, ("rep", "shard"))
    by_rep = P(None, "rep", None)
    vector = P("shard")
    matrix = P("shard", None)
    in_specs = (
        (rows, rows, flat, by_rep, by_rep, P(), vector)
        + (matrix,) * 5
        + (vector,)
        + (matrix,) * 3
        + (vector, vector)
    )
    out_specs = (
        (rows, flat, rows, vector) + (matrix,) * 5 + (vector,) + (matrix,) * 3 + (vector, vector)
    )
    return jax.shard_map(
        on_device, mesh=mesh, in_specs=in_specs, out_specs=out_specs, check_vma=False
    )
```

```python
import functools

import math

import jax
import jax.numpy as jnp
from jax import lax
from jax.experimental import pallas as pl
from jax.experimental.pallas import tpu as pltpu
from jax.sharding import PartitionSpec as P

EPSILON = 1e-06
HIGHEST = lax.Precision.HIGHEST
MASKED = -1000000000.0
BF16 = jnp.bfloat16
F32 = jnp.float32


def gelu_tanh(value):
    return jax.nn.gelu(value, approximate=True)


def rms_scale(hidden):
    return lax.rsqrt(jnp.mean(hidden * hidden, axis=-1, keepdims=True) + EPSILON)


def rms_back(hidden, scale_row, gain, upstream):
    scaled = upstream * gain
    return scale_row * scaled - hidden * (scale_row * scale_row * scale_row) * jnp.mean(
        hidden * scaled, axis=-1, keepdims=True
    )


def dot(left, right, kind=F32):
    return jnp.dot(left, right, preferred_element_type=F32).astype(kind)


def bias_kernel(rows_ref, slots_ref, out_ref):
    group = out_ref.shape[2]
    row = jnp.broadcast_to(rows_ref[0], (group, rows_ref.shape[2]))
    grid = pltpu.roll(row, group + 1, 1, stride=1, stride_axis=0)[:, :group].astype(BF16)
    tokens = slots_ref.shape[0]
    pick = (slots_ref[...] == lax.broadcasted_iota(jnp.int32, (tokens, group), 1)).astype(BF16)
    out_ref[0] = jnp.dot(pick, grid, preferred_element_type=F32).astype(BF16)


def bias_of_queries(bias_rows, slots, group):
    heads, width = bias_rows.shape
    tokens = slots.shape[0]
    return pl.pallas_call(
        bias_kernel,
        grid=(heads,),
        in_specs=[
            pl.BlockSpec((1, 1, width), lambda h: (h, 0, 0)),
            pl.BlockSpec((tokens, 1), lambda h: (0, 0)),
        ],
        out_specs=pl.BlockSpec((1, tokens, group), lambda h: (h, 0, 0)),
        out_shape=jax.ShapeDtypeStruct((heads, tokens, group), BF16),
    )(bias_rows.reshape(heads, 1, width), slots.reshape(tokens, 1))


def bias_fold(score_grads, slots):
    heads, local, group = score_grads[0].shape
    count = len(score_grads)

    def kernel(*refs):
        grad_refs, slots_ref, out_ref = refs[:count], refs[count], refs[count + 1]
        square = None
        for index, ref in enumerate(grad_refs):
            mine = slots_ref[:, index * local : (index + 1) * local]
            row = lax.broadcasted_iota(jnp.int32, (group, local), 0)
            place = (row == (group - 1) - mine).astype(BF16)
            part = jnp.dot(place, ref[0], preferred_element_type=F32)
            square = part if square is None else square + part
        wide = jnp.concatenate([square, jnp.zeros_like(square)], axis=1)
        rolled = pltpu.roll(wide, 0, 1, stride=1, stride_axis=0)
        out_ref[0] = jnp.sum(rolled, axis=0, keepdims=True)

    return pl.pallas_call(
        kernel,
        grid=(heads,),
        in_specs=[pl.BlockSpec((1, local, group), lambda h: (h, 0, 0))] * count
        + [pl.BlockSpec((1, count * local), lambda h: (0, 0))],
        out_specs=pl.BlockSpec((1, 1, 2 * group), lambda h: (h, 0, 0)),
        out_shape=jax.ShapeDtypeStruct((heads, 1, 2 * group), F32),
    )(*score_grads, slots.reshape(1, count * local)).reshape(heads, 2 * group)


def by_head(value, head, head_size):
    per_block = 128 // head_size
    start = head // per_block * 128
    lanes = lax.broadcasted_iota(jnp.int32, (1, 128), 1) // head_size
    block = value[:, start : start + 128]
    return jnp.where(lanes == head % per_block, block, jnp.zeros_like(block)), start


def dot_last(left, right):
    return lax.dot_general(left, right, (((1,), (1,)), ((), ())), preferred_element_type=F32)


def attention_call(micro, lengths, queries, pairs, own_slots, key_slots, bias):
    heads, rows, group = bias.shape
    double = pairs[0].shape[1]
    count = len(pairs)
    local = group // count
    proj = double // 2
    head_size = proj // heads

    def kernel(lengths_ref, query_ref, *rest):
        pair_refs = rest[:count]
        own_ref, key_ref, bias_ref, context_ref, prob_ref, packed_ref, arrived = rest[count:]
        for index, ref in enumerate(pair_refs):
            arrived[index * local : (index + 1) * local] = ref[...]
        place = (
            lax.broadcasted_iota(jnp.int32, (group, group), 0) == key_ref[...]
        ).astype(BF16)
        packed_ref[...] = jnp.dot(place, arrived[...], preferred_element_type=F32).astype(BF16)
        first = lengths_ref[0]
        key_seg = lax.broadcasted_iota(jnp.int32, (local, group), 1) >= first
        same = key_seg == (own_ref[...] >= first)
        per_block = 128 // head_size
        total = None
        for head in range(heads):
            query, start = by_head(query_ref[...], head, head_size)
            scores = dot_last(query, packed_ref[:, start : start + 128])
            scores = jnp.where(same, scores + bias_ref[head].astype(F32), MASKED)
            weights = jnp.exp(scores - jnp.max(scores, axis=1, keepdims=True))
            weights = (weights / jnp.sum(weights, axis=1, keepdims=True)).astype(BF16)
            prob_ref[head] = weights
            value, _ = by_head(packed_ref[:, proj:], head, head_size)
            part = jnp.dot(weights, value, preferred_element_type=F32)
            total = part if head % per_block == 0 else total + part
            if head % per_block == per_block - 1:
                context_ref[:, start : start + 128] = total.astype(BF16)

    return pl.pallas_call(
        kernel,
        grid=(1,),
        in_specs=[
            pl.BlockSpec(memory_space=pltpu.SMEM),
            pl.BlockSpec((local, proj), lambda i: (micro, 0)),
        ]
        + [pl.BlockSpec((local, double), lambda i: (micro, 0))] * count
        + [
            pl.BlockSpec((local, 1), lambda i: (micro, 0)),
            pl.BlockSpec((1, group), lambda i: (0, 0)),
            pl.BlockSpec((heads, local, group), lambda i: (0, micro, 0)),
        ],
        out_specs=[
            pl.BlockSpec((local, proj), lambda i: (0, 0)),
            pl.BlockSpec((heads, local, group), lambda i: (0, 0, 0)),
            pl.BlockSpec((group, double), lambda i: (0, 0)),
        ],
        out_shape=[
            jax.ShapeDtypeStruct((local, proj), BF16),
            jax.ShapeDtypeStruct((heads, local, group), BF16),
            jax.ShapeDtypeStruct((group, double), BF16),
        ],
        scratch_shapes=[pltpu.VMEM((group, double), BF16)],
        cost_estimate=pl.CostEstimate(
            flops=2 * group * group * double + 8 * local * group * proj,
            bytes_accessed=4 * group * double + 4 * heads * local * group,
            transcendentals=heads * local * group,
        ),
    )(lengths, queries, *pairs, own_slots, key_slots, bias)


def attention_back_call(micro, queries, context_grad, probs, packed, key_slots, shards):
    heads, local, group = probs.shape
    double = packed.shape[1]
    proj = double // 2
    head_size = proj // heads

    def kernel(query_ref, context_ref, prob_ref, packed_ref, key_ref, score_ref, dq_ref, *rest):
        part_refs, sums = rest[:shards], rest[shards]
        per_block = 128 // head_size
        for head in range(heads):
            context, start = by_head(context_ref[...], head, head_size)
            query, _ = by_head(query_ref[...], head, head_size)
            key, _ = by_head(packed_ref[:, :proj], head, head_size)
            weights = prob_ref[head]
            wide = weights.astype(F32)
            upstream = dot_last(context, packed_ref[:, proj + start : proj + start + 128])
            inner = jnp.sum(wide * upstream, axis=1, keepdims=True)
            grad = (wide * (upstream - inner)).astype(BF16)
            score_ref[head] = grad
            query_part = jnp.dot(grad, key, preferred_element_type=F32)
            key_part = jnp.dot(grad.T, query, preferred_element_type=F32)
            value_part = jnp.dot(weights.T, context, preferred_element_type=F32)
            if head % per_block == 0:
                totals = [query_part, key_part, value_part]
            else:
                totals = [
                    total + part
                    for total, part in zip(totals, (query_part, key_part, value_part))
                ]
            if head % per_block == per_block - 1:
                dq_ref[:, start : start + 128] = totals[0].astype(BF16)
                sums[:, start : start + 128] = totals[1].astype(BF16)
                sums[:, proj + start : proj + start + 128] = totals[2].astype(BF16)
        for index, ref in enumerate(part_refs):
            slots = key_ref[index * local : (index + 1) * local]
            pick = (lax.broadcasted_iota(jnp.int32, (local, group), 1) == slots).astype(BF16)
            ref[...] = jnp.dot(pick, sums[...], preferred_element_type=F32).astype(BF16)

    return pl.pallas_call(
        kernel,
        grid=(1,),
        in_specs=[
            pl.BlockSpec((local, proj), lambda i: (micro, 0)),
            pl.BlockSpec((local, proj), lambda i: (micro, 0)),
            pl.BlockSpec((heads, local, group), lambda i: (0, 0, 0)),
            pl.BlockSpec((group, double), lambda i: (0, 0)),
            pl.BlockSpec((group, 1), lambda i: (0, 0)),
        ],
        out_specs=[
            pl.BlockSpec((heads, local, group), lambda i: (0, 0, 0)),
            pl.BlockSpec((local, proj), lambda i: (0, 0)),
        ]
        + [pl.BlockSpec((local, double), lambda i: (0, 0))] * shards,
        out_shape=[
            jax.ShapeDtypeStruct((heads, local, group), BF16),
            jax.ShapeDtypeStruct((local, proj), BF16),
        ]
        + [jax.ShapeDtypeStruct((local, double), BF16)] * shards,
        scratch_shapes=[pltpu.VMEM((group, double), BF16)],
        cost_estimate=pl.CostEstimate(
            flops=2 * group * group * double + 16 * local * group * proj,
            bytes_accessed=4 * group * double + 4 * heads * local * group,
            transcendentals=0,
        ),
    )(queries, context_grad, probs, packed, key_slots)


def axis_ranks():
    return lax.axis_index("shard"), lax.axis_index("rep") // 2


def gelu_parts(value):
    inner = math.sqrt(2.0 / math.pi)
    square = value * value
    bend = jnp.tanh(inner * value * (1.0 + 0.044715 * square))
    outside = 0.5 * (1.0 + bend)
    slope = outside + 0.5 * value * (1.0 - bend * bend) * (inner * (1.0 + 0.134145 * square))
    return value * outside, slope


def run_copies(copies, sems):
    started = [pltpu.make_async_copy(src, dst, sems.at[i]) for i, (src, dst) in enumerate(copies)]
    for copy in started:
        copy.start()
    return started


ANY = pl.BlockSpec(memory_space=pl.ANY)
VMEM = pl.BlockSpec(memory_space=pltpu.VMEM)


def pick_kernel(gate_ref, up_ref, out_ref):
    core = lax.axis_index("rep") % 2
    inner = gate_ref.shape[1]
    shards = lax.axis_size("shard")
    unit = inner // shards
    half = unit // 2
    for index, ref in enumerate((gate_ref, up_ref)):
        parts = []
        for shard in range(shards):
            low = ref[:, shard * unit : shard * unit + half]
            high = ref[:, shard * unit + half : (shard + 1) * unit]
            parts.append(jnp.where(core == 0, low, high))
        out_ref[:, index * (inner // 2) : (index + 1) * (inner // 2)] = jnp.concatenate(parts, 1)


def pick_columns(w_gate, w_up):
    return pl.pallas_call(
        pick_kernel,
        in_specs=[VMEM, VMEM],
        out_specs=VMEM,
        out_shape=jax.ShapeDtypeStruct(w_gate.shape, BF16),
    )(w_gate, w_up)


def spread_kernel(low_ref, high_ref, gate_ref, up_ref):
    inner = gate_ref.shape[1]
    shards = lax.axis_size("shard")
    half = inner // shards // 2
    for index, ref in enumerate((gate_ref, up_ref)):
        parts = []
        for shard in range(shards):
            start = index * (inner // 2) + shard * half
            parts += [low_ref[:, start : start + half], high_ref[:, start : start + half]]
        ref[...] = jnp.concatenate(parts, 1).astype(F32)


def spread_columns(low, high):
    shape = jax.ShapeDtypeStruct(low.shape, F32)
    return pl.pallas_call(
        spread_kernel,
        in_specs=[VMEM, VMEM],
        out_specs=[VMEM, VMEM],
        out_shape=[shape, shape],
    )(low, high)


def project_call(tokens, gain, pieces, places, block, proj):
    rows, width = tokens.shape
    count = len(pieces)
    moves = 2 * sum(len(place) for place in places)

    def kernel(token_ref, gain_ref, *rest):
        piece_refs = rest[:count]
        normed_ref, query_ref, pair_ref, keep_ref, weights, sems = rest[count:]
        rank, rep = lax.axis_index("shard"), lax.axis_index("rep")
        copies = []
        for ref, place in zip(piece_refs, places):
            for index, where in place:
                source = ref if index is None else ref.at[index]
                for start, size, matrix, row in where(rank, rep):
                    copies.append(
                        (source.at[pl.ds(start, size)], weights.at[matrix, pl.ds(row, size)])
                    )
        copies = run_copies(copies, sems)
        hidden = token_ref[...].astype(F32)
        scale = lax.rsqrt(jnp.mean(hidden * hidden, axis=1, keepdims=True) + EPSILON)
        normed = (hidden * scale * gain_ref[...]).astype(BF16)
        normed_ref[...] = normed
        for copy in copies:
            copy.wait()
        keep = pltpu.make_async_copy(weights, keep_ref, sems.at[moves])
        keep.start()
        query_ref[...] = jnp.dot(normed, weights[0], preferred_element_type=F32).astype(BF16)
        pair_ref[:, :proj] = jnp.dot(normed, weights[1], preferred_element_type=F32).astype(BF16)
        pair_ref[:, proj:] = jnp.dot(normed, weights[2], preferred_element_type=F32).astype(BF16)
        keep.wait()

    return pl.pallas_call(
        kernel,
        in_specs=[VMEM, VMEM] + [ANY] * count,
        out_specs=[VMEM, VMEM, VMEM, ANY],
        out_shape=[
            jax.ShapeDtypeStruct((rows, width), BF16),
            jax.ShapeDtypeStruct((rows, proj), BF16),
            jax.ShapeDtypeStruct((rows, 2 * proj), BF16),
            jax.ShapeDtypeStruct((4, width, proj), BF16),
        ],
        scratch_shapes=[
            pltpu.VMEM((4, width, proj), BF16),
            pltpu.SemaphoreType.DMA((moves + 1,)),
        ],
        cost_estimate=pl.CostEstimate(
            flops=6 * rows * width * proj, bytes_accessed=16 * width * proj, transcendentals=0
        ),
    )(tokens, gain, *pieces)


def project_grad_call(normed, query_grad, pair_grad, out_grads, small, outputs):
    rows, width = normed.shape
    proj = query_grad.shape[1]
    count = len(outputs)
    moves = sum(len(items) for _, items in outputs)

    small_rows = small.shape[1]

    def kernel(normed_ref, query_ref, pair_ref, out_grad_ref, small_ref, *rest):
        out_refs, result, sems = rest[:count], rest[count], rest[count + 1]
        fourth = pltpu.make_async_copy(out_grad_ref, result.at[3], sems.at[2 * moves])
        fourth.start()
        for begin in range(0, width, 256):
            size = min(256, width - begin)
            turned = normed_ref[:, begin : begin + size].T
            for index in range(3):
                right = query_ref[...] if index == 0 else pair_ref[:, (index - 1) * proj : index * proj]
                result[index, begin : begin + size] = jnp.dot(
                    turned, right, preferred_element_type=F32
                ).astype(BF16)
        fourth.wait()
        rank, rep = lax.axis_index("shard"), lax.axis_index("rep")
        copies = []
        for ref, (shape, items) in zip(out_refs, outputs):
            for index, where, step in items:
                matrix, row = where(rank, rep)
                size = shape[-2] - (small_rows if step is not None else 0)
                copies.append((result.at[matrix, pl.ds(row, size)], ref.at[index + (pl.ds(0, size),)]))
                if step is not None:
                    copies.append(
                        (
                            small_ref.at[(rank - step) % lax.axis_size("shard")],
                            ref.at[index + (pl.ds(size, small_rows),)],
                        )
                    )
        for copy in run_copies(copies, sems):
            copy.wait()

    return pl.pallas_call(
        kernel,
        in_specs=[VMEM, VMEM, VMEM, ANY, VMEM],
        out_specs=[ANY] * count,
        out_shape=[jax.ShapeDtypeStruct(shape, BF16) for shape, _ in outputs],
        scratch_shapes=[
            pltpu.VMEM((4, width, proj), BF16),
            pltpu.SemaphoreType.DMA((2 * moves + 1,)),
        ],
        cost_estimate=pl.CostEstimate(
            flops=6 * rows * width * proj, bytes_accessed=16 * width * proj, transcendentals=0
        ),
    )(normed, query_grad, pair_grad, out_grads, small)


def part_of(ref, row, count, columns):
    if (row, count, columns) == (0,) + ref.shape:
        return ref
    return ref.at[pl.ds(row, count), pl.ds(0, columns)]


def gate_up_call(own, other, inner, pieces, moves):
    rows, width = own.shape
    count, steps = len(pieces), len(moves)
    half = inner // 2
    tile = 256

    def kernel(own_ref, other_ref, *rest):
        piece_refs = rest[:count]
        slope_ref, act_ref, hidden_ref, keep_ref, both, weights, sems = rest[count:]
        rank, chip = axis_ranks()
        copies = [(own_ref, both.at[:rows]), (other_ref, both.at[rows:])]
        for piece, row, size, columns, place in moves:
            to_row, to_column = place(rank, chip)
            copies.append(
                (
                    part_of(piece_refs[piece], row, size, columns),
                    weights.at[pl.ds(to_row, size), pl.ds(to_column, columns)],
                )
            )
        for copy in run_copies(copies, sems):
            copy.wait()
        keep = pltpu.make_async_copy(weights, keep_ref, sems.at[steps + 2])
        keep.start()

        def step(index, carry):
            start = pl.multiple_of(index * tile, tile)
            gate = jnp.dot(both[...], weights[:, pl.ds(start, tile)], preferred_element_type=F32)
            up = jnp.dot(
                both[...],
                weights[:, pl.ds(pl.multiple_of(half + start, tile), tile)],
                preferred_element_type=F32,
            )
            act, slope = gelu_parts(gate)
            act_ref[:, pl.ds(start, tile)] = act.astype(BF16)
            slope_ref[:, pl.ds(start, tile)] = (up * slope).astype(BF16)
            hidden_ref[:, pl.ds(start, tile)] = (act * up).astype(BF16)
            return carry

        lax.fori_loop(0, half // tile, step, 0)
        keep.wait()

    shape = jax.ShapeDtypeStruct((2 * rows, half), BF16)
    return pl.pallas_call(
        kernel,
        in_specs=[ANY] * (2 + count),
        out_specs=[VMEM, VMEM, VMEM, ANY],
        out_shape=[shape, shape, shape, jax.ShapeDtypeStruct((width, inner), BF16)],
        scratch_shapes=[
            pltpu.VMEM((2 * rows, width), BF16),
            pltpu.VMEM((width, inner), BF16),
            pltpu.SemaphoreType.DMA((steps + 3,)),
        ],
        cost_estimate=pl.CostEstimate(
            flops=4 * rows * width * inner,
            bytes_accessed=4 * width * inner + 6 * rows * inner,
            transcendentals=rows * inner,
        ),
    )(own, other, *pieces)


def col_tiles(width):
    return [(start, min(512, width - start)) for start in range(0, width, 512)]


def down_call(hidden, width, padded, pieces, moves):
    double, half = hidden.shape
    rows = double // 2
    count, steps = len(pieces), len(moves)

    def kernel(hidden_ref, *rest):
        piece_refs = rest[:count]
        own_ref, other_ref, keep_ref, weights, sems = rest[count:]
        rank, chip = axis_ranks()
        copies = []
        for piece, row, size, columns, place in moves:
            to_row, to_column = place(rank, chip)
            copies.append(
                (
                    part_of(piece_refs[piece], row, size, columns),
                    weights.at[pl.ds(to_row, size), pl.ds(to_column, columns)],
                )
            )
        for copy in run_copies(copies, sems):
            copy.wait()
        keep = pltpu.make_async_copy(weights, keep_ref, sems.at[steps])
        keep.start()
        for start, size in col_tiles(width):
            columns = slice(start, start + size)
            own_ref[:, columns] = jnp.dot(
                hidden_ref[:rows], weights[:, columns], preferred_element_type=F32
            )
            other_ref[:, columns] = jnp.dot(
                hidden_ref[rows:], weights[:, columns], preferred_element_type=F32
            ).astype(BF16)
        keep.wait()

    return pl.pallas_call(
        kernel,
        in_specs=[VMEM] + [ANY] * count,
        out_specs=[VMEM, VMEM, ANY],
        out_shape=[
            jax.ShapeDtypeStruct((rows, width), F32),
            jax.ShapeDtypeStruct((rows, width), BF16),
            jax.ShapeDtypeStruct((half, padded), BF16),
        ],
        scratch_shapes=[pltpu.VMEM((half, padded), BF16), pltpu.SemaphoreType.DMA((steps + 1,))],
        cost_estimate=pl.CostEstimate(
            flops=4 * rows * width * half, bytes_accessed=4 * width * half, transcendentals=0
        ),
    )(hidden, *pieces)


def finish_call(pieces, gate_up_moves, down_moves, block, inner, down_rows, width, padded):
    count = len(pieces)
    steps = len(gate_up_moves) + len(down_moves)

    def kernel(*refs):
        piece_refs = refs[:count]
        gate_ref, up_ref, down_ref, columns_of, rows_of, sems = refs[count:]
        chip, core = axis_ranks()[1], lax.axis_index("rep") % 2
        shards = lax.axis_size("shard")
        copies = []
        for piece, row, size, columns, place in gate_up_moves:
            to_core, to_row, to_column = place(core, chip)
            copies.append(
                (
                    part_of(piece_refs[piece], row, size, columns),
                    columns_of.at[to_core, pl.ds(to_row, size), pl.ds(to_column, columns)],
                )
            )
        for piece, row, size, columns, place in down_moves:
            to_row, to_column = place(core, chip)
            copies.append(
                (
                    part_of(piece_refs[piece], row, size, columns),
                    rows_of.at[pl.ds(to_row, size), pl.ds(to_column, columns)],
                )
            )
        for copy in run_copies(copies, sems):
            copy.wait()
        half = inner // shards // 2
        for index, ref in enumerate((gate_ref, up_ref)):
            for shard in range(shards):
                start = index * (inner // 2) + shard * half
                both = [columns_of[at, :, start : start + half] for at in range(2)]
                ref[:, 2 * half * shard : 2 * half * (shard + 1)] = jnp.concatenate(
                    both, 1
                ).astype(F32)
        down_ref[...] = rows_of[:, :width].astype(F32)

    return pl.pallas_call(
        kernel,
        in_specs=[ANY] * count,
        out_specs=[VMEM] * 3,
        out_shape=[
            jax.ShapeDtypeStruct((block, inner), F32),
            jax.ShapeDtypeStruct((block, inner), F32),
            jax.ShapeDtypeStruct((down_rows, width), F32),
        ],
        scratch_shapes=[
            pltpu.VMEM((2, block, inner), BF16),
            pltpu.VMEM((down_rows, padded), BF16),
            pltpu.SemaphoreType.DMA((steps,)),
        ],
    )(*pieces)


def attn_finish_call(pieces, moves, block, proj):
    count = len(pieces)

    def kernel(*refs):
        piece_refs = refs[:count]
        out_refs, whole, sems = refs[count : count + 4], refs[count + 4], refs[count + 5]
        rep = lax.axis_index("rep")
        copies = []
        for piece, index, place in moves:
            for start, size, matrix, row in place(rep):
                copies.append(
                    (
                        piece_refs[piece].at[index, pl.ds(start, size)],
                        whole.at[matrix, pl.ds(row, size)],
                    )
                )
        for copy in run_copies(copies, sems):
            copy.wait()
        for index, ref in enumerate(out_refs):
            ref[...] = whole[index].astype(F32)

    return pl.pallas_call(
        kernel,
        in_specs=[ANY] * count,
        out_specs=[VMEM] * 4,
        out_shape=[jax.ShapeDtypeStruct((block, proj), F32)] * 4,
        scratch_shapes=[
            pltpu.VMEM((4, block, proj), BF16),
            pltpu.SemaphoreType.DMA((2 * len(moves),)),
        ],
    )(*pieces)


def hidden_grad_call(own, other, down, slope, act):
    rows, width = own.shape
    half = down.shape[0]
    tile = 256

    def kernel(own_ref, other_ref, down_ref, slope_ref, act_ref, out_ref, both, sems):
        for copy in run_copies(
            [(own_ref, both.at[:rows]), (other_ref, both.at[rows:])], sems
        ):
            copy.wait()

        def step(index, carry):
            start = pl.multiple_of(index * tile, tile)
            upstream = lax.dot_general(
                both[...],
                down_ref[pl.ds(start, tile), :width],
                (((1,), (1,)), ((), ())),
                preferred_element_type=F32,
            )
            gate = upstream * slope_ref[:, pl.ds(start, tile)].astype(F32)
            up = upstream * act_ref[:, pl.ds(start, tile)].astype(F32)
            out_ref[:, pl.ds(start, tile)] = gate.astype(BF16)
            out_ref[:, pl.ds(pl.multiple_of(half + start, tile), tile)] = up.astype(BF16)
            return carry

        lax.fori_loop(0, half // tile, step, 0)

    return pl.pallas_call(
        kernel,
        in_specs=[ANY, ANY, VMEM, VMEM, VMEM],
        out_specs=VMEM,
        out_shape=jax.ShapeDtypeStruct((2 * rows, 2 * half), BF16),
        scratch_shapes=[pltpu.VMEM((2 * rows, width), BF16), pltpu.SemaphoreType.DMA((2,))],
        cost_estimate=pl.CostEstimate(
            flops=4 * rows * width * half,
            bytes_accessed=2 * width * half + 16 * rows * half,
            transcendentals=0,
        ),
    )(own, other, down, slope, act)


def weight_grad_call(left, right, outputs):
    left_own, left_other = left
    right_own, right_other = right
    rows = left_own.shape[0]
    depth, width = left_own.shape[1], right_own.shape[1]
    count = len(outputs)
    copies_out = sum(len(moves) for _, moves in outputs)
    split = left_other is not None
    total = 2 * rows if split else rows
    right_split = right_other is not None
    inputs = [left_own] + ([left_other] if split else []) + [right_own]
    inputs += [right_other] if right_split else []

    def kernel(*refs):
        in_refs = list(refs[: len(inputs)])
        out_refs = refs[len(inputs) : len(inputs) + count]
        lefts, rights, result, sems = refs[len(inputs) + count :]
        copies = []
        for target, parted in ((lefts, split), (rights, right_split)):
            first = in_refs.pop(0)
            size = first.shape[0]
            copies.append((first, target.at[:size]))
            if parted:
                copies.append((in_refs.pop(0), target.at[size:]))
        for copy in run_copies(copies, sems):
            copy.wait()
        tile = 512 if width % 512 == 0 else width
        for begin in range(0, depth, 256):
            size = min(256, depth - begin)
            turned = lefts[:, begin : begin + size].T
            if tile == width:
                for start, span in col_tiles(width):
                    result[begin : begin + size, start : start + span] = jnp.dot(
                        turned, rights[:, start : start + span], preferred_element_type=F32
                    ).astype(BF16)
            else:

                def step(index, carry):
                    start = pl.multiple_of(index * tile, tile)
                    result[begin : begin + size, pl.ds(start, tile)] = jnp.dot(
                        turned, rights[:, pl.ds(start, tile)], preferred_element_type=F32
                    ).astype(BF16)
                    return carry

                lax.fori_loop(0, width // tile, step, 0)
        rank, chip = axis_ranks()
        moves_out = []
        for ref, (shape, moves) in zip(out_refs, outputs):
            for index, place in moves:
                row, column = place(rank, chip)
                moves_out.append(
                    (result.at[pl.ds(row, shape[1]), pl.ds(column, shape[2])], ref.at[index])
                )
        for copy in run_copies(moves_out, sems):
            copy.wait()

    return pl.pallas_call(
        kernel,
        in_specs=[ANY] * len(inputs),
        out_specs=[ANY] * count,
        out_shape=[jax.ShapeDtypeStruct(shape, BF16) for shape, _ in outputs],
        scratch_shapes=[
            pltpu.VMEM((total, depth), BF16),
            pltpu.VMEM((total, width), BF16),
            pltpu.VMEM((depth, width), BF16),
            pltpu.SemaphoreType.DMA((max(4, copies_out),)),
        ],
        cost_estimate=pl.CostEstimate(
            flops=2 * total * depth * width,
            bytes_accessed=2 * (depth * width + total * (depth + width)),
            transcendentals=0,
        ),
    )(*inputs)


def on_device(
    tokens,
    cotangent,
    gate_cotangent,
    slot_of,
    seq_lengths,
    buckets,
    gain_attn,
    w_query,
    w_key,
    w_value,
    w_out,
    rel_bias,
    gain_ffn,
    w_gate,
    w_up,
    w_down,
    gain_delete,
    w_delete,
):
    shards = lax.axis_size("shard")
    reps = lax.axis_size("rep")
    chips = reps // 2
    rank = lax.axis_index("shard")
    rep_rank = lax.axis_index("rep")
    core = rep_rank % 2
    chip = rep_rank // 2
    micro_count, local_rows, width = tokens.shape
    group = local_rows * shards
    rows = micro_count * local_rows
    heads = rel_bias.shape[1]
    bucket_rows = rel_bias.shape[0]
    bucket_count = bucket_rows * shards
    proj = w_query.shape[1]
    head_size = proj // heads
    block = gain_attn.shape[0]
    inner = w_gate.shape[1]
    half_inner = inner // 2
    col_piece = inner // chips
    down_block = w_down.shape[0]
    down_half = down_block // 2
    down_piece = down_half // chips
    down_parts_count = -(-width // col_piece)
    padded = -(-width // 128) * 128
    aligned = reps == 8 and block % 16 == 0 and down_piece % 16 == 0 and col_piece % 128 == 0

    def swap(value, mask):
        return lax.ppermute(value, "rep", [(i, i ^ mask) for i in range(reps)])

    def shift(value, by=1):
        return lax.ppermute(value, "shard", [(i, (i + by) % shards) for i in range(shards)])

    def tie(value, moved):
        return lax.optimization_barrier((value, moved))

    def cut(count):
        half = count // 2
        return half // 16 * 16 if half >= 16 else half

    def gather_near(piece):
        if chips == 1:
            return []
        return [swap(piece, 2)] + ([swap(piece, 4)] if chips >= 4 else [])

    def gather_rest(near):
        if chips < 4:
            return []
        middle = cut(near[0].shape[0])
        return [swap(near[1][:middle], 2), swap(near[0][middle:], 4)]

    def gather_list(piece, near, rest):
        middle = cut(piece.shape[0])
        found = [(0, 0, piece)] + [(1 + i, 0, part) for i, part in enumerate(near)]
        found += [(3, i * middle, part) for i, part in enumerate(rest)]
        bit = 4
        while bit < chips:
            found += [
                (mask ^ bit, start, swap(part, 2 * bit)) for mask, start, part in found
            ]
            bit *= 2
        return found

    def plane_gather(piece):
        near = gather_near(piece)
        return gather_list(piece, near, gather_rest(near))

    def add(*values):
        return sum(value.astype(F32) for value in values).astype(BF16)

    def plane_reduce(parts, axis):
        state = reduce_begin(parts, axis)
        return reduce_end(reduce_middle(state, axis))

    def reduce_begin(parts, axis):
        def level(base, bit):
            if bit < 4:
                return lambda name: parts[base][name]
            lower, upper = level(base, bit // 2), level(base ^ bit, bit // 2)
            return lambda name: add(lower(name), swap(upper(name), 2 * bit))

        get = level(0, chips // 2)
        if chips < 4:
            return [get("own")] + ([swap(get("near"), 2)] if chips == 2 else [])
        return [get("own"), get("far"), get("near"), swap(get("top"), 2), swap(get("low"), 4)]

    def reduce_middle(state, axis):
        if chips < 4:
            return state
        own, far, near, top, low = state
        middle = top.shape[axis]

        def pair(value):
            return (
                lax.slice_in_dim(value, 0, middle, axis=axis),
                lax.slice_in_dim(value, middle, value.shape[axis], axis=axis),
            )

        (far_top, far_low), (near_top, near_low) = pair(far), pair(near)
        far = jnp.concatenate([add(far_top, top), far_low], axis)
        near = jnp.concatenate([near_top, add(near_low, low)], axis)
        return [own, swap(far, 4), swap(near, 2)]

    def reduce_end(state):
        return add(*state) if len(state) > 1 else state[0]

    names = {"own": 0, "near": 1, "far": 2, "top": 3, "low": 3}
    bases = [base for base in range(chips) if base & 3 == 0]
    used = ["own", "near", "far", "top", "low"] if chips >= 4 else ["own", "near"][:chips]

    def source(step):
        return (rank - step) % shards

    order = (rank - jnp.arange(shards, dtype=jnp.int32)) % shards
    per_matrix = reps // 4
    attn_rows = block // per_matrix
    if aligned:
        attn_rows = -(-attn_rows // 16) * 16
    last_row = block - attn_rows

    def part_row(part):
        return jnp.minimum(part * attn_rows, last_row)

    attn_own = jnp.stack([w_query, w_key, w_value, w_out.reshape(block, proj)])
    attn_piece = lax.dynamic_slice(
        attn_own,
        (rep_rank // per_matrix, part_row(rep_rank % per_matrix), 0),
        (1, attn_rows, proj),
    )[0]
    vector_pack = jnp.concatenate(
        [gain_attn, gain_ffn, gain_delete, w_delete, rel_bias.reshape(-1)]
    )
    pack_rows = -(-vector_pack.shape[0] // (16 * proj)) * 16
    vector_pack = jnp.pad(vector_pack, (0, pack_rows * proj - vector_pack.shape[0]))
    vector_pack = vector_pack.reshape(pack_rows, proj)
    attn_sent = jnp.concatenate([attn_piece, vector_pack])
    attn_arrived = [shift(attn_sent, step) for step in range(1, shards)]
    vectors = jnp.stack([vector_pack] + [part[attn_rows:] for part in attn_arrived])
    vectors = jnp.take(vectors, order, axis=0).reshape(shards, pack_rows * proj)
    attn_gain = vectors[:, :block].reshape(width).astype(F32)
    ffn_gain = vectors[:, block : 2 * block].reshape(width).astype(F32)
    delete_gain = vectors[:, 2 * block : 3 * block].reshape(width).astype(F32)
    delete_vec = vectors[:, 3 * block : 4 * block].reshape(width).astype(F32)
    bias_table = vectors[:, 4 * block : 4 * block + bucket_rows * heads]
    bias_table = bias_table.reshape(bucket_count, heads)
    stacked = jnp.stack([part[:attn_rows] for part in attn_arrived])

    def pack(gate_up_part, down_part):
        wide = jnp.pad(down_part, ((0, 0), (0, down_parts_count * col_piece - width)))
        cuts = [wide[:, i * col_piece : (i + 1) * col_piece] for i in range(down_parts_count)]
        return jnp.concatenate([gate_up_part] + cuts)

    def overlaps(start, count):
        bounds = [(None, 0, block)] + [
            (i, block + i * down_piece, block + (i + 1) * down_piece)
            for i in range(down_parts_count)
        ]
        found = []
        for part, low, high in bounds:
            first, last = max(low, start), min(high, start + count)
            if first < last:
                found.append((part, first - start, first - low, last - first))
        return found

    def part_columns(part):
        return min(col_piece, padded - part * col_piece)

    gate_up_own = pick_columns(w_gate, w_up)
    down_own = lax.dynamic_slice_in_dim(w_down, core * down_half, down_half, 0)
    packed_own = pack(
        lax.dynamic_slice_in_dim(gate_up_own, chip * col_piece, col_piece, 1),
        lax.dynamic_slice_in_dim(down_own, chip * down_piece, down_piece, 0),
    )
    packed_own, stacked = tie(packed_own, stacked)
    ring = [shift(packed_own)]
    for step in range(2, shards):
        ring.append(shift(ring[-1]))
    attn_plane = [stacked] + [swap(stacked, 2 * mask) for mask in range(1, chips)]
    attn_plane = jnp.stack(attn_plane)
    attn_other = swap(attn_plane, 1)

    def attn_place(mask, flip, step):
        def place(at, rep):
            owner = rep ^ (2 * mask + flip)
            row = (at - step) % shards * block + part_row(owner % per_matrix)
            return owner // per_matrix, pl.multiple_of(row, 16) if aligned else row

        return place

    shared = per_matrix * attn_rows - block

    def split_place(place, flip):
        def places_of(*at):
            matrix, row = place(*at)
            part = (at[-1] ^ flip) % per_matrix
            first = row - last_row * part
            moves = [
                (
                    pl.multiple_of(shared * part, 16),
                    attn_rows - shared,
                    matrix,
                    pl.multiple_of(first + attn_rows * part, 16),
                )
            ]
            if shared and flip == 0:
                moves.append(
                    (
                        pl.multiple_of(last_row * (1 - part), 16),
                        shared,
                        matrix,
                        pl.multiple_of(first + last_row, 16),
                    )
                )
            return moves

        return places_of

    attn_pieces = [w_query, w_key, w_value, attn_own[3]]
    attn_places = [
        [(None, lambda at, rep, matrix=matrix: [(0, block, matrix, pl.multiple_of(at * block, 16))])]
        for matrix in range(4)
    ]
    for flip, found in enumerate((attn_plane, attn_other)):
        attn_pieces.append(found)
        attn_places.append(
            [
                ((mask, step - 1), attn_place(mask, flip, step), flip)
                for mask in range(chips)
                for step in range(1, shards)
            ]
        )
    if not aligned:
        whole = jnp.zeros((4, width, proj), BF16)
        whole = lax.dynamic_update_slice(whole, attn_own, (0, rank * block, 0))
        for piece, place in zip(attn_pieces[4:], attn_places[4:]):
            for index, where, _ in place:
                matrix, row = where(rank, rep_rank)
                whole = lax.dynamic_update_slice(whole, piece[index][None], (matrix, row, 0))
        attn_pieces = [whole[matrix] for matrix in range(4)]
        attn_places = [
            [(None, lambda at, rep, matrix=matrix: [(0, width, matrix, 0)])] for matrix in range(4)
        ]
    else:
        attn_places[4:] = [
            [(index, split_place(where, flip)) for index, where, flip in place]
            for place in attn_places[4:]
        ]

    slots = slot_of[:, 0]
    own_slots = lax.dynamic_slice_in_dim(slots, rank * local_rows, local_rows, 1)
    key_slots = jnp.take(slots.reshape(micro_count, shards, local_rows), order, axis=1)
    key_slots = key_slots.reshape(micro_count, group)
    onehot = (buckets[:, None] == jnp.arange(bucket_count, dtype=jnp.int32)[None, :]).astype(F32)
    onehot = jnp.pad(onehot, ((0, 1), (0, 0)))
    bias_rows = jnp.dot(onehot, bias_table.astype(F32), precision=HIGHEST).T
    bias = bias_of_queries(bias_rows, own_slots.reshape(rows), group)
    first_len = seq_lengths[:, 0, 0]

    hidden_in = tokens.reshape(rows, width).astype(F32)
    scale_one = rms_scale(hidden_in)
    normed_one, queries, own_pairs, attn_full = project_call(
        tokens.reshape(rows, width), attn_gain[None], attn_pieces, attn_places, block, proj
    )
    query_full, key_full, value_full = attn_full[0], attn_full[1], attn_full[2]
    out_full = attn_full[3].reshape(proj, width)

    nears, rests = [], []
    ring[0], attn_plane = tie(ring[0], attn_plane)
    for step in range(1, shards):
        nears.append(gather_near(ring[step - 1]))
        rests.append(gather_rest(nears[-1]))
        if step < shards - 1:
            ring[step], rests = tie(ring[step], rests)
    own_pairs, (ring, nears[0]) = tie(own_pairs, (ring, nears[0]))
    pairs = [own_pairs]
    for step in range(1, shards):
        pairs.append(shift(pairs[-1]))
    pairs, (nears, rests[:-1]) = tie(pairs, (nears, rests[:-1]))
    contexts, probs, packed = [], [], []
    for micro in range(micro_count):
        context, prob, pair = attention_call(
            micro,
            first_len[micro : micro + 1],
            queries,
            pairs,
            own_slots.reshape(rows, 1),
            key_slots[micro : micro + 1],
            bias,
        )
        contexts.append(context)
        probs.append(prob)
        packed.append(pair)
    context = jnp.concatenate(contexts)
    hidden_mid = hidden_in + dot(context, out_full)

    scale_two = rms_scale(hidden_mid)
    normed_two = (hidden_mid * scale_two * ffn_gain).astype(BF16)
    normed_two_other = swap(normed_two, 1)
    pieces = [gate_up_own, jnp.pad(down_own, ((0, 0), (0, padded - width)))]
    gate_up_moves = [(0, 0, block, inner, lambda at, chip_at: (pl.multiple_of(at * block, 16), 0))]
    down_moves = [
        (1, 0, down_half, padded, lambda at, chip_at: (pl.multiple_of(at * down_half, 16), 0))
    ]

    def gate_up_place(step, mask, row):
        return lambda at, chip_at: (
            pl.multiple_of((at - step) % shards * block + row, 16),
            pl.multiple_of((chip_at ^ mask) * col_piece, 128),
        )

    def down_place(step, mask, row, part):
        return lambda at, chip_at: (
            pl.multiple_of((at - step) % shards * down_half + (chip_at ^ mask) * down_piece + row, 16),
            part * col_piece,
        )

    for step in range(1, shards):
        for mask, start, array in gather_list(ring[step - 1], nears[step - 1], rests[step - 1]):
            for part, here, there, size in overlaps(start, array.shape[0]):
                if part is None:
                    gate_up_moves.append(
                        (len(pieces), here, size, col_piece, gate_up_place(step, mask, there))
                    )
                else:
                    down_moves.append(
                        (
                            len(pieces),
                            here,
                            size,
                            part_columns(part),
                            down_place(step, mask, there, part),
                        )
                    )
            pieces.append(array)
    if not aligned:

        def put_together(moves, shape):
            whole = jnp.zeros(shape, BF16)
            for piece, row, size, columns, place in moves:
                value = pieces[piece][row : row + size, :columns]
                whole = lax.dynamic_update_slice(whole, value, place(rank, chip))
            return whole

        pieces = [
            put_together(gate_up_moves, (width, inner)),
            put_together(down_moves, (half_inner, padded)),
        ]
        gate_up_moves = [(0, 0, width, inner, lambda at, chip_at: (0, 0))]
        down_moves = [(1, 0, half_inner, padded, lambda at, chip_at: (0, 0))]
    gate_slope_act, gate_act, inner_act, gate_up = gate_up_call(
        normed_two, normed_two_other, inner, pieces, gate_up_moves
    )
    down_part, down_given, down = down_call(inner_act, width, padded, pieces, down_moves)
    hidden_out = hidden_mid + down_part + swap(down_given, 1).astype(F32)
    scale_three = rms_scale(hidden_out)
    delete_norm = hidden_out * scale_three * delete_gain
    sigmoid_val = jax.nn.sigmoid(jnp.sum(delete_norm * delete_vec, axis=-1))
    deleted = -30.0 * sigmoid_val

    gate_upstream = gate_cotangent.reshape(rows).astype(F32)
    gate_slope = gate_upstream * -30.0 * sigmoid_val * (1.0 - sigmoid_val)
    grad_delete_vec = jnp.sum(gate_slope[:, None] * delete_norm, axis=0)
    delete_up = gate_slope[:, None] * delete_vec
    grad_delete_gain = jnp.sum(delete_up * hidden_out * scale_three, axis=0)
    grad_out = cotangent.reshape(rows, width).astype(F32) + rms_back(
        hidden_out, scale_three, delete_gain, delete_up
    )
    down_up = grad_out.astype(BF16)
    down_up_other = swap(down_up, 1)

    def reduce_plan(piece_rows, piece_columns, place, groups):
        middle = cut(piece_rows)
        spans = {"own": (0, piece_rows), "near": (0, piece_rows), "far": (0, piece_rows)}
        spans["top"], spans["low"] = (0, middle), (middle, piece_rows - middle)
        plan = []
        for steps in groups:
            for base in bases:
                for name in used:
                    start, size = spans[name]
                    moves = [
                        (index, place(step % shards, base ^ names[name], start))
                        for index, step in enumerate(steps)
                    ]
                    plan.append(((len(moves), size, piece_columns), moves))
        return plan

    def reduce_run(plan, left, right):
        if aligned:
            buffers = weight_grad_call(left, right, plan)
        else:
            shape = (left[0].shape[1], right[0].shape[1])
            whole = weight_grad_call(
                left, right, [((1,) + shape, [(0, lambda at, chip_at: (0, 0))])]
            )[0][0]
            buffers = []
            for (_, size, columns), moves in plan:
                buffers.append(
                    jnp.stack(
                        [
                            lax.dynamic_slice(whole, place(rank, chip), (size, columns))
                            for _, place in moves
                        ]
                    )
                )
        return buffers

    def group_parts(buffers, group_index, group_count):
        each = len(buffers) // group_count
        chosen = buffers[group_index * each : (group_index + 1) * each]
        return {
            base: dict(zip(used, chosen[i * len(used) : (i + 1) * len(used)]))
            for i, base in enumerate(bases)
        }

    all_steps = [range(1, shards + 1)]
    two_steps = [range(1, shards // 2 + 1), range(shards // 2 + 1, shards + 1)]

    def send_blocks(state, steps):
        sent = []
        for index, step in enumerate(steps):
            total = reduce_end([value[index] for value in state])
            sent.append(shift(total, -step) if step < shards else total)
        return sent

    def down_grad_place(step, mask, start):
        return tile_hint(
            lambda at, chip_at: (
                (at - step) % shards * down_half + (chip_at ^ mask) * down_piece + start,
                0,
            ),
            16,
            128,
        ) if aligned else lambda at, chip_at: (
            (at - step) % shards * down_half + (chip_at ^ mask) * down_piece + start,
            0,
        )

    def gate_up_grad_place(step, mask, start):
        plain = lambda at, chip_at: (
            (at - step) % shards * block + start,
            (chip_at ^ mask) * col_piece,
        )
        return tile_hint(plain, 16, 128) if aligned else plain

    down_buffers = reduce_run(
        reduce_plan(down_piece, width, down_grad_place, all_steps),
        (inner_act, None),
        (down_up, down_up_other),
    )
    down_state = reduce_begin(group_parts(down_buffers, 0, 1), 1)
    both_grad = hidden_grad_call(down_up, down_up_other, down, gate_slope_act, gate_act)
    both_grad, down_state = tie(both_grad, down_state)
    gate_up_buffers = reduce_run(
        reduce_plan(block, col_piece, gate_up_grad_place, two_steps),
        (normed_two, normed_two_other),
        (both_grad, None),
    )
    down_state = reduce_middle(down_state, 1)
    partial = jnp.einsum("tf,df->td", both_grad, gate_up, preferred_element_type=F32)
    gate_up_state = reduce_begin(group_parts(gate_up_buffers, 0, 2), 1)
    partial_given = swap(partial[rows:].astype(BF16), 1)
    partial_given, down_state = tie(partial_given, down_state)
    normed_two_grad = partial[:rows] + partial_given.astype(F32)
    grad_ffn_gain = jnp.sum(normed_two_grad * hidden_mid * scale_two, axis=0)
    grad_mid = grad_out + rms_back(hidden_mid, scale_two, ffn_gain, normed_two_grad)
    out_grad = grad_mid.astype(BF16)
    grad_w_out = jnp.einsum("th,td->hd", context, out_grad, preferred_element_type=F32)
    context_grad = jnp.einsum("td,hd->th", out_grad, out_full, preferred_element_type=F32)
    context_grad = context_grad.astype(BF16)
    down_sent = send_blocks(down_state, all_steps[0])
    context_grad, gate_up_state = tie(context_grad, gate_up_state)
    gate_up_state = reduce_middle(gate_up_state, 1)
    score_grads, query_grads, pair_parts = [], [], []
    for micro in range(micro_count):
        score_grad, query_grad, *parts = attention_back_call(
            micro,
            queries,
            context_grad,
            probs[micro],
            packed[micro],
            key_slots[micro].reshape(group, 1),
            shards,
        )
        score_grads.append(score_grad)
        query_grads.append(query_grad)
        pair_parts.append(parts)
    pair_parts = [jnp.concatenate(parts) for parts in zip(*pair_parts)]
    pair_parts, down_sent = tie(pair_parts, down_sent)
    pair_sent = [shift(pair_parts[step], -step) for step in range(1, shards)]
    pair_sent, gate_up_state = tie(pair_sent, gate_up_state)
    gate_up_later = reduce_begin(group_parts(gate_up_buffers, 1, 2), 1)
    gate_up_sent = send_blocks(gate_up_state, two_steps[0])
    pair_sum = add(pair_parts[0], *pair_sent)
    down_sum = add(*down_sent)
    query_grad = jnp.concatenate(query_grads)
    grad_bias_rows = bias_fold(score_grads, own_slots.reshape(rows))
    grad_bias = jnp.einsum("ob,ho->bh", onehot, grad_bias_rows, precision=HIGHEST)

    normed_one_grad = (
        jnp.einsum("th,dh->td", query_grad, query_full, preferred_element_type=F32)
        + jnp.einsum("th,dh->td", pair_sum[:, :proj], key_full, preferred_element_type=F32)
        + jnp.einsum("th,dh->td", pair_sum[:, proj:], value_full, preferred_element_type=F32)
    )
    grad_attn_gain = jnp.sum(normed_one_grad * hidden_in * scale_one, axis=0)
    grad_in = grad_mid + rms_back(hidden_in, scale_one, attn_gain, normed_one_grad)

    small = jnp.concatenate(
        [
            grad_attn_gain.reshape(shards, block),
            grad_ffn_gain.reshape(shards, block),
            grad_delete_gain.reshape(shards, block),
            grad_delete_vec.reshape(shards, block),
            grad_bias.reshape(shards, bucket_rows * heads),
        ],
        axis=1,
    ).astype(BF16)
    small = jnp.pad(small, ((0, 0), (0, pack_rows * proj - small.shape[1])))
    small = small.reshape(shards, pack_rows, proj)

    out_grads = grad_w_out.astype(BF16).reshape(width, proj)
    attn_plan = [
        (
            (chips, shards, attn_rows + pack_rows, proj),
            [
                ((mask, step), attn_place(mask, flip, step), step)
                for mask in range(chips)
                for step in range(shards)
            ],
        )
        for flip in range(2)
    ]
    if aligned:
        kept, given = project_grad_call(
            normed_one, query_grad, pair_sum, out_grads, small, attn_plan
        )
    else:
        whole_plan = [
            (
                (4, width, proj),
                [((matrix,), lambda at, rep, matrix=matrix: (matrix, 0), None) for matrix in range(4)],
            )
        ]
        whole = project_grad_call(
            normed_one, query_grad, pair_sum, out_grads, small, whole_plan
        )[0]
        kept, given = [
            jnp.stack(
                [
                    jnp.concatenate(
                        [
                            lax.dynamic_slice(
                                whole, where(rank, rep_rank) + (0,), (1, attn_rows, proj)
                            )[0],
                            lax.dynamic_index_in_dim(small, source(step), 0, keepdims=False),
                        ]
                    )
                    for _, where, step in items
                ]
            ).reshape(shape)
            for shape, items in attn_plan
        ]
    given = swap(given, 1)
    given, gate_up_later = tie(given, gate_up_later)
    gate_up_later = reduce_middle(gate_up_later, 1)
    attn_own_sum = add(kept[0], given[0])
    attn_send = [add(kept[mask], given[mask]) for mask in range(1, chips)]
    attn_send, (gate_up_later, gate_up_sent) = tie(attn_send, (gate_up_later, gate_up_sent))
    attn_found = [swap(part, 2 * mask + 2) for mask, part in enumerate(attn_send)]
    gate_up_sent = gate_up_sent + send_blocks(gate_up_later, two_steps[1])
    attn_sum = add(attn_own_sum, *attn_found)
    attn_sum = add(attn_sum[0], *[shift(attn_sum[step], -step) for step in range(1, shards)])
    gate_up_sum = add(*gate_up_sent)
    total = attn_sum[attn_rows:].astype(F32).reshape(-1)
    attn_sum = attn_sum[:attn_rows]

    packed_sum = pack(gate_up_sum, down_sum)
    found = plane_gather(packed_sum)
    pieces, gate_up_moves, down_moves = [], [], []

    def gate_up_to(flip, mask, row):
        return lambda core_at, chip_at: (
            core_at ^ flip,
            row,
            pl.multiple_of((chip_at ^ mask) * col_piece, 128),
        )

    def down_to(flip, mask, row, part):
        return lambda core_at, chip_at: (
            pl.multiple_of((core_at ^ flip) * down_half + (chip_at ^ mask) * down_piece + row, 16),
            part * col_piece,
        )

    for flip in range(2):
        for mask, start, array in found:
            array = swap(array, 1) if flip else array
            for part, here, there, size in overlaps(start, array.shape[0]):
                if part is None:
                    gate_up_moves.append(
                        (len(pieces), here, size, col_piece, gate_up_to(flip, mask, there))
                    )
                else:
                    down_moves.append(
                        (
                            len(pieces),
                            here,
                            size,
                            part_columns(part),
                            down_to(flip, mask, there, part),
                        )
                    )
            pieces.append(array)
    if aligned:
        grad_gate, grad_up, grad_down_out = finish_call(
            pieces, gate_up_moves, down_moves, block, inner, down_block, width, padded
        )
    else:
        halves = jnp.zeros((2, block, inner), BF16)
        for piece, row, size, columns, place in gate_up_moves:
            value = pieces[piece][None, row : row + size, :columns]
            halves = lax.dynamic_update_slice(halves, value, place(core, chip))
        whole = jnp.zeros((down_block, padded), BF16)
        for piece, row, size, columns, place in down_moves:
            value = pieces[piece][row : row + size, :columns]
            whole = lax.dynamic_update_slice(whole, value, place(core, chip))
        grad_gate, grad_up = spread_columns(halves[0], halves[1])
        grad_down_out = whole[:, :width].astype(F32)

    attn_half = jnp.stack([attn_sum] + [swap(attn_sum, 2 * mask) for mask in range(1, chips)])
    attn_found = [attn_half, swap(attn_half, 1)]

    def attn_to(mask, flip):
        def place(rep):
            owner = rep ^ (2 * mask + flip)
            row = part_row(owner % per_matrix)
            return owner // per_matrix, pl.multiple_of(row, 16) if aligned else row

        return place

    attn_moves = [(flip, mask, attn_to(mask, flip)) for flip in range(2) for mask in range(chips)]
    if aligned:
        attn_moves = [
            (flip, mask, split_place(place, flip)) for flip, mask, place in attn_moves
        ]
        attn_shard = attn_finish_call(attn_found, attn_moves, block, proj)
    else:
        attn_shard = jnp.zeros((4, block, proj), BF16)
        for piece, index, place in attn_moves:
            attn_shard = lax.dynamic_update_slice(
                attn_shard, attn_found[piece][index][None], place(rep_rank) + (0,)
            )
        attn_shard = attn_shard.astype(F32)

    return (
        hidden_out.reshape(micro_count, local_rows, width),
        deleted.reshape(micro_count, local_rows),
        grad_in.astype(BF16).reshape(micro_count, local_rows, width),
        total[:block],
        attn_shard[0],
        attn_shard[1],
        attn_shard[2],
        attn_shard[3].reshape(proj // shards, width),
        total[4 * block : 4 * block + bucket_rows * heads].reshape(bucket_rows, heads),
        total[block : 2 * block],
        grad_gate,
        grad_up,
        grad_down_out,
        total[2 * block : 3 * block],
        total[3 * block : 4 * block],
    )


def tile_hint(place, row_unit, column_unit):
    def hinted(at, chip_at):
        row, column = place(at, chip_at)
        return pl.multiple_of(row, row_unit), pl.multiple_of(column, column_unit)

    return hinted


def solution(mesh):
    rows = P(None, ("rep", "shard"), None)
    flat = P(None, ("rep", "shard"))
    by_rep = P(None, "rep", None)
    vector = P("shard")
    matrix = P("shard", None)
    in_specs = (
        (rows, rows, flat, by_rep, by_rep, P(), vector)
        + (matrix,) * 5
        + (vector,)
        + (matrix,) * 3
        + (vector, vector)
    )
    out_specs = (
        (rows, flat, rows, vector) + (matrix,) * 5 + (vector,) + (matrix,) * 3 + (vector, vector)
    )
    return jax.shard_map(
        on_device, mesh=mesh, in_specs=in_specs, out_specs=out_specs, check_vma=False
    )
```

```python
import functools

import math

import jax
import jax.numpy as jnp
from jax import lax
from jax.experimental import pallas as pl
from jax.experimental.pallas import tpu as pltpu
from jax.sharding import PartitionSpec as P

EPSILON = 1e-06
HIGHEST = lax.Precision.HIGHEST
MASKED = -1000000000.0
BF16 = jnp.bfloat16
LIGHT = pl.CostEstimate(flops=1000, bytes_accessed=1000, transcendentals=0)
F32 = jnp.float32


ANY = pl.BlockSpec(memory_space=pl.ANY)
VMEM = pl.BlockSpec(memory_space=pltpu.VMEM)


def rms_scale(hidden):
    return lax.rsqrt(jnp.mean(hidden * hidden, axis=-1, keepdims=True) + EPSILON)


def rms_back(hidden, scale_row, gain, upstream):
    scaled = upstream * gain
    return scale_row * scaled - hidden * (scale_row * scale_row * scale_row) * jnp.mean(
        hidden * scaled, axis=-1, keepdims=True
    )


def bias_kernel(rows_ref, slots_ref, out_ref):
    group = out_ref.shape[2]
    row = jnp.broadcast_to(rows_ref[0], (group, rows_ref.shape[2]))
    grid = pltpu.roll(row, group + 1, 1, stride=1, stride_axis=0)[:, :group].astype(BF16)
    tokens = slots_ref.shape[0]
    pick = (slots_ref[...] == lax.broadcasted_iota(jnp.int32, (tokens, group), 1)).astype(BF16)
    out_ref[0] = jnp.dot(pick, grid, preferred_element_type=F32).astype(BF16)


def bias_of_queries(bias_rows, slots, group):
    heads, width = bias_rows.shape
    tokens = slots.shape[0]
    return pl.pallas_call(
        bias_kernel,
        grid=(heads,),
        in_specs=[
            pl.BlockSpec((1, 1, width), lambda h: (h, 0, 0)),
            pl.BlockSpec((tokens, 1), lambda h: (0, 0)),
        ],
        out_specs=pl.BlockSpec((1, tokens, group), lambda h: (h, 0, 0)),
        out_shape=jax.ShapeDtypeStruct((heads, tokens, group), BF16),
    )(bias_rows.reshape(heads, 1, width), slots.reshape(tokens, 1))


def bias_fold(score_grads, slots):
    heads, local, group = score_grads[0].shape
    count = len(score_grads)

    def kernel(*refs):
        grad_refs, slots_ref, out_ref = refs[:count], refs[count], refs[count + 1]
        square = None
        for index, ref in enumerate(grad_refs):
            mine = slots_ref[:, index * local : (index + 1) * local]
            row = lax.broadcasted_iota(jnp.int32, (group, local), 0)
            place = (row == (group - 1) - mine).astype(BF16)
            part = jnp.dot(place, ref[0], preferred_element_type=F32)
            square = part if square is None else square + part
        wide = jnp.concatenate([square, jnp.zeros_like(square)], axis=1)
        rolled = pltpu.roll(wide, 0, 1, stride=1, stride_axis=0)
        out_ref[0] = jnp.sum(rolled, axis=0, keepdims=True)

    return pl.pallas_call(
        kernel,
        grid=(heads,),
        in_specs=[pl.BlockSpec((1, local, group), lambda h: (h, 0, 0))] * count
        + [pl.BlockSpec((1, count * local), lambda h: (0, 0))],
        out_specs=pl.BlockSpec((1, 1, 2 * group), lambda h: (h, 0, 0)),
        out_shape=jax.ShapeDtypeStruct((heads, 1, 2 * group), F32),
    )(*score_grads, slots.reshape(1, count * local)).reshape(heads, 2 * group)


def by_head(value, head, head_size):
    per_block = 128 // head_size
    start = head // per_block * 128
    lanes = lax.broadcasted_iota(jnp.int32, (1, 128), 1) // head_size
    block = value[:, start : start + 128]
    return jnp.where(lanes == head % per_block, block, jnp.zeros_like(block)), start


def dot_last(left, right):
    return lax.dot_general(left, right, (((1,), (1,)), ((), ())), preferred_element_type=F32)


def attention_call(micro, lengths, queries, pairs, own_slots, key_slots, bias, context):
    heads, rows, group = bias.shape
    double = pairs[0].shape[1]
    count = len(pairs)
    local = group // count
    proj = double // 2
    head_size = proj // heads

    def kernel(lengths_ref, query_ref, *rest):
        pair_refs = rest[:count]
        own_ref, key_ref, bias_ref = rest[count : count + 3]
        context_ref, prob_ref, packed_ref, arrived = rest[-4:]
        for index, ref in enumerate(pair_refs):
            arrived[index * local : (index + 1) * local] = ref[...]
        place = (
            lax.broadcasted_iota(jnp.int32, (group, group), 0) == key_ref[...]
        ).astype(BF16)
        packed_ref[...] = jnp.dot(place, arrived[...], preferred_element_type=F32).astype(BF16)
        first = lengths_ref[0]
        key_seg = lax.broadcasted_iota(jnp.int32, (local, group), 1) >= first
        same = key_seg == (own_ref[...] >= first)
        per_block = 128 // head_size
        total = None
        for head in range(heads):
            query, start = by_head(query_ref[...], head, head_size)
            scores = dot_last(query, packed_ref[:, start : start + 128])
            scores = jnp.where(same, scores + bias_ref[head].astype(F32), MASKED)
            weights = jnp.exp(scores - jnp.max(scores, axis=1, keepdims=True))
            weights = (weights / jnp.sum(weights, axis=1, keepdims=True)).astype(BF16)
            prob_ref[head] = weights
            value, _ = by_head(packed_ref[:, proj:], head, head_size)
            part = jnp.dot(weights, value, preferred_element_type=F32)
            total = part if head % per_block == 0 else total + part
            if head % per_block == per_block - 1:
                context_ref[:, start : start + 128] = total.astype(BF16)

    return pl.pallas_call(
        kernel,
        grid=(1,),
        in_specs=[
            pl.BlockSpec(memory_space=pltpu.SMEM),
            pl.BlockSpec((local, proj), lambda i: (micro, 0)),
        ]
        + [pl.BlockSpec((local, double), lambda i: (micro, 0))] * count
        + [
            pl.BlockSpec((local, 1), lambda i: (micro, 0)),
            pl.BlockSpec((1, group), lambda i: (0, 0)),
            pl.BlockSpec((heads, local, group), lambda i: (0, micro, 0)),
        ]
        + [ANY] * len(context),
        out_specs=[
            pl.BlockSpec((local, proj), lambda i: (micro, 0)),
            pl.BlockSpec((heads, local, group), lambda i: (0, 0, 0)),
            pl.BlockSpec((group, double), lambda i: (0, 0)),
        ],
        out_shape=[
            jax.ShapeDtypeStruct(queries.shape, BF16),
            jax.ShapeDtypeStruct((heads, local, group), BF16),
            jax.ShapeDtypeStruct((group, double), BF16),
        ],
        input_output_aliases={count + 5: 0} if context else {},
        scratch_shapes=[pltpu.VMEM((group, double), BF16)],
        cost_estimate=LIGHT,
    )(lengths, queries, *pairs, own_slots, key_slots, bias, *context)


def attention_back_call(micro, queries, context_grad, probs, packed, key_slots, shards, sums):
    heads, local, group = probs.shape
    double = packed.shape[1]
    proj = double // 2
    head_size = proj // heads

    def kernel(query_ref, context_ref, prob_ref, packed_ref, key_ref, *rest):
        score_ref, dq_ref, part_ref, sums = rest[-4:]
        per_block = 128 // head_size
        for head in range(heads):
            context, start = by_head(context_ref[...], head, head_size)
            query, _ = by_head(query_ref[...], head, head_size)
            key, _ = by_head(packed_ref[:, :proj], head, head_size)
            weights = prob_ref[head]
            wide = weights.astype(F32)
            upstream = dot_last(context, packed_ref[:, proj + start : proj + start + 128])
            inner = jnp.sum(wide * upstream, axis=1, keepdims=True)
            grad = (wide * (upstream - inner)).astype(BF16)
            score_ref[head] = grad
            query_part = jnp.dot(grad, key, preferred_element_type=F32)
            key_part = jnp.dot(grad.T, query, preferred_element_type=F32)
            value_part = jnp.dot(weights.T, context, preferred_element_type=F32)
            if head % per_block == 0:
                totals = [query_part, key_part, value_part]
            else:
                totals = [
                    total + part
                    for total, part in zip(totals, (query_part, key_part, value_part))
                ]
            if head % per_block == per_block - 1:
                dq_ref[:, start : start + 128] = totals[0].astype(BF16)
                sums[:, start : start + 128] = totals[1].astype(BF16)
                sums[:, proj + start : proj + start + 128] = totals[2].astype(BF16)
        for index in range(shards):
            slots = key_ref[index * local : (index + 1) * local]
            pick = (lax.broadcasted_iota(jnp.int32, (local, group), 1) == slots).astype(BF16)
            part_ref[index] = jnp.dot(pick, sums[...], preferred_element_type=F32).astype(BF16)

    return pl.pallas_call(
        kernel,
        grid=(1,),
        in_specs=[
            pl.BlockSpec((local, proj), lambda i: (micro, 0)),
            pl.BlockSpec((local, proj), lambda i: (micro, 0)),
            pl.BlockSpec((heads, local, group), lambda i: (0, 0, 0)),
            pl.BlockSpec((group, double), lambda i: (0, 0)),
            pl.BlockSpec((group, 1), lambda i: (0, 0)),
        ]
        + [ANY] * len(sums),
        out_specs=[
            pl.BlockSpec((heads, local, group), lambda i: (0, 0, 0)),
            pl.BlockSpec((local, proj), lambda i: (micro, 0)),
            pl.BlockSpec((shards, local, double), lambda i: (0, micro, 0)),
        ],
        out_shape=[
            jax.ShapeDtypeStruct((heads, local, group), BF16),
            jax.ShapeDtypeStruct(queries.shape, BF16),
            jax.ShapeDtypeStruct((shards, queries.shape[0], double), BF16),
        ],
        input_output_aliases={5 + i: 1 + i for i in range(len(sums))},
        scratch_shapes=[pltpu.VMEM((group, double), BF16)],
        cost_estimate=LIGHT,
    )(queries, context_grad, probs, packed, key_slots, *sums)


def axis_ranks():
    return lax.axis_index("shard"), lax.axis_index("rep") // 2


def gelu_parts(value):
    inner = math.sqrt(2.0 / math.pi)
    square = value * value
    bend = jnp.tanh(inner * value * (1.0 + 0.044715 * square))
    outside = 0.5 * (1.0 + bend)
    slope = outside + 0.5 * value * (1.0 - bend * bend) * (inner * (1.0 + 0.134145 * square))
    return value * outside, slope


def run_copies(copies, sems):
    started = [pltpu.make_async_copy(src, dst, sems.at[i]) for i, (src, dst) in enumerate(copies)]
    for copy in started:
        copy.start()
    return started


def pick_kernel(gate_ref, up_ref, out_ref):
    core = lax.axis_index("rep") % 2
    inner = gate_ref.shape[1]
    shards = lax.axis_size("shard")
    unit = inner // shards
    half = unit // 2
    for index, ref in enumerate((gate_ref, up_ref)):
        parts = []
        for shard in range(shards):
            low = ref[:, shard * unit : shard * unit + half]
            high = ref[:, shard * unit + half : (shard + 1) * unit]
            parts.append(jnp.where(core == 0, low, high))
        out_ref[:, index * (inner // 2) : (index + 1) * (inner // 2)] = jnp.concatenate(parts, 1)


def pick_columns(w_gate, w_up):
    return pl.pallas_call(
        pick_kernel,
        in_specs=[VMEM, VMEM],
        out_specs=VMEM,
        out_shape=jax.ShapeDtypeStruct(w_gate.shape, BF16),
    )(w_gate, w_up)


def spread_kernel(low_ref, high_ref, gate_ref, up_ref):
    inner = gate_ref.shape[1]
    shards = lax.axis_size("shard")
    half = inner // shards // 2
    for index, ref in enumerate((gate_ref, up_ref)):
        parts = []
        for shard in range(shards):
            start = index * (inner // 2) + shard * half
            parts += [low_ref[:, start : start + half], high_ref[:, start : start + half]]
        ref[...] = jnp.concatenate(parts, 1).astype(F32)


def spread_columns(low, high):
    shape = jax.ShapeDtypeStruct(low.shape, F32)
    return pl.pallas_call(
        spread_kernel,
        in_specs=[VMEM, VMEM],
        out_specs=[VMEM, VMEM],
        out_shape=[shape, shape],
    )(low, high)


def project_call(tokens, gain, pieces, places, block, proj):
    rows, width = tokens.shape
    count = len(pieces)
    moves = 2 * sum(len(place) for place in places)

    def kernel(token_ref, gain_ref, *rest):
        piece_refs = rest[:count]
        normed_ref, query_ref, pair_ref, keep_ref, weights, sems = rest[count:]
        rank, rep = lax.axis_index("shard"), lax.axis_index("rep")
        copies = []
        for ref, place in zip(piece_refs, places):
            for index, where in place:
                source = ref if index is None else ref.at[index]
                for start, size, matrix, row in where(rank, rep):
                    copies.append(
                        (source.at[pl.ds(start, size)], weights.at[matrix, pl.ds(row, size)])
                    )
        copies = run_copies(copies, sems)
        hidden = token_ref[...].astype(F32)
        scale = lax.rsqrt(jnp.mean(hidden * hidden, axis=1, keepdims=True) + EPSILON)
        normed = (hidden * scale * gain_ref[...]).astype(BF16)
        normed_ref[...] = normed
        for copy in copies:
            copy.wait()
        keep = pltpu.make_async_copy(weights, keep_ref, sems.at[moves])
        keep.start()
        query_ref[...] = jnp.dot(normed, weights[0], preferred_element_type=F32).astype(BF16)
        pair_ref[:, :proj] = jnp.dot(normed, weights[1], preferred_element_type=F32).astype(BF16)
        pair_ref[:, proj:] = jnp.dot(normed, weights[2], preferred_element_type=F32).astype(BF16)
        keep.wait()

    return pl.pallas_call(
        kernel,
        in_specs=[VMEM, VMEM] + [ANY] * count,
        out_specs=[VMEM, VMEM, VMEM, ANY],
        out_shape=[
            jax.ShapeDtypeStruct((rows, width), BF16),
            jax.ShapeDtypeStruct((rows, proj), BF16),
            jax.ShapeDtypeStruct((rows, 2 * proj), BF16),
            jax.ShapeDtypeStruct((4, width, proj), BF16),
        ],
        scratch_shapes=[
            pltpu.VMEM((4, width, proj), BF16),
            pltpu.SemaphoreType.DMA((moves + 1,)),
        ],
        cost_estimate=LIGHT,
    )(tokens, gain, *pieces)


def project_grad_call(normed, query_grad, pair_grad, out_grads, small, outputs):
    rows, width = normed.shape
    proj = query_grad.shape[1]
    count = len(outputs)
    moves = sum(len(items) for _, items in outputs)

    small_rows = small.shape[1]

    def kernel(normed_ref, query_ref, pair_ref, out_grad_ref, small_ref, *rest):
        out_refs, result, sems = rest[:count], rest[count], rest[count + 1]
        fourth = pltpu.make_async_copy(out_grad_ref, result.at[3], sems.at[2 * moves])
        fourth.start()
        for begin in range(0, width, 256):
            size = min(256, width - begin)
            turned = normed_ref[:, begin : begin + size].T
            for index in range(3):
                right = query_ref[...] if index == 0 else pair_ref[:, (index - 1) * proj : index * proj]
                result[index, begin : begin + size] = jnp.dot(
                    turned, right, preferred_element_type=F32
                ).astype(BF16)
        fourth.wait()
        rank, rep = lax.axis_index("shard"), lax.axis_index("rep")
        copies = []
        for ref, (shape, items) in zip(out_refs, outputs):
            for index, where, step in items:
                matrix, row = where(rank, rep)
                size = shape[-2] - (small_rows if step is not None else 0)
                copies.append((result.at[matrix, pl.ds(row, size)], ref.at[index + (pl.ds(0, size),)]))
                if step is not None:
                    copies.append(
                        (
                            small_ref.at[step],
                            ref.at[index + (pl.ds(size, small_rows),)],
                        )
                    )
        for copy in run_copies(copies, sems):
            copy.wait()

    return pl.pallas_call(
        kernel,
        in_specs=[VMEM, VMEM, VMEM, ANY, VMEM],
        out_specs=[ANY] * count,
        out_shape=[jax.ShapeDtypeStruct(shape, BF16) for shape, _ in outputs],
        scratch_shapes=[
            pltpu.VMEM((4, width, proj), BF16),
            pltpu.SemaphoreType.DMA((2 * moves + 1,)),
        ],
        cost_estimate=LIGHT,
    )(normed, query_grad, pair_grad, out_grads, small)


def part_of(ref, row, count, columns):
    if (row, count, columns) == (0,) + ref.shape:
        return ref
    return ref.at[pl.ds(row, count), pl.ds(0, columns)]


def gate_up_call(own, other, width, inner, pieces, moves):
    rows, wide = own.shape
    count, steps = len(pieces), len(moves)
    half = inner // 2
    tile = 256

    def kernel(own_ref, other_ref, *rest):
        piece_refs = rest[:count]
        slope_ref, act_ref, hidden_ref, keep_ref, both, weights, sems = rest[count:]
        rank, chip = axis_ranks()
        copies = [(own_ref, both.at[:rows]), (other_ref, both.at[rows:])]
        for piece, row, size, columns, place in moves:
            to_row, to_column = place(rank, chip)
            copies.append(
                (
                    part_of(piece_refs[piece], row, size, columns),
                    weights.at[pl.ds(to_row, size), pl.ds(to_column, columns)],
                )
            )
        for copy in run_copies(copies, sems):
            copy.wait()
        keep = pltpu.make_async_copy(weights, keep_ref, sems.at[steps + 2])
        keep.start()

        def step(index, carry):
            start = pl.multiple_of(index * tile, tile)
            left = both[:, :width]
            gate = jnp.dot(left, weights[:, pl.ds(start, tile)], preferred_element_type=F32)
            up = jnp.dot(
                left,
                weights[:, pl.ds(pl.multiple_of(half + start, tile), tile)],
                preferred_element_type=F32,
            )
            act, slope = gelu_parts(gate)
            act_ref[:, pl.ds(start, tile)] = act.astype(BF16)
            slope_ref[:, pl.ds(start, tile)] = (up * slope).astype(BF16)
            hidden_ref[:, pl.ds(start, tile)] = (act * up).astype(BF16)
            return carry

        lax.fori_loop(0, half // tile, step, 0)
        keep.wait()

    shape = jax.ShapeDtypeStruct((2 * rows, half), BF16)
    return pl.pallas_call(
        kernel,
        in_specs=[ANY] * (2 + count),
        out_specs=[VMEM, VMEM, VMEM, ANY],
        out_shape=[shape, shape, shape, jax.ShapeDtypeStruct((width, inner), BF16)],
        scratch_shapes=[
            pltpu.VMEM((2 * rows, wide), BF16),
            pltpu.VMEM((width, inner), BF16),
            pltpu.SemaphoreType.DMA((steps + 3,)),
        ],
        cost_estimate=LIGHT,
    )(own, other, *pieces)


def col_tiles(width):
    return [(start, min(512, width - start)) for start in range(0, width, 512)]


def down_call(hidden, width, padded, pieces, moves):
    double, half = hidden.shape
    rows = double // 2
    count, steps = len(pieces), len(moves)

    def kernel(hidden_ref, *rest):
        piece_refs = rest[:count]
        own_ref, other_ref, keep_ref, weights, sems = rest[count:]
        rank, chip = axis_ranks()
        copies = []
        for piece, row, size, columns, place in moves:
            to_row, to_column = place(rank, chip)
            copies.append(
                (
                    part_of(piece_refs[piece], row, size, columns),
                    weights.at[pl.ds(to_row, size), pl.ds(to_column, columns)],
                )
            )
        for copy in run_copies(copies, sems):
            copy.wait()
        keep = pltpu.make_async_copy(weights, keep_ref, sems.at[steps])
        keep.start()
        for start, size in col_tiles(width):
            columns = slice(start, start + size)
            own_ref[:, columns] = jnp.dot(
                hidden_ref[:rows], weights[:, columns], preferred_element_type=F32
            )
            other_ref[:, columns] = jnp.dot(
                hidden_ref[rows:], weights[:, columns], preferred_element_type=F32
            ).astype(BF16)
        if padded > width:
            other_ref[:, width:] = jnp.zeros((rows, padded - width), BF16)
        keep.wait()

    return pl.pallas_call(
        kernel,
        in_specs=[VMEM] + [ANY] * count,
        out_specs=[VMEM, VMEM, ANY],
        out_shape=[
            jax.ShapeDtypeStruct((rows, width), F32),
            jax.ShapeDtypeStruct((rows, padded), BF16),
            jax.ShapeDtypeStruct((half, padded), BF16),
        ],
        scratch_shapes=[pltpu.VMEM((half, padded), BF16), pltpu.SemaphoreType.DMA((steps + 1,))],
        cost_estimate=LIGHT,
    )(hidden, *pieces)


def finish_call(pieces, gate_up_moves, down_moves, block, inner, down_rows, width, padded):
    count = len(pieces)
    steps = len(gate_up_moves) + len(down_moves)

    def kernel(*refs):
        piece_refs = refs[:count]
        gate_ref, up_ref, down_ref, columns_of, rows_of, sems = refs[count:]
        chip, core = axis_ranks()[1], lax.axis_index("rep") % 2
        shards = lax.axis_size("shard")
        copies = []
        for piece, row, size, columns, place in gate_up_moves:
            to_core, to_row, to_column = place(core, chip)
            copies.append(
                (
                    part_of(piece_refs[piece], row, size, columns),
                    columns_of.at[to_core, pl.ds(to_row, size), pl.ds(to_column, columns)],
                )
            )
        for piece, row, size, columns, place in down_moves:
            to_row, to_column = place(core, chip)
            copies.append(
                (
                    part_of(piece_refs[piece], row, size, columns),
                    rows_of.at[pl.ds(to_row, size), pl.ds(to_column, columns)],
                )
            )
        for copy in run_copies(copies, sems):
            copy.wait()
        half = inner // shards // 2
        for index, ref in enumerate((gate_ref, up_ref)):
            for shard in range(shards):
                start = index * (inner // 2) + shard * half
                both = [columns_of[at, :, start : start + half] for at in range(2)]
                ref[:, 2 * half * shard : 2 * half * (shard + 1)] = jnp.concatenate(
                    both, 1
                ).astype(F32)
        down_ref[...] = rows_of[...].T[:width].astype(F32)

    return pl.pallas_call(
        kernel,
        in_specs=[ANY] * count,
        out_specs=[VMEM] * 3,
        out_shape=[
            jax.ShapeDtypeStruct((block, inner), F32),
            jax.ShapeDtypeStruct((block, inner), F32),
            jax.ShapeDtypeStruct((width, down_rows), F32),
        ],
        scratch_shapes=[
            pltpu.VMEM((2, block, inner), BF16),
            pltpu.VMEM((down_rows, padded), BF16),
            pltpu.SemaphoreType.DMA((steps,)),
        ],
    )(*pieces)


def attn_finish_call(pieces, moves, block, proj):
    count = len(pieces)

    def kernel(*refs):
        piece_refs = refs[:count]
        out_refs, whole, sems = refs[count : count + 4], refs[count + 4], refs[count + 5]
        rep = lax.axis_index("rep")
        copies = []
        for piece, index, place in moves:
            for start, size, matrix, row in place(rep):
                copies.append(
                    (
                        piece_refs[piece].at[index, pl.ds(start, size)],
                        whole.at[matrix, pl.ds(row, size)],
                    )
                )
        for copy in run_copies(copies, sems):
            copy.wait()
        for index, ref in enumerate(out_refs):
            ref[...] = whole[index].astype(F32)

    return pl.pallas_call(
        kernel,
        in_specs=[ANY] * count,
        out_specs=[VMEM] * 4,
        out_shape=[jax.ShapeDtypeStruct((block, proj), F32)] * 4,
        scratch_shapes=[
            pltpu.VMEM((4, block, proj), BF16),
            pltpu.SemaphoreType.DMA((2 * len(moves),)),
        ],
    )(*pieces)


def hidden_grad_call(own, other, down, slope, act):
    rows, width = own.shape
    half = down.shape[0]
    tile = 256

    def kernel(own_ref, other_ref, down_ref, slope_ref, act_ref, gate_ref, up_ref):
        for index, ref in enumerate((own_ref, other_ref)):
            part = slice(index * rows, (index + 1) * rows)
            upstream = dot_last(ref[...], down_ref[...])
            gate_ref[part] = (upstream * slope_ref[part].astype(F32)).astype(BF16)
            up_ref[part] = (upstream * act_ref[part].astype(F32)).astype(BF16)

    whole = pl.BlockSpec((rows, width), lambda i: (0, 0))
    columns = pl.BlockSpec((2 * rows, tile), lambda i: (0, i))
    shape = jax.ShapeDtypeStruct((2 * rows, half), BF16)
    return pl.pallas_call(
        kernel,
        grid=(half // tile,),
        in_specs=[
            whole,
            whole,
            pl.BlockSpec((tile, down.shape[1]), lambda i: (i, 0)),
            columns,
            columns,
        ],
        out_specs=[columns, columns],
        out_shape=[shape, shape],
        cost_estimate=LIGHT,
    )(own, other, down, slope, act)


def normed_grad_call(gate, up, weights):
    double, half = gate.shape
    rows = double // 2
    width = weights.shape[0]
    tile = 256

    def kernel(gate_ref, up_ref, low_ref, high_ref, own_ref, other_ref):
        for index, ref in enumerate((own_ref, other_ref)):
            part = slice(index * rows, (index + 1) * rows)
            total = dot_last(gate_ref[part], low_ref[...]) + dot_last(up_ref[part], high_ref[...])
            ref[...] = total.astype(ref.dtype)

    whole = pl.BlockSpec((double, half), lambda i: (0, 0))
    return pl.pallas_call(
        kernel,
        grid=(pl.cdiv(width, tile),),
        in_specs=[
            whole,
            whole,
            pl.BlockSpec((tile, half), lambda i: (i, 0)),
            pl.BlockSpec((tile, half), lambda i: (i, 1)),
        ],
        out_specs=[pl.BlockSpec((rows, tile), lambda i: (0, i))] * 2,
        out_shape=[
            jax.ShapeDtypeStruct((rows, width), F32),
            jax.ShapeDtypeStruct((rows, lane_tiles(width)), BF16),
        ],
        cost_estimate=LIGHT,
    )(gate, up, weights, weights)


def row_specs(micro_count, local, width):
    return pl.BlockSpec((local, width), lambda i: (i, 0)), pl.BlockSpec((1, width), lambda i: (0, 0))


def sum_rows(ref, value):
    total = jnp.sum(value, axis=0, keepdims=True)

    @pl.when(pl.program_id(0) == 0)
    def _():
        ref[...] = total

    @pl.when(pl.program_id(0) > 0)
    def _():
        ref[...] += total


def put_padded(ref, value):
    width = value.shape[1]
    ref[:, :width] = value.astype(BF16)
    if ref.shape[1] > width:
        ref[:, width:] = jnp.zeros((value.shape[0], ref.shape[1] - width), BF16)


def lane_tiles(width):
    return -(-width // 128) * 128


def mid_call(tokens, context, w_out, gain, micro_count):
    rows, width = tokens.shape
    local = rows // micro_count
    by_row, vector = row_specs(micro_count, local, width)

    def kernel(token_ref, context_ref, out_ref, gain_ref, hidden_ref, normed_ref):
        hidden = token_ref[...].astype(F32) + jnp.dot(
            context_ref[...], out_ref[...], preferred_element_type=F32
        )
        hidden_ref[...] = hidden
        put_padded(normed_ref, hidden * rms_scale(hidden) * gain_ref[...])

    return pl.pallas_call(
        kernel,
        grid=(micro_count,),
        in_specs=[
            by_row,
            pl.BlockSpec((local, context.shape[1]), lambda i: (i, 0)),
            pl.BlockSpec(w_out.shape, lambda i: (0, 0)),
            vector,
        ],
        out_specs=[by_row, pl.BlockSpec((local, lane_tiles(width)), lambda i: (i, 0))],
        out_shape=[
            jax.ShapeDtypeStruct((rows, width), F32),
            jax.ShapeDtypeStruct((rows, lane_tiles(width)), BF16),
        ],
        cost_estimate=LIGHT,
    )(tokens, context, w_out, gain)


def out_call(hidden, part, given, cotangent, gate_cotangent, gain, vector_in, micro_count):
    rows, width = hidden.shape
    local = rows // micro_count
    by_row, vector = row_specs(micro_count, local, width)
    one = pl.BlockSpec((local, 1), lambda i: (i, 0))
    turned = pl.BlockSpec((1, width, local), lambda i: (i, 0, 0))
    padded = pl.BlockSpec((local, lane_tiles(width)), lambda i: (i, 0))

    def kernel(
        hidden_ref, part_ref, given_ref, up_ref, gate_ref, gain_ref, vector_ref,
        state_ref, deleted_ref, grad_ref, low_ref, gain_grad_ref, vector_grad_ref,
    ):
        state = hidden_ref[...] + part_ref[...] + given_ref[:, :width].astype(F32)
        state_ref[0] = state.T
        scale = rms_scale(state)
        normed = state * scale * gain_ref[...]
        logit = jnp.sum(normed * vector_ref[...], axis=1, keepdims=True)
        sigmoid = lax.logistic(logit)
        deleted_ref[...] = -30.0 * sigmoid
        slope = gate_ref[...] * -30.0 * sigmoid * (1.0 - sigmoid)
        upstream = slope * vector_ref[...]
        sum_rows(vector_grad_ref, slope * normed)
        sum_rows(gain_grad_ref, upstream * state * scale)
        grad = up_ref[...].astype(F32) + rms_back(state, scale, gain_ref[...], upstream)
        grad_ref[...] = grad
        put_padded(low_ref, grad)

    return pl.pallas_call(
        kernel,
        grid=(micro_count,),
        in_specs=[by_row, by_row, padded, by_row, one, vector, vector],
        out_specs=[turned, one, by_row, padded, vector, vector],
        out_shape=[
            jax.ShapeDtypeStruct((micro_count, width, local), F32),
            jax.ShapeDtypeStruct((rows, 1), F32),
            jax.ShapeDtypeStruct((rows, width), F32),
            jax.ShapeDtypeStruct((rows, lane_tiles(width)), BF16),
            jax.ShapeDtypeStruct((1, width), F32),
            jax.ShapeDtypeStruct((1, width), F32),
        ],
        cost_estimate=LIGHT,
    )(hidden, part, given, cotangent, gate_cotangent, gain, vector_in)


def back_call(part, given, grad_out, hidden, gain, context, w_out, micro_count):
    rows, width = hidden.shape
    local = rows // micro_count
    proj = context.shape[1]
    by_row, vector = row_specs(micro_count, local, width)
    by_proj = pl.BlockSpec((local, proj), lambda i: (i, 0))
    padded = pl.BlockSpec((local, lane_tiles(width)), lambda i: (i, 0))
    whole = pl.BlockSpec((proj, width), lambda i: (0, 0))

    def kernel(
        part_ref, given_ref, grad_ref, hidden_ref, gain_ref, context_ref, out_ref,
        mid_ref, context_grad_ref, out_grad_ref, gain_grad_ref, total,
    ):
        normed_grad = part_ref[...] + given_ref[:, :width].astype(F32)
        hidden = hidden_ref[...]
        scale = rms_scale(hidden)
        sum_rows(gain_grad_ref, normed_grad * hidden * scale)
        mid = grad_ref[...] + rms_back(hidden, scale, gain_ref[...], normed_grad)
        mid_ref[...] = mid
        low = mid.astype(BF16)
        context_grad_ref[...] = dot_last(low, out_ref[...]).astype(BF16)
        product = jnp.dot(context_ref[...].T, low, preferred_element_type=F32)
        step = pl.program_id(0)

        @pl.when(step == 0)
        def _():
            total[...] = product

        @pl.when(step > 0)
        def _():
            total[...] += product

        @pl.when(step == micro_count - 1)
        def _():
            out_grad_ref[...] = total[...].astype(BF16)

    return pl.pallas_call(
        kernel,
        grid=(micro_count,),
        in_specs=[by_row, padded, by_row, by_row, vector, by_proj, whole],
        out_specs=[by_row, by_proj, whole, vector],
        out_shape=[
            jax.ShapeDtypeStruct((rows, width), F32),
            jax.ShapeDtypeStruct((rows, proj), BF16),
            jax.ShapeDtypeStruct((proj, width), BF16),
            jax.ShapeDtypeStruct((1, width), F32),
        ],
        scratch_shapes=[pltpu.VMEM((proj, width), F32)],
        cost_estimate=LIGHT,
    )(part, given, grad_out, hidden, gain, context, w_out)


def in_call(query_grad, pair_parts, weights, grad_mid, tokens, gain, micro_count):
    rows, width = tokens.shape
    local = rows // micro_count
    proj = query_grad.shape[1]
    count = pair_parts.shape[0]
    by_row, vector = row_specs(micro_count, local, width)
    by_proj = pl.BlockSpec((local, proj), lambda i: (i, 0))
    by_pair = pl.BlockSpec((local, 2 * proj), lambda i: (i, 0))

    def kernel(
        query_ref, part_ref, wq_ref, wk_ref, wv_ref, mid_ref, token_ref, gain_ref,
        pair_ref, grad_ref, gain_grad_ref,
    ):
        pair = sum(part_ref[index].astype(F32) for index in range(count)).astype(BF16)
        pair_ref[...] = pair
        normed_grad = (
            dot_last(query_ref[...], wq_ref[0])
            + dot_last(pair[:, :proj], wk_ref[0])
            + dot_last(pair[:, proj:], wv_ref[0])
        )
        hidden = token_ref[...].astype(F32)
        scale = rms_scale(hidden)
        sum_rows(gain_grad_ref, normed_grad * hidden * scale)
        grad = mid_ref[...] + rms_back(hidden, scale, gain_ref[...], normed_grad)
        grad_ref[0] = grad.astype(BF16).T

    return pl.pallas_call(
        kernel,
        grid=(micro_count,),
        in_specs=[by_proj, pl.BlockSpec((count, local, 2 * proj), lambda i: (0, i, 0))]
        + [pl.BlockSpec((1, width, proj), lambda i, m=m: (m, 0, 0)) for m in range(3)]
        + [by_row, by_row, vector],
        out_specs=[by_pair, pl.BlockSpec((1, width, local), lambda i: (i, 0, 0)), vector],
        out_shape=[
            jax.ShapeDtypeStruct((rows, 2 * proj), BF16),
            jax.ShapeDtypeStruct((micro_count, width, local), BF16),
            jax.ShapeDtypeStruct((1, width), F32),
        ],
        cost_estimate=LIGHT,
    )(query_grad, pair_parts, weights, weights, weights, grad_mid, tokens, gain)


def weight_grad_call(left, right, depth, width, outputs):
    left_own, left_other = left
    right_own, right_other = right
    rows = left_own.shape[0]
    total = 2 * rows if left_other is not None else rows
    beside = right_other is not None and right_own.shape[0] == total
    right_width = right_own.shape[1] * (2 if beside else 1)
    count = len(outputs)
    copies_out = sum(len(moves) for _, moves in outputs)
    split = left_other is not None
    right_split = right_other is not None
    inputs = [left_own] + ([left_other] if split else []) + [right_own]
    inputs += [right_other] if right_split else []

    def kernel(*refs):
        in_refs = list(refs[: len(inputs)])
        out_refs = refs[len(inputs) : len(inputs) + count]
        lefts, rights, result, sems = refs[len(inputs) + count :]
        copies = []
        for target, parted, aside in ((lefts, split, False), (rights, right_split, beside)):
            first = in_refs.pop(0)
            size = first.shape[1] if aside else first.shape[0]
            if not parted:
                copies.append((first, target))
            elif aside:
                copies.append((first, target.at[:, :size]))
                copies.append((in_refs.pop(0), target.at[:, size:]))
            else:
                copies.append((first, target.at[:size]))
                copies.append((in_refs.pop(0), target.at[size:]))
        for copy in run_copies(copies, sems):
            copy.wait()
        tile = 512 if width % 512 == 0 else width
        for begin in range(0, depth, 256):
            size = min(256, depth - begin)
            turned = lefts[:, begin : begin + size].T
            if tile == width:
                for start, span in col_tiles(width):
                    result[begin : begin + size, start : start + span] = jnp.dot(
                        turned, rights[:, start : start + span], preferred_element_type=F32
                    ).astype(BF16)
            else:

                def step(index, carry):
                    start = pl.multiple_of(index * tile, tile)
                    result[begin : begin + size, pl.ds(start, tile)] = jnp.dot(
                        turned, rights[:, pl.ds(start, tile)], preferred_element_type=F32
                    ).astype(BF16)
                    return carry

                lax.fori_loop(0, width // tile, step, 0)
        rank, chip = axis_ranks()
        moves_out = []
        for ref, (shape, moves) in zip(out_refs, outputs):
            for index, place in moves:
                row, column = place(rank, chip)
                moves_out.append(
                    (result.at[pl.ds(row, shape[1]), pl.ds(column, shape[2])], ref.at[index])
                )
        for copy in run_copies(moves_out, sems):
            copy.wait()

    return pl.pallas_call(
        kernel,
        in_specs=[ANY] * len(inputs),
        out_specs=[ANY] * count,
        out_shape=[jax.ShapeDtypeStruct(shape, BF16) for shape, _ in outputs],
        scratch_shapes=[
            pltpu.VMEM((total, left_own.shape[1]), BF16),
            pltpu.VMEM((total, right_width), BF16),
            pltpu.VMEM((depth, width), BF16),
            pltpu.SemaphoreType.DMA((max(4, copies_out),)),
        ],
        cost_estimate=LIGHT,
    )(*inputs)


def on_device(
    tokens,
    cotangent,
    gate_cotangent,
    slot_of,
    seq_lengths,
    buckets,
    gain_attn,
    w_query,
    w_key,
    w_value,
    w_out,
    rel_bias,
    gain_ffn,
    w_gate,
    w_up,
    w_down,
    gain_delete,
    w_delete,
):
    shards = lax.axis_size("shard")
    reps = lax.axis_size("rep")
    chips = reps // 2
    rank = lax.axis_index("shard")
    rep_rank = lax.axis_index("rep")
    core = rep_rank % 2
    chip = rep_rank // 2
    micro_count, local_rows, width = tokens.shape
    group = local_rows * shards
    rows = micro_count * local_rows
    heads = rel_bias.shape[1]
    bucket_rows = rel_bias.shape[0]
    bucket_count = bucket_rows * shards
    proj = w_query.shape[1]
    head_size = proj // heads
    block = gain_attn.shape[0]
    inner = w_gate.shape[1]
    half_inner = inner // 2
    col_piece = inner // chips
    down_block = w_down.shape[0]
    down_half = down_block // 2
    down_piece = down_half // chips
    down_parts_count = -(-width // col_piece)
    padded = -(-width // 128) * 128
    aligned = reps == 8 and block % 16 == 0 and down_piece % 16 == 0 and col_piece % 128 == 0

    def swap(value, mask):
        return lax.ppermute(value, "rep", [(i, i ^ mask) for i in range(reps)])

    def shift(value, by=1):
        return lax.ppermute(value, "shard", [(i, (i + by) % shards) for i in range(shards)])

    def tie(value, moved):
        return lax.optimization_barrier((value, moved))

    def cut(count):
        half = count // 2
        return half // 16 * 16 if half >= 16 else half

    def gather_near(piece):
        if chips == 1:
            return []
        return [swap(piece, 2)] + ([swap(piece, 4)] if chips >= 4 else [])

    def gather_rest(near):
        if chips < 4:
            return []
        middle = cut(near[0].shape[0])
        return [swap(near[1][:middle], 2), swap(near[0][middle:], 4)]

    def gather_list(piece, near, rest):
        middle = cut(piece.shape[0])
        found = [(0, 0, piece)] + [(1 + i, 0, part) for i, part in enumerate(near)]
        found += [(3, i * middle, part) for i, part in enumerate(rest)]
        bit = 4
        while bit < chips:
            found += [
                (mask ^ bit, start, swap(part, 2 * bit)) for mask, start, part in found
            ]
            bit *= 2
        return found

    def plane_gather(piece):
        near = gather_near(piece)
        return gather_list(piece, near, gather_rest(near))

    def add(*values):
        return sum(value.astype(F32) for value in values).astype(BF16)

    def plane_reduce(parts, axis):
        state = reduce_begin(parts, axis)
        return reduce_end(reduce_middle(state, axis))

    def reduce_begin(parts, axis):
        def level(base, bit):
            if bit < 4:
                return lambda name: parts[base][name]
            lower, upper = level(base, bit // 2), level(base ^ bit, bit // 2)
            return lambda name: add(lower(name), swap(upper(name), 2 * bit))

        get = level(0, chips // 2)
        if chips < 4:
            return [get("own")] + ([swap(get("near"), 2)] if chips == 2 else [])
        return [get("own"), get("far"), get("near"), swap(get("top"), 2), swap(get("low"), 4)]

    def reduce_middle(state, axis):
        if chips < 4:
            return state
        own, far, near, top, low = state
        middle = top.shape[axis]

        def pair(value):
            return (
                lax.slice_in_dim(value, 0, middle, axis=axis),
                lax.slice_in_dim(value, middle, value.shape[axis], axis=axis),
            )

        (far_top, far_low), (near_top, near_low) = pair(far), pair(near)
        far = jnp.concatenate([add(far_top, top), far_low], axis)
        near = jnp.concatenate([near_top, add(near_low, low)], axis)
        return [own, swap(far, 4), swap(near, 2)]

    def reduce_end(state):
        return add(*state) if len(state) > 1 else state[0]

    names = {"own": 0, "near": 1, "far": 2, "top": 3, "low": 3}
    bases = [base for base in range(chips) if base & 3 == 0]
    used = ["own", "near", "far", "top", "low"] if chips >= 4 else ["own", "near"][:chips]

    def source(step):
        return (rank - step) % shards

    order = (rank - jnp.arange(shards, dtype=jnp.int32)) % shards
    per_matrix = reps // 4
    attn_rows = block // per_matrix
    if aligned:
        attn_rows = -(-attn_rows // 16) * 16
    last_row = block - attn_rows

    def part_row(part):
        return jnp.minimum(part * attn_rows, last_row)

    attn_own = jnp.stack([w_query, w_key, w_value, w_out.reshape(block, proj)])
    attn_piece = lax.dynamic_slice(
        attn_own,
        (rep_rank // per_matrix, part_row(rep_rank % per_matrix), 0),
        (1, attn_rows, proj),
    )[0]
    vector_pack = jnp.concatenate(
        [gain_attn, gain_ffn, gain_delete, w_delete, rel_bias.reshape(-1)]
    )
    pack_rows = -(-vector_pack.shape[0] // (16 * proj)) * 16
    vector_pack = jnp.pad(vector_pack, (0, pack_rows * proj - vector_pack.shape[0]))
    vector_pack = vector_pack.reshape(pack_rows, proj)
    attn_sent = jnp.concatenate([attn_piece, vector_pack])
    attn_arrived = [shift(attn_sent, step) for step in range(1, shards)]
    vectors = jnp.stack([vector_pack] + [part[attn_rows:] for part in attn_arrived])
    vectors = jnp.take(vectors, order, axis=0).reshape(shards, pack_rows * proj)
    attn_gain = vectors[:, :block].reshape(width).astype(F32)
    ffn_gain = vectors[:, block : 2 * block].reshape(width).astype(F32)
    delete_gain = vectors[:, 2 * block : 3 * block].reshape(width).astype(F32)
    delete_vec = vectors[:, 3 * block : 4 * block].reshape(width).astype(F32)
    bias_table = vectors[:, 4 * block : 4 * block + bucket_rows * heads]
    bias_table = bias_table.reshape(bucket_count, heads)
    stacked = jnp.stack([part[:attn_rows] for part in attn_arrived])

    def pack(gate_up_part, down_part):
        wide = jnp.pad(down_part, ((0, 0), (0, down_parts_count * col_piece - width)))
        cuts = [wide[:, i * col_piece : (i + 1) * col_piece] for i in range(down_parts_count)]
        return jnp.concatenate([gate_up_part] + cuts)

    def overlaps(start, count):
        bounds = [(None, 0, block)] + [
            (i, block + i * down_piece, block + (i + 1) * down_piece)
            for i in range(down_parts_count)
        ]
        found = []
        for part, low, high in bounds:
            first, last = max(low, start), min(high, start + count)
            if first < last:
                found.append((part, first - start, first - low, last - first))
        return found

    def part_columns(part):
        return min(col_piece, padded - part * col_piece)

    gate_up_own = pick_columns(w_gate, w_up)
    down_own = lax.dynamic_slice_in_dim(w_down, core * down_half, down_half, 0)
    packed_own = pack(
        lax.dynamic_slice_in_dim(gate_up_own, chip * col_piece, col_piece, 1),
        lax.dynamic_slice_in_dim(down_own, chip * down_piece, down_piece, 0),
    )
    packed_own, stacked = tie(packed_own, stacked)
    attn_plane = [stacked] + [swap(stacked, 2 * mask) for mask in range(1, chips)]
    attn_plane = jnp.stack(attn_plane)
    ring = [packed_own, shift(packed_own)]
    attn_plane, ring = tie(attn_plane, ring)
    nears, rests = [None] * shards, [None] * shards
    nears[1] = gather_near(ring[1])
    attn_other = swap(attn_plane, 1)

    def attn_place(mask, flip, step):
        def place(at, rep):
            owner = rep ^ (2 * mask + flip)
            row = (at - step) % shards * block + part_row(owner % per_matrix)
            return owner // per_matrix, pl.multiple_of(row, 16) if aligned else row

        return place

    shared = per_matrix * attn_rows - block

    def split_place(place, flip):
        def places_of(*at):
            matrix, row = place(*at)
            part = (at[-1] ^ flip) % per_matrix
            first = row - last_row * part
            moves = [
                (
                    pl.multiple_of(shared * part, 16),
                    attn_rows - shared,
                    matrix,
                    pl.multiple_of(first + attn_rows * part, 16),
                )
            ]
            if shared and flip == 0:
                moves.append(
                    (
                        pl.multiple_of(last_row * (1 - part), 16),
                        shared,
                        matrix,
                        pl.multiple_of(first + last_row, 16),
                    )
                )
            return moves

        return places_of

    attn_pieces = [w_query, w_key, w_value, attn_own[3]]
    attn_places = [
        [(None, lambda at, rep, matrix=matrix: [(0, block, matrix, pl.multiple_of(at * block, 16))])]
        for matrix in range(4)
    ]
    for flip, found in enumerate((attn_plane, attn_other)):
        attn_pieces.append(found)
        attn_places.append(
            [
                ((mask, step - 1), attn_place(mask, flip, step), flip)
                for mask in range(chips)
                for step in range(1, shards)
            ]
        )
    if not aligned:
        whole = jnp.zeros((4, width, proj), BF16)
        whole = lax.dynamic_update_slice(whole, attn_own, (0, rank * block, 0))
        for piece, place in zip(attn_pieces[4:], attn_places[4:]):
            for index, where, _ in place:
                matrix, row = where(rank, rep_rank)
                whole = lax.dynamic_update_slice(whole, piece[index][None], (matrix, row, 0))
        attn_pieces = [whole[matrix] for matrix in range(4)]
        attn_places = [
            [(None, lambda at, rep, matrix=matrix: [(0, width, matrix, 0)])] for matrix in range(4)
        ]
    else:
        attn_places[4:] = [
            [(index, split_place(where, flip)) for index, where, flip in place]
            for place in attn_places[4:]
        ]

    slots = slot_of[:, 0]
    own_slots = lax.dynamic_slice_in_dim(slots, rank * local_rows, local_rows, 1)
    key_slots = jnp.take(slots.reshape(micro_count, shards, local_rows), order, axis=1)
    key_slots = key_slots.reshape(micro_count, group)
    onehot = (buckets[:, None] == jnp.arange(bucket_count, dtype=jnp.int32)[None, :]).astype(F32)
    onehot = jnp.pad(onehot, ((0, 1), (0, 0)))
    bias_rows = jnp.dot(onehot, bias_table.astype(F32), precision=HIGHEST).T
    bias = bias_of_queries(bias_rows, own_slots.reshape(rows), group)
    first_len = seq_lengths[:, 0, 0]

    token_rows = tokens.reshape(rows, width)
    normed_one, queries, own_pairs, attn_full = project_call(
        token_rows, attn_gain[None], attn_pieces, attn_places, block, proj
    )
    out_full = attn_full[3].reshape(proj, width)

    for step in range(2, shards - 1):
        ring.append(shift(ring[-1]))
    own_pairs, ring = tie(own_pairs, ring)
    early = (
        out_full,
        jnp.pad(down_own, ((0, 0), (0, padded - width))),
        cotangent.reshape(rows, width),
        gate_cotangent.reshape(rows, 1).astype(F32),
        [value[None] for value in (ffn_gain, delete_gain, delete_vec)],
        [slots[micro].reshape(group, 1) for micro in range(micro_count)],
    )
    pairs = [own_pairs]
    for step in range(1, shards):
        pairs.append(shift(pairs[-1]))
        if step == 1:
            pairs[-1], (nears[1], bias) = tie(pairs[-1], (nears[1], bias))
            rests[1] = gather_rest(nears[1])
        if step == 2:
            pairs[-1], (rests[1], early) = tie(pairs[-1], (rests[1], early))
            ring[2], rests[1] = tie(ring[2], rests[1])
            nears[2] = gather_near(ring[2])
    ring[-1], pairs[-1] = tie(ring[-1], pairs[-1])
    last = shift(ring[-1][:block])
    context, probs, packed = [], [], []
    for micro in range(micro_count):
        if micro == micro_count - 1:
            context, nears[2] = tie(context, nears[2])
            rests[2] = gather_rest(nears[2])
        *context, prob, pair = attention_call(
            micro,
            first_len[micro : micro + 1],
            queries,
            pairs,
            own_slots.reshape(rows, 1),
            key_slots[micro : micro + 1],
            bias,
            context,
        )
        probs.append(prob)
        packed.append(pair)
    for step in range(3, shards - 1):
        ring[step], rests[step - 1] = tie(ring[step], rests[step - 1])
        nears[step] = gather_near(ring[step])
        rests[step] = gather_rest(nears[step])
    context, (last, rests[shards - 2]) = tie(context, (last, rests[shards - 2]))
    last_near = gather_near(last)
    last_down = shift(ring[-1][block:])
    (context,) = context
    out_full, down_wide, cotangent_rows, gate_rows, gains, key_columns = early
    ffn_gain, delete_gain, delete_vec = gains

    hidden_mid, normed_two = mid_call(token_rows, context, out_full, ffn_gain, micro_count)
    normed_two, (last_near, last_down) = tie(normed_two, (last_near, last_down))
    last_rest = gather_rest(last_near)
    normed_two_other = swap(normed_two, 1)
    normed_two_other, (last_rest, last_down) = tie(normed_two_other, (last_rest, last_down))
    last_down_found = [(mask, 0, swap(last_down, 2 * mask)) for mask in range(1, chips)]
    pieces = [gate_up_own, down_wide]
    gate_up_moves = [(0, 0, block, inner, lambda at, chip_at: (pl.multiple_of(at * block, 16), 0))]
    down_moves = [
        (1, 0, down_half, padded, lambda at, chip_at: (pl.multiple_of(at * down_half, 16), 0))
    ]

    def gate_up_place(step, mask, row):
        return lambda at, chip_at: (
            pl.multiple_of((at - step) % shards * block + row, 16),
            pl.multiple_of((chip_at ^ mask) * col_piece, 128),
        )

    def down_place(step, mask, row, part):
        return lambda at, chip_at: (
            pl.multiple_of((at - step) % shards * down_half + (chip_at ^ mask) * down_piece + row, 16),
            part * col_piece,
        )

    arrived = [
        (step, 0, gather_list(ring[step], nears[step], rests[step])) for step in range(1, shards - 1)
    ]
    arrived.append((shards - 1, 0, gather_list(last, last_near, last_rest)))
    arrived.append((shards - 1, block, [(0, 0, last_down)] + last_down_found))
    for step, below, found in arrived:
        for mask, start, array in found:
            for part, here, there, size in overlaps(below + start, array.shape[0]):
                if part is None:
                    gate_up_moves.append(
                        (len(pieces), here, size, col_piece, gate_up_place(step, mask, there))
                    )
                else:
                    down_moves.append(
                        (
                            len(pieces),
                            here,
                            size,
                            part_columns(part),
                            down_place(step, mask, there, part),
                        )
                    )
            pieces.append(array)
    if not aligned:

        def put_together(moves, shape):
            whole = jnp.zeros(shape, BF16)
            for piece, row, size, columns, place in moves:
                value = pieces[piece][row : row + size, :columns]
                whole = lax.dynamic_update_slice(whole, value, place(rank, chip))
            return whole

        pieces = [
            put_together(gate_up_moves, (width, inner)),
            put_together(down_moves, (half_inner, padded)),
        ]
        gate_up_moves = [(0, 0, width, inner, lambda at, chip_at: (0, 0))]
        down_moves = [(1, 0, half_inner, padded, lambda at, chip_at: (0, 0))]
    gate_up_pieces, gate_up_moves = used_by(pieces, gate_up_moves)
    down_pieces, down_moves = used_by(pieces, down_moves)
    gate_slope_act, gate_act, inner_act, gate_up = gate_up_call(
        normed_two, normed_two_other, width, inner, gate_up_pieces, gate_up_moves
    )
    down_part, down_given, down = down_call(inner_act, width, padded, down_pieces, down_moves)
    hidden_out, deleted, grad_out, down_up, grad_delete_gain, grad_delete_vec = out_call(
        hidden_mid,
        down_part,
        swap(down_given, 1),
        cotangent_rows,
        gate_rows,
        delete_gain,
        delete_vec,
        micro_count,
    )

    down_up_other = swap(down_up, 1)

    def reduce_plan(groups, piece_columns, place):
        plan = []
        for first, size in groups:
            middle = cut(size)
            spans = {"own": (0, size), "near": (0, size), "far": (0, size)}
            spans["top"], spans["low"] = (0, middle), (middle, size - middle)
            for base in bases:
                for name in used:
                    start, count = spans[name]
                    moves = [
                        (index, place(index, base ^ names[name], first + start))
                        for index in range(shards)
                    ]
                    plan.append(((shards, count, piece_columns), moves))
        return plan

    def reduce_run(plan, left, right, left_width, right_width):
        if aligned:
            buffers = weight_grad_call(left, right, left_width, right_width, plan)
        else:
            shape = (left_width, right_width)
            whole = weight_grad_call(
                left, right, left_width, right_width, [((1,) + shape, [(0, lambda at, chip_at: (0, 0))])]
            )[0][0]
            buffers = []
            for (_, size, columns), moves in plan:
                buffers.append(
                    jnp.stack(
                        [
                            lax.dynamic_slice(whole, place(rank, chip), (size, columns))
                            for _, place in moves
                        ]
                    )
                )
        return buffers

    def group_parts(buffers, group_index, group_count):
        each = len(buffers) // group_count
        chosen = buffers[group_index * each : (group_index + 1) * each]
        return {
            base: dict(zip(used, chosen[i * len(used) : (i + 1) * len(used)]))
            for i, base in enumerate(bases)
        }

    def exchange(value):
        return lax.all_to_all(value, "shard", split_axis=0, concat_axis=0, tiled=True)

    def total_of(arrived):
        return jnp.sum(arrived.astype(F32), axis=0).astype(BF16)

    def down_grad_place(index, mask, start):
        plain = lambda at, chip_at: (
            index * down_half + (chip_at ^ mask) * down_piece + start,
            0,
        )
        return tile_hint(plain, 16, 128) if aligned else plain

    def gate_up_grad_place(index, mask, start):
        plain = lambda at, chip_at: (index * block + start, (chip_at ^ mask) * col_piece)
        return tile_hint(plain, 16, 128) if aligned else plain

    down_buffers = reduce_run(
        reduce_plan([(0, down_piece)], width, down_grad_place),
        (inner_act, None),
        (down_up, down_up_other),
        half_inner,
        width,
    )
    down_state = reduce_begin(group_parts(down_buffers, 0, 1), 1)
    gate_grad, up_grad = hidden_grad_call(down_up, down_up_other, down, gate_slope_act, gate_act)
    gate_grad, down_state = tie(gate_grad, down_state)
    gate_up_buffers = reduce_run(
        reduce_plan([(0, cut(block)), (cut(block), block - cut(block))], col_piece, gate_up_grad_place),
        (normed_two, normed_two_other),
        (gate_grad, up_grad),
        width,
        inner,
    )
    down_state = reduce_middle(down_state, 1)
    gate_grad, (gate_up_buffers, down_state) = tie(gate_grad, (gate_up_buffers, down_state))
    gate_up_state = reduce_begin(group_parts(gate_up_buffers, 0, 2), 1)
    normed_part, normed_given = normed_grad_call(gate_grad, up_grad, gate_up)
    normed_given, gate_up_state = tie(normed_given, gate_up_state)
    gate_up_state = reduce_middle(gate_up_state, 1)
    normed_given = swap(normed_given, 1)
    down_arrived = exchange(reduce_end(down_state))
    grad_mid, context_grad, grad_w_out, grad_ffn_gain = back_call(
        normed_part,
        normed_given,
        grad_out,
        hidden_mid,
        ffn_gain,
        context,
        out_full,
        micro_count,
    )
    score_grads, sums = [], []
    for micro in range(micro_count):
        score_grad, *sums = attention_back_call(
            micro,
            queries,
            context_grad,
            probs[micro],
            packed[micro],
            key_columns[micro],
            shards,
            sums,
        )
        score_grads.append(score_grad)
    query_grad, pair_parts = sums
    gate_up_parts = group_parts(gate_up_buffers, 1, 2)
    pair_parts, gate_up_state = tie(pair_parts, gate_up_state)
    pair_arrived = exchange(pair_parts)
    gate_up_parts, gate_up_state = tie(gate_up_parts, gate_up_state)
    gate_up_later = reduce_begin(gate_up_parts, 1)
    grad_bias_rows = bias_fold(score_grads, own_slots.reshape(rows))
    grad_bias = jnp.einsum("ob,ho->bh", onehot, grad_bias_rows, precision=HIGHEST)
    out_grads = grad_w_out.reshape(width, proj)
    gate_up_later, (grad_bias, out_grads) = tie(gate_up_later, (grad_bias, out_grads))
    gate_up_later = reduce_middle(gate_up_later, 1)
    pair_arrived, (gate_up_later, down_arrived) = tie(pair_arrived, (gate_up_later, down_arrived))
    gate_up_arrived = exchange(reduce_end(gate_up_state))
    down_sum = total_of(down_arrived)
    pair_sum, grad_in, grad_attn_gain = in_call(
        query_grad,
        pair_arrived,
        attn_full,
        grad_mid,
        token_rows,
        attn_gain[None],
        micro_count,
    )

    small = jnp.concatenate(
        [
            grad_attn_gain.reshape(shards, block),
            grad_ffn_gain.reshape(shards, block),
            grad_delete_gain.reshape(shards, block),
            grad_delete_vec.reshape(shards, block),
            grad_bias.reshape(shards, bucket_rows * heads),
        ],
        axis=1,
    ).astype(BF16)
    small = jnp.pad(small, ((0, 0), (0, pack_rows * proj - small.shape[1])))
    small = small.reshape(shards, pack_rows, proj)

    def attn_grad_place(mask, flip, index):
        def place(at, rep):
            owner = rep ^ (2 * mask + flip)
            row = index * block + part_row(owner % per_matrix)
            return owner // per_matrix, pl.multiple_of(row, 16) if aligned else row

        return place

    attn_plan = [
        (
            (chips, shards, attn_rows + pack_rows, proj),
            [
                ((mask, index), attn_grad_place(mask, flip, index), index)
                for mask in range(chips)
                for index in range(shards)
            ],
        )
        for flip in range(2)
    ]
    if aligned:
        kept, given = project_grad_call(
            normed_one, query_grad, pair_sum, out_grads, small, attn_plan
        )
    else:
        whole_plan = [
            (
                (4, width, proj),
                [((matrix,), lambda at, rep, matrix=matrix: (matrix, 0), None) for matrix in range(4)],
            )
        ]
        whole = project_grad_call(
            normed_one, query_grad, pair_sum, out_grads, small, whole_plan
        )[0]
        kept, given = [
            jnp.stack(
                [
                    jnp.concatenate(
                        [
                            lax.dynamic_slice(
                                whole, where(rank, rep_rank) + (0,), (1, attn_rows, proj)
                            )[0],
                            small[index],
                        ]
                    )
                    for _, where, index in items
                ]
            ).reshape(shape)
            for shape, items in attn_plan
        ]
    given = swap(given, 1)
    attn_own_sum = add(kept[0], given[0])
    attn_send = [add(kept[mask], given[mask]) for mask in range(1, chips)]
    attn_found = [swap(part, 2 * mask + 2) for mask, part in enumerate(attn_send)]
    gate_up_rest = exchange(reduce_end(gate_up_later))
    attn_sum = add(attn_own_sum, *attn_found)
    attn_sum = total_of(exchange(attn_sum))
    gate_up_sum = jnp.concatenate([total_of(gate_up_arrived), total_of(gate_up_rest)])
    total = attn_sum[attn_rows:].astype(F32).reshape(-1)
    attn_sum = attn_sum[:attn_rows]

    packed_sum = pack(gate_up_sum, down_sum)
    near = gather_near(packed_sum)
    attn_sum, near = tie(attn_sum, near)
    found = gather_list(packed_sum, near, gather_rest(near))
    pieces, gate_up_moves, down_moves = [], [], []

    def gate_up_to(flip, mask, row):
        return lambda core_at, chip_at: (
            core_at ^ flip,
            row,
            pl.multiple_of((chip_at ^ mask) * col_piece, 128),
        )

    def down_to(flip, mask, row, part):
        return lambda core_at, chip_at: (
            pl.multiple_of((core_at ^ flip) * down_half + (chip_at ^ mask) * down_piece + row, 16),
            part * col_piece,
        )

    for flip in range(2):
        for mask, start, array in found:
            array = swap(array, 1) if flip else array
            for part, here, there, size in overlaps(start, array.shape[0]):
                if part is None:
                    gate_up_moves.append(
                        (len(pieces), here, size, col_piece, gate_up_to(flip, mask, there))
                    )
                else:
                    down_moves.append(
                        (
                            len(pieces),
                            here,
                            size,
                            part_columns(part),
                            down_to(flip, mask, there, part),
                        )
                    )
            pieces.append(array)
    if aligned:
        grad_gate, grad_up, grad_down_out = finish_call(
            pieces, gate_up_moves, down_moves, block, inner, down_block, width, padded
        )
        grad_down_out = grad_down_out.T
    else:
        halves = jnp.zeros((2, block, inner), BF16)
        for piece, row, size, columns, place in gate_up_moves:
            value = pieces[piece][None, row : row + size, :columns]
            halves = lax.dynamic_update_slice(halves, value, place(core, chip))
        whole = jnp.zeros((down_block, padded), BF16)
        for piece, row, size, columns, place in down_moves:
            value = pieces[piece][row : row + size, :columns]
            whole = lax.dynamic_update_slice(whole, value, place(core, chip))
        grad_gate, grad_up = spread_columns(halves[0], halves[1])
        grad_down_out = whole[:, :width].astype(F32)

    attn_half = jnp.stack([attn_sum] + [swap(attn_sum, 2 * mask) for mask in range(1, chips)])
    attn_found = [attn_half, swap(attn_half, 1)]

    def attn_to(mask, flip):
        def place(rep):
            owner = rep ^ (2 * mask + flip)
            row = part_row(owner % per_matrix)
            return owner // per_matrix, pl.multiple_of(row, 16) if aligned else row

        return place

    attn_moves = [(flip, mask, attn_to(mask, flip)) for flip in range(2) for mask in range(chips)]
    if aligned:
        attn_moves = [
            (flip, mask, split_place(place, flip)) for flip, mask, place in attn_moves
        ]
        attn_shard = attn_finish_call(attn_found, attn_moves, block, proj)
    else:
        attn_shard = jnp.zeros((4, block, proj), BF16)
        for piece, index, place in attn_moves:
            attn_shard = lax.dynamic_update_slice(
                attn_shard, attn_found[piece][index][None], place(rep_rank) + (0,)
            )
        attn_shard = attn_shard.astype(F32)

    return (
        jnp.swapaxes(hidden_out, 1, 2),
        deleted.reshape(micro_count, local_rows),
        jnp.swapaxes(grad_in, 1, 2),
        total[:block],
        attn_shard[0],
        attn_shard[1],
        attn_shard[2],
        attn_shard[3].reshape(proj // shards, width),
        total[4 * block : 4 * block + bucket_rows * heads].reshape(bucket_rows, heads),
        total[block : 2 * block],
        grad_gate,
        grad_up,
        grad_down_out,
        total[2 * block : 3 * block],
        total[3 * block : 4 * block],
    )


def used_by(pieces, moves):
    wanted = sorted({move[0] for move in moves})
    return [pieces[i] for i in wanted], [(wanted.index(move[0]),) + move[1:] for move in moves]


def tile_hint(place, row_unit, column_unit):
    def hinted(at, chip_at):
        row, column = place(at, chip_at)
        return pl.multiple_of(row, row_unit), pl.multiple_of(column, column_unit)

    return hinted


def solution(mesh):
    rows = P(None, ("rep", "shard"), None)
    flat = P(None, ("rep", "shard"))
    by_rep = P(None, "rep", None)
    vector = P("shard")
    matrix = P("shard", None)
    in_specs = (
        (rows, rows, flat, by_rep, by_rep, P(), vector)
        + (matrix,) * 5
        + (vector,)
        + (matrix,) * 3
        + (vector, vector)
    )
    out_specs = (
        (rows, flat, rows, vector) + (matrix,) * 5 + (vector,) + (matrix,) * 3 + (vector, vector)
    )
    return jax.shard_map(
        on_device, mesh=mesh, in_specs=in_specs, out_specs=out_specs, check_vma=False
    )
```

```python
import functools

import math

import jax
import jax.numpy as jnp
from jax import lax
from jax.experimental import pallas as pl
from jax.experimental.pallas import tpu as pltpu
from jax.sharding import PartitionSpec as P

EPSILON = 1e-06
HIGHEST = lax.Precision.HIGHEST
MASKED = -1000000000.0
BF16 = jnp.bfloat16
LIGHT = pl.CostEstimate(flops=1000, bytes_accessed=1000, transcendentals=0)
F32 = jnp.float32


ANY = pl.BlockSpec(memory_space=pl.ANY)
VMEM = pl.BlockSpec(memory_space=pltpu.VMEM)


def rms_scale(hidden):
    return lax.rsqrt(jnp.mean(hidden * hidden, axis=-1, keepdims=True) + EPSILON)


def rms_back(hidden, scale_row, gain, upstream):
    scaled = upstream * gain
    return scale_row * scaled - hidden * (scale_row * scale_row * scale_row) * jnp.mean(
        hidden * scaled, axis=-1, keepdims=True
    )


def bias_kernel(rows_ref, slots_ref, out_ref):
    group = out_ref.shape[2]
    row = jnp.broadcast_to(rows_ref[0], (group, rows_ref.shape[2]))
    grid = pltpu.roll(row, group + 1, 1, stride=1, stride_axis=0)[:, :group].astype(BF16)
    tokens = slots_ref.shape[0]
    pick = (slots_ref[...] == lax.broadcasted_iota(jnp.int32, (tokens, group), 1)).astype(BF16)
    out_ref[0] = jnp.dot(pick, grid, preferred_element_type=F32).astype(BF16)


def bias_of_queries(bias_rows, slots, group):
    heads, width = bias_rows.shape
    tokens = slots.shape[0]
    return pl.pallas_call(
        bias_kernel,
        grid=(heads,),
        in_specs=[
            pl.BlockSpec((1, 1, width), lambda h: (h, 0, 0)),
            pl.BlockSpec((tokens, 1), lambda h: (0, 0)),
        ],
        out_specs=pl.BlockSpec((1, tokens, group), lambda h: (h, 0, 0)),
        out_shape=jax.ShapeDtypeStruct((heads, tokens, group), BF16),
    )(bias_rows.reshape(heads, 1, width), slots.reshape(tokens, 1))


def bias_fold(score_grads, slots):
    heads, local, group = score_grads[0].shape
    count = len(score_grads)

    def kernel(*refs):
        grad_refs, slots_ref, out_ref = refs[:count], refs[count], refs[count + 1]
        square = None
        for index, ref in enumerate(grad_refs):
            mine = slots_ref[:, index * local : (index + 1) * local]
            row = lax.broadcasted_iota(jnp.int32, (group, local), 0)
            place = (row == (group - 1) - mine).astype(BF16)
            part = jnp.dot(place, ref[0], preferred_element_type=F32)
            square = part if square is None else square + part
        wide = jnp.concatenate([square, jnp.zeros_like(square)], axis=1)
        rolled = pltpu.roll(wide, 0, 1, stride=1, stride_axis=0)
        out_ref[0] = jnp.sum(rolled, axis=0, keepdims=True)

    return pl.pallas_call(
        kernel,
        grid=(heads,),
        in_specs=[pl.BlockSpec((1, local, group), lambda h: (h, 0, 0))] * count
        + [pl.BlockSpec((1, count * local), lambda h: (0, 0))],
        out_specs=pl.BlockSpec((1, 1, 2 * group), lambda h: (h, 0, 0)),
        out_shape=jax.ShapeDtypeStruct((heads, 1, 2 * group), F32),
    )(*score_grads, slots.reshape(1, count * local)).reshape(heads, 2 * group)


def by_head(value, head, head_size):
    per_block = 128 // head_size
    start = head // per_block * 128
    lanes = lax.broadcasted_iota(jnp.int32, (1, 128), 1) // head_size
    block = value[:, start : start + 128]
    return jnp.where(lanes == head % per_block, block, jnp.zeros_like(block)), start


def dot_last(left, right):
    return lax.dot_general(left, right, (((1,), (1,)), ((), ())), preferred_element_type=F32)


def attention_call(micro, lengths, queries, pairs, own_slots, key_slots, bias, context):
    heads, rows, group = bias.shape
    double = pairs[0].shape[1]
    count = len(pairs)
    local = group // count
    proj = double // 2
    head_size = proj // heads

    def kernel(lengths_ref, query_ref, *rest):
        pair_refs = rest[:count]
        own_ref, key_ref, bias_ref = rest[count : count + 3]
        context_ref, prob_ref, packed_ref, arrived = rest[-4:]
        for index, ref in enumerate(pair_refs):
            arrived[index * local : (index + 1) * local] = ref[...]
        place = (
            lax.broadcasted_iota(jnp.int32, (group, group), 0) == key_ref[...]
        ).astype(BF16)
        packed_ref[...] = jnp.dot(place, arrived[...], preferred_element_type=F32).astype(BF16)
        first = lengths_ref[0]
        key_seg = lax.broadcasted_iota(jnp.int32, (local, group), 1) >= first
        same = key_seg == (own_ref[...] >= first)
        per_block = 128 // head_size
        total = None
        for head in range(heads):
            query, start = by_head(query_ref[...], head, head_size)
            scores = dot_last(query, packed_ref[:, start : start + 128])
            scores = jnp.where(same, scores + bias_ref[head].astype(F32), MASKED)
            weights = jnp.exp(scores - jnp.max(scores, axis=1, keepdims=True))
            weights = (weights / jnp.sum(weights, axis=1, keepdims=True)).astype(BF16)
            prob_ref[head] = weights
            value, _ = by_head(packed_ref[:, proj:], head, head_size)
            part = jnp.dot(weights, value, preferred_element_type=F32)
            total = part if head % per_block == 0 else total + part
            if head % per_block == per_block - 1:
                context_ref[:, start : start + 128] = total.astype(BF16)

    return pl.pallas_call(
        kernel,
        grid=(1,),
        in_specs=[
            pl.BlockSpec(memory_space=pltpu.SMEM),
            pl.BlockSpec((local, proj), lambda i: (micro, 0)),
        ]
        + [pl.BlockSpec((local, double), lambda i: (micro, 0))] * count
        + [
            pl.BlockSpec((local, 1), lambda i: (micro, 0)),
            pl.BlockSpec((1, group), lambda i: (0, 0)),
            pl.BlockSpec((heads, local, group), lambda i: (0, micro, 0)),
        ]
        + [ANY] * len(context),
        out_specs=[
            pl.BlockSpec((local, proj), lambda i: (micro, 0)),
            pl.BlockSpec((heads, local, group), lambda i: (0, 0, 0)),
            pl.BlockSpec((group, double), lambda i: (0, 0)),
        ],
        out_shape=[
            jax.ShapeDtypeStruct(queries.shape, BF16),
            jax.ShapeDtypeStruct((heads, local, group), BF16),
            jax.ShapeDtypeStruct((group, double), BF16),
        ],
        input_output_aliases={count + 5: 0} if context else {},
        scratch_shapes=[pltpu.VMEM((group, double), BF16)],
        cost_estimate=LIGHT,
    )(lengths, queries, *pairs, own_slots, key_slots, bias, *context)


def attention_back_call(micro, queries, context_grad, probs, packed, key_slots, shards, sums):
    heads, local, group = probs.shape
    double = packed.shape[1]
    proj = double // 2
    head_size = proj // heads

    def kernel(query_ref, context_ref, prob_ref, packed_ref, key_ref, *rest):
        score_ref, dq_ref, part_ref, sums = rest[-4:]
        per_block = 128 // head_size
        for head in range(heads):
            context, start = by_head(context_ref[...], head, head_size)
            query, _ = by_head(query_ref[...], head, head_size)
            key, _ = by_head(packed_ref[:, :proj], head, head_size)
            weights = prob_ref[head]
            wide = weights.astype(F32)
            upstream = dot_last(context, packed_ref[:, proj + start : proj + start + 128])
            inner = jnp.sum(wide * upstream, axis=1, keepdims=True)
            grad = (wide * (upstream - inner)).astype(BF16)
            score_ref[head] = grad
            query_part = jnp.dot(grad, key, preferred_element_type=F32)
            key_part = jnp.dot(grad.T, query, preferred_element_type=F32)
            value_part = jnp.dot(weights.T, context, preferred_element_type=F32)
            if head % per_block == 0:
                totals = [query_part, key_part, value_part]
            else:
                totals = [
                    total + part
                    for total, part in zip(totals, (query_part, key_part, value_part))
                ]
            if head % per_block == per_block - 1:
                dq_ref[:, start : start + 128] = totals[0].astype(BF16)
                sums[:, start : start + 128] = totals[1].astype(BF16)
                sums[:, proj + start : proj + start + 128] = totals[2].astype(BF16)
        for index in range(shards):
            slots = key_ref[index * local : (index + 1) * local]
            pick = (lax.broadcasted_iota(jnp.int32, (local, group), 1) == slots).astype(BF16)
            part_ref[index] = jnp.dot(pick, sums[...], preferred_element_type=F32).astype(BF16)

    return pl.pallas_call(
        kernel,
        grid=(1,),
        in_specs=[
            pl.BlockSpec((local, proj), lambda i: (micro, 0)),
            pl.BlockSpec((local, proj), lambda i: (micro, 0)),
            pl.BlockSpec((heads, local, group), lambda i: (0, 0, 0)),
            pl.BlockSpec((group, double), lambda i: (0, 0)),
            pl.BlockSpec((group, 1), lambda i: (0, 0)),
        ]
        + [ANY] * len(sums),
        out_specs=[
            pl.BlockSpec((heads, local, group), lambda i: (0, 0, 0)),
            pl.BlockSpec((local, proj), lambda i: (micro, 0)),
            pl.BlockSpec((shards, local, double), lambda i: (0, micro, 0)),
        ],
        out_shape=[
            jax.ShapeDtypeStruct((heads, local, group), BF16),
            jax.ShapeDtypeStruct(queries.shape, BF16),
            jax.ShapeDtypeStruct((shards, queries.shape[0], double), BF16),
        ],
        input_output_aliases={5 + i: 1 + i for i in range(len(sums))},
        scratch_shapes=[pltpu.VMEM((group, double), BF16)],
        cost_estimate=LIGHT,
    )(queries, context_grad, probs, packed, key_slots, *sums)


def axis_ranks():
    return lax.axis_index("shard"), lax.axis_index("rep") // 2


def gelu_parts(value):
    inner = math.sqrt(2.0 / math.pi)
    square = value * value
    bend = jnp.tanh(inner * value * (1.0 + 0.044715 * square))
    outside = 0.5 * (1.0 + bend)
    slope = outside + 0.5 * value * (1.0 - bend * bend) * (inner * (1.0 + 0.134145 * square))
    return value * outside, slope


def run_copies(copies, sems):
    started = [pltpu.make_async_copy(src, dst, sems.at[i]) for i, (src, dst) in enumerate(copies)]
    for copy in started:
        copy.start()
    return started


def pick_kernel(gate_ref, up_ref, out_ref):
    core = lax.axis_index("rep") % 2
    inner = gate_ref.shape[1]
    shards = lax.axis_size("shard")
    unit = inner // shards
    half = unit // 2
    for index, ref in enumerate((gate_ref, up_ref)):
        parts = []
        for shard in range(shards):
            low = ref[:, shard * unit : shard * unit + half]
            high = ref[:, shard * unit + half : (shard + 1) * unit]
            parts.append(jnp.where(core == 0, low, high))
        out_ref[:, index * (inner // 2) : (index + 1) * (inner // 2)] = jnp.concatenate(parts, 1)


def pick_columns(w_gate, w_up):
    return pl.pallas_call(
        pick_kernel,
        in_specs=[VMEM, VMEM],
        out_specs=VMEM,
        out_shape=jax.ShapeDtypeStruct(w_gate.shape, BF16),
    )(w_gate, w_up)


def spread_kernel(low_ref, high_ref, gate_ref, up_ref):
    inner = gate_ref.shape[1]
    shards = lax.axis_size("shard")
    half = inner // shards // 2
    for index, ref in enumerate((gate_ref, up_ref)):
        parts = []
        for shard in range(shards):
            start = index * (inner // 2) + shard * half
            parts += [low_ref[:, start : start + half], high_ref[:, start : start + half]]
        ref[...] = jnp.concatenate(parts, 1).astype(F32)


def spread_columns(low, high):
    shape = jax.ShapeDtypeStruct(low.shape, F32)
    return pl.pallas_call(
        spread_kernel,
        in_specs=[VMEM, VMEM],
        out_specs=[VMEM, VMEM],
        out_shape=[shape, shape],
    )(low, high)


def project_call(tokens, gain, pieces, places, block, proj):
    rows, width = tokens.shape
    count = len(pieces)
    moves = 2 * sum(len(place) for place in places)

    def kernel(token_ref, gain_ref, *rest):
        piece_refs = rest[:count]
        normed_ref, query_ref, pair_ref, keep_ref, weights, sems = rest[count:]
        rank, rep = lax.axis_index("shard"), lax.axis_index("rep")
        copies = []
        for ref, place in zip(piece_refs, places):
            for index, where in place:
                source = ref if index is None else ref.at[index]
                for start, size, matrix, row in where(rank, rep):
                    copies.append(
                        (source.at[pl.ds(start, size)], weights.at[matrix, pl.ds(row, size)])
                    )
        copies = run_copies(copies, sems)
        hidden = token_ref[...].astype(F32)
        scale = lax.rsqrt(jnp.mean(hidden * hidden, axis=1, keepdims=True) + EPSILON)
        normed = (hidden * scale * gain_ref[...]).astype(BF16)
        normed_ref[...] = normed
        for copy in copies:
            copy.wait()
        keep = pltpu.make_async_copy(weights, keep_ref, sems.at[moves])
        keep.start()
        query_ref[...] = jnp.dot(normed, weights[0], preferred_element_type=F32).astype(BF16)
        pair_ref[:, :proj] = jnp.dot(normed, weights[1], preferred_element_type=F32).astype(BF16)
        pair_ref[:, proj:] = jnp.dot(normed, weights[2], preferred_element_type=F32).astype(BF16)
        keep.wait()

    return pl.pallas_call(
        kernel,
        in_specs=[VMEM, VMEM] + [ANY] * count,
        out_specs=[VMEM, VMEM, VMEM, ANY],
        out_shape=[
            jax.ShapeDtypeStruct((rows, width), BF16),
            jax.ShapeDtypeStruct((rows, proj), BF16),
            jax.ShapeDtypeStruct((rows, 2 * proj), BF16),
            jax.ShapeDtypeStruct((4, width, proj), BF16),
        ],
        scratch_shapes=[
            pltpu.VMEM((4, width, proj), BF16),
            pltpu.SemaphoreType.DMA((moves + 1,)),
        ],
        cost_estimate=LIGHT,
    )(tokens, gain, *pieces)


def project_grad_call(normed, query_grad, pair_grad, out_grads, small, outputs):
    rows, width = normed.shape
    proj = query_grad.shape[1]
    count = len(outputs)
    moves = sum(len(items) for _, items in outputs)

    small_rows = small.shape[1]

    def kernel(normed_ref, query_ref, pair_ref, out_grad_ref, small_ref, *rest):
        out_refs, result, sems = rest[:count], rest[count], rest[count + 1]
        fourth = pltpu.make_async_copy(out_grad_ref, result.at[3], sems.at[2 * moves])
        fourth.start()
        for begin in range(0, width, 256):
            size = min(256, width - begin)
            turned = normed_ref[:, begin : begin + size].T
            for index in range(3):
                right = query_ref[...] if index == 0 else pair_ref[:, (index - 1) * proj : index * proj]
                result[index, begin : begin + size] = jnp.dot(
                    turned, right, preferred_element_type=F32
                ).astype(BF16)
        fourth.wait()
        rank, rep = lax.axis_index("shard"), lax.axis_index("rep")
        copies = []
        for ref, (shape, items) in zip(out_refs, outputs):
            for index, where, step in items:
                matrix, row = where(rank, rep)
                size = shape[-2] - (small_rows if step is not None else 0)
                copies.append((result.at[matrix, pl.ds(row, size)], ref.at[index + (pl.ds(0, size),)]))
                if step is not None:
                    copies.append(
                        (
                            small_ref.at[step],
                            ref.at[index + (pl.ds(size, small_rows),)],
                        )
                    )
        for copy in run_copies(copies, sems):
            copy.wait()

    return pl.pallas_call(
        kernel,
        in_specs=[VMEM, VMEM, VMEM, ANY, VMEM],
        out_specs=[ANY] * count,
        out_shape=[jax.ShapeDtypeStruct(shape, BF16) for shape, _ in outputs],
        scratch_shapes=[
            pltpu.VMEM((4, width, proj), BF16),
            pltpu.SemaphoreType.DMA((2 * moves + 1,)),
        ],
        cost_estimate=LIGHT,
    )(normed, query_grad, pair_grad, out_grads, small)


def part_of(ref, row, count, columns):
    if (row, count, columns) == (0,) + ref.shape:
        return ref
    return ref.at[pl.ds(row, count), pl.ds(0, columns)]


def gate_up_call(own, other, width, inner, pieces, moves):
    rows, wide = own.shape
    count, steps = len(pieces), len(moves)
    half = inner // 2
    tile = 256

    def kernel(own_ref, other_ref, *rest):
        piece_refs = rest[:count]
        out_refs, keep_ref = rest[count : count + 3], rest[count + 3]
        both, weights, slopes, acts, hiddens, sems = rest[count + 4 :]
        results = (slopes, acts, hiddens)
        rank, chip = axis_ranks()
        copies = [(own_ref, both.at[:rows]), (other_ref, both.at[rows:])]
        for piece, row, size, columns, place in moves:
            to_row, to_column = place(rank, chip)
            copies.append(
                (
                    part_of(piece_refs[piece], row, size, columns),
                    weights.at[pl.ds(to_row, size), pl.ds(to_column, columns)],
                )
            )
        for copy in run_copies(copies, sems):
            copy.wait()
        keep = pltpu.make_async_copy(weights, keep_ref, sems.at[steps + 2])
        keep.start()

        def step(index, carry):
            start = pl.multiple_of(index * tile, tile)
            left = both[:, :width]
            gate = jnp.dot(left, weights[:, pl.ds(start, tile)], preferred_element_type=F32)
            up = jnp.dot(
                left,
                weights[:, pl.ds(pl.multiple_of(half + start, tile), tile)],
                preferred_element_type=F32,
            )
            act, slope = gelu_parts(gate)
            columns = pl.ds(start, tile)
            for number, value in enumerate((up * slope, act, act * up)):
                results[number][:, columns] = value.astype(BF16)
                pltpu.make_async_copy(
                    results[number].at[:, columns],
                    out_refs[number].at[:, columns],
                    sems.at[steps + 3 + number],
                ).start()
            return carry

        lax.fori_loop(0, half // tile, step, 0)
        keep.wait()
        for number in range(3):
            pltpu.make_async_copy(
                results[number], out_refs[number], sems.at[steps + 3 + number]
            ).wait()

    shape = jax.ShapeDtypeStruct((2 * rows, half), BF16)
    return pl.pallas_call(
        kernel,
        in_specs=[ANY] * (2 + count),
        out_specs=[ANY] * 4,
        out_shape=[shape, shape, shape, jax.ShapeDtypeStruct((width, inner), BF16)],
        scratch_shapes=[
            pltpu.VMEM((2 * rows, wide), BF16),
            pltpu.VMEM((width, inner), BF16),
        ]
        + [pltpu.VMEM((2 * rows, half), BF16)] * 3
        + [
            pltpu.SemaphoreType.DMA((steps + 6,)),
        ],
        cost_estimate=LIGHT,
    )(own, other, *pieces)


def col_tiles(width):
    return [(start, min(512, width - start)) for start in range(0, width, 512)]


def down_call(hidden, width, padded, pieces, moves):
    double, half = hidden.shape
    rows = double // 2
    count, steps = len(pieces), len(moves)

    def kernel(hidden_ref, *rest):
        piece_refs = rest[:count]
        own_ref, other_ref, keep_ref, weights, sems = rest[count:]
        rank, chip = axis_ranks()
        copies = []
        for piece, row, size, columns, place in moves:
            to_row, to_column = place(rank, chip)
            copies.append(
                (
                    part_of(piece_refs[piece], row, size, columns),
                    weights.at[pl.ds(to_row, size), pl.ds(to_column, columns)],
                )
            )
        for copy in run_copies(copies, sems):
            copy.wait()
        keep = pltpu.make_async_copy(weights, keep_ref, sems.at[steps])
        keep.start()
        for start, size in col_tiles(width):
            columns = slice(start, start + size)
            own_ref[:, columns] = jnp.dot(
                hidden_ref[:rows], weights[:, columns], preferred_element_type=F32
            )
            other_ref[:, columns] = jnp.dot(
                hidden_ref[rows:], weights[:, columns], preferred_element_type=F32
            ).astype(BF16)
        if padded > width:
            other_ref[:, width:] = jnp.zeros((rows, padded - width), BF16)
        keep.wait()

    return pl.pallas_call(
        kernel,
        in_specs=[VMEM] + [ANY] * count,
        out_specs=[VMEM, VMEM, ANY],
        out_shape=[
            jax.ShapeDtypeStruct((rows, width), F32),
            jax.ShapeDtypeStruct((rows, padded), BF16),
            jax.ShapeDtypeStruct((half, padded), BF16),
        ],
        scratch_shapes=[pltpu.VMEM((half, padded), BF16), pltpu.SemaphoreType.DMA((steps + 1,))],
        cost_estimate=LIGHT,
    )(hidden, *pieces)


def finish_call(pieces, gate_up_moves, down_moves, block, inner, down_rows, width, padded):
    count = len(pieces)
    steps = len(gate_up_moves) + len(down_moves)

    def kernel(*refs):
        piece_refs = refs[:count]
        out_refs = refs[count : count + 3]
        columns_of, rows_of, gate_ref, up_ref, down_ref, sems = refs[count + 3 :]
        chip, core = axis_ranks()[1], lax.axis_index("rep") % 2
        shards = lax.axis_size("shard")
        copies = []
        for piece, row, size, columns, place in gate_up_moves:
            to_core, to_row, to_column = place(core, chip)
            copies.append(
                (
                    part_of(piece_refs[piece], row, size, columns),
                    columns_of.at[to_core, pl.ds(to_row, size), pl.ds(to_column, columns)],
                )
            )
        for piece, row, size, columns, place in down_moves:
            to_row, to_column = place(core, chip)
            copies.append(
                (
                    part_of(piece_refs[piece], row, size, columns),
                    rows_of.at[pl.ds(to_row, size), pl.ds(to_column, columns)],
                )
            )
        copies = run_copies(copies, sems)
        for copy in copies[: len(gate_up_moves)]:
            copy.wait()
        half = inner // shards // 2
        outs = [
            pltpu.make_async_copy(ref, out, sems.at[steps + number])
            for number, (ref, out) in enumerate(zip((gate_ref, up_ref, down_ref), out_refs))
        ]
        for index, ref in enumerate((gate_ref, up_ref)):
            for shard in range(shards):
                start = index * (inner // 2) + shard * half
                both = [columns_of[at, :, start : start + half] for at in range(2)]
                ref[:, 2 * half * shard : 2 * half * (shard + 1)] = jnp.concatenate(
                    both, 1
                ).astype(F32)
            outs[index].start()
        for copy in copies[len(gate_up_moves) :]:
            copy.wait()
        down_ref[...] = rows_of[...].T[:width].astype(F32)
        outs[2].start()
        for copy in outs:
            copy.wait()

    return pl.pallas_call(
        kernel,
        in_specs=[ANY] * count,
        out_specs=[ANY] * 3,
        out_shape=[
            jax.ShapeDtypeStruct((block, inner), F32),
            jax.ShapeDtypeStruct((block, inner), F32),
            jax.ShapeDtypeStruct((width, down_rows), F32),
        ],
        scratch_shapes=[
            pltpu.VMEM((2, block, inner), BF16),
            pltpu.VMEM((down_rows, padded), BF16),
            pltpu.VMEM((block, inner), F32),
            pltpu.VMEM((block, inner), F32),
            pltpu.VMEM((width, down_rows), F32),
            pltpu.SemaphoreType.DMA((steps + 3,)),
        ],
    )(*pieces)


def attn_finish_call(pieces, moves, block, proj):
    count = len(pieces)

    def kernel(*refs):
        piece_refs = refs[:count]
        out_refs, whole, sems = refs[count : count + 4], refs[count + 4], refs[count + 5]
        rep = lax.axis_index("rep")
        copies = []
        for piece, index, place in moves:
            for start, size, matrix, row in place(rep):
                copies.append(
                    (
                        piece_refs[piece].at[index, pl.ds(start, size)],
                        whole.at[matrix, pl.ds(row, size)],
                    )
                )
        for copy in run_copies(copies, sems):
            copy.wait()
        for index, ref in enumerate(out_refs):
            ref[...] = whole[index].astype(F32)

    return pl.pallas_call(
        kernel,
        in_specs=[ANY] * count,
        out_specs=[VMEM] * 4,
        out_shape=[jax.ShapeDtypeStruct((block, proj), F32)] * 4,
        scratch_shapes=[
            pltpu.VMEM((4, block, proj), BF16),
            pltpu.SemaphoreType.DMA((2 * len(moves),)),
        ],
    )(*pieces)


def hidden_grad_call(own, other, down, slope, act):
    rows, width = own.shape
    half = down.shape[0]
    tile = 256

    def kernel(own_ref, other_ref, down_ref, slope_ref, act_ref, gate_ref, up_ref):
        for index, ref in enumerate((own_ref, other_ref)):
            part = slice(index * rows, (index + 1) * rows)
            upstream = dot_last(ref[...], down_ref[...])
            gate_ref[part] = (upstream * slope_ref[part].astype(F32)).astype(BF16)
            up_ref[part] = (upstream * act_ref[part].astype(F32)).astype(BF16)

    whole = pl.BlockSpec((rows, width), lambda i: (0, 0))
    columns = pl.BlockSpec((2 * rows, tile), lambda i: (0, i))
    shape = jax.ShapeDtypeStruct((2 * rows, half), BF16)
    return pl.pallas_call(
        kernel,
        grid=(half // tile,),
        in_specs=[
            whole,
            whole,
            pl.BlockSpec((tile, down.shape[1]), lambda i: (i, 0)),
            columns,
            columns,
        ],
        out_specs=[columns, columns],
        out_shape=[shape, shape],
        cost_estimate=LIGHT,
    )(own, other, down, slope, act)


def normed_grad_call(gate, up, weights):
    double, half = gate.shape
    rows = double // 2
    width = weights.shape[0]
    tile = 256

    def kernel(gate_ref, up_ref, low_ref, high_ref, own_ref, other_ref):
        for index, ref in enumerate((own_ref, other_ref)):
            part = slice(index * rows, (index + 1) * rows)
            total = dot_last(gate_ref[part], low_ref[...]) + dot_last(up_ref[part], high_ref[...])
            ref[...] = total.astype(ref.dtype)

    whole = pl.BlockSpec((double, half), lambda i: (0, 0))
    return pl.pallas_call(
        kernel,
        grid=(pl.cdiv(width, tile),),
        in_specs=[
            whole,
            whole,
            pl.BlockSpec((tile, half), lambda i: (i, 0)),
            pl.BlockSpec((tile, half), lambda i: (i, 1)),
        ],
        out_specs=[pl.BlockSpec((rows, tile), lambda i: (0, i))] * 2,
        out_shape=[
            jax.ShapeDtypeStruct((rows, width), F32),
            jax.ShapeDtypeStruct((rows, lane_tiles(width)), BF16),
        ],
        cost_estimate=LIGHT,
    )(gate, up, weights, weights)


def row_specs(micro_count, local, width):
    return pl.BlockSpec((local, width), lambda i: (i, 0)), pl.BlockSpec((1, width), lambda i: (0, 0))


def sum_rows(ref, value):
    total = jnp.sum(value, axis=0, keepdims=True)

    @pl.when(pl.program_id(0) == 0)
    def _():
        ref[...] = total

    @pl.when(pl.program_id(0) > 0)
    def _():
        ref[...] += total


def put_padded(ref, value):
    width = value.shape[1]
    ref[:, :width] = value.astype(BF16)
    if ref.shape[1] > width:
        ref[:, width:] = jnp.zeros((value.shape[0], ref.shape[1] - width), BF16)


def lane_tiles(width):
    return -(-width // 128) * 128


def mid_call(tokens, context, w_out, gain, micro_count):
    rows, width = tokens.shape
    local = rows // micro_count
    by_row, vector = row_specs(micro_count, local, width)

    def kernel(token_ref, context_ref, out_ref, gain_ref, hidden_ref, normed_ref):
        hidden = token_ref[...].astype(F32) + jnp.dot(
            context_ref[...], out_ref[...], preferred_element_type=F32
        )
        hidden_ref[...] = hidden
        put_padded(normed_ref, hidden * rms_scale(hidden) * gain_ref[...])

    return pl.pallas_call(
        kernel,
        grid=(micro_count,),
        in_specs=[
            by_row,
            pl.BlockSpec((local, context.shape[1]), lambda i: (i, 0)),
            pl.BlockSpec(w_out.shape, lambda i: (0, 0)),
            vector,
        ],
        out_specs=[by_row, pl.BlockSpec((local, lane_tiles(width)), lambda i: (i, 0))],
        out_shape=[
            jax.ShapeDtypeStruct((rows, width), F32),
            jax.ShapeDtypeStruct((rows, lane_tiles(width)), BF16),
        ],
        cost_estimate=LIGHT,
    )(tokens, context, w_out, gain)


def out_call(hidden, part, given, cotangent, gate_cotangent, gain, vector_in, micro_count):
    rows, width = hidden.shape
    local = rows // micro_count
    by_row, vector = row_specs(micro_count, local, width)
    one = pl.BlockSpec((local, 1), lambda i: (i, 0))
    turned = pl.BlockSpec((1, width, local), lambda i: (i, 0, 0))
    padded = pl.BlockSpec((local, lane_tiles(width)), lambda i: (i, 0))

    def kernel(
        hidden_ref, part_ref, given_ref, up_ref, gate_ref, gain_ref, vector_ref,
        state_ref, deleted_ref, grad_ref, low_ref, gain_grad_ref, vector_grad_ref,
    ):
        state = hidden_ref[...] + part_ref[...] + given_ref[:, :width].astype(F32)
        state_ref[0] = state.T
        scale = rms_scale(state)
        normed = state * scale * gain_ref[...]
        logit = jnp.sum(normed * vector_ref[...], axis=1, keepdims=True)
        sigmoid = lax.logistic(logit)
        deleted_ref[...] = -30.0 * sigmoid
        slope = gate_ref[...] * -30.0 * sigmoid * (1.0 - sigmoid)
        upstream = slope * vector_ref[...]
        sum_rows(vector_grad_ref, slope * normed)
        sum_rows(gain_grad_ref, upstream * state * scale)
        grad = up_ref[...].astype(F32) + rms_back(state, scale, gain_ref[...], upstream)
        grad_ref[...] = grad
        put_padded(low_ref, grad)

    return pl.pallas_call(
        kernel,
        grid=(micro_count,),
        in_specs=[by_row, by_row, padded, by_row, one, vector, vector],
        out_specs=[turned, one, by_row, padded, vector, vector],
        out_shape=[
            jax.ShapeDtypeStruct((micro_count, width, local), F32),
            jax.ShapeDtypeStruct((rows, 1), F32),
            jax.ShapeDtypeStruct((rows, width), F32),
            jax.ShapeDtypeStruct((rows, lane_tiles(width)), BF16),
            jax.ShapeDtypeStruct((1, width), F32),
            jax.ShapeDtypeStruct((1, width), F32),
        ],
        cost_estimate=LIGHT,
    )(hidden, part, given, cotangent, gate_cotangent, gain, vector_in)


def back_call(part, given, grad_out, hidden, gain, context, w_out, micro_count):
    rows, width = hidden.shape
    local = rows // micro_count
    proj = context.shape[1]
    by_row, vector = row_specs(micro_count, local, width)
    by_proj = pl.BlockSpec((local, proj), lambda i: (i, 0))
    padded = pl.BlockSpec((local, lane_tiles(width)), lambda i: (i, 0))
    whole = pl.BlockSpec((proj, width), lambda i: (0, 0))

    def kernel(
        part_ref, given_ref, grad_ref, hidden_ref, gain_ref, context_ref, out_ref,
        mid_ref, context_grad_ref, out_grad_ref, gain_grad_ref, total,
    ):
        normed_grad = part_ref[...] + given_ref[:, :width].astype(F32)
        hidden = hidden_ref[...]
        scale = rms_scale(hidden)
        sum_rows(gain_grad_ref, normed_grad * hidden * scale)
        mid = grad_ref[...] + rms_back(hidden, scale, gain_ref[...], normed_grad)
        mid_ref[...] = mid
        low = mid.astype(BF16)
        context_grad_ref[...] = dot_last(low, out_ref[...]).astype(BF16)
        product = jnp.dot(context_ref[...].T, low, preferred_element_type=F32)
        step = pl.program_id(0)

        @pl.when(step == 0)
        def _():
            total[...] = product

        @pl.when(step > 0)
        def _():
            total[...] += product

        @pl.when(step == micro_count - 1)
        def _():
            out_grad_ref[...] = total[...].astype(BF16)

    return pl.pallas_call(
        kernel,
        grid=(micro_count,),
        in_specs=[by_row, padded, by_row, by_row, vector, by_proj, whole],
        out_specs=[by_row, by_proj, whole, vector],
        out_shape=[
            jax.ShapeDtypeStruct((rows, width), F32),
            jax.ShapeDtypeStruct((rows, proj), BF16),
            jax.ShapeDtypeStruct((proj, width), BF16),
            jax.ShapeDtypeStruct((1, width), F32),
        ],
        scratch_shapes=[pltpu.VMEM((proj, width), F32)],
        cost_estimate=LIGHT,
    )(part, given, grad_out, hidden, gain, context, w_out)


def in_call(query_grad, pair_parts, weights, grad_mid, tokens, gain, micro_count):
    rows, width = tokens.shape
    local = rows // micro_count
    proj = query_grad.shape[1]
    count = pair_parts.shape[0]
    by_row, vector = row_specs(micro_count, local, width)
    by_proj = pl.BlockSpec((local, proj), lambda i: (i, 0))
    by_pair = pl.BlockSpec((local, 2 * proj), lambda i: (i, 0))

    def kernel(
        query_ref, part_ref, wq_ref, wk_ref, wv_ref, mid_ref, token_ref, gain_ref,
        pair_ref, grad_ref, gain_grad_ref,
    ):
        pair = sum(part_ref[index].astype(F32) for index in range(count)).astype(BF16)
        pair_ref[...] = pair
        normed_grad = (
            dot_last(query_ref[...], wq_ref[0])
            + dot_last(pair[:, :proj], wk_ref[0])
            + dot_last(pair[:, proj:], wv_ref[0])
        )
        hidden = token_ref[...].astype(F32)
        scale = rms_scale(hidden)
        sum_rows(gain_grad_ref, normed_grad * hidden * scale)
        grad = mid_ref[...] + rms_back(hidden, scale, gain_ref[...], normed_grad)
        grad_ref[0] = grad.astype(BF16).T

    return pl.pallas_call(
        kernel,
        grid=(micro_count,),
        in_specs=[by_proj, pl.BlockSpec((count, local, 2 * proj), lambda i: (0, i, 0))]
        + [pl.BlockSpec((1, width, proj), lambda i, m=m: (m, 0, 0)) for m in range(3)]
        + [by_row, by_row, vector],
        out_specs=[by_pair, pl.BlockSpec((1, width, local), lambda i: (i, 0, 0)), vector],
        out_shape=[
            jax.ShapeDtypeStruct((rows, 2 * proj), BF16),
            jax.ShapeDtypeStruct((micro_count, width, local), BF16),
            jax.ShapeDtypeStruct((1, width), F32),
        ],
        cost_estimate=LIGHT,
    )(query_grad, pair_parts, weights, weights, weights, grad_mid, tokens, gain)


def weight_grad_call(left, right, picks, width, outputs, in_halves):
    left_own, left_other = left
    right_own, right_other = right
    rows = left_own.shape[0]
    total = 2 * rows if left_other is not None else rows
    beside = right_other is not None and right_own.shape[0] == total
    right_width = right_own.shape[1] * (2 if beside else 1)
    count = len(outputs)
    copies_out = sum(len(moves) for _, moves, _ in outputs)
    depth = sum(size for _, size in picks)
    tile = 256
    split = left_other is not None
    right_split = right_other is not None
    inputs = [left_own] + ([left_other] if split else []) + [right_own]
    inputs += [right_other] if right_split else []

    def kernel(*refs):
        in_refs = list(refs[: len(inputs)])
        out_refs = refs[len(inputs) : len(inputs) + count]
        lefts, turned, rights, result, sems = refs[len(inputs) + count :]
        copies = []
        for target, parted, aside in ((lefts, split, False), (rights, right_split, beside)):
            first = in_refs.pop(0)
            size = first.shape[1] if aside else first.shape[0]
            if not parted:
                copies.append((first, target))
            elif aside:
                copies.append((first, target.at[:, :size]))
                copies.append((in_refs.pop(0), target.at[:, size:]))
            else:
                copies.append((first, target.at[:size]))
                copies.append((in_refs.pop(0), target.at[size:]))
        for copy in run_copies(copies, sems):
            copy.wait()
        to_row = 0
        for first, size in picks:
            for begin in range(0, size, tile):
                span = min(tile, size - begin)
                turned[to_row : to_row + span] = lefts[:, first + begin : first + begin + span].T
                to_row += span

        def product(start, size):
            result[:, pl.ds(start, size)] = jnp.dot(
                turned[...], rights[:, pl.ds(start, size)], preferred_element_type=F32
            ).astype(BF16)

        rank, chip = axis_ranks()
        started = []
        for half in range(2 if in_halves else 1):
            first = (chip // 2 ^ (1 - half)) * (width // 2) if in_halves else 0
            tiles = (width // 2 if in_halves else width) // tile

            def step(index, carry, first=first):
                product(pl.multiple_of(first + index * tile, tile), tile)
                return carry

            lax.fori_loop(0, tiles, step, 0)
            if not in_halves and width % tile:
                product(tiles * tile, width % tile)
            for ref, (shape, moves, mask) in zip(out_refs, outputs):
                if in_halves and mask & 2 == 2 * half:
                    continue
                for index, place in moves:
                    row, column = place(rank, chip)
                    copy = pltpu.make_async_copy(
                        result.at[pl.ds(row, shape[1]), pl.ds(column, shape[2])],
                        ref.at[index],
                        sems.at[len(started)],
                    )
                    copy.start()
                    started.append(copy)
        for copy in started:
            copy.wait()

    return pl.pallas_call(
        kernel,
        in_specs=[ANY] * len(inputs),
        out_specs=[ANY] * count,
        out_shape=[jax.ShapeDtypeStruct(shape, BF16) for shape, _, _ in outputs],
        scratch_shapes=[
            pltpu.VMEM((total, left_own.shape[1]), BF16),
            pltpu.VMEM((depth, total), BF16),
            pltpu.VMEM((total, right_width), BF16),
            pltpu.VMEM((depth, width), BF16),
            pltpu.SemaphoreType.DMA((max(4, copies_out),)),
        ],
        cost_estimate=LIGHT,
    )(*inputs)


def on_device(
    tokens,
    cotangent,
    gate_cotangent,
    slot_of,
    seq_lengths,
    buckets,
    gain_attn,
    w_query,
    w_key,
    w_value,
    w_out,
    rel_bias,
    gain_ffn,
    w_gate,
    w_up,
    w_down,
    gain_delete,
    w_delete,
):
    shards = lax.axis_size("shard")
    reps = lax.axis_size("rep")
    chips = reps // 2
    rank = lax.axis_index("shard")
    rep_rank = lax.axis_index("rep")
    core = rep_rank % 2
    chip = rep_rank // 2
    micro_count, local_rows, width = tokens.shape
    group = local_rows * shards
    rows = micro_count * local_rows
    heads = rel_bias.shape[1]
    bucket_rows = rel_bias.shape[0]
    bucket_count = bucket_rows * shards
    proj = w_query.shape[1]
    head_size = proj // heads
    block = gain_attn.shape[0]
    inner = w_gate.shape[1]
    half_inner = inner // 2
    col_piece = inner // chips
    down_block = w_down.shape[0]
    down_half = down_block // 2
    down_piece = down_half // chips
    down_parts_count = -(-width // col_piece)
    padded = -(-width // 128) * 128
    aligned = reps == 8 and block % 16 == 0 and down_piece % 16 == 0 and col_piece % 128 == 0

    def swap(value, mask):
        return lax.ppermute(value, "rep", [(i, i ^ mask) for i in range(reps)])

    def shift(value, by=1):
        return lax.ppermute(value, "shard", [(i, (i + by) % shards) for i in range(shards)])

    def tie(value, moved):
        return lax.optimization_barrier((value, moved))

    def cut(count):
        half = count // 2
        return half // 16 * 16 if half >= 16 else half

    def gather_near(piece):
        if chips == 1:
            return []
        return [swap(piece, 2)] + ([swap(piece, 4)] if chips >= 4 else [])

    def gather_rest(near):
        if chips < 4:
            return []
        middle = cut(near[0].shape[0])
        return [swap(near[1][:middle], 2), swap(near[0][middle:], 4)]

    def gather_list(piece, near, rest):
        middle = cut(piece.shape[0])
        found = [(0, 0, piece)] + [(1 + i, 0, part) for i, part in enumerate(near)]
        found += [(3, i * middle, part) for i, part in enumerate(rest)]
        bit = 4
        while bit < chips:
            found += [
                (mask ^ bit, start, swap(part, 2 * bit)) for mask, start, part in found
            ]
            bit *= 2
        return found

    def plane_gather(piece):
        near = gather_near(piece)
        return gather_list(piece, near, gather_rest(near))

    def add(*values):
        return sum(value.astype(F32) for value in values).astype(BF16)

    def plane_reduce(parts, axis):
        state = reduce_begin(parts, axis)
        return reduce_end(reduce_middle(state, axis))

    def reduce_begin(parts, axis):
        def level(base, bit):
            if bit < 4:
                return lambda name: parts[base][name]
            lower, upper = level(base, bit // 2), level(base ^ bit, bit // 2)
            return lambda name: add(lower(name), swap(upper(name), 2 * bit))

        get = level(0, chips // 2)
        if chips < 4:
            return [get("own")] + ([swap(get("near"), 2)] if chips == 2 else [])
        return [get("own"), get("far"), get("near"), swap(get("top"), 2), swap(get("low"), 4)]

    def reduce_middle(state, axis):
        if chips < 4:
            return state
        own, far, near, top, low = state
        middle = top.shape[axis]

        def pair(value):
            return (
                lax.slice_in_dim(value, 0, middle, axis=axis),
                lax.slice_in_dim(value, middle, value.shape[axis], axis=axis),
            )

        (far_top, far_low), (near_top, near_low) = pair(far), pair(near)
        far = jnp.concatenate([add(far_top, top), far_low], axis)
        near = jnp.concatenate([near_top, add(near_low, low)], axis)
        return [own, swap(far, 4), swap(near, 2)]

    def reduce_end(state):
        return add(*state) if len(state) > 1 else state[0]

    names = {"own": 0, "near": 1, "far": 2, "top": 3, "low": 3}
    bases = [base for base in range(chips) if base & 3 == 0]
    used = ["own", "near", "far", "top", "low"] if chips >= 4 else ["own", "near"][:chips]

    def source(step):
        return (rank - step) % shards

    order = (rank - jnp.arange(shards, dtype=jnp.int32)) % shards
    per_matrix = reps // 4
    attn_rows = block // per_matrix
    if aligned:
        attn_rows = -(-attn_rows // 16) * 16
    last_row = block - attn_rows

    def part_row(part):
        return jnp.minimum(part * attn_rows, last_row)

    attn_own = jnp.stack([w_query, w_key, w_value, w_out.reshape(block, proj)])
    attn_piece = lax.dynamic_slice(
        attn_own,
        (rep_rank // per_matrix, part_row(rep_rank % per_matrix), 0),
        (1, attn_rows, proj),
    )[0]
    vector_pack = jnp.concatenate(
        [gain_attn, gain_ffn, gain_delete, w_delete, rel_bias.reshape(-1)]
    )
    pack_rows = -(-vector_pack.shape[0] // (16 * proj)) * 16
    vector_pack = jnp.pad(vector_pack, (0, pack_rows * proj - vector_pack.shape[0]))
    vector_pack = vector_pack.reshape(pack_rows, proj)
    attn_sent = jnp.concatenate([attn_piece, vector_pack])
    attn_arrived = [shift(attn_sent, step) for step in range(1, shards)]
    vectors = jnp.stack([vector_pack] + [part[attn_rows:] for part in attn_arrived])
    vectors = jnp.take(vectors, order, axis=0).reshape(shards, pack_rows * proj)
    attn_gain = vectors[:, :block].reshape(width).astype(F32)
    ffn_gain = vectors[:, block : 2 * block].reshape(width).astype(F32)
    delete_gain = vectors[:, 2 * block : 3 * block].reshape(width).astype(F32)
    delete_vec = vectors[:, 3 * block : 4 * block].reshape(width).astype(F32)
    bias_table = vectors[:, 4 * block : 4 * block + bucket_rows * heads]
    bias_table = bias_table.reshape(bucket_count, heads)
    stacked = jnp.stack([part[:attn_rows] for part in attn_arrived])

    def pack(gate_up_part, down_part):
        wide = jnp.pad(down_part, ((0, 0), (0, down_parts_count * col_piece - width)))
        cuts = [wide[:, i * col_piece : (i + 1) * col_piece] for i in range(down_parts_count)]
        return jnp.concatenate([gate_up_part] + cuts)

    def overlaps(start, count):
        bounds = [(None, 0, block)] + [
            (i, block + i * down_piece, block + (i + 1) * down_piece)
            for i in range(down_parts_count)
        ]
        found = []
        for part, low, high in bounds:
            first, last = max(low, start), min(high, start + count)
            if first < last:
                found.append((part, first - start, first - low, last - first))
        return found

    def part_columns(part):
        return min(col_piece, padded - part * col_piece)

    gate_up_own = pick_columns(w_gate, w_up)
    down_own = lax.dynamic_slice_in_dim(w_down, core * down_half, down_half, 0)
    packed_own = pack(
        lax.dynamic_slice_in_dim(gate_up_own, chip * col_piece, col_piece, 1),
        lax.dynamic_slice_in_dim(down_own, chip * down_piece, down_piece, 0),
    )
    packed_own, stacked = tie(packed_own, stacked)
    attn_plane = [stacked] + [swap(stacked, 2 * mask) for mask in range(1, chips)]
    attn_plane = jnp.stack(attn_plane)
    ring = [packed_own, shift(packed_own)]
    attn_plane, ring = tie(attn_plane, ring)
    nears, rests = [None] * shards, [None] * shards
    nears[1] = gather_near(ring[1])
    attn_other = swap(attn_plane, 1)

    def attn_place(mask, flip, step):
        def place(at, rep):
            owner = rep ^ (2 * mask + flip)
            row = (at - step) % shards * block + part_row(owner % per_matrix)
            return owner // per_matrix, pl.multiple_of(row, 16) if aligned else row

        return place

    shared = per_matrix * attn_rows - block

    def split_place(place, flip):
        def places_of(*at):
            matrix, row = place(*at)
            part = (at[-1] ^ flip) % per_matrix
            first = row - last_row * part
            moves = [
                (
                    pl.multiple_of(shared * part, 16),
                    attn_rows - shared,
                    matrix,
                    pl.multiple_of(first + attn_rows * part, 16),
                )
            ]
            if shared and flip == 0:
                moves.append(
                    (
                        pl.multiple_of(last_row * (1 - part), 16),
                        shared,
                        matrix,
                        pl.multiple_of(first + last_row, 16),
                    )
                )
            return moves

        return places_of

    attn_pieces = [w_query, w_key, w_value, attn_own[3]]
    attn_places = [
        [(None, lambda at, rep, matrix=matrix: [(0, block, matrix, pl.multiple_of(at * block, 16))])]
        for matrix in range(4)
    ]
    for flip, found in enumerate((attn_plane, attn_other)):
        attn_pieces.append(found)
        attn_places.append(
            [
                ((mask, step - 1), attn_place(mask, flip, step), flip)
                for mask in range(chips)
                for step in range(1, shards)
            ]
        )
    if not aligned:
        whole = jnp.zeros((4, width, proj), BF16)
        whole = lax.dynamic_update_slice(whole, attn_own, (0, rank * block, 0))
        for piece, place in zip(attn_pieces[4:], attn_places[4:]):
            for index, where, _ in place:
                matrix, row = where(rank, rep_rank)
                whole = lax.dynamic_update_slice(whole, piece[index][None], (matrix, row, 0))
        attn_pieces = [whole[matrix] for matrix in range(4)]
        attn_places = [
            [(None, lambda at, rep, matrix=matrix: [(0, width, matrix, 0)])] for matrix in range(4)
        ]
    else:
        attn_places[4:] = [
            [(index, split_place(where, flip)) for index, where, flip in place]
            for place in attn_places[4:]
        ]

    slots = slot_of[:, 0]
    own_slots = lax.dynamic_slice_in_dim(slots, rank * local_rows, local_rows, 1)
    key_slots = jnp.take(slots.reshape(micro_count, shards, local_rows), order, axis=1)
    key_slots = key_slots.reshape(micro_count, group)
    onehot = (buckets[:, None] == jnp.arange(bucket_count, dtype=jnp.int32)[None, :]).astype(F32)
    onehot = jnp.pad(onehot, ((0, 1), (0, 0)))
    bias_rows = jnp.dot(onehot, bias_table.astype(F32), precision=HIGHEST).T
    bias = bias_of_queries(bias_rows, own_slots.reshape(rows), group)
    first_len = seq_lengths[:, 0, 0]

    token_rows = tokens.reshape(rows, width)
    normed_one, queries, own_pairs, attn_full = project_call(
        token_rows, attn_gain[None], attn_pieces, attn_places, block, proj
    )
    out_full = attn_full[3].reshape(proj, width)

    for step in range(2, shards - 1):
        ring.append(shift(ring[-1]))
    own_pairs, ring = tie(own_pairs, ring)
    early = (
        out_full,
        jnp.pad(down_own, ((0, 0), (0, padded - width))),
        cotangent.reshape(rows, width),
        gate_cotangent.reshape(rows, 1).astype(F32),
        [value[None] for value in (ffn_gain, delete_gain, delete_vec)],
        [slots[micro].reshape(group, 1) for micro in range(micro_count)],
    )
    pairs = [own_pairs]
    for step in range(1, shards):
        pairs.append(shift(pairs[-1]))
        if step == 1:
            pairs[-1], (nears[1], bias) = tie(pairs[-1], (nears[1], bias))
            rests[1] = gather_rest(nears[1])
        if step == 2:
            pairs[-1], (rests[1], early) = tie(pairs[-1], (rests[1], early))
            ring[2], rests[1] = tie(ring[2], rests[1])
            nears[2] = gather_near(ring[2])
    ring[-1], pairs[-1] = tie(ring[-1], pairs[-1])
    last = shift(ring[-1][:block])
    context, probs, packed = [], [], []
    for micro in range(micro_count):
        if micro == micro_count - 1:
            context, nears[2] = tie(context, nears[2])
            rests[2] = gather_rest(nears[2])
        *context, prob, pair = attention_call(
            micro,
            first_len[micro : micro + 1],
            queries,
            pairs,
            own_slots.reshape(rows, 1),
            key_slots[micro : micro + 1],
            bias,
            context,
        )
        probs.append(prob)
        packed.append(pair)
    for step in range(3, shards - 1):
        ring[step], rests[step - 1] = tie(ring[step], rests[step - 1])
        nears[step] = gather_near(ring[step])
        rests[step] = gather_rest(nears[step])
    context, (last, rests[shards - 2]) = tie(context, (last, rests[shards - 2]))
    last_near = gather_near(last)
    last_down = shift(ring[-1][block:])
    (context,) = context
    out_full, down_wide, cotangent_rows, gate_rows, gains, key_columns = early
    ffn_gain, delete_gain, delete_vec = gains

    hidden_mid, normed_two = mid_call(token_rows, context, out_full, ffn_gain, micro_count)
    normed_two, (last_near, last_down) = tie(normed_two, (last_near, last_down))
    last_rest = gather_rest(last_near)
    normed_two_other = swap(normed_two, 1)
    normed_two_other, (last_rest, last_down) = tie(normed_two_other, (last_rest, last_down))
    last_down_found = [(mask, 0, swap(last_down, 2 * mask)) for mask in range(1, chips)]
    pieces = [gate_up_own, down_wide]
    gate_up_moves = [(0, 0, block, inner, lambda at, chip_at: (pl.multiple_of(at * block, 16), 0))]
    down_moves = [
        (1, 0, down_half, padded, lambda at, chip_at: (pl.multiple_of(at * down_half, 16), 0))
    ]

    def gate_up_place(step, mask, row):
        return lambda at, chip_at: (
            pl.multiple_of((at - step) % shards * block + row, 16),
            pl.multiple_of((chip_at ^ mask) * col_piece, 128),
        )

    def down_place(step, mask, row, part):
        return lambda at, chip_at: (
            pl.multiple_of((at - step) % shards * down_half + (chip_at ^ mask) * down_piece + row, 16),
            part * col_piece,
        )

    arrived = [
        (step, 0, gather_list(ring[step], nears[step], rests[step])) for step in range(1, shards - 1)
    ]
    arrived.append((shards - 1, 0, gather_list(last, last_near, last_rest)))
    arrived.append((shards - 1, block, [(0, 0, last_down)] + last_down_found))
    for step, below, found in arrived:
        for mask, start, array in found:
            for part, here, there, size in overlaps(below + start, array.shape[0]):
                if part is None:
                    gate_up_moves.append(
                        (len(pieces), here, size, col_piece, gate_up_place(step, mask, there))
                    )
                else:
                    down_moves.append(
                        (
                            len(pieces),
                            here,
                            size,
                            part_columns(part),
                            down_place(step, mask, there, part),
                        )
                    )
            pieces.append(array)
    if not aligned:

        def put_together(moves, shape):
            whole = jnp.zeros(shape, BF16)
            for piece, row, size, columns, place in moves:
                value = pieces[piece][row : row + size, :columns]
                whole = lax.dynamic_update_slice(whole, value, place(rank, chip))
            return whole

        pieces = [
            put_together(gate_up_moves, (width, inner)),
            put_together(down_moves, (half_inner, padded)),
        ]
        gate_up_moves = [(0, 0, width, inner, lambda at, chip_at: (0, 0))]
        down_moves = [(1, 0, half_inner, padded, lambda at, chip_at: (0, 0))]
    gate_up_pieces, gate_up_moves = used_by(pieces, gate_up_moves)
    down_pieces, down_moves = used_by(pieces, down_moves)
    gate_slope_act, gate_act, inner_act, gate_up = gate_up_call(
        normed_two, normed_two_other, width, inner, gate_up_pieces, gate_up_moves
    )
    down_part, down_given, down = down_call(inner_act, width, padded, down_pieces, down_moves)
    hidden_out, deleted, grad_out, down_up, grad_delete_gain, grad_delete_vec = out_call(
        hidden_mid,
        down_part,
        swap(down_given, 1),
        cotangent_rows,
        gate_rows,
        delete_gain,
        delete_vec,
        micro_count,
    )

    down_up_other = swap(down_up, 1)

    def reduce_plan(size, piece_columns, place):
        middle = cut(size)
        spans = {"own": (0, size), "near": (0, size), "far": (0, size)}
        spans["top"], spans["low"] = (0, middle), (middle, size - middle)
        plan = []
        for base in bases:
            for name in used:
                start, count = spans[name]
                moves = [
                    (index, place(index, base ^ names[name], start)) for index in range(shards)
                ]
                plan.append(((shards, count, piece_columns), moves, base ^ names[name]))
        return plan

    def reduce_run(plan, left, right, picks, right_width, in_halves):
        if aligned:
            buffers = weight_grad_call(left, right, picks, right_width, plan, in_halves)
        else:
            shape = (sum(size for _, size in picks), right_width)
            whole = weight_grad_call(
                left, right, picks, right_width,
                [((1,) + shape, [(0, lambda at, chip_at: (0, 0))], 0)], False,
            )[0][0]
            buffers = []
            for (_, size, columns), moves, _ in plan:
                buffers.append(
                    jnp.stack(
                        [
                            lax.dynamic_slice(whole, place(rank, chip), (size, columns))
                            for _, place in moves
                        ]
                    )
                )
        return {
            base: dict(zip(used, buffers[i * len(used) : (i + 1) * len(used)]))
            for i, base in enumerate(bases)
        }

    def exchange(value):
        return lax.all_to_all(value, "shard", split_axis=0, concat_axis=0, tiled=True)

    def total_of(arrived):
        return jnp.sum(arrived.astype(F32), axis=0).astype(BF16)

    def down_grad_place(index, mask, start):
        plain = lambda at, chip_at: (
            index * down_half + (chip_at ^ mask) * down_piece + start,
            0,
        )
        return tile_hint(plain, 16, 128) if aligned else plain

    def gate_up_grads(first, size, left, right):
        def place(index, mask, start):
            plain = lambda at, chip_at: (index * size + start, (chip_at ^ mask) * col_piece)
            return tile_hint(plain, 16, 128) if aligned else plain

        return reduce_run(
            reduce_plan(size, col_piece, place),
            left,
            right,
            [(index * block + first, size) for index in range(shards)],
            inner,
            chips == 4 and half_inner % 256 == 0,
        )

    down_buffers = reduce_run(
        reduce_plan(down_piece, width, down_grad_place),
        (inner_act, None),
        (down_up, down_up_other),
        [(0, half_inner)],
        width,
        False,
    )
    down_state = reduce_begin(down_buffers, 1)
    gate_grad, up_grad = hidden_grad_call(down_up, down_up_other, down, gate_slope_act, gate_act)
    gate_grad, down_state = tie(gate_grad, down_state)
    down_state = reduce_middle(down_state, 1)
    normed_both = (normed_two, normed_two_other)
    gate_up_buffers = gate_up_grads(0, cut(block), normed_both, (gate_grad, up_grad))
    gate_grad, gate_up_buffers = tie(gate_grad, gate_up_buffers)
    normed_part, normed_given = normed_grad_call(gate_grad, up_grad, gate_up)
    normed_given, (down_state, gate_up_buffers) = tie(normed_given, (down_state, gate_up_buffers))
    gate_up_state = reduce_begin(gate_up_buffers, 1)
    down_arrived = exchange(reduce_end(down_state))
    normed_given = swap(normed_given, 1)
    grad_mid, context_grad, grad_w_out, grad_ffn_gain = back_call(
        normed_part,
        normed_given,
        grad_out,
        hidden_mid,
        ffn_gain,
        context,
        out_full,
        micro_count,
    )
    context_grad, gate_up_state = tie(context_grad, gate_up_state)
    gate_up_state = reduce_middle(gate_up_state, 1)
    score_grads, sums = [], []
    for micro in range(micro_count):
        score_grad, *sums = attention_back_call(
            micro,
            queries,
            context_grad,
            probs[micro],
            packed[micro],
            key_columns[micro],
            shards,
            sums,
        )
        score_grads.append(score_grad)
    query_grad, pair_parts = sums
    gate_grad, pair_parts = tie(gate_grad, pair_parts)
    pair_arrived = exchange(pair_parts)
    gate_up_buffers = gate_up_grads(
        cut(block), block - cut(block), normed_both, (gate_grad, up_grad)
    )
    gate_up_buffers, gate_up_state = tie(gate_up_buffers, gate_up_state)
    gate_up_later = reduce_begin(gate_up_buffers, 1)
    grad_bias_rows = bias_fold(score_grads, own_slots.reshape(rows))
    grad_bias = jnp.einsum("ob,ho->bh", onehot, grad_bias_rows, precision=HIGHEST)
    out_grads = grad_w_out.reshape(width, proj)
    gate_up_later, (grad_bias, out_grads) = tie(gate_up_later, (grad_bias, out_grads))
    gate_up_later = reduce_middle(gate_up_later, 1)
    pair_arrived, down_arrived = tie(pair_arrived, down_arrived)
    gate_up_arrived = exchange(reduce_end(gate_up_state))
    down_sum = total_of(down_arrived)
    pair_sum, grad_in, grad_attn_gain = in_call(
        query_grad,
        pair_arrived,
        attn_full,
        grad_mid,
        token_rows,
        attn_gain[None],
        micro_count,
    )
    pair_sum, gate_up_later = tie(pair_sum, gate_up_later)

    small = jnp.concatenate(
        [
            grad_attn_gain.reshape(shards, block),
            grad_ffn_gain.reshape(shards, block),
            grad_delete_gain.reshape(shards, block),
            grad_delete_vec.reshape(shards, block),
            grad_bias.reshape(shards, bucket_rows * heads),
        ],
        axis=1,
    ).astype(BF16)
    small = jnp.pad(small, ((0, 0), (0, pack_rows * proj - small.shape[1])))
    small = small.reshape(shards, pack_rows, proj)

    def attn_grad_place(mask, flip, index):
        def place(at, rep):
            owner = rep ^ (2 * mask + flip)
            row = index * block + part_row(owner % per_matrix)
            return owner // per_matrix, pl.multiple_of(row, 16) if aligned else row

        return place

    attn_plan = [
        (
            (chips, shards, attn_rows + pack_rows, proj),
            [
                ((mask, index), attn_grad_place(mask, flip, index), index)
                for mask in range(chips)
                for index in range(shards)
            ],
        )
        for flip in range(2)
    ]
    if aligned:
        kept, given = project_grad_call(
            normed_one, query_grad, pair_sum, out_grads, small, attn_plan
        )
    else:
        whole_plan = [
            (
                (4, width, proj),
                [((matrix,), lambda at, rep, matrix=matrix: (matrix, 0), None) for matrix in range(4)],
            )
        ]
        whole = project_grad_call(
            normed_one, query_grad, pair_sum, out_grads, small, whole_plan
        )[0]
        kept, given = [
            jnp.stack(
                [
                    jnp.concatenate(
                        [
                            lax.dynamic_slice(
                                whole, where(rank, rep_rank) + (0,), (1, attn_rows, proj)
                            )[0],
                            small[index],
                        ]
                    )
                    for _, where, index in items
                ]
            ).reshape(shape)
            for shape, items in attn_plan
        ]
    given = swap(given, 1)
    attn_own_sum = add(kept[0], given[0])
    attn_send = [add(kept[mask], given[mask]) for mask in range(1, chips)]
    attn_found = [swap(part, 2 * mask + 2) for mask, part in enumerate(attn_send)]
    gate_up_rest = exchange(reduce_end(gate_up_later))
    attn_found, gate_up_rest = tie(attn_found, gate_up_rest)
    attn_sum = add(attn_own_sum, *attn_found)
    attn_sum = total_of(exchange(attn_sum))
    gate_up_sum = jnp.concatenate([total_of(gate_up_arrived), total_of(gate_up_rest)])
    total = attn_sum[attn_rows:].astype(F32).reshape(-1)
    attn_sum = attn_sum[:attn_rows]

    packed_sum = pack(gate_up_sum, down_sum)
    near = gather_near(packed_sum)
    attn_sum, near = tie(attn_sum, near)
    rest = gather_rest(near)
    attn_half = [attn_sum] + [swap(attn_sum, 2 * mask) for mask in range(1, chips)]
    bounds = [0, block, 2 * block, 3 * block, 4 * block, 4 * block + bucket_rows * heads]
    totals = [total[low:high] for low, high in zip(bounds, bounds[1:])]
    totals[4] = totals[4].reshape(bucket_rows, heads)
    attn_half, (rest, totals) = tie(attn_half, (rest, totals))
    found = gather_list(packed_sum, near, rest)
    pieces, gate_up_moves, down_moves = [], [], []

    def gate_up_to(flip, mask, row):
        return lambda core_at, chip_at: (
            core_at ^ flip,
            row,
            pl.multiple_of((chip_at ^ mask) * col_piece, 128),
        )

    def down_to(flip, mask, row, part):
        return lambda core_at, chip_at: (
            pl.multiple_of((core_at ^ flip) * down_half + (chip_at ^ mask) * down_piece + row, 16),
            part * col_piece,
        )

    for flip in range(2):
        for mask, start, array in found:
            array = swap(array, 1) if flip else array
            for part, here, there, size in overlaps(start, array.shape[0]):
                if part is None:
                    gate_up_moves.append(
                        (len(pieces), here, size, col_piece, gate_up_to(flip, mask, there))
                    )
                else:
                    down_moves.append(
                        (
                            len(pieces),
                            here,
                            size,
                            part_columns(part),
                            down_to(flip, mask, there, part),
                        )
                    )
            pieces.append(array)
    if aligned:
        grad_gate, grad_up, grad_down_out = finish_call(
            pieces, gate_up_moves, down_moves, block, inner, down_block, width, padded
        )
        grad_down_out = grad_down_out.T
    else:
        halves = jnp.zeros((2, block, inner), BF16)
        for piece, row, size, columns, place in gate_up_moves:
            value = pieces[piece][None, row : row + size, :columns]
            halves = lax.dynamic_update_slice(halves, value, place(core, chip))
        whole = jnp.zeros((down_block, padded), BF16)
        for piece, row, size, columns, place in down_moves:
            value = pieces[piece][row : row + size, :columns]
            whole = lax.dynamic_update_slice(whole, value, place(core, chip))
        grad_gate, grad_up = spread_columns(halves[0], halves[1])
        grad_down_out = whole[:, :width].astype(F32)

    attn_half = jnp.stack(attn_half)
    attn_found = [attn_half, swap(attn_half, 1)]

    def attn_to(mask, flip):
        def place(rep):
            owner = rep ^ (2 * mask + flip)
            row = part_row(owner % per_matrix)
            return owner // per_matrix, pl.multiple_of(row, 16) if aligned else row

        return place

    attn_moves = [(flip, mask, attn_to(mask, flip)) for flip in range(2) for mask in range(chips)]
    if aligned:
        attn_moves = [
            (flip, mask, split_place(place, flip)) for flip, mask, place in attn_moves
        ]
        attn_shard = attn_finish_call(attn_found, attn_moves, block, proj)
    else:
        attn_shard = jnp.zeros((4, block, proj), BF16)
        for piece, index, place in attn_moves:
            attn_shard = lax.dynamic_update_slice(
                attn_shard, attn_found[piece][index][None], place(rep_rank) + (0,)
            )
        attn_shard = attn_shard.astype(F32)

    return (
        jnp.swapaxes(hidden_out, 1, 2),
        deleted.reshape(micro_count, local_rows),
        jnp.swapaxes(grad_in, 1, 2),
        totals[0],
        attn_shard[0],
        attn_shard[1],
        attn_shard[2],
        attn_shard[3].reshape(proj // shards, width),
        totals[4],
        totals[1],
        grad_gate,
        grad_up,
        grad_down_out,
        totals[2],
        totals[3],
    )


def used_by(pieces, moves):
    wanted = sorted({move[0] for move in moves})
    return [pieces[i] for i in wanted], [(wanted.index(move[0]),) + move[1:] for move in moves]


def tile_hint(place, row_unit, column_unit):
    def hinted(at, chip_at):
        row, column = place(at, chip_at)
        return pl.multiple_of(row, row_unit), pl.multiple_of(column, column_unit)

    return hinted


def solution(mesh):
    rows = P(None, ("rep", "shard"), None)
    flat = P(None, ("rep", "shard"))
    by_rep = P(None, "rep", None)
    vector = P("shard")
    matrix = P("shard", None)
    in_specs = (
        (rows, rows, flat, by_rep, by_rep, P(), vector)
        + (matrix,) * 5
        + (vector,)
        + (matrix,) * 3
        + (vector, vector)
    )
    out_specs = (
        (rows, flat, rows, vector) + (matrix,) * 5 + (vector,) + (matrix,) * 3 + (vector, vector)
    )
    return jax.shard_map(
        on_device, mesh=mesh, in_specs=in_specs, out_specs=out_specs, check_vma=False
    )
```

```python
import functools

import math

import jax
import jax.numpy as jnp
from jax import lax
from jax.experimental import pallas as pl
from jax.experimental.pallas import tpu as pltpu
from jax.sharding import PartitionSpec as P

EPSILON = 1e-06
HIGHEST = lax.Precision.HIGHEST
MASKED = -1000000000.0
BF16 = jnp.bfloat16
LIGHT = pl.CostEstimate(flops=1000, bytes_accessed=1000, transcendentals=0)
F32 = jnp.float32


ANY = pl.BlockSpec(memory_space=pl.ANY)
VMEM = pl.BlockSpec(memory_space=pltpu.VMEM)


def rms_scale(hidden):
    return lax.rsqrt(jnp.mean(hidden * hidden, axis=-1, keepdims=True) + EPSILON)


def rms_back(hidden, scale_row, gain, upstream):
    scaled = upstream * gain
    return scale_row * scaled - hidden * (scale_row * scale_row * scale_row) * jnp.mean(
        hidden * scaled, axis=-1, keepdims=True
    )


def bias_kernel(rows_ref, slots_ref, out_ref):
    group = out_ref.shape[2]
    row = jnp.broadcast_to(rows_ref[0], (group, rows_ref.shape[2]))
    grid = pltpu.roll(row, group + 1, 1, stride=1, stride_axis=0)[:, :group].astype(BF16)
    tokens = slots_ref.shape[0]
    pick = (slots_ref[...] == lax.broadcasted_iota(jnp.int32, (tokens, group), 1)).astype(BF16)
    out_ref[0] = jnp.dot(pick, grid, preferred_element_type=F32).astype(BF16)


def bias_of_queries(bias_rows, slots, group):
    heads, width = bias_rows.shape
    tokens = slots.shape[0]
    return pl.pallas_call(
        bias_kernel,
        grid=(heads,),
        in_specs=[
            pl.BlockSpec((1, 1, width), lambda h: (h, 0, 0)),
            pl.BlockSpec((tokens, 1), lambda h: (0, 0)),
        ],
        out_specs=pl.BlockSpec((1, tokens, group), lambda h: (h, 0, 0)),
        out_shape=jax.ShapeDtypeStruct((heads, tokens, group), BF16),
    )(bias_rows.reshape(heads, 1, width), slots.reshape(tokens, 1))


def bias_fold(score_grads, slots):
    heads, local, group = score_grads[0].shape
    count = len(score_grads)

    def kernel(*refs):
        grad_refs, slots_ref, out_ref = refs[:count], refs[count], refs[count + 1]
        square = None
        for index, ref in enumerate(grad_refs):
            mine = slots_ref[:, index * local : (index + 1) * local]
            row = lax.broadcasted_iota(jnp.int32, (group, local), 0)
            place = (row == (group - 1) - mine).astype(BF16)
            part = jnp.dot(place, ref[0], preferred_element_type=F32)
            square = part if square is None else square + part
        wide = jnp.concatenate([square, jnp.zeros_like(square)], axis=1)
        rolled = pltpu.roll(wide, 0, 1, stride=1, stride_axis=0)
        out_ref[0] = jnp.sum(rolled, axis=0, keepdims=True)

    return pl.pallas_call(
        kernel,
        grid=(heads,),
        in_specs=[pl.BlockSpec((1, local, group), lambda h: (h, 0, 0))] * count
        + [pl.BlockSpec((1, count * local), lambda h: (0, 0))],
        out_specs=pl.BlockSpec((1, 1, 2 * group), lambda h: (h, 0, 0)),
        out_shape=jax.ShapeDtypeStruct((heads, 1, 2 * group), F32),
    )(*score_grads, slots.reshape(1, count * local)).reshape(heads, 2 * group)


def by_head(value, head, head_size):
    per_block = 128 // head_size
    start = head // per_block * 128
    lanes = lax.broadcasted_iota(jnp.int32, (1, 128), 1) // head_size
    block = value[:, start : start + 128]
    return jnp.where(lanes == head % per_block, block, jnp.zeros_like(block)), start


def dot_last(left, right):
    return lax.dot_general(left, right, (((1,), (1,)), ((), ())), preferred_element_type=F32)


def attention_call(micro, lengths, queries, pairs, own_slots, key_slots, bias, context):
    heads, rows, group = bias.shape
    double = pairs[0].shape[1]
    count = len(pairs)
    local = group // count
    proj = double // 2
    head_size = proj // heads

    def kernel(lengths_ref, query_ref, *rest):
        pair_refs = rest[:count]
        own_ref, key_ref, bias_ref = rest[count : count + 3]
        context_ref, prob_ref, packed_ref, arrived = rest[-4:]
        for index, ref in enumerate(pair_refs):
            arrived[index * local : (index + 1) * local] = ref[...]
        place = (
            lax.broadcasted_iota(jnp.int32, (group, group), 0) == key_ref[...]
        ).astype(BF16)
        packed_ref[...] = jnp.dot(place, arrived[...], preferred_element_type=F32).astype(BF16)
        first = lengths_ref[0]
        key_seg = lax.broadcasted_iota(jnp.int32, (local, group), 1) >= first
        same = key_seg == (own_ref[...] >= first)
        per_block = 128 // head_size
        total = None
        for head in range(heads):
            query, start = by_head(query_ref[...], head, head_size)
            scores = dot_last(query, packed_ref[:, start : start + 128])
            scores = jnp.where(same, scores + bias_ref[head].astype(F32), MASKED)
            weights = jnp.exp(scores - jnp.max(scores, axis=1, keepdims=True))
            weights = (weights / jnp.sum(weights, axis=1, keepdims=True)).astype(BF16)
            prob_ref[head] = weights
            value, _ = by_head(packed_ref[:, proj:], head, head_size)
            part = jnp.dot(weights, value, preferred_element_type=F32)
            total = part if head % per_block == 0 else total + part
            if head % per_block == per_block - 1:
                context_ref[:, start : start + 128] = total.astype(BF16)

    return pl.pallas_call(
        kernel,
        grid=(1,),
        in_specs=[
            pl.BlockSpec(memory_space=pltpu.SMEM),
            pl.BlockSpec((local, proj), lambda i: (micro, 0)),
        ]
        + [pl.BlockSpec((local, double), lambda i: (micro, 0))] * count
        + [
            pl.BlockSpec((local, 1), lambda i: (micro, 0)),
            pl.BlockSpec((1, group), lambda i: (0, 0)),
            pl.BlockSpec((heads, local, group), lambda i: (0, micro, 0)),
        ]
        + [ANY] * len(context),
        out_specs=[
            pl.BlockSpec((local, proj), lambda i: (micro, 0)),
            pl.BlockSpec((heads, local, group), lambda i: (0, 0, 0)),
            pl.BlockSpec((group, double), lambda i: (0, 0)),
        ],
        out_shape=[
            jax.ShapeDtypeStruct(queries.shape, BF16),
            jax.ShapeDtypeStruct((heads, local, group), BF16),
            jax.ShapeDtypeStruct((group, double), BF16),
        ],
        input_output_aliases={count + 5: 0} if context else {},
        scratch_shapes=[pltpu.VMEM((group, double), BF16)],
        cost_estimate=LIGHT,
    )(lengths, queries, *pairs, own_slots, key_slots, bias, *context)


def attention_back_call(micro, queries, context_grad, probs, packed, key_slots, shards, sums):
    heads, local, group = probs.shape
    double = packed.shape[1]
    proj = double // 2
    head_size = proj // heads

    def kernel(query_ref, context_ref, prob_ref, packed_ref, key_ref, *rest):
        score_ref, dq_ref, part_ref, sums = rest[-4:]
        per_block = 128 // head_size
        for head in range(heads):
            context, start = by_head(context_ref[...], head, head_size)
            query, _ = by_head(query_ref[...], head, head_size)
            key, _ = by_head(packed_ref[:, :proj], head, head_size)
            weights = prob_ref[head]
            wide = weights.astype(F32)
            upstream = dot_last(context, packed_ref[:, proj + start : proj + start + 128])
            inner = jnp.sum(wide * upstream, axis=1, keepdims=True)
            grad = (wide * (upstream - inner)).astype(BF16)
            score_ref[head] = grad
            query_part = jnp.dot(grad, key, preferred_element_type=F32)
            key_part = jnp.dot(grad.T, query, preferred_element_type=F32)
            value_part = jnp.dot(weights.T, context, preferred_element_type=F32)
            if head % per_block == 0:
                totals = [query_part, key_part, value_part]
            else:
                totals = [
                    total + part
                    for total, part in zip(totals, (query_part, key_part, value_part))
                ]
            if head % per_block == per_block - 1:
                dq_ref[:, start : start + 128] = totals[0].astype(BF16)
                sums[:, start : start + 128] = totals[1].astype(BF16)
                sums[:, proj + start : proj + start + 128] = totals[2].astype(BF16)
        for index in range(shards):
            slots = key_ref[index * local : (index + 1) * local]
            pick = (lax.broadcasted_iota(jnp.int32, (local, group), 1) == slots).astype(BF16)
            part_ref[index] = jnp.dot(pick, sums[...], preferred_element_type=F32).astype(BF16)

    return pl.pallas_call(
        kernel,
        grid=(1,),
        in_specs=[
            pl.BlockSpec((local, proj), lambda i: (micro, 0)),
            pl.BlockSpec((local, proj), lambda i: (micro, 0)),
            pl.BlockSpec((heads, local, group), lambda i: (0, 0, 0)),
            pl.BlockSpec((group, double), lambda i: (0, 0)),
            pl.BlockSpec((group, 1), lambda i: (0, 0)),
        ]
        + [ANY] * len(sums),
        out_specs=[
            pl.BlockSpec((heads, local, group), lambda i: (0, 0, 0)),
            pl.BlockSpec((local, proj), lambda i: (micro, 0)),
            pl.BlockSpec((shards, local, double), lambda i: (0, micro, 0)),
        ],
        out_shape=[
            jax.ShapeDtypeStruct((heads, local, group), BF16),
            jax.ShapeDtypeStruct(queries.shape, BF16),
            jax.ShapeDtypeStruct((shards, queries.shape[0], double), BF16),
        ],
        input_output_aliases={5 + i: 1 + i for i in range(len(sums))},
        scratch_shapes=[pltpu.VMEM((group, double), BF16)],
        cost_estimate=LIGHT,
    )(queries, context_grad, probs, packed, key_slots, *sums)


def axis_ranks():
    return lax.axis_index("shard"), lax.axis_index("rep") // 2


def gelu_parts(value):
    inner = math.sqrt(2.0 / math.pi)
    square = value * value
    bend = jnp.tanh(inner * value * (1.0 + 0.044715 * square))
    outside = 0.5 * (1.0 + bend)
    slope = outside + 0.5 * value * (1.0 - bend * bend) * (inner * (1.0 + 0.134145 * square))
    return value * outside, slope


def run_copies(copies, sems):
    started = [pltpu.make_async_copy(src, dst, sems.at[i]) for i, (src, dst) in enumerate(copies)]
    for copy in started:
        copy.start()
    return started


def pick_kernel(gate_ref, up_ref, out_ref):
    core = lax.axis_index("rep") % 2
    inner = gate_ref.shape[1]
    shards = lax.axis_size("shard")
    unit = inner // shards
    half = unit // 2
    for index, ref in enumerate((gate_ref, up_ref)):
        parts = []
        for shard in range(shards):
            low = ref[:, shard * unit : shard * unit + half]
            high = ref[:, shard * unit + half : (shard + 1) * unit]
            parts.append(jnp.where(core == 0, low, high))
        out_ref[:, index * (inner // 2) : (index + 1) * (inner // 2)] = jnp.concatenate(parts, 1)


def pick_columns(w_gate, w_up):
    return pl.pallas_call(
        pick_kernel,
        in_specs=[VMEM, VMEM],
        out_specs=VMEM,
        out_shape=jax.ShapeDtypeStruct(w_gate.shape, BF16),
    )(w_gate, w_up)


def spread_kernel(low_ref, high_ref, gate_ref, up_ref):
    inner = gate_ref.shape[1]
    shards = lax.axis_size("shard")
    half = inner // shards // 2
    for index, ref in enumerate((gate_ref, up_ref)):
        parts = []
        for shard in range(shards):
            start = index * (inner // 2) + shard * half
            parts += [low_ref[:, start : start + half], high_ref[:, start : start + half]]
        ref[...] = jnp.concatenate(parts, 1).astype(F32)


def spread_columns(low, high):
    shape = jax.ShapeDtypeStruct(low.shape, F32)
    return pl.pallas_call(
        spread_kernel,
        in_specs=[VMEM, VMEM],
        out_specs=[VMEM, VMEM],
        out_shape=[shape, shape],
    )(low, high)


def project_call(tokens, gain, pieces, places, block, proj):
    rows, width = tokens.shape
    count = len(pieces)
    moves = 2 * sum(len(place) for place in places)

    def kernel(token_ref, gain_ref, *rest):
        piece_refs = rest[:count]
        normed_ref, query_ref, pair_ref, keep_ref, weights, sems = rest[count:]
        rank, rep = lax.axis_index("shard"), lax.axis_index("rep")
        copies = []
        for ref, place in zip(piece_refs, places):
            for index, where in place:
                source = ref if index is None else ref.at[index]
                for start, size, matrix, row in where(rank, rep):
                    copies.append(
                        (source.at[pl.ds(start, size)], weights.at[matrix, pl.ds(row, size)])
                    )
        copies = run_copies(copies, sems)
        hidden = token_ref[...].astype(F32)
        scale = lax.rsqrt(jnp.mean(hidden * hidden, axis=1, keepdims=True) + EPSILON)
        normed = (hidden * scale * gain_ref[...]).astype(BF16)
        normed_ref[...] = normed
        for copy in copies:
            copy.wait()
        keep = pltpu.make_async_copy(weights, keep_ref, sems.at[moves])
        keep.start()
        query_ref[...] = jnp.dot(normed, weights[0], preferred_element_type=F32).astype(BF16)
        pair_ref[:, :proj] = jnp.dot(normed, weights[1], preferred_element_type=F32).astype(BF16)
        pair_ref[:, proj:] = jnp.dot(normed, weights[2], preferred_element_type=F32).astype(BF16)
        keep.wait()

    return pl.pallas_call(
        kernel,
        in_specs=[VMEM, VMEM] + [ANY] * count,
        out_specs=[VMEM, VMEM, VMEM, ANY],
        out_shape=[
            jax.ShapeDtypeStruct((rows, width), BF16),
            jax.ShapeDtypeStruct((rows, proj), BF16),
            jax.ShapeDtypeStruct((rows, 2 * proj), BF16),
            jax.ShapeDtypeStruct((4, width, proj), BF16),
        ],
        scratch_shapes=[
            pltpu.VMEM((4, width, proj), BF16),
            pltpu.SemaphoreType.DMA((moves + 1,)),
        ],
        cost_estimate=LIGHT,
    )(tokens, gain, *pieces)


def project_grad_call(normed, query_grad, pair_grad, out_grads, small, outputs):
    rows, width = normed.shape
    proj = query_grad.shape[1]
    count = len(outputs)
    moves = sum(len(items) for _, items in outputs)

    small_rows = small.shape[1]

    def kernel(normed_ref, query_ref, pair_ref, out_grad_ref, small_ref, *rest):
        out_refs, result, sems = rest[:count], rest[count], rest[count + 1]
        fourth = pltpu.make_async_copy(out_grad_ref, result.at[3], sems.at[2 * moves])
        fourth.start()
        for begin in range(0, width, 256):
            size = min(256, width - begin)
            turned = normed_ref[:, begin : begin + size].T
            for index in range(3):
                right = query_ref[...] if index == 0 else pair_ref[:, (index - 1) * proj : index * proj]
                result[index, begin : begin + size] = jnp.dot(
                    turned, right, preferred_element_type=F32
                ).astype(BF16)
        fourth.wait()
        rank, rep = lax.axis_index("shard"), lax.axis_index("rep")
        copies = []
        for ref, (shape, items) in zip(out_refs, outputs):
            for index, where, step in items:
                matrix, row = where(rank, rep)
                size = shape[-2] - (small_rows if step is not None else 0)
                copies.append((result.at[matrix, pl.ds(row, size)], ref.at[index + (pl.ds(0, size),)]))
                if step is not None:
                    copies.append(
                        (
                            small_ref.at[step],
                            ref.at[index + (pl.ds(size, small_rows),)],
                        )
                    )
        for copy in run_copies(copies, sems):
            copy.wait()

    return pl.pallas_call(
        kernel,
        in_specs=[VMEM, VMEM, VMEM, ANY, VMEM],
        out_specs=[ANY] * count,
        out_shape=[jax.ShapeDtypeStruct(shape, BF16) for shape, _ in outputs],
        scratch_shapes=[
            pltpu.VMEM((4, width, proj), BF16),
            pltpu.SemaphoreType.DMA((2 * moves + 1,)),
        ],
        cost_estimate=LIGHT,
    )(normed, query_grad, pair_grad, out_grads, small)


def part_of(ref, row, count, columns):
    if (row, count, columns) == (0,) + ref.shape:
        return ref
    return ref.at[pl.ds(row, count), pl.ds(0, columns)]


def gate_up_call(own, other, width, inner, pieces, moves):
    rows, wide = own.shape
    count, steps = len(pieces), len(moves)
    half = inner // 2
    tile = 256

    def kernel(own_ref, other_ref, *rest):
        piece_refs = rest[:count]
        out_refs, keep_ref = rest[count : count + 3], rest[count + 3]
        both, weights, slopes, acts, hiddens, sems = rest[count + 4 :]
        results = (slopes, acts, hiddens)
        rank, chip = axis_ranks()
        copies = [(own_ref, both.at[:rows]), (other_ref, both.at[rows:])]
        for piece, row, size, columns, place in moves:
            to_row, to_column = place(rank, chip)
            copies.append(
                (
                    part_of(piece_refs[piece], row, size, columns),
                    weights.at[pl.ds(to_row, size), pl.ds(to_column, columns)],
                )
            )
        for copy in run_copies(copies, sems):
            copy.wait()
        keep = pltpu.make_async_copy(weights, keep_ref, sems.at[steps + 2])
        keep.start()

        def step(index, carry):
            start = pl.multiple_of(index * tile, tile)
            left = both[:, :width]
            gate = jnp.dot(left, weights[:, pl.ds(start, tile)], preferred_element_type=F32)
            up = jnp.dot(
                left,
                weights[:, pl.ds(pl.multiple_of(half + start, tile), tile)],
                preferred_element_type=F32,
            )
            act, slope = gelu_parts(gate)
            columns = pl.ds(start, tile)
            for number, value in enumerate((up * slope, act, act * up)):
                results[number][:, columns] = value.astype(BF16)
                pltpu.make_async_copy(
                    results[number].at[:, columns],
                    out_refs[number].at[:, columns],
                    sems.at[steps + 3 + number],
                ).start()
            return carry

        lax.fori_loop(0, half // tile, step, 0)
        keep.wait()
        for number in range(3):
            pltpu.make_async_copy(
                results[number], out_refs[number], sems.at[steps + 3 + number]
            ).wait()

    shape = jax.ShapeDtypeStruct((2 * rows, half), BF16)
    return pl.pallas_call(
        kernel,
        in_specs=[ANY] * (2 + count),
        out_specs=[ANY] * 4,
        out_shape=[shape, shape, shape, jax.ShapeDtypeStruct((width, inner), BF16)],
        scratch_shapes=[
            pltpu.VMEM((2 * rows, wide), BF16),
            pltpu.VMEM((width, inner), BF16),
        ]
        + [pltpu.VMEM((2 * rows, half), BF16)] * 3
        + [
            pltpu.SemaphoreType.DMA((steps + 6,)),
        ],
        cost_estimate=LIGHT,
    )(own, other, *pieces)


def col_tiles(width):
    return [(start, min(512, width - start)) for start in range(0, width, 512)]


def down_call(hidden, width, padded, pieces, moves):
    double, half = hidden.shape
    rows = double // 2
    count, steps = len(pieces), len(moves)

    def kernel(hidden_ref, *rest):
        piece_refs = rest[:count]
        own_ref, other_ref, keep_ref, weights, sems = rest[count:]
        rank, chip = axis_ranks()
        copies = []
        for piece, row, size, columns, place in moves:
            to_row, to_column = place(rank, chip)
            copies.append(
                (
                    part_of(piece_refs[piece], row, size, columns),
                    weights.at[pl.ds(to_row, size), pl.ds(to_column, columns)],
                )
            )
        for copy in run_copies(copies, sems):
            copy.wait()
        keep = pltpu.make_async_copy(weights, keep_ref, sems.at[steps])
        keep.start()
        for start, size in col_tiles(width):
            columns = slice(start, start + size)
            own_ref[:, columns] = jnp.dot(
                hidden_ref[:rows], weights[:, columns], preferred_element_type=F32
            )
            other_ref[:, columns] = jnp.dot(
                hidden_ref[rows:], weights[:, columns], preferred_element_type=F32
            ).astype(BF16)
        if padded > width:
            other_ref[:, width:] = jnp.zeros((rows, padded - width), BF16)
        keep.wait()

    return pl.pallas_call(
        kernel,
        in_specs=[VMEM] + [ANY] * count,
        out_specs=[VMEM, VMEM, ANY],
        out_shape=[
            jax.ShapeDtypeStruct((rows, width), F32),
            jax.ShapeDtypeStruct((rows, padded), BF16),
            jax.ShapeDtypeStruct((half, padded), BF16),
        ],
        scratch_shapes=[pltpu.VMEM((half, padded), BF16), pltpu.SemaphoreType.DMA((steps + 1,))],
        cost_estimate=LIGHT,
    )(hidden, *pieces)


def finish_call(pieces, gate_up_moves, down_moves, block, inner, down_rows, width, padded):
    count = len(pieces)
    steps = len(gate_up_moves) + len(down_moves)

    def kernel(*refs):
        piece_refs = refs[:count]
        out_refs = refs[count : count + 3]
        columns_of, rows_of, gate_ref, up_ref, down_ref, sems = refs[count + 3 :]
        chip, core = axis_ranks()[1], lax.axis_index("rep") % 2
        shards = lax.axis_size("shard")
        copies = []
        for piece, row, size, columns, place in gate_up_moves:
            to_core, to_row, to_column = place(core, chip)
            copies.append(
                (
                    part_of(piece_refs[piece], row, size, columns),
                    columns_of.at[to_core, pl.ds(to_row, size), pl.ds(to_column, columns)],
                )
            )
        for piece, row, size, columns, place in down_moves:
            to_row, to_column = place(core, chip)
            copies.append(
                (
                    part_of(piece_refs[piece], row, size, columns),
                    rows_of.at[pl.ds(to_row, size), pl.ds(to_column, columns)],
                )
            )
        copies = run_copies(copies, sems)
        for copy in copies[: len(gate_up_moves)]:
            copy.wait()
        half = inner // shards // 2
        outs = [
            pltpu.make_async_copy(ref, out, sems.at[steps + number])
            for number, (ref, out) in enumerate(zip((gate_ref, up_ref, down_ref), out_refs))
        ]
        for index, ref in enumerate((gate_ref, up_ref)):
            for shard in range(shards):
                start = index * (inner // 2) + shard * half
                both = [columns_of[at, :, start : start + half] for at in range(2)]
                ref[:, 2 * half * shard : 2 * half * (shard + 1)] = jnp.concatenate(
                    both, 1
                ).astype(F32)
            outs[index].start()
        for copy in copies[len(gate_up_moves) :]:
            copy.wait()
        down_ref[...] = rows_of[...].T[:width].astype(F32)
        outs[2].start()
        for copy in outs:
            copy.wait()

    return pl.pallas_call(
        kernel,
        in_specs=[ANY] * count,
        out_specs=[ANY] * 3,
        out_shape=[
            jax.ShapeDtypeStruct((block, inner), F32),
            jax.ShapeDtypeStruct((block, inner), F32),
            jax.ShapeDtypeStruct((width, down_rows), F32),
        ],
        scratch_shapes=[
            pltpu.VMEM((2, block, inner), BF16),
            pltpu.VMEM((down_rows, padded), BF16),
            pltpu.VMEM((block, inner), F32),
            pltpu.VMEM((block, inner), F32),
            pltpu.VMEM((width, down_rows), F32),
            pltpu.SemaphoreType.DMA((steps + 3,)),
        ],
    )(*pieces)


def attn_finish_call(pieces, moves, block, proj):
    count = len(pieces)

    def kernel(*refs):
        piece_refs = refs[:count]
        out_refs, whole, sems = refs[count : count + 4], refs[count + 4], refs[count + 5]
        rep = lax.axis_index("rep")
        copies = []
        for piece, index, place in moves:
            for start, size, matrix, row in place(rep):
                copies.append(
                    (
                        piece_refs[piece].at[index, pl.ds(start, size)],
                        whole.at[matrix, pl.ds(row, size)],
                    )
                )
        for copy in run_copies(copies, sems):
            copy.wait()
        for index, ref in enumerate(out_refs):
            ref[...] = whole[index].astype(F32)

    return pl.pallas_call(
        kernel,
        in_specs=[ANY] * count,
        out_specs=[VMEM] * 4,
        out_shape=[jax.ShapeDtypeStruct((block, proj), F32)] * 4,
        scratch_shapes=[
            pltpu.VMEM((4, block, proj), BF16),
            pltpu.SemaphoreType.DMA((2 * len(moves),)),
        ],
    )(*pieces)


def hidden_grad_call(own, other, down, slope, act):
    rows, width = own.shape
    half = down.shape[0]
    tile = 256

    def kernel(own_ref, other_ref, down_ref, slope_ref, act_ref, gate_ref, up_ref):
        for index, ref in enumerate((own_ref, other_ref)):
            part = slice(index * rows, (index + 1) * rows)
            upstream = dot_last(ref[...], down_ref[...])
            gate_ref[part] = (upstream * slope_ref[part].astype(F32)).astype(BF16)
            up_ref[part] = (upstream * act_ref[part].astype(F32)).astype(BF16)

    whole = pl.BlockSpec((rows, width), lambda i: (0, 0))
    columns = pl.BlockSpec((2 * rows, tile), lambda i: (0, i))
    shape = jax.ShapeDtypeStruct((2 * rows, half), BF16)
    return pl.pallas_call(
        kernel,
        grid=(half // tile,),
        in_specs=[
            whole,
            whole,
            pl.BlockSpec((tile, down.shape[1]), lambda i: (i, 0)),
            columns,
            columns,
        ],
        out_specs=[columns, columns],
        out_shape=[shape, shape],
        cost_estimate=LIGHT,
    )(own, other, down, slope, act)


def normed_grad_call(gate, up, weights):
    double, half = gate.shape
    rows = double // 2
    width = weights.shape[0]
    tile = 256

    def kernel(gate_ref, up_ref, low_ref, high_ref, own_ref, other_ref):
        for index, ref in enumerate((own_ref, other_ref)):
            part = slice(index * rows, (index + 1) * rows)
            total = dot_last(gate_ref[part], low_ref[...]) + dot_last(up_ref[part], high_ref[...])
            ref[...] = total.astype(ref.dtype)

    whole = pl.BlockSpec((double, half), lambda i: (0, 0))
    return pl.pallas_call(
        kernel,
        grid=(pl.cdiv(width, tile),),
        in_specs=[
            whole,
            whole,
            pl.BlockSpec((tile, half), lambda i: (i, 0)),
            pl.BlockSpec((tile, half), lambda i: (i, 1)),
        ],
        out_specs=[pl.BlockSpec((rows, tile), lambda i: (0, i))] * 2,
        out_shape=[
            jax.ShapeDtypeStruct((rows, width), F32),
            jax.ShapeDtypeStruct((rows, lane_tiles(width)), BF16),
        ],
        cost_estimate=LIGHT,
    )(gate, up, weights, weights)


def row_specs(micro_count, local, width):
    return pl.BlockSpec((local, width), lambda i: (i, 0)), pl.BlockSpec((1, width), lambda i: (0, 0))


def sum_rows(ref, value):
    total = jnp.sum(value, axis=0, keepdims=True)

    @pl.when(pl.program_id(0) == 0)
    def _():
        ref[...] = total

    @pl.when(pl.program_id(0) > 0)
    def _():
        ref[...] += total


def put_padded(ref, value):
    width = value.shape[1]
    ref[:, :width] = value.astype(BF16)
    if ref.shape[1] > width:
        ref[:, width:] = jnp.zeros((value.shape[0], ref.shape[1] - width), BF16)


def lane_tiles(width):
    return -(-width // 128) * 128


def mid_call(tokens, context, w_out, gain, micro_count):
    rows, width = tokens.shape
    local = rows // micro_count
    by_row, vector = row_specs(micro_count, local, width)

    def kernel(token_ref, context_ref, out_ref, gain_ref, hidden_ref, normed_ref):
        hidden = token_ref[...].astype(F32) + jnp.dot(
            context_ref[...], out_ref[...], preferred_element_type=F32
        )
        hidden_ref[...] = hidden
        put_padded(normed_ref, hidden * rms_scale(hidden) * gain_ref[...])

    return pl.pallas_call(
        kernel,
        grid=(micro_count,),
        in_specs=[
            by_row,
            pl.BlockSpec((local, context.shape[1]), lambda i: (i, 0)),
            pl.BlockSpec(w_out.shape, lambda i: (0, 0)),
            vector,
        ],
        out_specs=[by_row, pl.BlockSpec((local, lane_tiles(width)), lambda i: (i, 0))],
        out_shape=[
            jax.ShapeDtypeStruct((rows, width), F32),
            jax.ShapeDtypeStruct((rows, lane_tiles(width)), BF16),
        ],
        cost_estimate=LIGHT,
    )(tokens, context, w_out, gain)


def out_call(hidden, part, given, cotangent, gate_cotangent, gain, vector_in, micro_count):
    rows, width = hidden.shape
    local = rows // micro_count
    by_row, vector = row_specs(micro_count, local, width)
    one = pl.BlockSpec((local, 1), lambda i: (i, 0))
    turned = pl.BlockSpec((1, width, local), lambda i: (i, 0, 0))
    padded = pl.BlockSpec((local, lane_tiles(width)), lambda i: (i, 0))

    def kernel(
        hidden_ref, part_ref, given_ref, up_ref, gate_ref, gain_ref, vector_ref,
        state_ref, deleted_ref, grad_ref, low_ref, gain_grad_ref, vector_grad_ref,
    ):
        state = hidden_ref[...] + part_ref[...] + given_ref[:, :width].astype(F32)
        state_ref[0] = state.T
        scale = rms_scale(state)
        normed = state * scale * gain_ref[...]
        logit = jnp.sum(normed * vector_ref[...], axis=1, keepdims=True)
        sigmoid = lax.logistic(logit)
        deleted_ref[...] = -30.0 * sigmoid
        slope = gate_ref[...] * -30.0 * sigmoid * (1.0 - sigmoid)
        upstream = slope * vector_ref[...]
        sum_rows(vector_grad_ref, slope * normed)
        sum_rows(gain_grad_ref, upstream * state * scale)
        grad = up_ref[...].astype(F32) + rms_back(state, scale, gain_ref[...], upstream)
        grad_ref[...] = grad
        put_padded(low_ref, grad)

    return pl.pallas_call(
        kernel,
        grid=(micro_count,),
        in_specs=[by_row, by_row, padded, by_row, one, vector, vector],
        out_specs=[turned, one, by_row, padded, vector, vector],
        out_shape=[
            jax.ShapeDtypeStruct((micro_count, width, local), F32),
            jax.ShapeDtypeStruct((rows, 1), F32),
            jax.ShapeDtypeStruct((rows, width), F32),
            jax.ShapeDtypeStruct((rows, lane_tiles(width)), BF16),
            jax.ShapeDtypeStruct((1, width), F32),
            jax.ShapeDtypeStruct((1, width), F32),
        ],
        cost_estimate=LIGHT,
    )(hidden, part, given, cotangent, gate_cotangent, gain, vector_in)


def back_call(part, given, grad_out, hidden, gain, context, w_out, micro_count):
    rows, width = hidden.shape
    local = rows // micro_count
    proj = context.shape[1]
    by_row, vector = row_specs(micro_count, local, width)
    by_proj = pl.BlockSpec((local, proj), lambda i: (i, 0))
    padded = pl.BlockSpec((local, lane_tiles(width)), lambda i: (i, 0))
    whole = pl.BlockSpec((proj, width), lambda i: (0, 0))

    def kernel(
        part_ref, given_ref, grad_ref, hidden_ref, gain_ref, context_ref, out_ref,
        mid_ref, context_grad_ref, out_grad_ref, gain_grad_ref, total,
    ):
        normed_grad = part_ref[...] + given_ref[:, :width].astype(F32)
        hidden = hidden_ref[...]
        scale = rms_scale(hidden)
        sum_rows(gain_grad_ref, normed_grad * hidden * scale)
        mid = grad_ref[...] + rms_back(hidden, scale, gain_ref[...], normed_grad)
        mid_ref[...] = mid
        low = mid.astype(BF16)
        context_grad_ref[...] = dot_last(low, out_ref[...]).astype(BF16)
        product = jnp.dot(context_ref[...].T, low, preferred_element_type=F32)
        step = pl.program_id(0)

        @pl.when(step == 0)
        def _():
            total[...] = product

        @pl.when(step > 0)
        def _():
            total[...] += product

        @pl.when(step == micro_count - 1)
        def _():
            out_grad_ref[...] = total[...].astype(BF16)

    return pl.pallas_call(
        kernel,
        grid=(micro_count,),
        in_specs=[by_row, padded, by_row, by_row, vector, by_proj, whole],
        out_specs=[by_row, by_proj, whole, vector],
        out_shape=[
            jax.ShapeDtypeStruct((rows, width), F32),
            jax.ShapeDtypeStruct((rows, proj), BF16),
            jax.ShapeDtypeStruct((proj, width), BF16),
            jax.ShapeDtypeStruct((1, width), F32),
        ],
        scratch_shapes=[pltpu.VMEM((proj, width), F32)],
        cost_estimate=LIGHT,
    )(part, given, grad_out, hidden, gain, context, w_out)


def in_call(query_grad, pair_parts, weights, grad_mid, tokens, gain, micro_count):
    rows, width = tokens.shape
    local = rows // micro_count
    proj = query_grad.shape[1]
    count = pair_parts.shape[0]
    by_row, vector = row_specs(micro_count, local, width)
    by_proj = pl.BlockSpec((local, proj), lambda i: (i, 0))
    by_pair = pl.BlockSpec((local, 2 * proj), lambda i: (i, 0))

    def kernel(
        query_ref, part_ref, wq_ref, wk_ref, wv_ref, mid_ref, token_ref, gain_ref,
        pair_ref, grad_ref, gain_grad_ref,
    ):
        pair = sum(part_ref[index].astype(F32) for index in range(count)).astype(BF16)
        pair_ref[...] = pair
        normed_grad = (
            dot_last(query_ref[...], wq_ref[0])
            + dot_last(pair[:, :proj], wk_ref[0])
            + dot_last(pair[:, proj:], wv_ref[0])
        )
        hidden = token_ref[...].astype(F32)
        scale = rms_scale(hidden)
        sum_rows(gain_grad_ref, normed_grad * hidden * scale)
        grad = mid_ref[...] + rms_back(hidden, scale, gain_ref[...], normed_grad)
        grad_ref[0] = grad.astype(BF16).T

    return pl.pallas_call(
        kernel,
        grid=(micro_count,),
        in_specs=[by_proj, pl.BlockSpec((count, local, 2 * proj), lambda i: (0, i, 0))]
        + [pl.BlockSpec((1, width, proj), lambda i, m=m: (m, 0, 0)) for m in range(3)]
        + [by_row, by_row, vector],
        out_specs=[by_pair, pl.BlockSpec((1, width, local), lambda i: (i, 0, 0)), vector],
        out_shape=[
            jax.ShapeDtypeStruct((rows, 2 * proj), BF16),
            jax.ShapeDtypeStruct((micro_count, width, local), BF16),
            jax.ShapeDtypeStruct((1, width), F32),
        ],
        cost_estimate=LIGHT,
    )(query_grad, pair_parts, weights, weights, weights, grad_mid, tokens, gain)


def weight_grad_call(left, right, picks, width, outputs, in_halves):
    left_own, left_other = left
    right_own, right_other = right
    rows = left_own.shape[0]
    total = 2 * rows if left_other is not None else rows
    beside = right_other is not None and right_own.shape[0] == total
    right_width = right_own.shape[1] * (2 if beside else 1)
    count = len(outputs)
    copies_out = sum(len(moves) for _, moves, _ in outputs)
    depth = sum(size for _, size in picks)
    tile = 256
    split = left_other is not None
    right_split = right_other is not None
    inputs = [left_own] + ([left_other] if split else []) + [right_own]
    inputs += [right_other] if right_split else []

    def kernel(*refs):
        in_refs = list(refs[: len(inputs)])
        out_refs = refs[len(inputs) : len(inputs) + count]
        lefts, turned, rights, result, sems = refs[len(inputs) + count :]
        copies = []
        for target, parted, aside in ((lefts, split, False), (rights, right_split, beside)):
            first = in_refs.pop(0)
            size = first.shape[1] if aside else first.shape[0]
            if not parted:
                copies.append((first, target))
            elif aside:
                copies.append((first, target.at[:, :size]))
                copies.append((in_refs.pop(0), target.at[:, size:]))
            else:
                copies.append((first, target.at[:size]))
                copies.append((in_refs.pop(0), target.at[size:]))
        for copy in run_copies(copies, sems):
            copy.wait()
        to_row = 0
        for first, size in picks:
            for begin in range(0, size, tile):
                span = min(tile, size - begin)
                turned[to_row : to_row + span] = lefts[:, first + begin : first + begin + span].T
                to_row += span

        def product(start, size):
            result[:, pl.ds(start, size)] = jnp.dot(
                turned[...], rights[:, pl.ds(start, size)], preferred_element_type=F32
            ).astype(BF16)

        rank, chip = axis_ranks()
        started = []
        for half in range(2 if in_halves else 1):
            first = (chip // 2 ^ (1 - half)) * (width // 2) if in_halves else 0
            tiles = (width // 2 if in_halves else width) // tile

            def step(index, carry, first=first):
                product(pl.multiple_of(first + index * tile, tile), tile)
                return carry

            lax.fori_loop(0, tiles, step, 0)
            if not in_halves and width % tile:
                product(tiles * tile, width % tile)
            for ref, (shape, moves, mask) in zip(out_refs, outputs):
                if in_halves and mask & 2 == 2 * half:
                    continue
                for index, place in moves:
                    row, column = place(rank, chip)
                    copy = pltpu.make_async_copy(
                        result.at[pl.ds(row, shape[1]), pl.ds(column, shape[2])],
                        ref.at[index],
                        sems.at[len(started)],
                    )
                    copy.start()
                    started.append(copy)
        for copy in started:
            copy.wait()

    return pl.pallas_call(
        kernel,
        in_specs=[ANY] * len(inputs),
        out_specs=[ANY] * count,
        out_shape=[jax.ShapeDtypeStruct(shape, BF16) for shape, _, _ in outputs],
        scratch_shapes=[
            pltpu.VMEM((total, left_own.shape[1]), BF16),
            pltpu.VMEM((depth, total), BF16),
            pltpu.VMEM((total, right_width), BF16),
            pltpu.VMEM((depth, width), BF16),
            pltpu.SemaphoreType.DMA((max(4, copies_out),)),
        ],
        cost_estimate=LIGHT,
    )(*inputs)


def on_device(
    tokens,
    cotangent,
    gate_cotangent,
    slot_of,
    seq_lengths,
    buckets,
    gain_attn,
    w_query,
    w_key,
    w_value,
    w_out,
    rel_bias,
    gain_ffn,
    w_gate,
    w_up,
    w_down,
    gain_delete,
    w_delete,
):
    shards = lax.axis_size("shard")
    reps = lax.axis_size("rep")
    chips = reps // 2
    rank = lax.axis_index("shard")
    rep_rank = lax.axis_index("rep")
    core = rep_rank % 2
    chip = rep_rank // 2
    micro_count, local_rows, width = tokens.shape
    group = local_rows * shards
    rows = micro_count * local_rows
    heads = rel_bias.shape[1]
    bucket_rows = rel_bias.shape[0]
    bucket_count = bucket_rows * shards
    proj = w_query.shape[1]
    head_size = proj // heads
    block = gain_attn.shape[0]
    inner = w_gate.shape[1]
    half_inner = inner // 2
    col_piece = inner // chips
    down_block = w_down.shape[0]
    down_half = down_block // 2
    down_piece = down_half // chips
    down_parts_count = -(-width // col_piece)
    padded = -(-width // 128) * 128
    aligned = reps == 8 and block % 16 == 0 and down_piece % 16 == 0 and col_piece % 128 == 0

    def swap(value, mask):
        return lax.ppermute(value, "rep", [(i, i ^ mask) for i in range(reps)])

    def shift(value, by=1):
        return lax.ppermute(value, "shard", [(i, (i + by) % shards) for i in range(shards)])

    def tie(value, moved):
        return lax.optimization_barrier((value, moved))

    def cut(count):
        half = count // 2
        return half // 16 * 16 if half >= 16 else half

    def gather_near(piece):
        if chips == 1:
            return []
        return [swap(piece, 2)] + ([swap(piece, 4)] if chips >= 4 else [])

    def gather_rest(near):
        if chips < 4:
            return []
        middle = cut(near[0].shape[0])
        return [swap(near[1][:middle], 2), swap(near[0][middle:], 4)]

    def gather_list(piece, near, rest):
        middle = cut(piece.shape[0])
        found = [(0, 0, piece)] + [(1 + i, 0, part) for i, part in enumerate(near)]
        found += [(3, i * middle, part) for i, part in enumerate(rest)]
        bit = 4
        while bit < chips:
            found += [
                (mask ^ bit, start, swap(part, 2 * bit)) for mask, start, part in found
            ]
            bit *= 2
        return found

    def plane_gather(piece):
        near = gather_near(piece)
        return gather_list(piece, near, gather_rest(near))

    def add(*values):
        return sum(value.astype(F32) for value in values).astype(BF16)

    def plane_reduce(parts, axis):
        state = reduce_begin(parts, axis)
        return reduce_end(reduce_middle(state, axis))

    def reduce_begin(parts, axis):
        def level(base, bit):
            if bit < 4:
                return lambda name: parts[base][name]
            lower, upper = level(base, bit // 2), level(base ^ bit, bit // 2)
            return lambda name: add(lower(name), swap(upper(name), 2 * bit))

        get = level(0, chips // 2)
        if chips < 4:
            return [get("own")] + ([swap(get("near"), 2)] if chips == 2 else [])
        return [get("own"), get("far"), get("near"), swap(get("top"), 2), swap(get("low"), 4)]

    def reduce_middle(state, axis):
        if chips < 4:
            return state
        own, far, near, top, low = state
        middle = top.shape[axis]

        def pair(value):
            return (
                lax.slice_in_dim(value, 0, middle, axis=axis),
                lax.slice_in_dim(value, middle, value.shape[axis], axis=axis),
            )

        (far_top, far_low), (near_top, near_low) = pair(far), pair(near)
        far = jnp.concatenate([add(far_top, top), far_low], axis)
        near = jnp.concatenate([near_top, add(near_low, low)], axis)
        return [own, swap(far, 4), swap(near, 2)]

    def reduce_end(state):
        return add(*state) if len(state) > 1 else state[0]

    names = {"own": 0, "near": 1, "far": 2, "top": 3, "low": 3}
    bases = [base for base in range(chips) if base & 3 == 0]
    used = ["own", "near", "far", "top", "low"] if chips >= 4 else ["own", "near"][:chips]

    def source(step):
        return (rank - step) % shards

    order = (rank - jnp.arange(shards, dtype=jnp.int32)) % shards
    per_matrix = reps // 4
    attn_rows = block // per_matrix
    if aligned:
        attn_rows = -(-attn_rows // 16) * 16
    last_row = block - attn_rows

    def part_row(part):
        return jnp.minimum(part * attn_rows, last_row)

    attn_own = jnp.stack([w_query, w_key, w_value, w_out.reshape(block, proj)])
    attn_piece = lax.dynamic_slice(
        attn_own,
        (rep_rank // per_matrix, part_row(rep_rank % per_matrix), 0),
        (1, attn_rows, proj),
    )[0]
    vector_pack = jnp.concatenate(
        [gain_attn, gain_ffn, gain_delete, w_delete, rel_bias.reshape(-1)]
    )
    pack_rows = -(-vector_pack.shape[0] // (16 * proj)) * 16
    vector_pack = jnp.pad(vector_pack, (0, pack_rows * proj - vector_pack.shape[0]))
    vector_pack = vector_pack.reshape(pack_rows, proj)
    attn_sent = jnp.concatenate([attn_piece, vector_pack])
    attn_arrived = [shift(attn_sent, step) for step in range(1, shards)]
    token_rows = tokens.reshape(rows, width)
    attn_arrived, (token_rows, attn_own) = tie(attn_arrived, (token_rows, attn_own))
    vectors = jnp.stack([vector_pack] + [part[attn_rows:] for part in attn_arrived])
    vectors = jnp.take(vectors, order, axis=0).reshape(shards, pack_rows * proj)
    attn_gain = vectors[:, :block].reshape(width).astype(F32)
    ffn_gain = vectors[:, block : 2 * block].reshape(width).astype(F32)
    delete_gain = vectors[:, 2 * block : 3 * block].reshape(width).astype(F32)
    delete_vec = vectors[:, 3 * block : 4 * block].reshape(width).astype(F32)
    bias_table = vectors[:, 4 * block : 4 * block + bucket_rows * heads]
    bias_table = bias_table.reshape(bucket_count, heads)
    stacked = jnp.stack([part[:attn_rows] for part in attn_arrived])

    def pack(gate_up_part, down_part):
        wide = jnp.pad(down_part, ((0, 0), (0, down_parts_count * col_piece - width)))
        cuts = [wide[:, i * col_piece : (i + 1) * col_piece] for i in range(down_parts_count)]
        return jnp.concatenate([gate_up_part] + cuts)

    def overlaps(start, count):
        bounds = [(None, 0, block)] + [
            (i, block + i * down_piece, block + (i + 1) * down_piece)
            for i in range(down_parts_count)
        ]
        found = []
        for part, low, high in bounds:
            first, last = max(low, start), min(high, start + count)
            if first < last:
                found.append((part, first - start, first - low, last - first))
        return found

    def part_columns(part):
        return min(col_piece, padded - part * col_piece)

    gate_up_own = pick_columns(w_gate, w_up)
    down_own = lax.dynamic_slice_in_dim(w_down, core * down_half, down_half, 0)
    packed_own = pack(
        lax.dynamic_slice_in_dim(gate_up_own, chip * col_piece, col_piece, 1),
        lax.dynamic_slice_in_dim(down_own, chip * down_piece, down_piece, 0),
    )
    packed_own, stacked = tie(packed_own, stacked)
    attn_plane = [stacked] + [swap(stacked, 2 * mask) for mask in range(1, chips)]
    attn_plane = jnp.stack(attn_plane)
    ring = [packed_own, shift(packed_own)]
    attn_plane, ring = tie(attn_plane, ring)
    nears, rests = [None] * shards, [None] * shards
    nears[1] = gather_near(ring[1])
    attn_other = swap(attn_plane, 1)

    def attn_place(mask, flip, step):
        def place(at, rep):
            owner = rep ^ (2 * mask + flip)
            row = (at - step) % shards * block + part_row(owner % per_matrix)
            return owner // per_matrix, pl.multiple_of(row, 16) if aligned else row

        return place

    shared = per_matrix * attn_rows - block

    def split_place(place, flip):
        def places_of(*at):
            matrix, row = place(*at)
            part = (at[-1] ^ flip) % per_matrix
            first = row - last_row * part
            moves = [
                (
                    pl.multiple_of(shared * part, 16),
                    attn_rows - shared,
                    matrix,
                    pl.multiple_of(first + attn_rows * part, 16),
                )
            ]
            if shared and flip == 0:
                moves.append(
                    (
                        pl.multiple_of(last_row * (1 - part), 16),
                        shared,
                        matrix,
                        pl.multiple_of(first + last_row, 16),
                    )
                )
            return moves

        return places_of

    attn_pieces = [w_query, w_key, w_value, attn_own[3]]
    attn_places = [
        [(None, lambda at, rep, matrix=matrix: [(0, block, matrix, pl.multiple_of(at * block, 16))])]
        for matrix in range(4)
    ]
    for flip, found in enumerate((attn_plane, attn_other)):
        attn_pieces.append(found)
        attn_places.append(
            [
                ((mask, step - 1), attn_place(mask, flip, step), flip)
                for mask in range(chips)
                for step in range(1, shards)
            ]
        )
    if not aligned:
        whole = jnp.zeros((4, width, proj), BF16)
        whole = lax.dynamic_update_slice(whole, attn_own, (0, rank * block, 0))
        for piece, place in zip(attn_pieces[4:], attn_places[4:]):
            for index, where, _ in place:
                matrix, row = where(rank, rep_rank)
                whole = lax.dynamic_update_slice(whole, piece[index][None], (matrix, row, 0))
        attn_pieces = [whole[matrix] for matrix in range(4)]
        attn_places = [
            [(None, lambda at, rep, matrix=matrix: [(0, width, matrix, 0)])] for matrix in range(4)
        ]
    else:
        attn_places[4:] = [
            [(index, split_place(where, flip)) for index, where, flip in place]
            for place in attn_places[4:]
        ]

    slots = slot_of[:, 0]
    own_slots = lax.dynamic_slice_in_dim(slots, rank * local_rows, local_rows, 1)
    key_slots = jnp.take(slots.reshape(micro_count, shards, local_rows), order, axis=1)
    key_slots = key_slots.reshape(micro_count, group)
    onehot = (buckets[:, None] == jnp.arange(bucket_count, dtype=jnp.int32)[None, :]).astype(F32)
    onehot = jnp.pad(onehot, ((0, 1), (0, 0)))
    bias_rows = jnp.dot(onehot, bias_table.astype(F32), precision=HIGHEST).T
    bias = bias_of_queries(bias_rows, own_slots.reshape(rows), group)
    first_len = seq_lengths[:, 0, 0]

    normed_one, queries, own_pairs, attn_full = project_call(
        token_rows, attn_gain[None], attn_pieces, attn_places, block, proj
    )
    out_full = attn_full[3].reshape(proj, width)

    for step in range(2, shards - 1):
        ring.append(shift(ring[-1]))
    own_pairs, ring = tie(own_pairs, ring)
    early = (
        out_full,
        jnp.pad(down_own, ((0, 0), (0, padded - width))),
        cotangent.reshape(rows, width),
        gate_cotangent.reshape(rows, 1).astype(F32),
        [value[None] for value in (ffn_gain, delete_gain, delete_vec)],
        [slots[micro].reshape(group, 1) for micro in range(micro_count)],
    )
    pairs = [own_pairs]
    for step in range(1, shards):
        pairs.append(shift(pairs[-1]))
        if step == 1:
            pairs[-1], (nears[1], bias) = tie(pairs[-1], (nears[1], bias))
            rests[1] = gather_rest(nears[1])
        if step == 2:
            pairs[-1], (rests[1], early) = tie(pairs[-1], (rests[1], early))
            ring[2], rests[1] = tie(ring[2], rests[1])
            nears[2] = gather_near(ring[2])
    ring[-1], pairs[-1] = tie(ring[-1], pairs[-1])
    last = shift(ring[-1][:block])
    pairs, nears[2] = tie(pairs, nears[2])
    rests[2] = gather_rest(nears[2])
    context, probs, packed = [], [], []
    for micro in range(micro_count):
        if micro == micro_count - 1:
            context, (rests[2], last) = tie(context, (rests[2], last))
            last_near = gather_near(last)
        *context, prob, pair = attention_call(
            micro,
            first_len[micro : micro + 1],
            queries,
            pairs,
            own_slots.reshape(rows, 1),
            key_slots[micro : micro + 1],
            bias,
            context,
        )
        probs.append(prob)
        packed.append(pair)
    for step in range(3, shards - 1):
        ring[step], rests[step - 1] = tie(ring[step], rests[step - 1])
        nears[step] = gather_near(ring[step])
        rests[step] = gather_rest(nears[step])
    if shards > 4:
        context, rests[shards - 2] = tie(context, rests[shards - 2])
    last_piece, last = tie(ring[-1][block:], last)
    last_down = shift(last_piece)
    (context,) = context
    out_full, down_wide, cotangent_rows, gate_rows, gains, key_columns = early
    ffn_gain, delete_gain, delete_vec = gains

    hidden_mid, normed_two = mid_call(token_rows, context, out_full, ffn_gain, micro_count)
    normed_two, (last_near, last_down) = tie(normed_two, (last_near, last_down))
    last_rest = gather_rest(last_near)
    normed_two_other = swap(normed_two, 1)
    normed_two_other, (last_rest, last_down) = tie(normed_two_other, (last_rest, last_down))
    last_down_found = [(mask, 0, swap(last_down, 2 * mask)) for mask in range(1, chips)]
    pieces = [gate_up_own, down_wide]
    gate_up_moves = [(0, 0, block, inner, lambda at, chip_at: (pl.multiple_of(at * block, 16), 0))]
    down_moves = [
        (1, 0, down_half, padded, lambda at, chip_at: (pl.multiple_of(at * down_half, 16), 0))
    ]

    def gate_up_place(step, mask, row):
        return lambda at, chip_at: (
            pl.multiple_of((at - step) % shards * block + row, 16),
            pl.multiple_of((chip_at ^ mask) * col_piece, 128),
        )

    def down_place(step, mask, row, part):
        return lambda at, chip_at: (
            pl.multiple_of((at - step) % shards * down_half + (chip_at ^ mask) * down_piece + row, 16),
            part * col_piece,
        )

    arrived = [
        (step, 0, gather_list(ring[step], nears[step], rests[step])) for step in range(1, shards - 1)
    ]
    arrived.append((shards - 1, 0, gather_list(last, last_near, last_rest)))
    arrived.append((shards - 1, block, [(0, 0, last_down)] + last_down_found))
    for step, below, found in arrived:
        for mask, start, array in found:
            for part, here, there, size in overlaps(below + start, array.shape[0]):
                if part is None:
                    gate_up_moves.append(
                        (len(pieces), here, size, col_piece, gate_up_place(step, mask, there))
                    )
                else:
                    down_moves.append(
                        (
                            len(pieces),
                            here,
                            size,
                            part_columns(part),
                            down_place(step, mask, there, part),
                        )
                    )
            pieces.append(array)
    if not aligned:

        def put_together(moves, shape):
            whole = jnp.zeros(shape, BF16)
            for piece, row, size, columns, place in moves:
                value = pieces[piece][row : row + size, :columns]
                whole = lax.dynamic_update_slice(whole, value, place(rank, chip))
            return whole

        pieces = [
            put_together(gate_up_moves, (width, inner)),
            put_together(down_moves, (half_inner, padded)),
        ]
        gate_up_moves = [(0, 0, width, inner, lambda at, chip_at: (0, 0))]
        down_moves = [(1, 0, half_inner, padded, lambda at, chip_at: (0, 0))]
    gate_up_pieces, gate_up_moves = used_by(pieces, gate_up_moves)
    down_pieces, down_moves = used_by(pieces, down_moves)
    gate_slope_act, gate_act, inner_act, gate_up = gate_up_call(
        normed_two, normed_two_other, width, inner, gate_up_pieces, gate_up_moves
    )
    down_part, down_given, down = down_call(inner_act, width, padded, down_pieces, down_moves)
    hidden_out, deleted, grad_out, down_up, grad_delete_gain, grad_delete_vec = out_call(
        hidden_mid,
        down_part,
        swap(down_given, 1),
        cotangent_rows,
        gate_rows,
        delete_gain,
        delete_vec,
        micro_count,
    )

    down_up_other = swap(down_up, 1)

    def reduce_plan(size, piece_columns, place):
        middle = cut(size)
        spans = {"own": (0, size), "near": (0, size), "far": (0, size)}
        spans["top"], spans["low"] = (0, middle), (middle, size - middle)
        plan = []
        for base in bases:
            for name in used:
                start, count = spans[name]
                moves = [
                    (index, place(index, base ^ names[name], start)) for index in range(shards)
                ]
                plan.append(((shards, count, piece_columns), moves, base ^ names[name]))
        return plan

    def reduce_run(plan, left, right, picks, right_width, in_halves):
        if aligned:
            buffers = weight_grad_call(left, right, picks, right_width, plan, in_halves)
        else:
            shape = (sum(size for _, size in picks), right_width)
            whole = weight_grad_call(
                left, right, picks, right_width,
                [((1,) + shape, [(0, lambda at, chip_at: (0, 0))], 0)], False,
            )[0][0]
            buffers = []
            for (_, size, columns), moves, _ in plan:
                buffers.append(
                    jnp.stack(
                        [
                            lax.dynamic_slice(whole, place(rank, chip), (size, columns))
                            for _, place in moves
                        ]
                    )
                )
        return {
            base: dict(zip(used, buffers[i * len(used) : (i + 1) * len(used)]))
            for i, base in enumerate(bases)
        }

    def exchange(value):
        return lax.all_to_all(value, "shard", split_axis=0, concat_axis=0, tiled=True)

    def total_of(arrived):
        return jnp.sum(arrived.astype(F32), axis=0).astype(BF16)

    def down_grad_place(index, mask, start):
        plain = lambda at, chip_at: (
            index * down_half + (chip_at ^ mask) * down_piece + start,
            0,
        )
        return tile_hint(plain, 16, 128) if aligned else plain

    def gate_up_grads(first, size, left, right):
        def place(index, mask, start):
            plain = lambda at, chip_at: (index * size + start, (chip_at ^ mask) * col_piece)
            return tile_hint(plain, 16, 128) if aligned else plain

        return reduce_run(
            reduce_plan(size, col_piece, place),
            left,
            right,
            [(index * block + first, size) for index in range(shards)],
            inner,
            chips == 4 and half_inner % 256 == 0,
        )

    down_buffers = reduce_run(
        reduce_plan(down_piece, width, down_grad_place),
        (inner_act, None),
        (down_up, down_up_other),
        [(0, half_inner)],
        width,
        False,
    )
    down_state = reduce_begin(down_buffers, 1)
    gate_grad, up_grad = hidden_grad_call(down_up, down_up_other, down, gate_slope_act, gate_act)
    gate_grad, down_state = tie(gate_grad, down_state)
    down_state = reduce_middle(down_state, 1)
    normed_both = (normed_two, normed_two_other)
    gate_up_buffers = gate_up_grads(0, cut(block), normed_both, (gate_grad, up_grad))
    gate_grad, gate_up_buffers = tie(gate_grad, gate_up_buffers)
    normed_part, normed_given = normed_grad_call(gate_grad, up_grad, gate_up)
    normed_given, (down_state, gate_up_buffers) = tie(normed_given, (down_state, gate_up_buffers))
    gate_up_state = reduce_begin(gate_up_buffers, 1)
    down_arrived = exchange(reduce_end(down_state))
    normed_given = swap(normed_given, 1)
    grad_mid, context_grad, grad_w_out, grad_ffn_gain = back_call(
        normed_part,
        normed_given,
        grad_out,
        hidden_mid,
        ffn_gain,
        context,
        out_full,
        micro_count,
    )
    context_grad, gate_up_state = tie(context_grad, gate_up_state)
    gate_up_state = reduce_middle(gate_up_state, 1)
    score_grads, sums = [], []
    for micro in range(micro_count):
        score_grad, *sums = attention_back_call(
            micro,
            queries,
            context_grad,
            probs[micro],
            packed[micro],
            key_columns[micro],
            shards,
            sums,
        )
        score_grads.append(score_grad)
    query_grad, pair_parts = sums
    gate_grad, pair_parts = tie(gate_grad, pair_parts)
    pair_arrived = exchange(pair_parts)
    gate_up_buffers = gate_up_grads(
        cut(block), block - cut(block), normed_both, (gate_grad, up_grad)
    )
    gate_up_buffers, gate_up_state = tie(gate_up_buffers, gate_up_state)
    gate_up_later = reduce_begin(gate_up_buffers, 1)
    grad_bias_rows = bias_fold(score_grads, own_slots.reshape(rows))
    grad_bias = jnp.einsum("ob,ho->bh", onehot, grad_bias_rows, precision=HIGHEST)
    out_grads = grad_w_out.reshape(width, proj)
    gate_up_later, (grad_bias, out_grads) = tie(gate_up_later, (grad_bias, out_grads))
    gate_up_later = reduce_middle(gate_up_later, 1)
    pair_arrived, down_arrived = tie(pair_arrived, down_arrived)
    gate_up_arrived = exchange(reduce_end(gate_up_state))
    down_sum = total_of(down_arrived)
    pair_sum, grad_in, grad_attn_gain = in_call(
        query_grad,
        pair_arrived,
        attn_full,
        grad_mid,
        token_rows,
        attn_gain[None],
        micro_count,
    )
    pair_sum, gate_up_later = tie(pair_sum, gate_up_later)

    small = jnp.concatenate(
        [
            grad_attn_gain.reshape(shards, block),
            grad_ffn_gain.reshape(shards, block),
            grad_delete_gain.reshape(shards, block),
            grad_delete_vec.reshape(shards, block),
            grad_bias.reshape(shards, bucket_rows * heads),
        ],
        axis=1,
    ).astype(BF16)
    small = jnp.pad(small, ((0, 0), (0, pack_rows * proj - small.shape[1])))
    small = small.reshape(shards, pack_rows, proj)

    def attn_grad_place(mask, flip, index):
        def place(at, rep):
            owner = rep ^ (2 * mask + flip)
            row = index * block + part_row(owner % per_matrix)
            return owner // per_matrix, pl.multiple_of(row, 16) if aligned else row

        return place

    attn_plan = [
        (
            (chips, shards, attn_rows + pack_rows, proj),
            [
                ((mask, index), attn_grad_place(mask, flip, index), index)
                for mask in range(chips)
                for index in range(shards)
            ],
        )
        for flip in range(2)
    ]
    if aligned:
        kept, given = project_grad_call(
            normed_one, query_grad, pair_sum, out_grads, small, attn_plan
        )
    else:
        whole_plan = [
            (
                (4, width, proj),
                [((matrix,), lambda at, rep, matrix=matrix: (matrix, 0), None) for matrix in range(4)],
            )
        ]
        whole = project_grad_call(
            normed_one, query_grad, pair_sum, out_grads, small, whole_plan
        )[0]
        kept, given = [
            jnp.stack(
                [
                    jnp.concatenate(
                        [
                            lax.dynamic_slice(
                                whole, where(rank, rep_rank) + (0,), (1, attn_rows, proj)
                            )[0],
                            small[index],
                        ]
                    )
                    for _, where, index in items
                ]
            ).reshape(shape)
            for shape, items in attn_plan
        ]
    given = swap(given, 1)
    attn_own_sum = add(kept[0], given[0])
    attn_send = [add(kept[mask], given[mask]) for mask in range(1, chips)]
    attn_found = [swap(part, 2 * mask + 2) for mask, part in enumerate(attn_send)]
    gate_up_rest = exchange(reduce_end(gate_up_later))
    attn_found, gate_up_rest = tie(attn_found, gate_up_rest)
    attn_sum = add(attn_own_sum, *attn_found)
    attn_sum = total_of(exchange(attn_sum))
    gate_up_sum = jnp.concatenate([total_of(gate_up_arrived), total_of(gate_up_rest)])
    total = attn_sum[attn_rows:].astype(F32).reshape(-1)
    attn_sum = attn_sum[:attn_rows]

    packed_sum = pack(gate_up_sum, down_sum)
    near = gather_near(packed_sum)
    attn_sum, near = tie(attn_sum, near)
    rest = gather_rest(near)
    attn_half = [attn_sum] + [swap(attn_sum, 2 * mask) for mask in range(1, chips)]
    bounds = [0, block, 2 * block, 3 * block, 4 * block, 4 * block + bucket_rows * heads]
    totals = [total[low:high] for low, high in zip(bounds, bounds[1:])]
    totals[4] = totals[4].reshape(bucket_rows, heads)
    attn_half, (rest, totals) = tie(attn_half, (rest, totals))
    found = gather_list(packed_sum, near, rest)
    pieces, gate_up_moves, down_moves = [], [], []

    def gate_up_to(flip, mask, row):
        return lambda core_at, chip_at: (
            core_at ^ flip,
            row,
            pl.multiple_of((chip_at ^ mask) * col_piece, 128),
        )

    def down_to(flip, mask, row, part):
        return lambda core_at, chip_at: (
            pl.multiple_of((core_at ^ flip) * down_half + (chip_at ^ mask) * down_piece + row, 16),
            part * col_piece,
        )

    for flip in range(2):
        for mask, start, array in found:
            array = swap(array, 1) if flip else array
            for part, here, there, size in overlaps(start, array.shape[0]):
                if part is None:
                    gate_up_moves.append(
                        (len(pieces), here, size, col_piece, gate_up_to(flip, mask, there))
                    )
                else:
                    down_moves.append(
                        (
                            len(pieces),
                            here,
                            size,
                            part_columns(part),
                            down_to(flip, mask, there, part),
                        )
                    )
            pieces.append(array)
    if aligned:
        grad_gate, grad_up, grad_down_out = finish_call(
            pieces, gate_up_moves, down_moves, block, inner, down_block, width, padded
        )
        grad_down_out = grad_down_out.T
    else:
        halves = jnp.zeros((2, block, inner), BF16)
        for piece, row, size, columns, place in gate_up_moves:
            value = pieces[piece][None, row : row + size, :columns]
            halves = lax.dynamic_update_slice(halves, value, place(core, chip))
        whole = jnp.zeros((down_block, padded), BF16)
        for piece, row, size, columns, place in down_moves:
            value = pieces[piece][row : row + size, :columns]
            whole = lax.dynamic_update_slice(whole, value, place(core, chip))
        grad_gate, grad_up = spread_columns(halves[0], halves[1])
        grad_down_out = whole[:, :width].astype(F32)

    attn_half = jnp.stack(attn_half)
    attn_found = [attn_half, swap(attn_half, 1)]

    def attn_to(mask, flip):
        def place(rep):
            owner = rep ^ (2 * mask + flip)
            row = part_row(owner % per_matrix)
            return owner // per_matrix, pl.multiple_of(row, 16) if aligned else row

        return place

    attn_moves = [(flip, mask, attn_to(mask, flip)) for flip in range(2) for mask in range(chips)]
    if aligned:
        attn_moves = [
            (flip, mask, split_place(place, flip)) for flip, mask, place in attn_moves
        ]
        attn_shard = attn_finish_call(attn_found, attn_moves, block, proj)
    else:
        attn_shard = jnp.zeros((4, block, proj), BF16)
        for piece, index, place in attn_moves:
            attn_shard = lax.dynamic_update_slice(
                attn_shard, attn_found[piece][index][None], place(rep_rank) + (0,)
            )
        attn_shard = attn_shard.astype(F32)

    return (
        jnp.swapaxes(hidden_out, 1, 2),
        deleted.reshape(micro_count, local_rows),
        jnp.swapaxes(grad_in, 1, 2),
        totals[0],
        attn_shard[0],
        attn_shard[1],
        attn_shard[2],
        attn_shard[3].reshape(proj // shards, width),
        totals[4],
        totals[1],
        grad_gate,
        grad_up,
        grad_down_out,
        totals[2],
        totals[3],
    )


def used_by(pieces, moves):
    wanted = sorted({move[0] for move in moves})
    return [pieces[i] for i in wanted], [(wanted.index(move[0]),) + move[1:] for move in moves]


def tile_hint(place, row_unit, column_unit):
    def hinted(at, chip_at):
        row, column = place(at, chip_at)
        return pl.multiple_of(row, row_unit), pl.multiple_of(column, column_unit)

    return hinted


def solution(mesh):
    rows = P(None, ("rep", "shard"), None)
    flat = P(None, ("rep", "shard"))
    by_rep = P(None, "rep", None)
    vector = P("shard")
    matrix = P("shard", None)
    in_specs = (
        (rows, rows, flat, by_rep, by_rep, P(), vector)
        + (matrix,) * 5
        + (vector,)
        + (matrix,) * 3
        + (vector, vector)
    )
    out_specs = (
        (rows, flat, rows, vector) + (matrix,) * 5 + (vector,) + (matrix,) * 3 + (vector, vector)
    )
    return jax.shard_map(
        on_device, mesh=mesh, in_specs=in_specs, out_specs=out_specs, check_vma=False
    )
```

```python
import functools

import math

import jax
import jax.numpy as jnp
from jax import lax
from jax.experimental import pallas as pl
from jax.experimental.pallas import tpu as pltpu
from jax.sharding import PartitionSpec as P

EPSILON = 1e-06
HIGHEST = lax.Precision.HIGHEST
MASKED = -1000000000.0
BF16 = jnp.bfloat16
LIGHT = pl.CostEstimate(flops=1000, bytes_accessed=1000, transcendentals=0)
F32 = jnp.float32


ANY = pl.BlockSpec(memory_space=pl.ANY)
VMEM = pl.BlockSpec(memory_space=pltpu.VMEM)


def rms_scale(hidden):
    return lax.rsqrt(jnp.mean(hidden * hidden, axis=-1, keepdims=True) + EPSILON)


def rms_back(hidden, scale_row, gain, upstream):
    scaled = upstream * gain
    return scale_row * scaled - hidden * (scale_row * scale_row * scale_row) * jnp.mean(
        hidden * scaled, axis=-1, keepdims=True
    )


def bias_kernel(rows_ref, slots_ref, out_ref):
    group = out_ref.shape[2]
    row = jnp.broadcast_to(rows_ref[0], (group, rows_ref.shape[2]))
    grid = pltpu.roll(row, group + 1, 1, stride=1, stride_axis=0)[:, :group].astype(BF16)
    tokens = slots_ref.shape[0]
    pick = (slots_ref[...] == lax.broadcasted_iota(jnp.int32, (tokens, group), 1)).astype(BF16)
    out_ref[0] = jnp.dot(pick, grid, preferred_element_type=F32).astype(BF16)


def bias_of_queries(bias_rows, slots, group):
    heads, width = bias_rows.shape
    tokens = slots.shape[0]
    return pl.pallas_call(
        bias_kernel,
        grid=(heads,),
        in_specs=[
            pl.BlockSpec((1, 1, width), lambda h: (h, 0, 0)),
            pl.BlockSpec((tokens, 1), lambda h: (0, 0)),
        ],
        out_specs=pl.BlockSpec((1, tokens, group), lambda h: (h, 0, 0)),
        out_shape=jax.ShapeDtypeStruct((heads, tokens, group), BF16),
    )(bias_rows.reshape(heads, 1, width), slots.reshape(tokens, 1))


def bias_fold(score_grads, slots):
    count, heads, local, group = score_grads.shape

    def kernel(*refs):
        grad_refs, slots_ref, out_ref = refs[:count], refs[count], refs[count + 1]
        square = None
        for index, ref in enumerate(grad_refs):
            mine = slots_ref[:, index * local : (index + 1) * local]
            row = lax.broadcasted_iota(jnp.int32, (group, local), 0)
            place = (row == (group - 1) - mine).astype(BF16)
            part = jnp.dot(place, ref[0, 0], preferred_element_type=F32)
            square = part if square is None else square + part
        wide = jnp.concatenate([square, jnp.zeros_like(square)], axis=1)
        rolled = pltpu.roll(wide, 0, 1, stride=1, stride_axis=0)
        out_ref[0] = jnp.sum(rolled, axis=0, keepdims=True)

    return pl.pallas_call(
        kernel,
        grid=(heads,),
        in_specs=[
            pl.BlockSpec((1, 1, local, group), lambda h, m=m: (m, h, 0, 0)) for m in range(count)
        ]
        + [pl.BlockSpec((1, count * local), lambda h: (0, 0))],
        out_specs=pl.BlockSpec((1, 1, 2 * group), lambda h: (h, 0, 0)),
        out_shape=jax.ShapeDtypeStruct((heads, 1, 2 * group), F32),
    )(*[score_grads] * count, slots.reshape(1, count * local)).reshape(heads, 2 * group)


def by_head(value, head, head_size):
    per_block = 128 // head_size
    start = head // per_block * 128
    lanes = lax.broadcasted_iota(jnp.int32, (1, 128), 1) // head_size
    block = value[:, start : start + 128]
    return jnp.where(lanes == head % per_block, block, jnp.zeros_like(block)), start


def dot_last(left, right):
    return lax.dot_general(left, right, (((1,), (1,)), ((), ())), preferred_element_type=F32)


def attention_call(micro, micro_count, lengths, queries, pairs, own_slots, key_slots, bias, into):
    heads, rows, group = bias.shape
    double = pairs[0].shape[1]
    count = len(pairs)
    local = group // count
    proj = double // 2
    head_size = proj // heads

    def kernel(lengths_ref, query_ref, *rest):
        pair_refs = rest[:count]
        own_ref, key_ref, bias_ref = rest[count : count + 3]
        context_ref, prob_ref, packed_ref, arrived = rest[-4:]
        prob_ref, packed_ref = prob_ref.at[0], packed_ref.at[0]
        for index, ref in enumerate(pair_refs):
            arrived[index * local : (index + 1) * local] = ref[...]
        place = (
            lax.broadcasted_iota(jnp.int32, (group, group), 0) == key_ref[...]
        ).astype(BF16)
        packed_ref[...] = jnp.dot(place, arrived[...], preferred_element_type=F32).astype(BF16)
        first = lengths_ref[0]
        key_seg = lax.broadcasted_iota(jnp.int32, (local, group), 1) >= first
        same = key_seg == (own_ref[...] >= first)
        per_block = 128 // head_size
        total = None
        for head in range(heads):
            query, start = by_head(query_ref[...], head, head_size)
            scores = dot_last(query, packed_ref[:, start : start + 128])
            scores = jnp.where(same, scores + bias_ref[head].astype(F32), MASKED)
            weights = jnp.exp(scores - jnp.max(scores, axis=1, keepdims=True))
            weights = (weights / jnp.sum(weights, axis=1, keepdims=True)).astype(BF16)
            prob_ref[head] = weights
            value, _ = by_head(packed_ref[:, proj:], head, head_size)
            part = jnp.dot(weights, value, preferred_element_type=F32)
            total = part if head % per_block == 0 else total + part
            if head % per_block == per_block - 1:
                context_ref[:, start : start + 128] = total.astype(BF16)

    return pl.pallas_call(
        kernel,
        grid=(1,),
        in_specs=[
            pl.BlockSpec(memory_space=pltpu.SMEM),
            pl.BlockSpec((local, proj), lambda i: (micro, 0)),
        ]
        + [pl.BlockSpec((local, double), lambda i: (micro, 0))] * count
        + [
            pl.BlockSpec((local, 1), lambda i: (micro, 0)),
            pl.BlockSpec((1, group), lambda i: (0, 0)),
            pl.BlockSpec((heads, local, group), lambda i: (0, micro, 0)),
        ]
        + [ANY] * len(into),
        out_specs=[
            pl.BlockSpec((local, proj), lambda i: (micro, 0)),
            pl.BlockSpec((1, heads, local, group), lambda i: (micro, 0, 0, 0)),
            pl.BlockSpec((1, group, double), lambda i: (micro, 0, 0)),
        ],
        out_shape=[
            jax.ShapeDtypeStruct(queries.shape, BF16),
            jax.ShapeDtypeStruct((micro_count, heads, local, group), BF16),
            jax.ShapeDtypeStruct((micro_count, group, double), BF16),
        ],
        input_output_aliases={count + 5 + i: i for i in range(len(into))},
        scratch_shapes=[pltpu.VMEM((group, double), BF16)],
        cost_estimate=LIGHT,
    )(lengths, queries, *pairs, own_slots, key_slots, bias, *into)


def attention_back_call(queries, context_grad, probs, packed, key_slots, shards):
    micro_count, heads, local, group = probs.shape
    double = packed.shape[2]
    proj = double // 2
    head_size = proj // heads

    def kernel(query_ref, context_ref, prob_ref, packed_ref, key_ref, *rest):
        score_ref, dq_ref, part_ref, sums = rest
        score_ref, prob_ref, packed_ref = score_ref.at[0], prob_ref.at[0], packed_ref.at[0]
        per_block = 128 // head_size
        for head in range(heads):
            context, start = by_head(context_ref[...], head, head_size)
            query, _ = by_head(query_ref[...], head, head_size)
            key, _ = by_head(packed_ref[:, :proj], head, head_size)
            weights = prob_ref[head]
            wide = weights.astype(F32)
            upstream = dot_last(context, packed_ref[:, proj + start : proj + start + 128])
            inner = jnp.sum(wide * upstream, axis=1, keepdims=True)
            grad = (wide * (upstream - inner)).astype(BF16)
            score_ref[head] = grad
            query_part = jnp.dot(grad, key, preferred_element_type=F32)
            key_part = jnp.dot(grad.T, query, preferred_element_type=F32)
            value_part = jnp.dot(weights.T, context, preferred_element_type=F32)
            if head % per_block == 0:
                totals = [query_part, key_part, value_part]
            else:
                totals = [
                    total + part
                    for total, part in zip(totals, (query_part, key_part, value_part))
                ]
            if head % per_block == per_block - 1:
                dq_ref[:, start : start + 128] = totals[0].astype(BF16)
                sums[:, start : start + 128] = totals[1].astype(BF16)
                sums[:, proj + start : proj + start + 128] = totals[2].astype(BF16)
        for index in range(shards):
            slots = key_ref[index * local : (index + 1) * local]
            pick = (lax.broadcasted_iota(jnp.int32, (local, group), 1) == slots).astype(BF16)
            part_ref[index] = jnp.dot(pick, sums[...], preferred_element_type=F32).astype(BF16)

    by_scores = pl.BlockSpec((1, heads, local, group), lambda i: (i, 0, 0, 0))
    by_proj = pl.BlockSpec((local, proj), lambda i: (i, 0))
    return pl.pallas_call(
        kernel,
        grid=(micro_count,),
        in_specs=[
            by_proj,
            by_proj,
            by_scores,
            pl.BlockSpec((1, group, double), lambda i: (i, 0, 0)),
            pl.BlockSpec((group, 1), lambda i: (i, 0)),
        ],
        out_specs=[
            by_scores,
            by_proj,
            pl.BlockSpec((shards, local, double), lambda i: (0, i, 0)),
        ],
        out_shape=[
            jax.ShapeDtypeStruct(probs.shape, BF16),
            jax.ShapeDtypeStruct(queries.shape, BF16),
            jax.ShapeDtypeStruct((shards, queries.shape[0], double), BF16),
        ],
        scratch_shapes=[pltpu.VMEM((group, double), BF16)],
        cost_estimate=LIGHT,
    )(queries, context_grad, probs, packed, key_slots)


def axis_ranks():
    return lax.axis_index("shard"), lax.axis_index("rep") // 2


def gelu_parts(value):
    inner = math.sqrt(2.0 / math.pi)
    square = value * value
    bend = jnp.tanh(inner * value * (1.0 + 0.044715 * square))
    outside = 0.5 * (1.0 + bend)
    slope = outside + 0.5 * value * (1.0 - bend * bend) * (inner * (1.0 + 0.134145 * square))
    return value * outside, slope


def run_copies(copies, sems):
    started = [pltpu.make_async_copy(src, dst, sems.at[i]) for i, (src, dst) in enumerate(copies)]
    for copy in started:
        copy.start()
    return started


def pick_kernel(gate_ref, up_ref, out_ref):
    core = lax.axis_index("rep") % 2
    inner = gate_ref.shape[1]
    shards = lax.axis_size("shard")
    unit = inner // shards
    half = unit // 2
    for index, ref in enumerate((gate_ref, up_ref)):
        parts = []
        for shard in range(shards):
            low = ref[:, shard * unit : shard * unit + half]
            high = ref[:, shard * unit + half : (shard + 1) * unit]
            parts.append(jnp.where(core == 0, low, high))
        out_ref[:, index * (inner // 2) : (index + 1) * (inner // 2)] = jnp.concatenate(parts, 1)


def pick_columns(w_gate, w_up):
    return pl.pallas_call(
        pick_kernel,
        in_specs=[VMEM, VMEM],
        out_specs=VMEM,
        out_shape=jax.ShapeDtypeStruct(w_gate.shape, BF16),
    )(w_gate, w_up)


def spread_kernel(low_ref, high_ref, gate_ref, up_ref):
    inner = gate_ref.shape[1]
    shards = lax.axis_size("shard")
    half = inner // shards // 2
    for index, ref in enumerate((gate_ref, up_ref)):
        parts = []
        for shard in range(shards):
            start = index * (inner // 2) + shard * half
            parts += [low_ref[:, start : start + half], high_ref[:, start : start + half]]
        ref[...] = jnp.concatenate(parts, 1).astype(F32)


def spread_columns(low, high):
    shape = jax.ShapeDtypeStruct(low.shape, F32)
    return pl.pallas_call(
        spread_kernel,
        in_specs=[VMEM, VMEM],
        out_specs=[VMEM, VMEM],
        out_shape=[shape, shape],
    )(low, high)


def project_call(tokens, gain, pieces, places, block, proj):
    rows, width = tokens.shape
    count = len(pieces)
    moves = 2 * sum(len(place) for place in places)

    def kernel(token_ref, gain_ref, *rest):
        piece_refs = rest[:count]
        normed_ref, query_ref, pair_ref, keep_ref, weights, sems = rest[count:]
        rank, rep = lax.axis_index("shard"), lax.axis_index("rep")
        copies = []
        for ref, place in zip(piece_refs, places):
            for index, where in place:
                source = ref if index is None else ref.at[index]
                for start, size, matrix, row in where(rank, rep):
                    copies.append(
                        (source.at[pl.ds(start, size)], weights.at[matrix, pl.ds(row, size)])
                    )
        copies = run_copies(copies, sems)
        hidden = token_ref[...].astype(F32)
        scale = lax.rsqrt(jnp.mean(hidden * hidden, axis=1, keepdims=True) + EPSILON)
        normed = (hidden * scale * gain_ref[...]).astype(BF16)
        normed_ref[...] = normed
        for copy in copies:
            copy.wait()
        keep = pltpu.make_async_copy(weights, keep_ref, sems.at[moves])
        keep.start()
        query_ref[...] = jnp.dot(normed, weights[0], preferred_element_type=F32).astype(BF16)
        pair_ref[:, :proj] = jnp.dot(normed, weights[1], preferred_element_type=F32).astype(BF16)
        pair_ref[:, proj:] = jnp.dot(normed, weights[2], preferred_element_type=F32).astype(BF16)
        keep.wait()

    return pl.pallas_call(
        kernel,
        in_specs=[VMEM, VMEM] + [ANY] * count,
        out_specs=[VMEM, VMEM, VMEM, ANY],
        out_shape=[
            jax.ShapeDtypeStruct((rows, width), BF16),
            jax.ShapeDtypeStruct((rows, proj), BF16),
            jax.ShapeDtypeStruct((rows, 2 * proj), BF16),
            jax.ShapeDtypeStruct((4, width, proj), BF16),
        ],
        scratch_shapes=[
            pltpu.VMEM((4, width, proj), BF16),
            pltpu.SemaphoreType.DMA((moves + 1,)),
        ],
        cost_estimate=LIGHT,
    )(tokens, gain, *pieces)


def project_grad_call(normed, query_grad, pair_grad, out_grads, small, outputs):
    rows, width = normed.shape
    proj = query_grad.shape[1]
    count = len(outputs)
    moves = sum(len(items) for _, items in outputs)

    small_rows = small.shape[1]

    def kernel(normed_ref, query_ref, pair_ref, out_grad_ref, small_ref, *rest):
        out_refs, result, sems = rest[:count], rest[count], rest[count + 1]
        fourth = pltpu.make_async_copy(out_grad_ref, result.at[3], sems.at[2 * moves])
        fourth.start()
        for begin in range(0, width, 256):
            size = min(256, width - begin)
            turned = normed_ref[:, begin : begin + size].T
            for index in range(3):
                right = query_ref[...] if index == 0 else pair_ref[:, (index - 1) * proj : index * proj]
                result[index, begin : begin + size] = jnp.dot(
                    turned, right, preferred_element_type=F32
                ).astype(BF16)
        fourth.wait()
        rank, rep = lax.axis_index("shard"), lax.axis_index("rep")
        copies = []
        for ref, (shape, items) in zip(out_refs, outputs):
            for index, where, step in items:
                matrix, row = where(rank, rep)
                size = shape[-2] - (small_rows if step is not None else 0)
                copies.append((result.at[matrix, pl.ds(row, size)], ref.at[index + (pl.ds(0, size),)]))
                if step is not None:
                    copies.append(
                        (
                            small_ref.at[step],
                            ref.at[index + (pl.ds(size, small_rows),)],
                        )
                    )
        for copy in run_copies(copies, sems):
            copy.wait()

    return pl.pallas_call(
        kernel,
        in_specs=[VMEM, VMEM, VMEM, ANY, VMEM],
        out_specs=[ANY] * count,
        out_shape=[jax.ShapeDtypeStruct(shape, BF16) for shape, _ in outputs],
        scratch_shapes=[
            pltpu.VMEM((4, width, proj), BF16),
            pltpu.SemaphoreType.DMA((2 * moves + 1,)),
        ],
        cost_estimate=LIGHT,
    )(normed, query_grad, pair_grad, out_grads, small)


def part_of(ref, row, count, columns):
    if (row, count, columns) == (0,) + ref.shape:
        return ref
    return ref.at[pl.ds(row, count), pl.ds(0, columns)]


def gate_up_call(own, other, width, inner, pieces, moves):
    rows, wide = own.shape
    count, steps = len(pieces), len(moves)
    half = inner // 2
    tile = 256

    def kernel(own_ref, other_ref, *rest):
        piece_refs = rest[:count]
        out_refs, keep_ref = rest[count : count + 3], rest[count + 3]
        both, weights, slopes, acts, hiddens, sems = rest[count + 4 :]
        results = (slopes, acts, hiddens)
        rank, chip = axis_ranks()
        copies = [(own_ref, both.at[:rows]), (other_ref, both.at[rows:])]
        for piece, row, size, columns, place in moves:
            to_row, to_column = place(rank, chip)
            copies.append(
                (
                    part_of(piece_refs[piece], row, size, columns),
                    weights.at[pl.ds(to_row, size), pl.ds(to_column, columns)],
                )
            )
        for copy in run_copies(copies, sems):
            copy.wait()
        keep = pltpu.make_async_copy(weights, keep_ref, sems.at[steps + 2])
        keep.start()

        def step(index, carry):
            start = pl.multiple_of(index * tile, tile)
            left = both[:, :width]
            gate = jnp.dot(left, weights[:, pl.ds(start, tile)], preferred_element_type=F32)
            up = jnp.dot(
                left,
                weights[:, pl.ds(pl.multiple_of(half + start, tile), tile)],
                preferred_element_type=F32,
            )
            act, slope = gelu_parts(gate)
            columns = pl.ds(start, tile)
            for number, value in enumerate((up * slope, act, act * up)):
                results[number][:, columns] = value.astype(BF16)
                pltpu.make_async_copy(
                    results[number].at[:, columns],
                    out_refs[number].at[:, columns],
                    sems.at[steps + 3 + number],
                ).start()
            return carry

        lax.fori_loop(0, half // tile, step, 0)
        keep.wait()
        for number in range(3):
            pltpu.make_async_copy(
                results[number], out_refs[number], sems.at[steps + 3 + number]
            ).wait()

    shape = jax.ShapeDtypeStruct((2 * rows, half), BF16)
    return pl.pallas_call(
        kernel,
        in_specs=[ANY] * (2 + count),
        out_specs=[ANY] * 4,
        out_shape=[shape, shape, shape, jax.ShapeDtypeStruct((width, inner), BF16)],
        scratch_shapes=[
            pltpu.VMEM((2 * rows, wide), BF16),
            pltpu.VMEM((width, inner), BF16),
        ]
        + [pltpu.VMEM((2 * rows, half), BF16)] * 3
        + [
            pltpu.SemaphoreType.DMA((steps + 6,)),
        ],
        cost_estimate=LIGHT,
    )(own, other, *pieces)


def col_tiles(width):
    return [(start, min(512, width - start)) for start in range(0, width, 512)]


def down_call(hidden, width, padded, pieces, moves):
    double, half = hidden.shape
    rows = double // 2
    count, steps = len(pieces), len(moves)

    def kernel(hidden_ref, *rest):
        piece_refs = rest[:count]
        own_ref, other_ref, keep_ref, weights, sems = rest[count:]
        rank, chip = axis_ranks()
        copies = []
        for piece, row, size, columns, place in moves:
            to_row, to_column = place(rank, chip)
            copies.append(
                (
                    part_of(piece_refs[piece], row, size, columns),
                    weights.at[pl.ds(to_row, size), pl.ds(to_column, columns)],
                )
            )
        for copy in run_copies(copies, sems):
            copy.wait()
        keep = pltpu.make_async_copy(weights, keep_ref, sems.at[steps])
        keep.start()
        for start, size in col_tiles(width):
            columns = slice(start, start + size)
            own_ref[:, columns] = jnp.dot(
                hidden_ref[:rows], weights[:, columns], preferred_element_type=F32
            )
            other_ref[:, columns] = jnp.dot(
                hidden_ref[rows:], weights[:, columns], preferred_element_type=F32
            ).astype(BF16)
        if padded > width:
            other_ref[:, width:] = jnp.zeros((rows, padded - width), BF16)
        keep.wait()

    return pl.pallas_call(
        kernel,
        in_specs=[VMEM] + [ANY] * count,
        out_specs=[VMEM, VMEM, ANY],
        out_shape=[
            jax.ShapeDtypeStruct((rows, width), F32),
            jax.ShapeDtypeStruct((rows, padded), BF16),
            jax.ShapeDtypeStruct((half, padded), BF16),
        ],
        scratch_shapes=[pltpu.VMEM((half, padded), BF16), pltpu.SemaphoreType.DMA((steps + 1,))],
        cost_estimate=LIGHT,
    )(hidden, *pieces)


def finish_call(pieces, gate_up_moves, down_moves, block, inner, down_rows, width, padded):
    count = len(pieces)
    steps = len(gate_up_moves) + len(down_moves)

    def kernel(*refs):
        piece_refs = refs[:count]
        out_refs = refs[count : count + 3]
        columns_of, rows_of, gate_ref, up_ref, down_ref, sems = refs[count + 3 :]
        chip, core = axis_ranks()[1], lax.axis_index("rep") % 2
        shards = lax.axis_size("shard")
        copies = []
        for piece, row, size, columns, place in gate_up_moves:
            to_core, to_row, to_column = place(core, chip)
            copies.append(
                (
                    part_of(piece_refs[piece], row, size, columns),
                    columns_of.at[to_core, pl.ds(to_row, size), pl.ds(to_column, columns)],
                )
            )
        for piece, row, size, columns, place in down_moves:
            to_row, to_column = place(core, chip)
            copies.append(
                (
                    part_of(piece_refs[piece], row, size, columns),
                    rows_of.at[pl.ds(to_row, size), pl.ds(to_column, columns)],
                )
            )
        copies = run_copies(copies, sems)
        for copy in copies[: len(gate_up_moves)]:
            copy.wait()
        half = inner // shards // 2
        outs = [
            pltpu.make_async_copy(ref, out, sems.at[steps + number])
            for number, (ref, out) in enumerate(zip((gate_ref, up_ref, down_ref), out_refs))
        ]
        for index, ref in enumerate((gate_ref, up_ref)):
            for shard in range(shards):
                start = index * (inner // 2) + shard * half
                both = [columns_of[at, :, start : start + half] for at in range(2)]
                ref[:, 2 * half * shard : 2 * half * (shard + 1)] = jnp.concatenate(
                    both, 1
                ).astype(F32)
            outs[index].start()
        for copy in copies[len(gate_up_moves) :]:
            copy.wait()
        down_ref[...] = rows_of[...].T[:width].astype(F32)
        outs[2].start()
        for copy in outs:
            copy.wait()

    return pl.pallas_call(
        kernel,
        in_specs=[ANY] * count,
        out_specs=[ANY] * 3,
        out_shape=[
            jax.ShapeDtypeStruct((block, inner), F32),
            jax.ShapeDtypeStruct((block, inner), F32),
            jax.ShapeDtypeStruct((width, down_rows), F32),
        ],
        scratch_shapes=[
            pltpu.VMEM((2, block, inner), BF16),
            pltpu.VMEM((down_rows, padded), BF16),
            pltpu.VMEM((block, inner), F32),
            pltpu.VMEM((block, inner), F32),
            pltpu.VMEM((width, down_rows), F32),
            pltpu.SemaphoreType.DMA((steps + 3,)),
        ],
    )(*pieces)


def attn_finish_call(pieces, moves, block, proj):
    count = len(pieces)

    def kernel(*refs):
        piece_refs = refs[:count]
        out_refs, whole, sems = refs[count : count + 4], refs[count + 4], refs[count + 5]
        rep = lax.axis_index("rep")
        copies = []
        for piece, index, place in moves:
            for start, size, matrix, row in place(rep):
                copies.append(
                    (
                        piece_refs[piece].at[index, pl.ds(start, size)],
                        whole.at[matrix, pl.ds(row, size)],
                    )
                )
        for copy in run_copies(copies, sems):
            copy.wait()
        for index, ref in enumerate(out_refs):
            ref[...] = whole[index].astype(F32)

    return pl.pallas_call(
        kernel,
        in_specs=[ANY] * count,
        out_specs=[VMEM] * 4,
        out_shape=[jax.ShapeDtypeStruct((block, proj), F32)] * 4,
        scratch_shapes=[
            pltpu.VMEM((4, block, proj), BF16),
            pltpu.SemaphoreType.DMA((2 * len(moves),)),
        ],
    )(*pieces)


def hidden_grad_call(own, other, down, slope, act):
    rows, width = own.shape
    half = down.shape[0]
    tile = 256

    def kernel(own_ref, other_ref, down_ref, slope_ref, act_ref, gate_ref, up_ref):
        for index, ref in enumerate((own_ref, other_ref)):
            part = slice(index * rows, (index + 1) * rows)
            upstream = dot_last(ref[...], down_ref[...])
            gate_ref[part] = (upstream * slope_ref[part].astype(F32)).astype(BF16)
            up_ref[part] = (upstream * act_ref[part].astype(F32)).astype(BF16)

    whole = pl.BlockSpec((rows, width), lambda i: (0, 0))
    columns = pl.BlockSpec((2 * rows, tile), lambda i: (0, i))
    shape = jax.ShapeDtypeStruct((2 * rows, half), BF16)
    return pl.pallas_call(
        kernel,
        grid=(half // tile,),
        in_specs=[
            whole,
            whole,
            pl.BlockSpec((tile, down.shape[1]), lambda i: (i, 0)),
            columns,
            columns,
        ],
        out_specs=[columns, columns],
        out_shape=[shape, shape],
        cost_estimate=LIGHT,
    )(own, other, down, slope, act)


def normed_grad_call(gate, up, weights):
    double, half = gate.shape
    rows = double // 2
    width = weights.shape[0]
    tile = 256

    def kernel(gate_ref, up_ref, low_ref, high_ref, own_ref, other_ref):
        for index, ref in enumerate((own_ref, other_ref)):
            part = slice(index * rows, (index + 1) * rows)
            total = dot_last(gate_ref[part], low_ref[...]) + dot_last(up_ref[part], high_ref[...])
            ref[...] = total.astype(ref.dtype)

    whole = pl.BlockSpec((double, half), lambda i: (0, 0))
    return pl.pallas_call(
        kernel,
        grid=(pl.cdiv(width, tile),),
        in_specs=[
            whole,
            whole,
            pl.BlockSpec((tile, half), lambda i: (i, 0)),
            pl.BlockSpec((tile, half), lambda i: (i, 1)),
        ],
        out_specs=[pl.BlockSpec((rows, tile), lambda i: (0, i))] * 2,
        out_shape=[
            jax.ShapeDtypeStruct((rows, width), F32),
            jax.ShapeDtypeStruct((rows, lane_tiles(width)), BF16),
        ],
        cost_estimate=LIGHT,
    )(gate, up, weights, weights)


def row_specs(micro_count, local, width):
    return pl.BlockSpec((local, width), lambda i: (i, 0)), pl.BlockSpec((1, width), lambda i: (0, 0))


def sum_rows(ref, value):
    total = jnp.sum(value, axis=0, keepdims=True)

    @pl.when(pl.program_id(0) == 0)
    def _():
        ref[...] = total

    @pl.when(pl.program_id(0) > 0)
    def _():
        ref[...] += total


def put_padded(ref, value):
    width = value.shape[1]
    ref[:, :width] = value.astype(BF16)
    if ref.shape[1] > width:
        ref[:, width:] = jnp.zeros((value.shape[0], ref.shape[1] - width), BF16)


def lane_tiles(width):
    return -(-width // 128) * 128


def mid_call(tokens, context, w_out, gain, micro_count):
    rows, width = tokens.shape
    local = rows // micro_count
    by_row, vector = row_specs(micro_count, local, width)

    def kernel(token_ref, context_ref, out_ref, gain_ref, hidden_ref, normed_ref):
        hidden = token_ref[...].astype(F32) + jnp.dot(
            context_ref[...], out_ref[...], preferred_element_type=F32
        )
        hidden_ref[...] = hidden
        put_padded(normed_ref, hidden * rms_scale(hidden) * gain_ref[...])

    return pl.pallas_call(
        kernel,
        grid=(micro_count,),
        in_specs=[
            by_row,
            pl.BlockSpec((local, context.shape[1]), lambda i: (i, 0)),
            pl.BlockSpec(w_out.shape, lambda i: (0, 0)),
            vector,
        ],
        out_specs=[by_row, pl.BlockSpec((local, lane_tiles(width)), lambda i: (i, 0))],
        out_shape=[
            jax.ShapeDtypeStruct((rows, width), F32),
            jax.ShapeDtypeStruct((rows, lane_tiles(width)), BF16),
        ],
        cost_estimate=LIGHT,
    )(tokens, context, w_out, gain)


def out_call(hidden, part, given, cotangent, gate_cotangent, gain, vector_in, micro_count):
    rows, width = hidden.shape
    local = rows // micro_count
    by_row, vector = row_specs(micro_count, local, width)
    one = pl.BlockSpec((local, 1), lambda i: (i, 0))
    turned = pl.BlockSpec((1, width, local), lambda i: (i, 0, 0))
    padded = pl.BlockSpec((local, lane_tiles(width)), lambda i: (i, 0))

    def kernel(
        hidden_ref, part_ref, given_ref, up_ref, gate_ref, gain_ref, vector_ref,
        state_ref, deleted_ref, grad_ref, low_ref, gain_grad_ref, vector_grad_ref,
    ):
        state = hidden_ref[...] + part_ref[...] + given_ref[:, :width].astype(F32)
        state_ref[0] = state.T
        scale = rms_scale(state)
        normed = state * scale * gain_ref[...]
        logit = jnp.sum(normed * vector_ref[...], axis=1, keepdims=True)
        sigmoid = lax.logistic(logit)
        deleted_ref[...] = -30.0 * sigmoid
        slope = gate_ref[...] * -30.0 * sigmoid * (1.0 - sigmoid)
        upstream = slope * vector_ref[...]
        sum_rows(vector_grad_ref, slope * normed)
        sum_rows(gain_grad_ref, upstream * state * scale)
        grad = up_ref[...].astype(F32) + rms_back(state, scale, gain_ref[...], upstream)
        grad_ref[...] = grad
        put_padded(low_ref, grad)

    return pl.pallas_call(
        kernel,
        grid=(micro_count,),
        in_specs=[by_row, by_row, padded, by_row, one, vector, vector],
        out_specs=[turned, one, by_row, padded, vector, vector],
        out_shape=[
            jax.ShapeDtypeStruct((micro_count, width, local), F32),
            jax.ShapeDtypeStruct((rows, 1), F32),
            jax.ShapeDtypeStruct((rows, width), F32),
            jax.ShapeDtypeStruct((rows, lane_tiles(width)), BF16),
            jax.ShapeDtypeStruct((1, width), F32),
            jax.ShapeDtypeStruct((1, width), F32),
        ],
        cost_estimate=LIGHT,
    )(hidden, part, given, cotangent, gate_cotangent, gain, vector_in)


def back_call(part, given, grad_out, hidden, gain, context, w_out, micro_count):
    rows, width = hidden.shape
    local = rows // micro_count
    proj = context.shape[1]
    by_row, vector = row_specs(micro_count, local, width)
    by_proj = pl.BlockSpec((local, proj), lambda i: (i, 0))
    padded = pl.BlockSpec((local, lane_tiles(width)), lambda i: (i, 0))
    whole = pl.BlockSpec((proj, width), lambda i: (0, 0))

    def kernel(
        part_ref, given_ref, grad_ref, hidden_ref, gain_ref, context_ref, out_ref,
        mid_ref, context_grad_ref, out_grad_ref, gain_grad_ref, total,
    ):
        normed_grad = part_ref[...] + given_ref[:, :width].astype(F32)
        hidden = hidden_ref[...]
        scale = rms_scale(hidden)
        sum_rows(gain_grad_ref, normed_grad * hidden * scale)
        mid = grad_ref[...] + rms_back(hidden, scale, gain_ref[...], normed_grad)
        mid_ref[...] = mid
        low = mid.astype(BF16)
        context_grad_ref[...] = dot_last(low, out_ref[...]).astype(BF16)
        product = jnp.dot(context_ref[...].T, low, preferred_element_type=F32)
        step = pl.program_id(0)

        @pl.when(step == 0)
        def _():
            total[...] = product

        @pl.when(step > 0)
        def _():
            total[...] += product

        @pl.when(step == micro_count - 1)
        def _():
            out_grad_ref[...] = total[...].astype(BF16)

    return pl.pallas_call(
        kernel,
        grid=(micro_count,),
        in_specs=[by_row, padded, by_row, by_row, vector, by_proj, whole],
        out_specs=[by_row, by_proj, whole, vector],
        out_shape=[
            jax.ShapeDtypeStruct((rows, width), F32),
            jax.ShapeDtypeStruct((rows, proj), BF16),
            jax.ShapeDtypeStruct((proj, width), BF16),
            jax.ShapeDtypeStruct((1, width), F32),
        ],
        scratch_shapes=[pltpu.VMEM((proj, width), F32)],
        cost_estimate=LIGHT,
    )(part, given, grad_out, hidden, gain, context, w_out)


def in_call(query_grad, pair_parts, weights, grad_mid, tokens, gain, micro_count):
    rows, width = tokens.shape
    local = rows // micro_count
    proj = query_grad.shape[1]
    count = pair_parts.shape[0]
    by_row, vector = row_specs(micro_count, local, width)
    by_proj = pl.BlockSpec((local, proj), lambda i: (i, 0))
    by_pair = pl.BlockSpec((local, 2 * proj), lambda i: (i, 0))

    def kernel(
        query_ref, part_ref, wq_ref, wk_ref, wv_ref, mid_ref, token_ref, gain_ref,
        pair_ref, grad_ref, gain_grad_ref,
    ):
        pair = sum(part_ref[index].astype(F32) for index in range(count)).astype(BF16)
        pair_ref[...] = pair
        normed_grad = (
            dot_last(query_ref[...], wq_ref[0])
            + dot_last(pair[:, :proj], wk_ref[0])
            + dot_last(pair[:, proj:], wv_ref[0])
        )
        hidden = token_ref[...].astype(F32)
        scale = rms_scale(hidden)
        sum_rows(gain_grad_ref, normed_grad * hidden * scale)
        grad = mid_ref[...] + rms_back(hidden, scale, gain_ref[...], normed_grad)
        grad_ref[0] = grad.astype(BF16).T

    return pl.pallas_call(
        kernel,
        grid=(micro_count,),
        in_specs=[by_proj, pl.BlockSpec((count, local, 2 * proj), lambda i: (0, i, 0))]
        + [pl.BlockSpec((1, width, proj), lambda i, m=m: (m, 0, 0)) for m in range(3)]
        + [by_row, by_row, vector],
        out_specs=[by_pair, pl.BlockSpec((1, width, local), lambda i: (i, 0, 0)), vector],
        out_shape=[
            jax.ShapeDtypeStruct((rows, 2 * proj), BF16),
            jax.ShapeDtypeStruct((micro_count, width, local), BF16),
            jax.ShapeDtypeStruct((1, width), F32),
        ],
        cost_estimate=LIGHT,
    )(query_grad, pair_parts, weights, weights, weights, grad_mid, tokens, gain)


def weight_grad_call(left, right, picks, width, outputs, in_halves):
    left_own, left_other = left
    right_own, right_other = right
    rows = left_own.shape[0]
    total = 2 * rows if left_other is not None else rows
    beside = right_other is not None and right_own.shape[0] == total
    right_width = right_own.shape[1] * (2 if beside else 1)
    count = len(outputs)
    copies_out = sum(len(moves) for _, moves, _ in outputs)
    depth = sum(size for _, size in picks)
    tile = 256
    split = left_other is not None
    right_split = right_other is not None
    inputs = [left_own] + ([left_other] if split else []) + [right_own]
    inputs += [right_other] if right_split else []

    def kernel(*refs):
        in_refs = list(refs[: len(inputs)])
        out_refs = refs[len(inputs) : len(inputs) + count]
        lefts, turned, rights, result, sems = refs[len(inputs) + count :]
        copies = []
        for target, parted, aside in ((lefts, split, False), (rights, right_split, beside)):
            first = in_refs.pop(0)
            size = first.shape[1] if aside else first.shape[0]
            if not parted:
                copies.append((first, target))
            elif aside:
                copies.append((first, target.at[:, :size]))
                copies.append((in_refs.pop(0), target.at[:, size:]))
            else:
                copies.append((first, target.at[:size]))
                copies.append((in_refs.pop(0), target.at[size:]))
        for copy in run_copies(copies, sems):
            copy.wait()
        to_row = 0
        for first, size in picks:
            for begin in range(0, size, tile):
                span = min(tile, size - begin)
                turned[to_row : to_row + span] = lefts[:, first + begin : first + begin + span].T
                to_row += span

        def product(start, size):
            result[:, pl.ds(start, size)] = jnp.dot(
                turned[...], rights[:, pl.ds(start, size)], preferred_element_type=F32
            ).astype(BF16)

        rank, chip = axis_ranks()
        started = []
        for half in range(2 if in_halves else 1):
            first = (chip // 2 ^ (1 - half)) * (width // 2) if in_halves else 0
            tiles = (width // 2 if in_halves else width) // tile

            def step(index, carry, first=first):
                product(pl.multiple_of(first + index * tile, tile), tile)
                return carry

            lax.fori_loop(0, tiles, step, 0)
            if not in_halves and width % tile:
                product(tiles * tile, width % tile)
            for ref, (shape, moves, mask) in zip(out_refs, outputs):
                if in_halves and mask & 2 == 2 * half:
                    continue
                for index, place in moves:
                    row, column = place(rank, chip)
                    copy = pltpu.make_async_copy(
                        result.at[pl.ds(row, shape[1]), pl.ds(column, shape[2])],
                        ref.at[index],
                        sems.at[len(started)],
                    )
                    copy.start()
                    started.append(copy)
        for copy in started:
            copy.wait()

    return pl.pallas_call(
        kernel,
        in_specs=[ANY] * len(inputs),
        out_specs=[ANY] * count,
        out_shape=[jax.ShapeDtypeStruct(shape, BF16) for shape, _, _ in outputs],
        scratch_shapes=[
            pltpu.VMEM((total, left_own.shape[1]), BF16),
            pltpu.VMEM((depth, total), BF16),
            pltpu.VMEM((total, right_width), BF16),
            pltpu.VMEM((depth, width), BF16),
            pltpu.SemaphoreType.DMA((max(4, copies_out),)),
        ],
        cost_estimate=LIGHT,
    )(*inputs)


def on_device(
    tokens,
    cotangent,
    gate_cotangent,
    slot_of,
    seq_lengths,
    buckets,
    gain_attn,
    w_query,
    w_key,
    w_value,
    w_out,
    rel_bias,
    gain_ffn,
    w_gate,
    w_up,
    w_down,
    gain_delete,
    w_delete,
):
    shards = lax.axis_size("shard")
    reps = lax.axis_size("rep")
    chips = reps // 2
    rank = lax.axis_index("shard")
    rep_rank = lax.axis_index("rep")
    core = rep_rank % 2
    chip = rep_rank // 2
    micro_count, local_rows, width = tokens.shape
    group = local_rows * shards
    rows = micro_count * local_rows
    heads = rel_bias.shape[1]
    bucket_rows = rel_bias.shape[0]
    bucket_count = bucket_rows * shards
    proj = w_query.shape[1]
    head_size = proj // heads
    block = gain_attn.shape[0]
    inner = w_gate.shape[1]
    half_inner = inner // 2
    col_piece = inner // chips
    down_block = w_down.shape[0]
    down_half = down_block // 2
    down_piece = down_half // chips
    down_parts_count = -(-width // col_piece)
    padded = -(-width // 128) * 128
    aligned = reps == 8 and block % 16 == 0 and down_piece % 16 == 0 and col_piece % 128 == 0

    def swap(value, mask):
        return lax.ppermute(value, "rep", [(i, i ^ mask) for i in range(reps)])

    def shift(value, by=1):
        return lax.ppermute(value, "shard", [(i, (i + by) % shards) for i in range(shards)])

    def tie(value, moved):
        return lax.optimization_barrier((value, moved))

    def cut(count):
        half = count // 2
        return half // 16 * 16 if half >= 16 else half

    def gather_near(piece):
        if chips == 1:
            return []
        return [swap(piece, 2)] + ([swap(piece, 4)] if chips >= 4 else [])

    def gather_rest(near):
        if chips < 4:
            return []
        middle = cut(near[0].shape[0])
        return [swap(near[1][:middle], 2), swap(near[0][middle:], 4)]

    def gather_list(piece, near, rest):
        middle = cut(piece.shape[0])
        found = [(0, 0, piece)] + [(1 + i, 0, part) for i, part in enumerate(near)]
        found += [(3, i * middle, part) for i, part in enumerate(rest)]
        bit = 4
        while bit < chips:
            found += [
                (mask ^ bit, start, swap(part, 2 * bit)) for mask, start, part in found
            ]
            bit *= 2
        return found

    def plane_gather(piece):
        near = gather_near(piece)
        return gather_list(piece, near, gather_rest(near))

    def add(*values):
        return sum(value.astype(F32) for value in values).astype(BF16)

    def plane_reduce(parts, axis):
        state = reduce_begin(parts, axis)
        return reduce_end(reduce_middle(state, axis))

    def reduce_begin(parts, axis):
        def level(base, bit):
            if bit < 4:
                return lambda name: parts[base][name]
            lower, upper = level(base, bit // 2), level(base ^ bit, bit // 2)
            return lambda name: add(lower(name), swap(upper(name), 2 * bit))

        get = level(0, chips // 2)
        if chips < 4:
            return [get("own")] + ([swap(get("near"), 2)] if chips == 2 else [])
        return [get("own"), get("far"), get("near"), swap(get("top"), 2), swap(get("low"), 4)]

    def reduce_middle(state, axis):
        if chips < 4:
            return state
        own, far, near, top, low = state
        middle = top.shape[axis]

        def pair(value):
            return (
                lax.slice_in_dim(value, 0, middle, axis=axis),
                lax.slice_in_dim(value, middle, value.shape[axis], axis=axis),
            )

        (far_top, far_low), (near_top, near_low) = pair(far), pair(near)
        far = jnp.concatenate([add(far_top, top), far_low], axis)
        near = jnp.concatenate([near_top, add(near_low, low)], axis)
        return [own, swap(far, 4), swap(near, 2)]

    def reduce_end(state):
        return add(*state) if len(state) > 1 else state[0]

    names = {"own": 0, "near": 1, "far": 2, "top": 3, "low": 3}
    bases = [base for base in range(chips) if base & 3 == 0]
    used = ["own", "near", "far", "top", "low"] if chips >= 4 else ["own", "near"][:chips]

    def source(step):
        return (rank - step) % shards

    order = (rank - jnp.arange(shards, dtype=jnp.int32)) % shards
    per_matrix = reps // 4
    attn_rows = block // per_matrix
    if aligned:
        attn_rows = -(-attn_rows // 16) * 16
    last_row = block - attn_rows

    def part_row(part):
        return jnp.minimum(part * attn_rows, last_row)

    attn_own = jnp.stack([w_query, w_key, w_value, w_out.reshape(block, proj)])
    attn_piece = lax.dynamic_slice(
        attn_own,
        (rep_rank // per_matrix, part_row(rep_rank % per_matrix), 0),
        (1, attn_rows, proj),
    )[0]
    vector_pack = jnp.concatenate(
        [gain_attn, gain_ffn, gain_delete, w_delete, rel_bias.reshape(-1)]
    )
    pack_rows = -(-vector_pack.shape[0] // (16 * proj)) * 16
    vector_pack = jnp.pad(vector_pack, (0, pack_rows * proj - vector_pack.shape[0]))
    vector_pack = vector_pack.reshape(pack_rows, proj)
    attn_sent = jnp.concatenate([attn_piece, vector_pack])
    attn_arrived = [shift(attn_sent, step) for step in range(1, shards)]
    token_rows = tokens.reshape(rows, width)
    attn_arrived, (token_rows, attn_own) = tie(attn_arrived, (token_rows, attn_own))
    vectors = jnp.stack([vector_pack] + [part[attn_rows:] for part in attn_arrived])
    vectors = jnp.take(vectors, order, axis=0).reshape(shards, pack_rows * proj)
    attn_gain = vectors[:, :block].reshape(width).astype(F32)
    ffn_gain = vectors[:, block : 2 * block].reshape(width).astype(F32)
    delete_gain = vectors[:, 2 * block : 3 * block].reshape(width).astype(F32)
    delete_vec = vectors[:, 3 * block : 4 * block].reshape(width).astype(F32)
    bias_table = vectors[:, 4 * block : 4 * block + bucket_rows * heads]
    bias_table = bias_table.reshape(bucket_count, heads)
    stacked = jnp.stack([part[:attn_rows] for part in attn_arrived])

    def pack(gate_up_part, down_part):
        wide = jnp.pad(down_part, ((0, 0), (0, down_parts_count * col_piece - width)))
        cuts = [wide[:, i * col_piece : (i + 1) * col_piece] for i in range(down_parts_count)]
        return jnp.concatenate([gate_up_part] + cuts)

    def overlaps(start, count):
        bounds = [(None, 0, block)] + [
            (i, block + i * down_piece, block + (i + 1) * down_piece)
            for i in range(down_parts_count)
        ]
        found = []
        for part, low, high in bounds:
            first, last = max(low, start), min(high, start + count)
            if first < last:
                found.append((part, first - start, first - low, last - first))
        return found

    def part_columns(part):
        return min(col_piece, padded - part * col_piece)

    gate_up_own = pick_columns(w_gate, w_up)
    down_own = lax.dynamic_slice_in_dim(w_down, core * down_half, down_half, 0)
    packed_own = pack(
        lax.dynamic_slice_in_dim(gate_up_own, chip * col_piece, col_piece, 1),
        lax.dynamic_slice_in_dim(down_own, chip * down_piece, down_piece, 0),
    )
    packed_own, stacked = tie(packed_own, stacked)
    attn_plane = [stacked] + [swap(stacked, 2 * mask) for mask in range(1, chips)]
    attn_plane = jnp.stack(attn_plane)
    ring = [packed_own, shift(packed_own)]
    attn_plane, ring = tie(attn_plane, ring)
    nears, rests = [None] * shards, [None] * shards
    nears[1] = gather_near(ring[1])
    attn_other = swap(attn_plane, 1)

    def attn_place(mask, flip, step):
        def place(at, rep):
            owner = rep ^ (2 * mask + flip)
            row = (at - step) % shards * block + part_row(owner % per_matrix)
            return owner // per_matrix, pl.multiple_of(row, 16) if aligned else row

        return place

    shared = per_matrix * attn_rows - block

    def split_place(place, flip):
        def places_of(*at):
            matrix, row = place(*at)
            part = (at[-1] ^ flip) % per_matrix
            first = row - last_row * part
            moves = [
                (
                    pl.multiple_of(shared * part, 16),
                    attn_rows - shared,
                    matrix,
                    pl.multiple_of(first + attn_rows * part, 16),
                )
            ]
            if shared and flip == 0:
                moves.append(
                    (
                        pl.multiple_of(last_row * (1 - part), 16),
                        shared,
                        matrix,
                        pl.multiple_of(first + last_row, 16),
                    )
                )
            return moves

        return places_of

    attn_pieces = [w_query, w_key, w_value, attn_own[3]]
    attn_places = [
        [(None, lambda at, rep, matrix=matrix: [(0, block, matrix, pl.multiple_of(at * block, 16))])]
        for matrix in range(4)
    ]
    for flip, found in enumerate((attn_plane, attn_other)):
        attn_pieces.append(found)
        attn_places.append(
            [
                ((mask, step - 1), attn_place(mask, flip, step), flip)
                for mask in range(chips)
                for step in range(1, shards)
            ]
        )
    if not aligned:
        whole = jnp.zeros((4, width, proj), BF16)
        whole = lax.dynamic_update_slice(whole, attn_own, (0, rank * block, 0))
        for piece, place in zip(attn_pieces[4:], attn_places[4:]):
            for index, where, _ in place:
                matrix, row = where(rank, rep_rank)
                whole = lax.dynamic_update_slice(whole, piece[index][None], (matrix, row, 0))
        attn_pieces = [whole[matrix] for matrix in range(4)]
        attn_places = [
            [(None, lambda at, rep, matrix=matrix: [(0, width, matrix, 0)])] for matrix in range(4)
        ]
    else:
        attn_places[4:] = [
            [(index, split_place(where, flip)) for index, where, flip in place]
            for place in attn_places[4:]
        ]

    slots = slot_of[:, 0]
    own_slots = lax.dynamic_slice_in_dim(slots, rank * local_rows, local_rows, 1)
    key_slots = jnp.take(slots.reshape(micro_count, shards, local_rows), order, axis=1)
    key_slots = key_slots.reshape(micro_count, group)
    onehot = (buckets[:, None] == jnp.arange(bucket_count, dtype=jnp.int32)[None, :]).astype(F32)
    onehot = jnp.pad(onehot, ((0, 1), (0, 0)))
    bias_rows = jnp.dot(onehot, bias_table.astype(F32), precision=HIGHEST).T
    bias = bias_of_queries(bias_rows, own_slots.reshape(rows), group)
    first_len = seq_lengths[:, 0, 0]

    normed_one, queries, own_pairs, attn_full = project_call(
        token_rows, attn_gain[None], attn_pieces, attn_places, block, proj
    )
    out_full = attn_full[3].reshape(proj, width)

    for step in range(2, shards - 1):
        ring.append(shift(ring[-1]))
    own_pairs, ring = tie(own_pairs, ring)
    early = (
        out_full,
        jnp.pad(down_own, ((0, 0), (0, padded - width))),
        cotangent.reshape(rows, width),
        gate_cotangent.reshape(rows, 1).astype(F32),
        [value[None] for value in (ffn_gain, delete_gain, delete_vec)],
        slots.reshape(micro_count * group, 1),
    )
    pairs = [own_pairs]
    for step in range(1, shards):
        pairs.append(shift(pairs[-1]))
        if step == 1:
            pairs[-1], (nears[1], bias) = tie(pairs[-1], (nears[1], bias))
            rests[1] = gather_rest(nears[1])
        if step == 2:
            pairs[-1], (rests[1], early) = tie(pairs[-1], (rests[1], early))
            ring[2], rests[1] = tie(ring[2], rests[1])
            nears[2] = gather_near(ring[2])
    ring[-1], pairs[-1] = tie(ring[-1], pairs[-1])
    last = shift(ring[-1][:block])
    pairs, nears[2] = tie(pairs, nears[2])
    rests[2] = gather_rest(nears[2])
    made = []
    for micro in range(micro_count):
        if micro == micro_count - 1:
            made, (rests[2], last) = tie(made, (rests[2], last))
            last_near = gather_near(last)
        made = attention_call(
            micro,
            micro_count,
            first_len[micro : micro + 1],
            queries,
            pairs,
            own_slots.reshape(rows, 1),
            key_slots[micro : micro + 1],
            bias,
            made,
        )
    context, probs, packed = made
    for step in range(3, shards - 1):
        ring[step], rests[step - 1] = tie(ring[step], rests[step - 1])
        nears[step] = gather_near(ring[step])
        rests[step] = gather_rest(nears[step])
    if shards > 4:
        context, rests[shards - 2] = tie(context, rests[shards - 2])
    last_piece, last = tie(ring[-1][block:], last)
    last_down = shift(last_piece)
    out_full, down_wide, cotangent_rows, gate_rows, gains, key_columns = early
    ffn_gain, delete_gain, delete_vec = gains

    hidden_mid, normed_two = mid_call(token_rows, context, out_full, ffn_gain, micro_count)
    normed_two, (last_near, last_down) = tie(normed_two, (last_near, last_down))
    last_rest = gather_rest(last_near)
    normed_two_other = swap(normed_two, 1)
    normed_two_other, (last_rest, last_down) = tie(normed_two_other, (last_rest, last_down))
    last_down_found = [(mask, 0, swap(last_down, 2 * mask)) for mask in range(1, chips)]
    pieces = [gate_up_own, down_wide]
    gate_up_moves = [(0, 0, block, inner, lambda at, chip_at: (pl.multiple_of(at * block, 16), 0))]
    down_moves = [
        (1, 0, down_half, padded, lambda at, chip_at: (pl.multiple_of(at * down_half, 16), 0))
    ]

    def gate_up_place(step, mask, row):
        return lambda at, chip_at: (
            pl.multiple_of((at - step) % shards * block + row, 16),
            pl.multiple_of((chip_at ^ mask) * col_piece, 128),
        )

    def down_place(step, mask, row, part):
        return lambda at, chip_at: (
            pl.multiple_of((at - step) % shards * down_half + (chip_at ^ mask) * down_piece + row, 16),
            part * col_piece,
        )

    arrived = [
        (step, 0, gather_list(ring[step], nears[step], rests[step])) for step in range(1, shards - 1)
    ]
    arrived.append((shards - 1, 0, gather_list(last, last_near, last_rest)))
    arrived.append((shards - 1, block, [(0, 0, last_down)] + last_down_found))
    for step, below, found in arrived:
        for mask, start, array in found:
            for part, here, there, size in overlaps(below + start, array.shape[0]):
                if part is None:
                    gate_up_moves.append(
                        (len(pieces), here, size, col_piece, gate_up_place(step, mask, there))
                    )
                else:
                    down_moves.append(
                        (
                            len(pieces),
                            here,
                            size,
                            part_columns(part),
                            down_place(step, mask, there, part),
                        )
                    )
            pieces.append(array)
    if not aligned:

        def put_together(moves, shape):
            whole = jnp.zeros(shape, BF16)
            for piece, row, size, columns, place in moves:
                value = pieces[piece][row : row + size, :columns]
                whole = lax.dynamic_update_slice(whole, value, place(rank, chip))
            return whole

        pieces = [
            put_together(gate_up_moves, (width, inner)),
            put_together(down_moves, (half_inner, padded)),
        ]
        gate_up_moves = [(0, 0, width, inner, lambda at, chip_at: (0, 0))]
        down_moves = [(1, 0, half_inner, padded, lambda at, chip_at: (0, 0))]
    gate_up_pieces, gate_up_moves = used_by(pieces, gate_up_moves)
    down_pieces, down_moves = used_by(pieces, down_moves)
    gate_slope_act, gate_act, inner_act, gate_up = gate_up_call(
        normed_two, normed_two_other, width, inner, gate_up_pieces, gate_up_moves
    )
    down_part, down_given, down = down_call(inner_act, width, padded, down_pieces, down_moves)
    hidden_out, deleted, grad_out, down_up, grad_delete_gain, grad_delete_vec = out_call(
        hidden_mid,
        down_part,
        swap(down_given, 1),
        cotangent_rows,
        gate_rows,
        delete_gain,
        delete_vec,
        micro_count,
    )

    down_up_other = swap(down_up, 1)

    def reduce_plan(size, piece_columns, place):
        middle = cut(size)
        spans = {"own": (0, size), "near": (0, size), "far": (0, size)}
        spans["top"], spans["low"] = (0, middle), (middle, size - middle)
        plan = []
        for base in bases:
            for name in used:
                start, count = spans[name]
                moves = [
                    (index, place(index, base ^ names[name], start)) for index in range(shards)
                ]
                plan.append(((shards, count, piece_columns), moves, base ^ names[name]))
        return plan

    def reduce_run(plan, left, right, picks, right_width, in_halves):
        if aligned:
            buffers = weight_grad_call(left, right, picks, right_width, plan, in_halves)
        else:
            shape = (sum(size for _, size in picks), right_width)
            whole = weight_grad_call(
                left, right, picks, right_width,
                [((1,) + shape, [(0, lambda at, chip_at: (0, 0))], 0)], False,
            )[0][0]
            buffers = []
            for (_, size, columns), moves, _ in plan:
                buffers.append(
                    jnp.stack(
                        [
                            lax.dynamic_slice(whole, place(rank, chip), (size, columns))
                            for _, place in moves
                        ]
                    )
                )
        return {
            base: dict(zip(used, buffers[i * len(used) : (i + 1) * len(used)]))
            for i, base in enumerate(bases)
        }

    def exchange(value):
        return lax.all_to_all(value, "shard", split_axis=0, concat_axis=0, tiled=True)

    def total_of(arrived):
        return jnp.sum(arrived.astype(F32), axis=0).astype(BF16)

    def down_grad_place(index, mask, start):
        plain = lambda at, chip_at: (
            index * down_half + (chip_at ^ mask) * down_piece + start,
            0,
        )
        return tile_hint(plain, 16, 128) if aligned else plain

    def gate_up_grads(first, size, left, right):
        def place(index, mask, start):
            plain = lambda at, chip_at: (index * size + start, (chip_at ^ mask) * col_piece)
            return tile_hint(plain, 16, 128) if aligned else plain

        return reduce_run(
            reduce_plan(size, col_piece, place),
            left,
            right,
            [(index * block + first, size) for index in range(shards)],
            inner,
            chips == 4 and half_inner % 256 == 0,
        )

    down_buffers = reduce_run(
        reduce_plan(down_piece, width, down_grad_place),
        (inner_act, None),
        (down_up, down_up_other),
        [(0, half_inner)],
        width,
        False,
    )
    down_state = reduce_begin(down_buffers, 1)
    gate_grad, up_grad = hidden_grad_call(down_up, down_up_other, down, gate_slope_act, gate_act)
    gate_grad, down_state = tie(gate_grad, down_state)
    down_state = reduce_middle(down_state, 1)
    normed_both = (normed_two, normed_two_other)
    gate_up_buffers = gate_up_grads(0, cut(block), normed_both, (gate_grad, up_grad))
    gate_grad, gate_up_buffers = tie(gate_grad, gate_up_buffers)
    normed_part, normed_given = normed_grad_call(gate_grad, up_grad, gate_up)
    normed_given, (down_state, gate_up_buffers) = tie(normed_given, (down_state, gate_up_buffers))
    gate_up_state = reduce_begin(gate_up_buffers, 1)
    down_arrived = exchange(reduce_end(down_state))
    normed_given = swap(normed_given, 1)
    grad_mid, context_grad, grad_w_out, grad_ffn_gain = back_call(
        normed_part,
        normed_given,
        grad_out,
        hidden_mid,
        ffn_gain,
        context,
        out_full,
        micro_count,
    )
    context_grad, gate_up_state = tie(context_grad, gate_up_state)
    gate_up_state = reduce_middle(gate_up_state, 1)
    score_grads, query_grad, pair_parts = attention_back_call(
        queries, context_grad, probs, packed, key_columns, shards
    )
    gate_grad, pair_parts = tie(gate_grad, pair_parts)
    pair_arrived = exchange(pair_parts)
    gate_up_buffers = gate_up_grads(
        cut(block), block - cut(block), normed_both, (gate_grad, up_grad)
    )
    gate_up_buffers, gate_up_state = tie(gate_up_buffers, gate_up_state)
    gate_up_later = reduce_begin(gate_up_buffers, 1)
    grad_bias_rows = bias_fold(score_grads, own_slots.reshape(rows))
    grad_bias = jnp.einsum("ob,ho->bh", onehot, grad_bias_rows, precision=HIGHEST)
    out_grads = grad_w_out.reshape(width, proj)
    gate_up_later, (grad_bias, out_grads) = tie(gate_up_later, (grad_bias, out_grads))
    gate_up_later = reduce_middle(gate_up_later, 1)
    pair_arrived, down_arrived = tie(pair_arrived, down_arrived)
    gate_up_arrived = exchange(reduce_end(gate_up_state))
    down_sum = total_of(down_arrived)
    pair_sum, grad_in, grad_attn_gain = in_call(
        query_grad,
        pair_arrived,
        attn_full,
        grad_mid,
        token_rows,
        attn_gain[None],
        micro_count,
    )
    pair_sum, gate_up_later = tie(pair_sum, gate_up_later)

    small = jnp.concatenate(
        [
            grad_attn_gain.reshape(shards, block),
            grad_ffn_gain.reshape(shards, block),
            grad_delete_gain.reshape(shards, block),
            grad_delete_vec.reshape(shards, block),
            grad_bias.reshape(shards, bucket_rows * heads),
        ],
        axis=1,
    ).astype(BF16)
    small = jnp.pad(small, ((0, 0), (0, pack_rows * proj - small.shape[1])))
    small = small.reshape(shards, pack_rows, proj)

    def attn_grad_place(mask, flip, index):
        def place(at, rep):
            owner = rep ^ (2 * mask + flip)
            row = index * block + part_row(owner % per_matrix)
            return owner // per_matrix, pl.multiple_of(row, 16) if aligned else row

        return place

    attn_plan = [
        (
            (chips, shards, attn_rows + pack_rows, proj),
            [
                ((mask, index), attn_grad_place(mask, flip, index), index)
                for mask in range(chips)
                for index in range(shards)
            ],
        )
        for flip in range(2)
    ]
    if aligned:
        kept, given = project_grad_call(
            normed_one, query_grad, pair_sum, out_grads, small, attn_plan
        )
    else:
        whole_plan = [
            (
                (4, width, proj),
                [((matrix,), lambda at, rep, matrix=matrix: (matrix, 0), None) for matrix in range(4)],
            )
        ]
        whole = project_grad_call(
            normed_one, query_grad, pair_sum, out_grads, small, whole_plan
        )[0]
        kept, given = [
            jnp.stack(
                [
                    jnp.concatenate(
                        [
                            lax.dynamic_slice(
                                whole, where(rank, rep_rank) + (0,), (1, attn_rows, proj)
                            )[0],
                            small[index],
                        ]
                    )
                    for _, where, index in items
                ]
            ).reshape(shape)
            for shape, items in attn_plan
        ]
    given = swap(given, 1)
    attn_own_sum = add(kept[0], given[0])
    attn_send = [add(kept[mask], given[mask]) for mask in range(1, chips)]
    attn_found = [swap(part, 2 * mask + 2) for mask, part in enumerate(attn_send)]
    gate_up_rest = exchange(reduce_end(gate_up_later))
    attn_found, gate_up_rest = tie(attn_found, gate_up_rest)
    attn_sum = add(attn_own_sum, *attn_found)
    attn_sum = total_of(exchange(attn_sum))
    gate_up_sum = jnp.concatenate([total_of(gate_up_arrived), total_of(gate_up_rest)])
    total = attn_sum[attn_rows:].astype(F32).reshape(-1)
    attn_sum = attn_sum[:attn_rows]

    packed_sum = pack(gate_up_sum, down_sum)
    near = gather_near(packed_sum)
    attn_sum, near = tie(attn_sum, near)
    rest = gather_rest(near)
    attn_half = [attn_sum] + [swap(attn_sum, 2 * mask) for mask in range(1, chips)]
    bounds = [0, block, 2 * block, 3 * block, 4 * block, 4 * block + bucket_rows * heads]
    totals = [total[low:high] for low, high in zip(bounds, bounds[1:])]
    totals[4] = totals[4].reshape(bucket_rows, heads)
    attn_half, (rest, totals) = tie(attn_half, (rest, totals))
    found = gather_list(packed_sum, near, rest)
    pieces, gate_up_moves, down_moves = [], [], []

    def gate_up_to(flip, mask, row):
        return lambda core_at, chip_at: (
            core_at ^ flip,
            row,
            pl.multiple_of((chip_at ^ mask) * col_piece, 128),
        )

    def down_to(flip, mask, row, part):
        return lambda core_at, chip_at: (
            pl.multiple_of((core_at ^ flip) * down_half + (chip_at ^ mask) * down_piece + row, 16),
            part * col_piece,
        )

    for flip in range(2):
        for mask, start, array in found:
            array = swap(array, 1) if flip else array
            for part, here, there, size in overlaps(start, array.shape[0]):
                if part is None:
                    gate_up_moves.append(
                        (len(pieces), here, size, col_piece, gate_up_to(flip, mask, there))
                    )
                else:
                    down_moves.append(
                        (
                            len(pieces),
                            here,
                            size,
                            part_columns(part),
                            down_to(flip, mask, there, part),
                        )
                    )
            pieces.append(array)
    if aligned:
        grad_gate, grad_up, grad_down_out = finish_call(
            pieces, gate_up_moves, down_moves, block, inner, down_block, width, padded
        )
        grad_down_out = grad_down_out.T
    else:
        halves = jnp.zeros((2, block, inner), BF16)
        for piece, row, size, columns, place in gate_up_moves:
            value = pieces[piece][None, row : row + size, :columns]
            halves = lax.dynamic_update_slice(halves, value, place(core, chip))
        whole = jnp.zeros((down_block, padded), BF16)
        for piece, row, size, columns, place in down_moves:
            value = pieces[piece][row : row + size, :columns]
            whole = lax.dynamic_update_slice(whole, value, place(core, chip))
        grad_gate, grad_up = spread_columns(halves[0], halves[1])
        grad_down_out = whole[:, :width].astype(F32)

    attn_half = jnp.stack(attn_half)
    attn_found = [attn_half, swap(attn_half, 1)]

    def attn_to(mask, flip):
        def place(rep):
            owner = rep ^ (2 * mask + flip)
            row = part_row(owner % per_matrix)
            return owner // per_matrix, pl.multiple_of(row, 16) if aligned else row

        return place

    attn_moves = [(flip, mask, attn_to(mask, flip)) for flip in range(2) for mask in range(chips)]
    if aligned:
        attn_moves = [
            (flip, mask, split_place(place, flip)) for flip, mask, place in attn_moves
        ]
        attn_shard = attn_finish_call(attn_found, attn_moves, block, proj)
    else:
        attn_shard = jnp.zeros((4, block, proj), BF16)
        for piece, index, place in attn_moves:
            attn_shard = lax.dynamic_update_slice(
                attn_shard, attn_found[piece][index][None], place(rep_rank) + (0,)
            )
        attn_shard = attn_shard.astype(F32)

    return (
        jnp.swapaxes(hidden_out, 1, 2),
        deleted.reshape(micro_count, local_rows),
        jnp.swapaxes(grad_in, 1, 2),
        totals[0],
        attn_shard[0],
        attn_shard[1],
        attn_shard[2],
        attn_shard[3].reshape(proj // shards, width),
        totals[4],
        totals[1],
        grad_gate,
        grad_up,
        grad_down_out,
        totals[2],
        totals[3],
    )


def used_by(pieces, moves):
    wanted = sorted({move[0] for move in moves})
    return [pieces[i] for i in wanted], [(wanted.index(move[0]),) + move[1:] for move in moves]


def tile_hint(place, row_unit, column_unit):
    def hinted(at, chip_at):
        row, column = place(at, chip_at)
        return pl.multiple_of(row, row_unit), pl.multiple_of(column, column_unit)

    return hinted


def solution(mesh):
    rows = P(None, ("rep", "shard"), None)
    flat = P(None, ("rep", "shard"))
    by_rep = P(None, "rep", None)
    vector = P("shard")
    matrix = P("shard", None)
    in_specs = (
        (rows, rows, flat, by_rep, by_rep, P(), vector)
        + (matrix,) * 5
        + (vector,)
        + (matrix,) * 3
        + (vector, vector)
    )
    out_specs = (
        (rows, flat, rows, vector) + (matrix,) * 5 + (vector,) + (matrix,) * 3 + (vector, vector)
    )
    return jax.shard_map(
        on_device, mesh=mesh, in_specs=in_specs, out_specs=out_specs, check_vma=False
    )
```

```python
import functools

import math

import jax
import jax.numpy as jnp
from jax import lax
from jax.experimental import pallas as pl
from jax.experimental.pallas import tpu as pltpu
from jax.sharding import PartitionSpec as P

EPSILON = 1e-06
HIGHEST = lax.Precision.HIGHEST
MASKED = -1000000000.0
BF16 = jnp.bfloat16
LIGHT = pl.CostEstimate(flops=1000, bytes_accessed=1000, transcendentals=0)
F32 = jnp.float32


ANY = pl.BlockSpec(memory_space=pl.ANY)
VMEM = pl.BlockSpec(memory_space=pltpu.VMEM)


def rms_scale(hidden):
    return lax.rsqrt(jnp.mean(hidden * hidden, axis=-1, keepdims=True) + EPSILON)


def rms_back(hidden, scale_row, gain, upstream):
    scaled = upstream * gain
    return scale_row * scaled - hidden * (scale_row * scale_row * scale_row) * jnp.mean(
        hidden * scaled, axis=-1, keepdims=True
    )


def bias_kernel(rows_ref, slots_ref, out_ref):
    group = out_ref.shape[2]
    row = jnp.broadcast_to(rows_ref[0], (group, rows_ref.shape[2]))
    grid = pltpu.roll(row, group + 1, 1, stride=1, stride_axis=0)[:, :group].astype(BF16)
    tokens = slots_ref.shape[0]
    pick = (slots_ref[...] == lax.broadcasted_iota(jnp.int32, (tokens, group), 1)).astype(BF16)
    out_ref[0] = jnp.dot(pick, grid, preferred_element_type=F32).astype(BF16)


def bias_of_queries(bias_rows, slots, group):
    heads, width = bias_rows.shape
    tokens = slots.shape[0]
    return pl.pallas_call(
        bias_kernel,
        grid=(heads,),
        in_specs=[
            pl.BlockSpec((1, 1, width), lambda h: (h, 0, 0)),
            pl.BlockSpec((tokens, 1), lambda h: (0, 0)),
        ],
        out_specs=pl.BlockSpec((1, tokens, group), lambda h: (h, 0, 0)),
        out_shape=jax.ShapeDtypeStruct((heads, tokens, group), BF16),
    )(bias_rows.reshape(heads, 1, width), slots.reshape(tokens, 1))


def bias_fold(score_grads, slots):
    count, heads, local, group = score_grads.shape

    def kernel(*refs):
        grad_refs, slots_ref, out_ref = refs[:count], refs[count], refs[count + 1]
        square = None
        for index, ref in enumerate(grad_refs):
            mine = slots_ref[:, index * local : (index + 1) * local]
            row = lax.broadcasted_iota(jnp.int32, (group, local), 0)
            place = (row == (group - 1) - mine).astype(BF16)
            part = jnp.dot(place, ref[0, 0], preferred_element_type=F32)
            square = part if square is None else square + part
        wide = jnp.concatenate([square, jnp.zeros_like(square)], axis=1)
        rolled = pltpu.roll(wide, 0, 1, stride=1, stride_axis=0)
        out_ref[0] = jnp.sum(rolled, axis=0, keepdims=True)

    return pl.pallas_call(
        kernel,
        grid=(heads,),
        in_specs=[
            pl.BlockSpec((1, 1, local, group), lambda h, m=m: (m, h, 0, 0)) for m in range(count)
        ]
        + [pl.BlockSpec((1, count * local), lambda h: (0, 0))],
        out_specs=pl.BlockSpec((1, 1, 2 * group), lambda h: (h, 0, 0)),
        out_shape=jax.ShapeDtypeStruct((heads, 1, 2 * group), F32),
    )(*[score_grads] * count, slots.reshape(1, count * local)).reshape(heads, 2 * group)


def by_head(value, head, head_size):
    per_block = 128 // head_size
    start = head // per_block * 128
    lanes = lax.broadcasted_iota(jnp.int32, (1, 128), 1) // head_size
    block = value[:, start : start + 128]
    return jnp.where(lanes == head % per_block, block, jnp.zeros_like(block)), start


def dot_last(left, right):
    return lax.dot_general(left, right, (((1,), (1,)), ((), ())), preferred_element_type=F32)


def attention_call(micro, micro_count, lengths, queries, pairs, own_slots, key_slots, bias, into):
    heads, rows, group = bias.shape
    double = pairs[0].shape[1]
    count = len(pairs)
    local = group // count
    proj = double // 2
    head_size = proj // heads

    def kernel(lengths_ref, query_ref, *rest):
        pair_refs = rest[:count]
        own_ref, key_ref, bias_ref = rest[count : count + 3]
        context_ref, prob_ref, packed_ref, arrived = rest[-4:]
        prob_ref, packed_ref = prob_ref.at[0], packed_ref.at[0]
        for index, ref in enumerate(pair_refs):
            arrived[index * local : (index + 1) * local] = ref[...]
        place = (
            lax.broadcasted_iota(jnp.int32, (group, group), 0) == key_ref[...]
        ).astype(BF16)
        packed_ref[...] = jnp.dot(place, arrived[...], preferred_element_type=F32).astype(BF16)
        first = lengths_ref[0]
        key_seg = lax.broadcasted_iota(jnp.int32, (local, group), 1) >= first
        same = key_seg == (own_ref[...] >= first)
        per_block = 128 // head_size
        total = None
        for head in range(heads):
            query, start = by_head(query_ref[...], head, head_size)
            scores = dot_last(query, packed_ref[:, start : start + 128])
            scores = jnp.where(same, scores + bias_ref[head].astype(F32), MASKED)
            weights = jnp.exp(scores - jnp.max(scores, axis=1, keepdims=True))
            weights = (weights / jnp.sum(weights, axis=1, keepdims=True)).astype(BF16)
            prob_ref[head] = weights
            value, _ = by_head(packed_ref[:, proj:], head, head_size)
            part = jnp.dot(weights, value, preferred_element_type=F32)
            total = part if head % per_block == 0 else total + part
            if head % per_block == per_block - 1:
                context_ref[:, start : start + 128] = total.astype(BF16)

    return pl.pallas_call(
        kernel,
        grid=(1,),
        in_specs=[
            pl.BlockSpec(memory_space=pltpu.SMEM),
            pl.BlockSpec((local, proj), lambda i: (micro, 0)),
        ]
        + [pl.BlockSpec((local, double), lambda i: (micro, 0))] * count
        + [
            pl.BlockSpec((local, 1), lambda i: (micro, 0)),
            pl.BlockSpec((1, group), lambda i: (0, 0)),
            pl.BlockSpec((heads, local, group), lambda i: (0, micro, 0)),
        ]
        + [ANY] * len(into),
        out_specs=[
            pl.BlockSpec((local, proj), lambda i: (micro, 0)),
            pl.BlockSpec((1, heads, local, group), lambda i: (micro, 0, 0, 0)),
            pl.BlockSpec((1, group, double), lambda i: (micro, 0, 0)),
        ],
        out_shape=[
            jax.ShapeDtypeStruct(queries.shape, BF16),
            jax.ShapeDtypeStruct((micro_count, heads, local, group), BF16),
            jax.ShapeDtypeStruct((micro_count, group, double), BF16),
        ],
        input_output_aliases={count + 5 + i: i for i in range(len(into))},
        scratch_shapes=[pltpu.VMEM((group, double), BF16)],
        cost_estimate=LIGHT,
    )(lengths, queries, *pairs, own_slots, key_slots, bias, *into)


def attention_back_call(queries, context_grad, probs, packed, key_slots, shards):
    micro_count, heads, local, group = probs.shape
    double = packed.shape[2]
    proj = double // 2
    head_size = proj // heads

    def kernel(query_ref, context_ref, prob_ref, packed_ref, key_ref, *rest):
        score_ref, dq_ref, part_ref, sums = rest
        score_ref, prob_ref, packed_ref = score_ref.at[0], prob_ref.at[0], packed_ref.at[0]
        per_block = 128 // head_size
        for head in range(heads):
            context, start = by_head(context_ref[...], head, head_size)
            query, _ = by_head(query_ref[...], head, head_size)
            key, _ = by_head(packed_ref[:, :proj], head, head_size)
            weights = prob_ref[head]
            wide = weights.astype(F32)
            upstream = dot_last(context, packed_ref[:, proj + start : proj + start + 128])
            inner = jnp.sum(wide * upstream, axis=1, keepdims=True)
            grad = (wide * (upstream - inner)).astype(BF16)
            score_ref[head] = grad
            query_part = jnp.dot(grad, key, preferred_element_type=F32)
            key_part = jnp.dot(grad.T, query, preferred_element_type=F32)
            value_part = jnp.dot(weights.T, context, preferred_element_type=F32)
            if head % per_block == 0:
                totals = [query_part, key_part, value_part]
            else:
                totals = [
                    total + part
                    for total, part in zip(totals, (query_part, key_part, value_part))
                ]
            if head % per_block == per_block - 1:
                dq_ref[:, start : start + 128] = totals[0].astype(BF16)
                sums[:, start : start + 128] = totals[1].astype(BF16)
                sums[:, proj + start : proj + start + 128] = totals[2].astype(BF16)
        for index in range(shards):
            slots = key_ref[index * local : (index + 1) * local]
            pick = (lax.broadcasted_iota(jnp.int32, (local, group), 1) == slots).astype(BF16)
            part_ref[index] = jnp.dot(pick, sums[...], preferred_element_type=F32).astype(BF16)

    by_scores = pl.BlockSpec((1, heads, local, group), lambda i: (i, 0, 0, 0))
    by_proj = pl.BlockSpec((local, proj), lambda i: (i, 0))
    return pl.pallas_call(
        kernel,
        grid=(micro_count,),
        in_specs=[
            by_proj,
            by_proj,
            by_scores,
            pl.BlockSpec((1, group, double), lambda i: (i, 0, 0)),
            pl.BlockSpec((group, 1), lambda i: (i, 0)),
        ],
        out_specs=[
            by_scores,
            by_proj,
            pl.BlockSpec((shards, local, double), lambda i: (0, i, 0)),
        ],
        out_shape=[
            jax.ShapeDtypeStruct(probs.shape, BF16),
            jax.ShapeDtypeStruct(queries.shape, BF16),
            jax.ShapeDtypeStruct((shards, queries.shape[0], double), BF16),
        ],
        scratch_shapes=[pltpu.VMEM((group, double), BF16)],
        cost_estimate=LIGHT,
    )(queries, context_grad, probs, packed, key_slots)


def axis_ranks():
    return lax.axis_index("shard"), lax.axis_index("rep") // 2


def gelu_parts(value):
    inner = math.sqrt(2.0 / math.pi)
    square = value * value
    bend = jnp.tanh(inner * value * (1.0 + 0.044715 * square))
    outside = 0.5 * (1.0 + bend)
    slope = outside + 0.5 * value * (1.0 - bend * bend) * (inner * (1.0 + 0.134145 * square))
    return value * outside, slope


def run_copies(copies, sems):
    started = [pltpu.make_async_copy(src, dst, sems.at[i]) for i, (src, dst) in enumerate(copies)]
    for copy in started:
        copy.start()
    return started


def pick_kernel(gate_ref, up_ref, out_ref):
    core = lax.axis_index("rep") % 2
    inner = gate_ref.shape[1]
    shards = lax.axis_size("shard")
    unit = inner // shards
    half = unit // 2
    for index, ref in enumerate((gate_ref, up_ref)):
        parts = []
        for shard in range(shards):
            low = ref[:, shard * unit : shard * unit + half]
            high = ref[:, shard * unit + half : (shard + 1) * unit]
            parts.append(jnp.where(core == 0, low, high))
        out_ref[:, index * (inner // 2) : (index + 1) * (inner // 2)] = jnp.concatenate(parts, 1)


def pick_columns(w_gate, w_up):
    return pl.pallas_call(
        pick_kernel,
        in_specs=[VMEM, VMEM],
        out_specs=VMEM,
        out_shape=jax.ShapeDtypeStruct(w_gate.shape, BF16),
    )(w_gate, w_up)


def spread_kernel(low_ref, high_ref, gate_ref, up_ref):
    inner = gate_ref.shape[1]
    shards = lax.axis_size("shard")
    half = inner // shards // 2
    for index, ref in enumerate((gate_ref, up_ref)):
        parts = []
        for shard in range(shards):
            start = index * (inner // 2) + shard * half
            parts += [low_ref[:, start : start + half], high_ref[:, start : start + half]]
        ref[...] = jnp.concatenate(parts, 1).astype(F32)


def spread_columns(low, high):
    shape = jax.ShapeDtypeStruct(low.shape, F32)
    return pl.pallas_call(
        spread_kernel,
        in_specs=[VMEM, VMEM],
        out_specs=[VMEM, VMEM],
        out_shape=[shape, shape],
    )(low, high)


def project_call(tokens, gain, pieces, places, block, proj):
    rows, width = tokens.shape
    count = len(pieces)
    moves = 2 * sum(len(place) for place in places)

    def kernel(token_ref, gain_ref, *rest):
        piece_refs = rest[:count]
        normed_ref, query_ref, pair_ref, keep_ref, weights, sems = rest[count:]
        rank, rep = lax.axis_index("shard"), lax.axis_index("rep")
        copies = []
        for ref, place in zip(piece_refs, places):
            for index, where in place:
                source = ref if index is None else ref.at[index]
                for start, size, matrix, row in where(rank, rep):
                    copies.append(
                        (source.at[pl.ds(start, size)], weights.at[matrix, pl.ds(row, size)])
                    )
        copies = run_copies(copies, sems)
        hidden = token_ref[...].astype(F32)
        scale = lax.rsqrt(jnp.mean(hidden * hidden, axis=1, keepdims=True) + EPSILON)
        normed = (hidden * scale * gain_ref[...]).astype(BF16)
        normed_ref[...] = normed
        for copy in copies:
            copy.wait()
        keep = pltpu.make_async_copy(weights, keep_ref, sems.at[moves])
        keep.start()
        query_ref[...] = jnp.dot(normed, weights[0], preferred_element_type=F32).astype(BF16)
        pair_ref[:, :proj] = jnp.dot(normed, weights[1], preferred_element_type=F32).astype(BF16)
        pair_ref[:, proj:] = jnp.dot(normed, weights[2], preferred_element_type=F32).astype(BF16)
        keep.wait()

    return pl.pallas_call(
        kernel,
        in_specs=[VMEM, VMEM] + [ANY] * count,
        out_specs=[VMEM, VMEM, VMEM, ANY],
        out_shape=[
            jax.ShapeDtypeStruct((rows, width), BF16),
            jax.ShapeDtypeStruct((rows, proj), BF16),
            jax.ShapeDtypeStruct((rows, 2 * proj), BF16),
            jax.ShapeDtypeStruct((4, width, proj), BF16),
        ],
        scratch_shapes=[
            pltpu.VMEM((4, width, proj), BF16),
            pltpu.SemaphoreType.DMA((moves + 1,)),
        ],
        cost_estimate=LIGHT,
    )(tokens, gain, *pieces)


def project_grad_call(normed, query_grad, pair_grad, out_grads, small, outputs):
    rows, width = normed.shape
    proj = query_grad.shape[1]
    count = len(outputs)
    moves = sum(len(items) for _, items in outputs)

    small_rows = small.shape[1]

    def kernel(normed_ref, query_ref, pair_ref, out_grad_ref, small_ref, *rest):
        out_refs, result, sems = rest[:count], rest[count], rest[count + 1]
        fourth = pltpu.make_async_copy(out_grad_ref, result.at[3], sems.at[2 * moves])
        fourth.start()
        for begin in range(0, width, 256):
            size = min(256, width - begin)
            turned = normed_ref[:, begin : begin + size].T
            for index in range(3):
                right = query_ref[...] if index == 0 else pair_ref[:, (index - 1) * proj : index * proj]
                result[index, begin : begin + size] = jnp.dot(
                    turned, right, preferred_element_type=F32
                ).astype(BF16)
        fourth.wait()
        rank, rep = lax.axis_index("shard"), lax.axis_index("rep")
        copies = []
        for ref, (shape, items) in zip(out_refs, outputs):
            for index, where, step in items:
                matrix, row = where(rank, rep)
                size = shape[-2] - (small_rows if step is not None else 0)
                copies.append((result.at[matrix, pl.ds(row, size)], ref.at[index + (pl.ds(0, size),)]))
                if step is not None:
                    copies.append(
                        (
                            small_ref.at[step],
                            ref.at[index + (pl.ds(size, small_rows),)],
                        )
                    )
        for copy in run_copies(copies, sems):
            copy.wait()

    return pl.pallas_call(
        kernel,
        in_specs=[VMEM, VMEM, VMEM, ANY, VMEM],
        out_specs=[ANY] * count,
        out_shape=[jax.ShapeDtypeStruct(shape, BF16) for shape, _ in outputs],
        scratch_shapes=[
            pltpu.VMEM((4, width, proj), BF16),
            pltpu.SemaphoreType.DMA((2 * moves + 1,)),
        ],
        cost_estimate=LIGHT,
    )(normed, query_grad, pair_grad, out_grads, small)


def part_of(ref, row, count, columns):
    if (row, count, columns) == (0,) + ref.shape:
        return ref
    return ref.at[pl.ds(row, count), pl.ds(0, columns)]


def gate_up_call(own, other, width, inner, pieces, moves):
    rows, wide = own.shape
    count, steps = len(pieces), len(moves)
    half = inner // 2
    tile = 256

    def kernel(own_ref, other_ref, *rest):
        piece_refs = rest[:count]
        out_refs, keep_ref = rest[count : count + 3], rest[count + 3]
        both, weights, slopes, acts, hiddens, sems = rest[count + 4 :]
        results = (slopes, acts, hiddens)
        rank, chip = axis_ranks()
        copies = [(own_ref, both.at[:rows]), (other_ref, both.at[rows:])]
        for piece, row, size, columns, place in moves:
            to_row, to_column = place(rank, chip)
            copies.append(
                (
                    part_of(piece_refs[piece], row, size, columns),
                    weights.at[pl.ds(to_row, size), pl.ds(to_column, columns)],
                )
            )
        for copy in run_copies(copies, sems):
            copy.wait()
        keep = pltpu.make_async_copy(weights, keep_ref, sems.at[steps + 2])
        keep.start()

        def step(index, carry):
            start = pl.multiple_of(index * tile, tile)
            left = both[:, :width]
            gate = jnp.dot(left, weights[:, pl.ds(start, tile)], preferred_element_type=F32)
            up = jnp.dot(
                left,
                weights[:, pl.ds(pl.multiple_of(half + start, tile), tile)],
                preferred_element_type=F32,
            )
            act, slope = gelu_parts(gate)
            columns = pl.ds(start, tile)
            for number, value in enumerate((up * slope, act, act * up)):
                results[number][:, columns] = value.astype(BF16)
                pltpu.make_async_copy(
                    results[number].at[:, columns],
                    out_refs[number].at[:, columns],
                    sems.at[steps + 3 + number],
                ).start()
            return carry

        lax.fori_loop(0, half // tile, step, 0)
        keep.wait()
        for number in range(3):
            pltpu.make_async_copy(
                results[number], out_refs[number], sems.at[steps + 3 + number]
            ).wait()

    shape = jax.ShapeDtypeStruct((2 * rows, half), BF16)
    return pl.pallas_call(
        kernel,
        in_specs=[ANY] * (2 + count),
        out_specs=[ANY] * 4,
        out_shape=[shape, shape, shape, jax.ShapeDtypeStruct((width, inner), BF16)],
        scratch_shapes=[
            pltpu.VMEM((2 * rows, wide), BF16),
            pltpu.VMEM((width, inner), BF16),
        ]
        + [pltpu.VMEM((2 * rows, half), BF16)] * 3
        + [
            pltpu.SemaphoreType.DMA((steps + 6,)),
        ],
        cost_estimate=LIGHT,
    )(own, other, *pieces)


def col_tiles(width):
    return [(start, min(512, width - start)) for start in range(0, width, 512)]


def down_call(hidden, width, padded, pieces, moves):
    double, half = hidden.shape
    rows = double // 2
    count, steps = len(pieces), len(moves)

    def kernel(hidden_ref, *rest):
        piece_refs = rest[:count]
        own_ref, other_ref, keep_ref, weights, sems = rest[count:]
        rank, chip = axis_ranks()
        copies = []
        for piece, row, size, columns, place in moves:
            to_row, to_column = place(rank, chip)
            copies.append(
                (
                    part_of(piece_refs[piece], row, size, columns),
                    weights.at[pl.ds(to_row, size), pl.ds(to_column, columns)],
                )
            )
        for copy in run_copies(copies, sems):
            copy.wait()
        keep = pltpu.make_async_copy(weights, keep_ref, sems.at[steps])
        keep.start()
        for start, size in col_tiles(width):
            columns = slice(start, start + size)
            own_ref[:, columns] = jnp.dot(
                hidden_ref[:rows], weights[:, columns], preferred_element_type=F32
            )
            other_ref[:, columns] = jnp.dot(
                hidden_ref[rows:], weights[:, columns], preferred_element_type=F32
            ).astype(BF16)
        if padded > width:
            other_ref[:, width:] = jnp.zeros((rows, padded - width), BF16)
        keep.wait()

    return pl.pallas_call(
        kernel,
        in_specs=[VMEM] + [ANY] * count,
        out_specs=[VMEM, VMEM, ANY],
        out_shape=[
            jax.ShapeDtypeStruct((rows, width), F32),
            jax.ShapeDtypeStruct((rows, padded), BF16),
            jax.ShapeDtypeStruct((half, padded), BF16),
        ],
        scratch_shapes=[pltpu.VMEM((half, padded), BF16), pltpu.SemaphoreType.DMA((steps + 1,))],
        cost_estimate=LIGHT,
    )(hidden, *pieces)


def finish_call(pieces, gate_up_moves, down_moves, block, inner, down_rows, width, padded):
    count = len(pieces)
    steps = len(gate_up_moves) + len(down_moves)

    def kernel(*refs):
        piece_refs = refs[:count]
        out_refs = refs[count : count + 3]
        columns_of, rows_of, gate_ref, up_ref, down_ref, sems = refs[count + 3 :]
        chip, core = axis_ranks()[1], lax.axis_index("rep") % 2
        shards = lax.axis_size("shard")
        copies = []
        for piece, row, size, columns, place in gate_up_moves:
            to_core, to_row, to_column = place(core, chip)
            copies.append(
                (
                    part_of(piece_refs[piece], row, size, columns),
                    columns_of.at[to_core, pl.ds(to_row, size), pl.ds(to_column, columns)],
                )
            )
        for piece, row, size, columns, place in down_moves:
            to_row, to_column = place(core, chip)
            copies.append(
                (
                    part_of(piece_refs[piece], row, size, columns),
                    rows_of.at[pl.ds(to_row, size), pl.ds(to_column, columns)],
                )
            )
        copies = run_copies(copies, sems)
        for copy in copies[: len(gate_up_moves)]:
            copy.wait()
        half = inner // shards // 2
        outs = [
            pltpu.make_async_copy(ref, out, sems.at[steps + number])
            for number, (ref, out) in enumerate(zip((gate_ref, up_ref, down_ref), out_refs))
        ]
        for index, ref in enumerate((gate_ref, up_ref)):
            for shard in range(shards):
                start = index * (inner // 2) + shard * half
                both = [columns_of[at, :, start : start + half] for at in range(2)]
                ref[:, 2 * half * shard : 2 * half * (shard + 1)] = jnp.concatenate(
                    both, 1
                ).astype(F32)
            outs[index].start()
        for copy in copies[len(gate_up_moves) :]:
            copy.wait()
        down_ref[...] = rows_of[...].T[:width].astype(F32)
        outs[2].start()
        for copy in outs:
            copy.wait()

    return pl.pallas_call(
        kernel,
        in_specs=[ANY] * count,
        out_specs=[ANY] * 3,
        out_shape=[
            jax.ShapeDtypeStruct((block, inner), F32),
            jax.ShapeDtypeStruct((block, inner), F32),
            jax.ShapeDtypeStruct((width, down_rows), F32),
        ],
        scratch_shapes=[
            pltpu.VMEM((2, block, inner), BF16),
            pltpu.VMEM((down_rows, padded), BF16),
            pltpu.VMEM((block, inner), F32),
            pltpu.VMEM((block, inner), F32),
            pltpu.VMEM((width, down_rows), F32),
            pltpu.SemaphoreType.DMA((steps + 3,)),
        ],
    )(*pieces)


def attn_finish_call(pieces, moves, block, proj):
    count = len(pieces)

    def kernel(*refs):
        piece_refs = refs[:count]
        out_refs, whole, sems = refs[count : count + 4], refs[count + 4], refs[count + 5]
        rep = lax.axis_index("rep")
        copies = []
        for piece, index, place in moves:
            for start, size, matrix, row in place(rep):
                copies.append(
                    (
                        piece_refs[piece].at[index, pl.ds(start, size)],
                        whole.at[matrix, pl.ds(row, size)],
                    )
                )
        for copy in run_copies(copies, sems):
            copy.wait()
        for index, ref in enumerate(out_refs):
            ref[...] = whole[index].astype(F32)

    return pl.pallas_call(
        kernel,
        in_specs=[ANY] * count,
        out_specs=[VMEM] * 4,
        out_shape=[jax.ShapeDtypeStruct((block, proj), F32)] * 4,
        scratch_shapes=[
            pltpu.VMEM((4, block, proj), BF16),
            pltpu.SemaphoreType.DMA((2 * len(moves),)),
        ],
    )(*pieces)


def hidden_grad_call(own, other, down, slope, act):
    rows, width = own.shape
    half = down.shape[0]
    tile = 256

    def kernel(own_ref, other_ref, down_ref, slope_ref, act_ref, gate_ref, up_ref):
        for index, ref in enumerate((own_ref, other_ref)):
            part = slice(index * rows, (index + 1) * rows)
            upstream = dot_last(ref[...], down_ref[...])
            gate_ref[part] = (upstream * slope_ref[part].astype(F32)).astype(BF16)
            up_ref[part] = (upstream * act_ref[part].astype(F32)).astype(BF16)

    whole = pl.BlockSpec((rows, width), lambda i: (0, 0))
    columns = pl.BlockSpec((2 * rows, tile), lambda i: (0, i))
    shape = jax.ShapeDtypeStruct((2 * rows, half), BF16)
    return pl.pallas_call(
        kernel,
        grid=(half // tile,),
        in_specs=[
            whole,
            whole,
            pl.BlockSpec((tile, down.shape[1]), lambda i: (i, 0)),
            columns,
            columns,
        ],
        out_specs=[columns, columns],
        out_shape=[shape, shape],
        cost_estimate=LIGHT,
    )(own, other, down, slope, act)


def normed_grad_call(gate, up, weights):
    double, half = gate.shape
    rows = double // 2
    width = weights.shape[0]
    tile = 256

    def kernel(gate_ref, up_ref, low_ref, high_ref, own_ref, other_ref):
        for index, ref in enumerate((own_ref, other_ref)):
            part = slice(index * rows, (index + 1) * rows)
            total = dot_last(gate_ref[part], low_ref[...]) + dot_last(up_ref[part], high_ref[...])
            ref[...] = total.astype(ref.dtype)

    whole = pl.BlockSpec((double, half), lambda i: (0, 0))
    return pl.pallas_call(
        kernel,
        grid=(pl.cdiv(width, tile),),
        in_specs=[
            whole,
            whole,
            pl.BlockSpec((tile, half), lambda i: (i, 0)),
            pl.BlockSpec((tile, half), lambda i: (i, 1)),
        ],
        out_specs=[pl.BlockSpec((rows, tile), lambda i: (0, i))] * 2,
        out_shape=[
            jax.ShapeDtypeStruct((rows, width), F32),
            jax.ShapeDtypeStruct((rows, lane_tiles(width)), BF16),
        ],
        cost_estimate=LIGHT,
    )(gate, up, weights, weights)


def row_specs(micro_count, local, width):
    return pl.BlockSpec((local, width), lambda i: (i, 0)), pl.BlockSpec((1, width), lambda i: (0, 0))


def sum_rows(ref, value):
    total = jnp.sum(value, axis=0, keepdims=True)

    @pl.when(pl.program_id(0) == 0)
    def _():
        ref[...] = total

    @pl.when(pl.program_id(0) > 0)
    def _():
        ref[...] += total


def put_padded(ref, value):
    width = value.shape[1]
    ref[:, :width] = value.astype(BF16)
    if ref.shape[1] > width:
        ref[:, width:] = jnp.zeros((value.shape[0], ref.shape[1] - width), BF16)


def lane_tiles(width):
    return -(-width // 128) * 128


def mid_call(tokens, context, w_out, gain, micro_count):
    rows, width = tokens.shape
    local = rows // micro_count
    by_row, vector = row_specs(micro_count, local, width)

    def kernel(token_ref, context_ref, out_ref, gain_ref, hidden_ref, normed_ref):
        hidden = token_ref[...].astype(F32) + jnp.dot(
            context_ref[...], out_ref[...], preferred_element_type=F32
        )
        hidden_ref[...] = hidden
        put_padded(normed_ref, hidden * rms_scale(hidden) * gain_ref[...])

    return pl.pallas_call(
        kernel,
        grid=(micro_count,),
        in_specs=[
            by_row,
            pl.BlockSpec((local, context.shape[1]), lambda i: (i, 0)),
            pl.BlockSpec(w_out.shape, lambda i: (0, 0)),
            vector,
        ],
        out_specs=[by_row, pl.BlockSpec((local, lane_tiles(width)), lambda i: (i, 0))],
        out_shape=[
            jax.ShapeDtypeStruct((rows, width), F32),
            jax.ShapeDtypeStruct((rows, lane_tiles(width)), BF16),
        ],
        cost_estimate=LIGHT,
    )(tokens, context, w_out, gain)


def out_call(hidden, part, given, cotangent, gate_cotangent, gain, vector_in, micro_count):
    rows, width = hidden.shape
    local = rows // micro_count
    by_row, vector = row_specs(micro_count, local, width)
    one = pl.BlockSpec((local, 1), lambda i: (i, 0))
    turned = pl.BlockSpec((1, width, local), lambda i: (i, 0, 0))
    padded = pl.BlockSpec((local, lane_tiles(width)), lambda i: (i, 0))

    def kernel(
        hidden_ref, part_ref, given_ref, up_ref, gate_ref, gain_ref, vector_ref,
        state_ref, deleted_ref, grad_ref, low_ref, gain_grad_ref, vector_grad_ref,
    ):
        state = hidden_ref[...] + part_ref[...] + given_ref[:, :width].astype(F32)
        state_ref[0] = state.T
        scale = rms_scale(state)
        normed = state * scale * gain_ref[...]
        logit = jnp.sum(normed * vector_ref[...], axis=1, keepdims=True)
        sigmoid = lax.logistic(logit)
        deleted_ref[...] = -30.0 * sigmoid
        slope = gate_ref[...] * -30.0 * sigmoid * (1.0 - sigmoid)
        upstream = slope * vector_ref[...]
        sum_rows(vector_grad_ref, slope * normed)
        sum_rows(gain_grad_ref, upstream * state * scale)
        grad = up_ref[...].astype(F32) + rms_back(state, scale, gain_ref[...], upstream)
        grad_ref[...] = grad
        put_padded(low_ref, grad)

    return pl.pallas_call(
        kernel,
        grid=(micro_count,),
        in_specs=[by_row, by_row, padded, by_row, one, vector, vector],
        out_specs=[turned, one, by_row, padded, vector, vector],
        out_shape=[
            jax.ShapeDtypeStruct((micro_count, width, local), F32),
            jax.ShapeDtypeStruct((rows, 1), F32),
            jax.ShapeDtypeStruct((rows, width), F32),
            jax.ShapeDtypeStruct((rows, lane_tiles(width)), BF16),
            jax.ShapeDtypeStruct((1, width), F32),
            jax.ShapeDtypeStruct((1, width), F32),
        ],
        cost_estimate=LIGHT,
    )(hidden, part, given, cotangent, gate_cotangent, gain, vector_in)


def back_call(part, given, grad_out, hidden, gain, context, w_out, micro_count):
    rows, width = hidden.shape
    local = rows // micro_count
    proj = context.shape[1]
    by_row, vector = row_specs(micro_count, local, width)
    by_proj = pl.BlockSpec((local, proj), lambda i: (i, 0))
    padded = pl.BlockSpec((local, lane_tiles(width)), lambda i: (i, 0))
    whole = pl.BlockSpec((proj, width), lambda i: (0, 0))

    def kernel(
        part_ref, given_ref, grad_ref, hidden_ref, gain_ref, context_ref, out_ref,
        mid_ref, context_grad_ref, out_grad_ref, gain_grad_ref, total,
    ):
        normed_grad = part_ref[...] + given_ref[:, :width].astype(F32)
        hidden = hidden_ref[...]
        scale = rms_scale(hidden)
        sum_rows(gain_grad_ref, normed_grad * hidden * scale)
        mid = grad_ref[...] + rms_back(hidden, scale, gain_ref[...], normed_grad)
        mid_ref[...] = mid
        low = mid.astype(BF16)
        context_grad_ref[...] = dot_last(low, out_ref[...]).astype(BF16)
        product = jnp.dot(context_ref[...].T, low, preferred_element_type=F32)
        step = pl.program_id(0)

        @pl.when(step == 0)
        def _():
            total[...] = product

        @pl.when(step > 0)
        def _():
            total[...] += product

        @pl.when(step == micro_count - 1)
        def _():
            out_grad_ref[...] = total[...].astype(BF16)

    return pl.pallas_call(
        kernel,
        grid=(micro_count,),
        in_specs=[by_row, padded, by_row, by_row, vector, by_proj, whole],
        out_specs=[by_row, by_proj, whole, vector],
        out_shape=[
            jax.ShapeDtypeStruct((rows, width), F32),
            jax.ShapeDtypeStruct((rows, proj), BF16),
            jax.ShapeDtypeStruct((proj, width), BF16),
            jax.ShapeDtypeStruct((1, width), F32),
        ],
        scratch_shapes=[pltpu.VMEM((proj, width), F32)],
        cost_estimate=LIGHT,
    )(part, given, grad_out, hidden, gain, context, w_out)


def in_call(query_grad, pair_parts, weights, grad_mid, tokens, gain, micro_count):
    rows, width = tokens.shape
    local = rows // micro_count
    proj = query_grad.shape[1]
    count = pair_parts.shape[0]
    by_row, vector = row_specs(micro_count, local, width)
    by_proj = pl.BlockSpec((local, proj), lambda i: (i, 0))
    by_pair = pl.BlockSpec((local, 2 * proj), lambda i: (i, 0))

    def kernel(
        query_ref, part_ref, wq_ref, wk_ref, wv_ref, mid_ref, token_ref, gain_ref,
        pair_ref, grad_ref, gain_grad_ref,
    ):
        pair = sum(part_ref[index].astype(F32) for index in range(count)).astype(BF16)
        pair_ref[...] = pair
        normed_grad = (
            dot_last(query_ref[...], wq_ref[0])
            + dot_last(pair[:, :proj], wk_ref[0])
            + dot_last(pair[:, proj:], wv_ref[0])
        )
        hidden = token_ref[...].astype(F32)
        scale = rms_scale(hidden)
        sum_rows(gain_grad_ref, normed_grad * hidden * scale)
        grad = mid_ref[...] + rms_back(hidden, scale, gain_ref[...], normed_grad)
        grad_ref[0] = grad.astype(BF16).T

    return pl.pallas_call(
        kernel,
        grid=(micro_count,),
        in_specs=[by_proj, pl.BlockSpec((count, local, 2 * proj), lambda i: (0, i, 0))]
        + [pl.BlockSpec((1, width, proj), lambda i, m=m: (m, 0, 0)) for m in range(3)]
        + [by_row, by_row, vector],
        out_specs=[by_pair, pl.BlockSpec((1, width, local), lambda i: (i, 0, 0)), vector],
        out_shape=[
            jax.ShapeDtypeStruct((rows, 2 * proj), BF16),
            jax.ShapeDtypeStruct((micro_count, width, local), BF16),
            jax.ShapeDtypeStruct((1, width), F32),
        ],
        cost_estimate=LIGHT,
    )(query_grad, pair_parts, weights, weights, weights, grad_mid, tokens, gain)


def weight_grad_call(left, right, picks, width, outputs, in_halves):
    left_own, left_other = left
    right_own, right_other = right
    rows = left_own.shape[0]
    total = 2 * rows if left_other is not None else rows
    beside = right_other is not None and right_own.shape[0] == total
    right_width = right_own.shape[1] * (2 if beside else 1)
    count = len(outputs)
    copies_out = sum(len(moves) for _, moves, _ in outputs)
    depth = sum(size for _, size in picks)
    tile = 256
    split = left_other is not None
    right_split = right_other is not None
    inputs = [left_own] + ([left_other] if split else []) + [right_own]
    inputs += [right_other] if right_split else []

    def kernel(*refs):
        in_refs = list(refs[: len(inputs)])
        out_refs = refs[len(inputs) : len(inputs) + count]
        lefts, turned, rights, result, sems = refs[len(inputs) + count :]
        copies = []
        for target, parted, aside in ((lefts, split, False), (rights, right_split, beside)):
            first = in_refs.pop(0)
            size = first.shape[1] if aside else first.shape[0]
            if not parted:
                copies.append((first, target))
            elif aside:
                copies.append((first, target.at[:, :size]))
                copies.append((in_refs.pop(0), target.at[:, size:]))
            else:
                copies.append((first, target.at[:size]))
                copies.append((in_refs.pop(0), target.at[size:]))
        for copy in run_copies(copies, sems):
            copy.wait()
        to_row = 0
        for first, size in picks:
            for begin in range(0, size, tile):
                span = min(tile, size - begin)
                turned[to_row : to_row + span] = lefts[:, first + begin : first + begin + span].T
                to_row += span

        def product(start, size):
            result[:, pl.ds(start, size)] = jnp.dot(
                turned[...], rights[:, pl.ds(start, size)], preferred_element_type=F32
            ).astype(BF16)

        if not in_halves:
            for begin in range(0, depth, tile):
                span = min(tile, depth - begin)
                for start, size in col_tiles(width):
                    result[begin : begin + span, start : start + size] = jnp.dot(
                        turned[begin : begin + span],
                        rights[:, start : start + size],
                        preferred_element_type=F32,
                    ).astype(BF16)
        rank, chip = axis_ranks()
        started = []
        for half in range(2 if in_halves else 1):
            first = (chip // 2 ^ (1 - half)) * (width // 2) if in_halves else 0
            tiles = (width // 2 if in_halves else width) // tile

            def step(index, carry, first=first):
                product(pl.multiple_of(first + index * tile, tile), tile)
                return carry

            if in_halves:
                lax.fori_loop(0, tiles, step, 0)
            for ref, (shape, moves, mask) in zip(out_refs, outputs):
                if in_halves and mask & 2 == 2 * half:
                    continue
                for index, place in moves:
                    row, column = place(rank, chip)
                    copy = pltpu.make_async_copy(
                        result.at[pl.ds(row, shape[1]), pl.ds(column, shape[2])],
                        ref.at[index],
                        sems.at[len(started)],
                    )
                    copy.start()
                    started.append(copy)
        for copy in started:
            copy.wait()

    return pl.pallas_call(
        kernel,
        in_specs=[ANY] * len(inputs),
        out_specs=[ANY] * count,
        out_shape=[jax.ShapeDtypeStruct(shape, BF16) for shape, _, _ in outputs],
        scratch_shapes=[
            pltpu.VMEM((total, left_own.shape[1]), BF16),
            pltpu.VMEM((depth, total), BF16),
            pltpu.VMEM((total, right_width), BF16),
            pltpu.VMEM((depth, width), BF16),
            pltpu.SemaphoreType.DMA((max(4, copies_out),)),
        ],
        cost_estimate=LIGHT,
    )(*inputs)


def on_device(
    tokens,
    cotangent,
    gate_cotangent,
    slot_of,
    seq_lengths,
    buckets,
    gain_attn,
    w_query,
    w_key,
    w_value,
    w_out,
    rel_bias,
    gain_ffn,
    w_gate,
    w_up,
    w_down,
    gain_delete,
    w_delete,
):
    shards = lax.axis_size("shard")
    reps = lax.axis_size("rep")
    chips = reps // 2
    rank = lax.axis_index("shard")
    rep_rank = lax.axis_index("rep")
    core = rep_rank % 2
    chip = rep_rank // 2
    micro_count, local_rows, width = tokens.shape
    group = local_rows * shards
    rows = micro_count * local_rows
    heads = rel_bias.shape[1]
    bucket_rows = rel_bias.shape[0]
    bucket_count = bucket_rows * shards
    proj = w_query.shape[1]
    head_size = proj // heads
    block = gain_attn.shape[0]
    inner = w_gate.shape[1]
    half_inner = inner // 2
    col_piece = inner // chips
    down_block = w_down.shape[0]
    down_half = down_block // 2
    down_piece = down_half // chips
    down_parts_count = -(-width // col_piece)
    padded = -(-width // 128) * 128
    aligned = reps == 8 and block % 16 == 0 and down_piece % 16 == 0 and col_piece % 128 == 0

    def swap(value, mask):
        return lax.ppermute(value, "rep", [(i, i ^ mask) for i in range(reps)])

    def shift(value, by=1):
        return lax.ppermute(value, "shard", [(i, (i + by) % shards) for i in range(shards)])

    def tie(value, moved):
        return lax.optimization_barrier((value, moved))

    def cut(count):
        half = count // 2
        return half // 16 * 16 if half >= 16 else half

    def gather_near(piece):
        if chips == 1:
            return []
        return [swap(piece, 2)] + ([swap(piece, 4)] if chips >= 4 else [])

    def gather_rest(near):
        if chips < 4:
            return []
        middle = cut(near[0].shape[0])
        return [swap(near[1][:middle], 2), swap(near[0][middle:], 4)]

    def gather_list(piece, near, rest):
        middle = cut(piece.shape[0])
        found = [(0, 0, piece)] + [(1 + i, 0, part) for i, part in enumerate(near)]
        found += [(3, i * middle, part) for i, part in enumerate(rest)]
        bit = 4
        while bit < chips:
            found += [
                (mask ^ bit, start, swap(part, 2 * bit)) for mask, start, part in found
            ]
            bit *= 2
        return found

    def plane_gather(piece):
        near = gather_near(piece)
        return gather_list(piece, near, gather_rest(near))

    def add(*values):
        return sum(value.astype(F32) for value in values).astype(BF16)

    def plane_reduce(parts, axis):
        state = reduce_begin(parts, axis)
        return reduce_end(reduce_middle(state, axis))

    def reduce_begin(parts, axis):
        def level(base, bit):
            if bit < 4:
                return lambda name: parts[base][name]
            lower, upper = level(base, bit // 2), level(base ^ bit, bit // 2)
            return lambda name: add(lower(name), swap(upper(name), 2 * bit))

        get = level(0, chips // 2)
        if chips < 4:
            return [get("own")] + ([swap(get("near"), 2)] if chips == 2 else [])
        return [get("own"), get("far"), get("near"), swap(get("top"), 2), swap(get("low"), 4)]

    def reduce_middle(state, axis):
        if chips < 4:
            return state
        own, far, near, top, low = state
        middle = top.shape[axis]

        def pair(value):
            return (
                lax.slice_in_dim(value, 0, middle, axis=axis),
                lax.slice_in_dim(value, middle, value.shape[axis], axis=axis),
            )

        (far_top, far_low), (near_top, near_low) = pair(far), pair(near)
        far = jnp.concatenate([add(far_top, top), far_low], axis)
        near = jnp.concatenate([near_top, add(near_low, low)], axis)
        return [own, swap(far, 4), swap(near, 2)]

    def reduce_end(state):
        return add(*state) if len(state) > 1 else state[0]

    names = {"own": 0, "near": 1, "far": 2, "top": 3, "low": 3}
    bases = [base for base in range(chips) if base & 3 == 0]
    used = ["own", "near", "far", "top", "low"] if chips >= 4 else ["own", "near"][:chips]

    def source(step):
        return (rank - step) % shards

    order = (rank - jnp.arange(shards, dtype=jnp.int32)) % shards
    per_matrix = reps // 4
    attn_rows = block // per_matrix
    if aligned:
        attn_rows = -(-attn_rows // 16) * 16
    last_row = block - attn_rows

    def part_row(part):
        return jnp.minimum(part * attn_rows, last_row)

    attn_own = jnp.stack([w_query, w_key, w_value, w_out.reshape(block, proj)])
    attn_piece = lax.dynamic_slice(
        attn_own,
        (rep_rank // per_matrix, part_row(rep_rank % per_matrix), 0),
        (1, attn_rows, proj),
    )[0]
    vector_pack = jnp.concatenate(
        [gain_attn, gain_ffn, gain_delete, w_delete, rel_bias.reshape(-1)]
    )
    pack_rows = -(-vector_pack.shape[0] // (16 * proj)) * 16
    vector_pack = jnp.pad(vector_pack, (0, pack_rows * proj - vector_pack.shape[0]))
    vector_pack = vector_pack.reshape(pack_rows, proj)
    attn_sent = jnp.concatenate([attn_piece, vector_pack])
    attn_arrived = [shift(attn_sent, step) for step in range(1, shards)]
    token_rows = tokens.reshape(rows, width)
    attn_arrived, (token_rows, attn_own) = tie(attn_arrived, (token_rows, attn_own))
    vectors = jnp.stack([vector_pack] + [part[attn_rows:] for part in attn_arrived])
    vectors = jnp.take(vectors, order, axis=0).reshape(shards, pack_rows * proj)
    attn_gain = vectors[:, :block].reshape(width).astype(F32)
    ffn_gain = vectors[:, block : 2 * block].reshape(width).astype(F32)
    delete_gain = vectors[:, 2 * block : 3 * block].reshape(width).astype(F32)
    delete_vec = vectors[:, 3 * block : 4 * block].reshape(width).astype(F32)
    bias_table = vectors[:, 4 * block : 4 * block + bucket_rows * heads]
    bias_table = bias_table.reshape(bucket_count, heads)
    stacked = jnp.stack([part[:attn_rows] for part in attn_arrived])

    def pack(gate_up_part, down_part):
        wide = jnp.pad(down_part, ((0, 0), (0, down_parts_count * col_piece - width)))
        cuts = [wide[:, i * col_piece : (i + 1) * col_piece] for i in range(down_parts_count)]
        return jnp.concatenate([gate_up_part] + cuts)

    def overlaps(start, count):
        bounds = [(None, 0, block)] + [
            (i, block + i * down_piece, block + (i + 1) * down_piece)
            for i in range(down_parts_count)
        ]
        found = []
        for part, low, high in bounds:
            first, last = max(low, start), min(high, start + count)
            if first < last:
                found.append((part, first - start, first - low, last - first))
        return found

    def part_columns(part):
        return min(col_piece, padded - part * col_piece)

    gate_up_own = pick_columns(w_gate, w_up)
    down_own = lax.dynamic_slice_in_dim(w_down, core * down_half, down_half, 0)
    packed_own = pack(
        lax.dynamic_slice_in_dim(gate_up_own, chip * col_piece, col_piece, 1),
        lax.dynamic_slice_in_dim(down_own, chip * down_piece, down_piece, 0),
    )
    packed_own, stacked = tie(packed_own, stacked)
    attn_plane = [stacked] + [swap(stacked, 2 * mask) for mask in range(1, chips)]
    attn_plane = jnp.stack(attn_plane)
    ring = [packed_own, shift(packed_own)]
    attn_plane, ring = tie(attn_plane, ring)
    nears, rests = [None] * shards, [None] * shards
    nears[1] = gather_near(ring[1])
    attn_other = swap(attn_plane, 1)

    def attn_place(mask, flip, step):
        def place(at, rep):
            owner = rep ^ (2 * mask + flip)
            row = (at - step) % shards * block + part_row(owner % per_matrix)
            return owner // per_matrix, pl.multiple_of(row, 16) if aligned else row

        return place

    shared = per_matrix * attn_rows - block

    def split_place(place, flip):
        def places_of(*at):
            matrix, row = place(*at)
            part = (at[-1] ^ flip) % per_matrix
            first = row - last_row * part
            moves = [
                (
                    pl.multiple_of(shared * part, 16),
                    attn_rows - shared,
                    matrix,
                    pl.multiple_of(first + attn_rows * part, 16),
                )
            ]
            if shared and flip == 0:
                moves.append(
                    (
                        pl.multiple_of(last_row * (1 - part), 16),
                        shared,
                        matrix,
                        pl.multiple_of(first + last_row, 16),
                    )
                )
            return moves

        return places_of

    attn_pieces = [w_query, w_key, w_value, attn_own[3]]
    attn_places = [
        [(None, lambda at, rep, matrix=matrix: [(0, block, matrix, pl.multiple_of(at * block, 16))])]
        for matrix in range(4)
    ]
    for flip, found in enumerate((attn_plane, attn_other)):
        attn_pieces.append(found)
        attn_places.append(
            [
                ((mask, step - 1), attn_place(mask, flip, step), flip)
                for mask in range(chips)
                for step in range(1, shards)
            ]
        )
    if not aligned:
        whole = jnp.zeros((4, width, proj), BF16)
        whole = lax.dynamic_update_slice(whole, attn_own, (0, rank * block, 0))
        for piece, place in zip(attn_pieces[4:], attn_places[4:]):
            for index, where, _ in place:
                matrix, row = where(rank, rep_rank)
                whole = lax.dynamic_update_slice(whole, piece[index][None], (matrix, row, 0))
        attn_pieces = [whole[matrix] for matrix in range(4)]
        attn_places = [
            [(None, lambda at, rep, matrix=matrix: [(0, width, matrix, 0)])] for matrix in range(4)
        ]
    else:
        attn_places[4:] = [
            [(index, split_place(where, flip)) for index, where, flip in place]
            for place in attn_places[4:]
        ]

    slots = slot_of[:, 0]
    own_slots = lax.dynamic_slice_in_dim(slots, rank * local_rows, local_rows, 1)
    key_slots = jnp.take(slots.reshape(micro_count, shards, local_rows), order, axis=1)
    key_slots = key_slots.reshape(micro_count, group)
    onehot = (buckets[:, None] == jnp.arange(bucket_count, dtype=jnp.int32)[None, :]).astype(F32)
    onehot = jnp.pad(onehot, ((0, 1), (0, 0)))
    bias_rows = jnp.dot(onehot, bias_table.astype(F32), precision=HIGHEST).T
    bias = bias_of_queries(bias_rows, own_slots.reshape(rows), group)
    first_len = seq_lengths[:, 0, 0]

    normed_one, queries, own_pairs, attn_full = project_call(
        token_rows, attn_gain[None], attn_pieces, attn_places, block, proj
    )
    out_full = attn_full[3].reshape(proj, width)

    for step in range(2, shards - 1):
        ring.append(shift(ring[-1]))
    own_pairs, ring = tie(own_pairs, ring)
    early = (
        out_full,
        jnp.pad(down_own, ((0, 0), (0, padded - width))),
        cotangent.reshape(rows, width),
        gate_cotangent.reshape(rows, 1).astype(F32),
        [value[None] for value in (ffn_gain, delete_gain, delete_vec)],
        slots.reshape(micro_count * group, 1),
    )
    pairs = [own_pairs]
    for step in range(1, shards):
        pairs.append(shift(pairs[-1]))
        if step == 1:
            pairs[-1], (nears[1], bias) = tie(pairs[-1], (nears[1], bias))
            rests[1] = gather_rest(nears[1])
        if step == 2:
            pairs[-1], (rests[1], early) = tie(pairs[-1], (rests[1], early))
            ring[2], rests[1] = tie(ring[2], rests[1])
            nears[2] = gather_near(ring[2])
    ring[-1], pairs[-1] = tie(ring[-1], pairs[-1])
    last = shift(ring[-1][:block])
    pairs, nears[2] = tie(pairs, nears[2])
    rests[2] = gather_rest(nears[2])
    made = []
    for micro in range(micro_count):
        if micro == micro_count - 1:
            made, (rests[2], last) = tie(made, (rests[2], last))
            last_near = gather_near(last)
        made = attention_call(
            micro,
            micro_count,
            first_len[micro : micro + 1],
            queries,
            pairs,
            own_slots.reshape(rows, 1),
            key_slots[micro : micro + 1],
            bias,
            made,
        )
    context, probs, packed = made
    for step in range(3, shards - 1):
        ring[step], rests[step - 1] = tie(ring[step], rests[step - 1])
        nears[step] = gather_near(ring[step])
        rests[step] = gather_rest(nears[step])
    if shards > 4:
        context, rests[shards - 2] = tie(context, rests[shards - 2])
    last_piece, last = tie(ring[-1][block:], last)
    last_down = shift(last_piece)
    out_full, down_wide, cotangent_rows, gate_rows, gains, key_columns = early
    ffn_gain, delete_gain, delete_vec = gains

    hidden_mid, normed_two = mid_call(token_rows, context, out_full, ffn_gain, micro_count)
    normed_two, (last_near, last_down) = tie(normed_two, (last_near, last_down))
    last_rest = gather_rest(last_near)
    normed_two_other = swap(normed_two, 1)
    normed_two_other, (last_rest, last_down) = tie(normed_two_other, (last_rest, last_down))
    last_down_found = [(mask, 0, swap(last_down, 2 * mask)) for mask in range(1, chips)]
    pieces = [gate_up_own, down_wide]
    gate_up_moves = [(0, 0, block, inner, lambda at, chip_at: (pl.multiple_of(at * block, 16), 0))]
    down_moves = [
        (1, 0, down_half, padded, lambda at, chip_at: (pl.multiple_of(at * down_half, 16), 0))
    ]

    def gate_up_place(step, mask, row):
        return lambda at, chip_at: (
            pl.multiple_of((at - step) % shards * block + row, 16),
            pl.multiple_of((chip_at ^ mask) * col_piece, 128),
        )

    def down_place(step, mask, row, part):
        return lambda at, chip_at: (
            pl.multiple_of((at - step) % shards * down_half + (chip_at ^ mask) * down_piece + row, 16),
            part * col_piece,
        )

    arrived = [
        (step, 0, gather_list(ring[step], nears[step], rests[step])) for step in range(1, shards - 1)
    ]
    arrived.append((shards - 1, 0, gather_list(last, last_near, last_rest)))
    arrived.append((shards - 1, block, [(0, 0, last_down)] + last_down_found))
    for step, below, found in arrived:
        for mask, start, array in found:
            for part, here, there, size in overlaps(below + start, array.shape[0]):
                if part is None:
                    gate_up_moves.append(
                        (len(pieces), here, size, col_piece, gate_up_place(step, mask, there))
                    )
                else:
                    down_moves.append(
                        (
                            len(pieces),
                            here,
                            size,
                            part_columns(part),
                            down_place(step, mask, there, part),
                        )
                    )
            pieces.append(array)
    if not aligned:

        def put_together(moves, shape):
            whole = jnp.zeros(shape, BF16)
            for piece, row, size, columns, place in moves:
                value = pieces[piece][row : row + size, :columns]
                whole = lax.dynamic_update_slice(whole, value, place(rank, chip))
            return whole

        pieces = [
            put_together(gate_up_moves, (width, inner)),
            put_together(down_moves, (half_inner, padded)),
        ]
        gate_up_moves = [(0, 0, width, inner, lambda at, chip_at: (0, 0))]
        down_moves = [(1, 0, half_inner, padded, lambda at, chip_at: (0, 0))]
    gate_up_pieces, gate_up_moves = used_by(pieces, gate_up_moves)
    down_pieces, down_moves = used_by(pieces, down_moves)
    gate_slope_act, gate_act, inner_act, gate_up = gate_up_call(
        normed_two, normed_two_other, width, inner, gate_up_pieces, gate_up_moves
    )
    down_part, down_given, down = down_call(inner_act, width, padded, down_pieces, down_moves)
    hidden_out, deleted, grad_out, down_up, grad_delete_gain, grad_delete_vec = out_call(
        hidden_mid,
        down_part,
        swap(down_given, 1),
        cotangent_rows,
        gate_rows,
        delete_gain,
        delete_vec,
        micro_count,
    )

    down_up_other = swap(down_up, 1)

    def reduce_plan(size, piece_columns, place):
        middle = cut(size)
        spans = {"own": (0, size), "near": (0, size), "far": (0, size)}
        spans["top"], spans["low"] = (0, middle), (middle, size - middle)
        plan = []
        for base in bases:
            for name in used:
                start, count = spans[name]
                moves = [
                    (index, place(index, base ^ names[name], start)) for index in range(shards)
                ]
                plan.append(((shards, count, piece_columns), moves, base ^ names[name]))
        return plan

    def reduce_run(plan, left, right, picks, right_width, in_halves):
        if aligned:
            buffers = weight_grad_call(left, right, picks, right_width, plan, in_halves)
        else:
            shape = (sum(size for _, size in picks), right_width)
            whole = weight_grad_call(
                left, right, picks, right_width,
                [((1,) + shape, [(0, lambda at, chip_at: (0, 0))], 0)], False,
            )[0][0]
            buffers = []
            for (_, size, columns), moves, _ in plan:
                buffers.append(
                    jnp.stack(
                        [
                            lax.dynamic_slice(whole, place(rank, chip), (size, columns))
                            for _, place in moves
                        ]
                    )
                )
        return {
            base: dict(zip(used, buffers[i * len(used) : (i + 1) * len(used)]))
            for i, base in enumerate(bases)
        }

    def exchange(value):
        return lax.all_to_all(value, "shard", split_axis=0, concat_axis=0, tiled=True)

    def total_of(arrived):
        return jnp.sum(arrived.astype(F32), axis=0).astype(BF16)

    def down_grad_place(index, mask, start):
        plain = lambda at, chip_at: (
            index * down_half + (chip_at ^ mask) * down_piece + start,
            0,
        )
        return tile_hint(plain, 16, 128) if aligned else plain

    def gate_up_grads(first, size, left, right):
        def place(index, mask, start):
            plain = lambda at, chip_at: (index * size + start, (chip_at ^ mask) * col_piece)
            return tile_hint(plain, 16, 128) if aligned else plain

        return reduce_run(
            reduce_plan(size, col_piece, place),
            left,
            right,
            [(index * block + first, size) for index in range(shards)],
            inner,
            chips == 4 and half_inner % 256 == 0,
        )

    down_buffers = reduce_run(
        reduce_plan(down_piece, width, down_grad_place),
        (inner_act, None),
        (down_up, down_up_other),
        [(0, half_inner)],
        width,
        False,
    )
    down_state = reduce_begin(down_buffers, 1)
    gate_grad, up_grad = hidden_grad_call(down_up, down_up_other, down, gate_slope_act, gate_act)
    gate_grad, down_state = tie(gate_grad, down_state)
    down_state = reduce_middle(down_state, 1)
    normed_both = (normed_two, normed_two_other)
    gate_up_buffers = gate_up_grads(0, cut(block), normed_both, (gate_grad, up_grad))
    gate_grad, gate_up_buffers = tie(gate_grad, gate_up_buffers)
    normed_part, normed_given = normed_grad_call(gate_grad, up_grad, gate_up)
    normed_given, (down_state, gate_up_buffers) = tie(normed_given, (down_state, gate_up_buffers))
    gate_up_state = reduce_begin(gate_up_buffers, 1)
    down_arrived = exchange(reduce_end(down_state))
    normed_given = swap(normed_given, 1)
    grad_mid, context_grad, grad_w_out, grad_ffn_gain = back_call(
        normed_part,
        normed_given,
        grad_out,
        hidden_mid,
        ffn_gain,
        context,
        out_full,
        micro_count,
    )
    context_grad, gate_up_state = tie(context_grad, gate_up_state)
    gate_up_state = reduce_middle(gate_up_state, 1)
    score_grads, query_grad, pair_parts = attention_back_call(
        queries, context_grad, probs, packed, key_columns, shards
    )
    gate_grad, pair_parts = tie(gate_grad, pair_parts)
    pair_arrived = exchange(pair_parts)
    gate_up_buffers = gate_up_grads(
        cut(block), block - cut(block), normed_both, (gate_grad, up_grad)
    )
    gate_up_buffers, gate_up_state = tie(gate_up_buffers, gate_up_state)
    gate_up_later = reduce_begin(gate_up_buffers, 1)
    grad_bias_rows = bias_fold(score_grads, own_slots.reshape(rows))
    grad_bias = jnp.einsum("ob,ho->bh", onehot, grad_bias_rows, precision=HIGHEST)
    out_grads = grad_w_out.reshape(width, proj)
    gate_up_later, (grad_bias, out_grads) = tie(gate_up_later, (grad_bias, out_grads))
    gate_up_later = reduce_middle(gate_up_later, 1)
    pair_arrived, down_arrived = tie(pair_arrived, down_arrived)
    gate_up_arrived = exchange(reduce_end(gate_up_state))
    down_sum = total_of(down_arrived)
    pair_sum, grad_in, grad_attn_gain = in_call(
        query_grad,
        pair_arrived,
        attn_full,
        grad_mid,
        token_rows,
        attn_gain[None],
        micro_count,
    )
    pair_sum, gate_up_later = tie(pair_sum, gate_up_later)

    small = jnp.concatenate(
        [
            grad_attn_gain.reshape(shards, block),
            grad_ffn_gain.reshape(shards, block),
            grad_delete_gain.reshape(shards, block),
            grad_delete_vec.reshape(shards, block),
            grad_bias.reshape(shards, bucket_rows * heads),
        ],
        axis=1,
    ).astype(BF16)
    small = jnp.pad(small, ((0, 0), (0, pack_rows * proj - small.shape[1])))
    small = small.reshape(shards, pack_rows, proj)

    def attn_grad_place(mask, flip, index):
        def place(at, rep):
            owner = rep ^ (2 * mask + flip)
            row = index * block + part_row(owner % per_matrix)
            return owner // per_matrix, pl.multiple_of(row, 16) if aligned else row

        return place

    attn_plan = [
        (
            (chips, shards, attn_rows + pack_rows, proj),
            [
                ((mask, index), attn_grad_place(mask, flip, index), index)
                for mask in range(chips)
                for index in range(shards)
            ],
        )
        for flip in range(2)
    ]
    if aligned:
        kept, given = project_grad_call(
            normed_one, query_grad, pair_sum, out_grads, small, attn_plan
        )
    else:
        whole_plan = [
            (
                (4, width, proj),
                [((matrix,), lambda at, rep, matrix=matrix: (matrix, 0), None) for matrix in range(4)],
            )
        ]
        whole = project_grad_call(
            normed_one, query_grad, pair_sum, out_grads, small, whole_plan
        )[0]
        kept, given = [
            jnp.stack(
                [
                    jnp.concatenate(
                        [
                            lax.dynamic_slice(
                                whole, where(rank, rep_rank) + (0,), (1, attn_rows, proj)
                            )[0],
                            small[index],
                        ]
                    )
                    for _, where, index in items
                ]
            ).reshape(shape)
            for shape, items in attn_plan
        ]
    given = swap(given, 1)
    attn_own_sum = add(kept[0], given[0])
    attn_send = [add(kept[mask], given[mask]) for mask in range(1, chips)]
    attn_found = [swap(part, 2 * mask + 2) for mask, part in enumerate(attn_send)]
    gate_up_rest = exchange(reduce_end(gate_up_later))
    attn_found, gate_up_rest = tie(attn_found, gate_up_rest)
    attn_sum = add(attn_own_sum, *attn_found)
    attn_sum = total_of(exchange(attn_sum))
    gate_up_sum = jnp.concatenate([total_of(gate_up_arrived), total_of(gate_up_rest)])
    total = attn_sum[attn_rows:].astype(F32).reshape(-1)
    attn_sum = attn_sum[:attn_rows]

    packed_sum = pack(gate_up_sum, down_sum)
    near = gather_near(packed_sum)
    attn_sum, near = tie(attn_sum, near)
    rest = gather_rest(near)
    attn_half = [attn_sum] + [swap(attn_sum, 2 * mask) for mask in range(1, chips)]
    bounds = [0, block, 2 * block, 3 * block, 4 * block, 4 * block + bucket_rows * heads]
    totals = [total[low:high] for low, high in zip(bounds, bounds[1:])]
    totals[4] = totals[4].reshape(bucket_rows, heads)
    attn_half, (rest, totals) = tie(attn_half, (rest, totals))
    found = gather_list(packed_sum, near, rest)
    pieces, gate_up_moves, down_moves = [], [], []

    def gate_up_to(flip, mask, row):
        return lambda core_at, chip_at: (
            core_at ^ flip,
            row,
            pl.multiple_of((chip_at ^ mask) * col_piece, 128),
        )

    def down_to(flip, mask, row, part):
        return lambda core_at, chip_at: (
            pl.multiple_of((core_at ^ flip) * down_half + (chip_at ^ mask) * down_piece + row, 16),
            part * col_piece,
        )

    for flip in range(2):
        for mask, start, array in found:
            array = swap(array, 1) if flip else array
            for part, here, there, size in overlaps(start, array.shape[0]):
                if part is None:
                    gate_up_moves.append(
                        (len(pieces), here, size, col_piece, gate_up_to(flip, mask, there))
                    )
                else:
                    down_moves.append(
                        (
                            len(pieces),
                            here,
                            size,
                            part_columns(part),
                            down_to(flip, mask, there, part),
                        )
                    )
            pieces.append(array)
    if aligned:
        grad_gate, grad_up, grad_down_out = finish_call(
            pieces, gate_up_moves, down_moves, block, inner, down_block, width, padded
        )
        grad_down_out = grad_down_out.T
    else:
        halves = jnp.zeros((2, block, inner), BF16)
        for piece, row, size, columns, place in gate_up_moves:
            value = pieces[piece][None, row : row + size, :columns]
            halves = lax.dynamic_update_slice(halves, value, place(core, chip))
        whole = jnp.zeros((down_block, padded), BF16)
        for piece, row, size, columns, place in down_moves:
            value = pieces[piece][row : row + size, :columns]
            whole = lax.dynamic_update_slice(whole, value, place(core, chip))
        grad_gate, grad_up = spread_columns(halves[0], halves[1])
        grad_down_out = whole[:, :width].astype(F32)

    attn_half = jnp.stack(attn_half)
    attn_found = [attn_half, swap(attn_half, 1)]

    def attn_to(mask, flip):
        def place(rep):
            owner = rep ^ (2 * mask + flip)
            row = part_row(owner % per_matrix)
            return owner // per_matrix, pl.multiple_of(row, 16) if aligned else row

        return place

    attn_moves = [(flip, mask, attn_to(mask, flip)) for flip in range(2) for mask in range(chips)]
    if aligned:
        attn_moves = [
            (flip, mask, split_place(place, flip)) for flip, mask, place in attn_moves
        ]
        attn_shard = attn_finish_call(attn_found, attn_moves, block, proj)
    else:
        attn_shard = jnp.zeros((4, block, proj), BF16)
        for piece, index, place in attn_moves:
            attn_shard = lax.dynamic_update_slice(
                attn_shard, attn_found[piece][index][None], place(rep_rank) + (0,)
            )
        attn_shard = attn_shard.astype(F32)

    return (
        jnp.swapaxes(hidden_out, 1, 2),
        deleted.reshape(micro_count, local_rows),
        jnp.swapaxes(grad_in, 1, 2),
        totals[0],
        attn_shard[0],
        attn_shard[1],
        attn_shard[2],
        attn_shard[3].reshape(proj // shards, width),
        totals[4],
        totals[1],
        grad_gate,
        grad_up,
        grad_down_out,
        totals[2],
        totals[3],
    )


def used_by(pieces, moves):
    wanted = sorted({move[0] for move in moves})
    return [pieces[i] for i in wanted], [(wanted.index(move[0]),) + move[1:] for move in moves]


def tile_hint(place, row_unit, column_unit):
    def hinted(at, chip_at):
        row, column = place(at, chip_at)
        return pl.multiple_of(row, row_unit), pl.multiple_of(column, column_unit)

    return hinted


def solution(mesh):
    rows = P(None, ("rep", "shard"), None)
    flat = P(None, ("rep", "shard"))
    by_rep = P(None, "rep", None)
    vector = P("shard")
    matrix = P("shard", None)
    in_specs = (
        (rows, rows, flat, by_rep, by_rep, P(), vector)
        + (matrix,) * 5
        + (vector,)
        + (matrix,) * 3
        + (vector, vector)
    )
    out_specs = (
        (rows, flat, rows, vector) + (matrix,) * 5 + (vector,) + (matrix,) * 3 + (vector, vector)
    )
    return jax.shard_map(
        on_device, mesh=mesh, in_specs=in_specs, out_specs=out_specs, check_vma=False
    )
```
